32 devices in a mesh: dp: 8 (over z, x), fsdp: 4 (over y, core).
Axes of the slice: x: 2, y: 2, z: 4, core: 2. Of those that a mesh axis runs over, the one named last changes fastest.
Arguments:
- tokens: bfloat16 [2, 4096, 2048], P(None, ('dp', 'fsdp')), may hold values from -6 to 6
- membership: int32 [8, 2, 16], P('dp'), may hold values from 0 to 4, as said below
- d_output: bfloat16 [2, 4096, 2048], P(None, ('dp', 'fsdp')), may hold values from -6 to 6
- gain_attn: bfloat16 [2048], P(('dp', 'fsdp')), may hold values from 0.25 to 1.75
- w_qa: bfloat16 [2048, 1024], P(('dp', 'fsdp')), may hold values from -0.125 to 0.125
- gain_latent: bfloat16 [1024], P(('dp', 'fsdp')), may hold values from 0.25 to 1.75
- w_qb: bfloat16 [1024, 4096], P('dp', 'fsdp'), may hold values from -0.1875 to 0.1875
- w_key: bfloat16 [2048, 256], P(('dp', 'fsdp')), may hold values from -0.125 to 0.125
- w_value: bfloat16 [2048, 256], P(('dp', 'fsdp')), may hold values from -0.125 to 0.125
- w_out: bfloat16 [2048, 4096], P('dp', 'fsdp'), may hold values from -0.5 to 0.5
- gain_ffn: bfloat16 [2048], P(('dp', 'fsdp')), may hold values from 0.25 to 1.75
- w_gate: bfloat16 [2048, 5632], P('dp', 'fsdp'), may hold values from -0.125 to 0.125
- w_up: bfloat16 [2048, 5632], P('dp', 'fsdp'), may hold values from -0.125 to 0.125
- w_down: bfloat16 [2048, 5632], P('dp', 'fsdp'), may hold values from -0.078125 to 0.078125
Outputs:
- output: bfloat16 [2, 4096, 2048], P(None, ('dp', 'fsdp'))
- input_grad: bfloat16 [2, 4096, 2048], P(None, ('dp', 'fsdp'))
- grad_gain_attn: float32 [2048], P(('dp', 'fsdp'))
- grad_w_qa: float32 [2048, 1024], P(('dp', 'fsdp'))
- grad_gain_latent: float32 [1024], P(('dp', 'fsdp'))
- grad_w_qb: float32 [1024, 4096], P('dp', 'fsdp')
- grad_w_key: float32 [2048, 256], P(('dp', 'fsdp'))
- grad_w_value: float32 [2048, 256], P(('dp', 'fsdp'))
- grad_w_out: float32 [2048, 4096], P('dp', 'fsdp')
- grad_gain_ffn: float32 [2048], P(('dp', 'fsdp'))
- grad_w_gate: float32 [2048, 5632], P('dp', 'fsdp')
- grad_w_up: float32 [2048, 5632], P('dp', 'fsdp')
- grad_w_down: float32 [2048, 5632], P('dp', 'fsdp')
The draws below stay inside these ranges and needn't reach their ends.
Inputs may be any that keep to these rules, and one draw needn't show every extreme that they name: `membership`: in each group's row the first 8 entries are 0 (the prompt); the last 8 entries name continuations 1 to 4 in increasing order, each a run of whole blocks; the runs have 4, 2, 1 and 1 blocks, in an order drawn for each group.
All inputs are finite; a program needn't handle non-finite values.
Results may differ from the reference program's by a relative error of at most 0.02.
Values may be sent and summed in bfloat16 or wider, within the bound.
A program may use at most 192 MiB of HBM per device.

```python
import jax
import jax.numpy as jnp
from jax import lax

D = 2048
QR = 1024
H = 16
HD = 256
FF = 5632
MICRO = 2
BLK = 32
CBLK = 8
GTOK = 512
NBLK = 16
N_DP = 8


def draw_membership(key, part):
    group_keys = jax.random.split(key, N_DP * MICRO)
    run_lengths = jnp.array([4, 2, 1, 1], jnp.int32)

    def one_group(group_key):
        shuffled = jax.random.permutation(group_key, run_lengths)
        run_ends = jnp.cumsum(shuffled)
        block_ids = jnp.arange(CBLK, dtype=jnp.int32)
        labels = 1 + jnp.sum((block_ids[:, None] >= run_ends[None, :3]).astype(jnp.int32), axis=1)
        return jnp.concatenate([jnp.zeros((NBLK - CBLK,), jnp.int32), labels.astype(jnp.int32)])
    return jax.vmap(one_group)(group_keys).reshape(N_DP, MICRO, NBLK)


def block_scale(rng, dims, cuts, low, top_value):
    level = 1.0
    for position, shards_of in cuts:
        draws = jax.random.uniform(jax.random.fold_in(jax.random.fold_in(rng, 6), position), (shards_of,), jnp.float32, low / len(cuts), top_value / len(cuts))
        level = level * jnp.repeat(jnp.exp(draws), dims[position] // shards_of).reshape((-1,) + (1,) * (len(dims) - 1 - position))
    return level


def normal_values(stream_key, shape, scale, bound, cuts=(), held_as=jnp.bfloat16):
    values = jax.random.normal(stream_key, shape, jnp.float32) * scale
    if len(cuts) > 0:
        values = block_scale(stream_key, shape, cuts, -0.22, 0.18) * values
    return jnp.clip(values, min=-bound, max=bound).astype(held_as)


def setup_inputs(seed: int = 0) -> dict:
    seeds = jax.random.split(jax.random.key(seed), 15)
    tokens = normal_values(seeds[0], (MICRO, N_DP * GTOK, D), 1.0, 6.0, ((1, 32),))
    membership = draw_membership(jax.random.fold_in(seeds[14], 71), 0)
    d_output = normal_values(seeds[2], (MICRO, N_DP * GTOK, D), 1.0, 6.0, ((1, 32),))
    gain_attn = jnp.clip(1.0 + 0.15 * jax.random.normal(seeds[3], (D,), jnp.float32), 0.25, 1.75).astype(jnp.bfloat16)
    w_qa = normal_values(seeds[4], (D, QR), D ** -0.5, 0.125, ((0, 32),))
    gain_latent = jnp.clip(1.0 + 0.15 * jax.random.normal(seeds[5], (QR,), jnp.float32), 0.25, 1.75).astype(jnp.bfloat16)
    w_qb = normal_values(seeds[6], (QR, H * HD), QR ** -0.5, 0.1875, ((0, 8), (1, 4)))
    w_key = normal_values(seeds[7], (D, HD), D ** -0.5, 0.125, ((0, 32),))
    w_value = normal_values(seeds[8], (D, HD), D ** -0.5, 0.125, ((0, 32),))
    w_out = normal_values(seeds[9], (D, H * HD), (H * HD * 16 // GTOK) ** -0.5, 0.5, ((0, 8), (1, 4)))
    gain_ffn = jnp.clip(1.0 + 0.15 * jax.random.normal(seeds[10], (D,), jnp.float32), 0.25, 1.75).astype(jnp.bfloat16)
    w_gate = normal_values(seeds[11], (D, FF), D ** -0.5, 0.125, ((0, 8), (1, 4)))
    w_up = normal_values(seeds[12], (D, FF), D ** -0.5, 0.125, ((0, 8), (1, 4)))
    w_down = normal_values(seeds[13], (D, FF), FF ** -0.5, 0.078125, ((0, 8), (1, 4)))
    return {"tokens": tokens, "membership": membership, "d_output": d_output, "gain_attn": gain_attn, "w_qa": w_qa, "gain_latent": gain_latent, "w_qb": w_qb, "w_key": w_key, "w_value": w_value, "w_out": w_out, "gain_ffn": gain_ffn, "w_gate": w_gate, "w_up": w_up, "w_down": w_down}


EPSILON = 1e-05
ROPE_BASE = 10000.0
MASK_FILL = -1e+30

@jax.custom_vjp
def low(v):
    return lax.optimization_barrier(v.astype(jnp.bfloat16)).astype(jnp.float32)

@jax.custom_vjp
def low_back(v):
    return v

def low_keep(v):
    return (low(v), None)

def low_pass(kept, grad):
    return (grad,)

def back_keep(v):
    return (v, None)

def back_low(kept, grad):
    return (low(grad),)
low.defvjp(low_keep, low_pass)
low_back.defvjp(back_keep, back_low)

def precise(left, right):
    return jnp.dot(left, right, precision=lax.Precision.HIGHEST, preferred_element_type=jnp.float32)

def rms_norm(values, gain):
    return values * lax.rsqrt(lax.optimization_barrier(jnp.mean(values * values, axis=-1, keepdims=True)) + EPSILON) * gain

def layout(member_row, block_len):
    count_blocks = member_row.shape[0]
    block_ids = jnp.arange(count_blocks, dtype=jnp.int32)
    same_run = (member_row[None, :] == member_row[:, None]) & (block_ids[None, :] < block_ids[:, None])
    earlier = lax.optimization_barrier(jnp.sum(same_run.astype(jnp.int32), axis=1))
    prompt_len = jnp.sum((member_row == 0).astype(jnp.int32)) * block_len
    labels = jnp.repeat(member_row, block_len)
    within = jnp.arange(count_blocks * block_len, dtype=jnp.int32) % block_len
    positions = (labels > 0).astype(jnp.int32) * prompt_len + jnp.repeat(earlier, block_len) * block_len + within
    return (labels, positions)

def rope_tables(positions, head_width):
    half_width = head_width // 2
    frequency = ROPE_BASE ** (-(jnp.arange(half_width, dtype=jnp.float32) * (2.0 / head_width)))
    angles = positions.astype(jnp.float32)[:, None] * frequency[None, :]
    return (jnp.cos(angles), jnp.sin(angles))

def rotate(vector, cos_tab, sin_tab):
    half_width = vector.shape[-1] // 2
    lower_half = vector[..., :half_width]
    upper_half = vector[..., half_width:]
    return jnp.concatenate([lower_half * cos_tab - upper_half * sin_tab, upper_half * cos_tab + lower_half * sin_tab], axis=-1)

def group_forward(inputs, gain_attn, w_qa, gain_latent, w_qb, w_key, w_value, w_out, gain_ffn, w_gate, w_up, w_down, labels, positions):
    group_len = inputs.shape[0]
    cos_tab, sin_tab = rope_tables(positions, HD)
    normed = low(rms_norm(inputs, gain_attn))
    latent = low_back(precise(normed, w_qa))
    latent_n = low(rms_norm(latent, gain_latent))
    keys_all = low(rotate(low_back(precise(normed, w_key)), cos_tab, sin_tab))
    values_all = low(low_back(precise(normed, w_value)))
    queries = low_back(precise(latent_n, w_qb)).reshape(group_len, H, HD)
    queries = low(rotate(queries, cos_tab[:, None, :], sin_tab[:, None, :]))
    q_block = min(256, group_len)
    n_blocks = group_len // q_block
    key_index = jnp.arange(group_len, dtype=jnp.int32)

    def attend(block_items):
        query_part, label_part, index_part = block_items
        scores = jnp.einsum('qhd,kd->qhk', query_part, keys_all, precision=lax.Precision.HIGHEST) * HD ** (-0.5)
        scores = low_back(scores)
        allowed = (key_index[None, :] <= index_part[:, None]) & ((labels[None, :] == 0) | (labels[None, :] == label_part[:, None]))
        scores = jnp.where(allowed[:, None, :], scores, MASK_FILL)
        attn_probs = low(jax.nn.softmax(scores, axis=-1))
        return jnp.einsum('qhk,kd->qhd', attn_probs, values_all, precision=lax.Precision.HIGHEST)
    mixed_rows = lax.map(jax.checkpoint(attend), (queries.reshape(n_blocks, q_block, H, HD), labels.reshape(n_blocks, q_block), key_index.reshape(n_blocks, q_block)))
    mixed_rows = low(low_back(mixed_rows.reshape(group_len, H * HD)))
    attn_out = low_back(jnp.dot(mixed_rows, w_out.T, precision=lax.Precision.HIGHEST, preferred_element_type=jnp.float32))
    middle = inputs + attn_out
    normed_two = low(rms_norm(middle, gain_ffn))
    gate_pre = low_back(precise(normed_two, w_gate))
    up_pre = low_back(precise(normed_two, w_up))
    hidden = low(jax.nn.silu(gate_pre) * up_pre)
    ffn_out = low_back(jnp.dot(hidden, w_down.T, precision=lax.Precision.HIGHEST, preferred_element_type=jnp.float32))
    return middle + ffn_out

def reference(tokens, membership, d_output, gain_attn, w_qa, gain_latent, w_qb, w_key, w_value, w_out, gain_ffn, w_gate, w_up, w_down):
    weights = tuple((weight.astype(jnp.float32) for weight in (gain_attn, w_qa, gain_latent, w_qb, w_key, w_value, w_out, gain_ffn, w_gate, w_up, w_down)))
    groups_here = MICRO * N_DP
    inputs = tokens.reshape(groups_here, GTOK, D)
    cotangent = d_output.reshape(groups_here, GTOK, D)
    members = jnp.transpose(membership, (1, 0, 2)).reshape(groups_here, NBLK)

    def group_step(carried, group_item):
        part_in, part_cot, member_row = group_item
        labels, positions = layout(member_row, BLK)

        def forward(values, p_ga, p_qa, p_gl, p_qb, p_key, p_value, p_out, p_gf, p_gate, p_up, p_down):
            return group_forward(values, p_ga, p_qa, p_gl, p_qb, p_key, p_value, p_out, p_gf, p_gate, p_up, p_down, labels, positions)
        result, pullback = jax.vjp(forward, part_in.astype(jnp.float32), weights[0], weights[1], weights[2], weights[3], weights[4], weights[5], weights[6], weights[7], weights[8], weights[9], weights[10])
        gradients = pullback(part_cot.astype(jnp.float32))
        carried = tuple((running + latest for running, latest in zip(carried, gradients[1:])))
        return (carried, (result.astype(jnp.bfloat16), gradients[0].astype(jnp.bfloat16)))
    zero_sums = tuple((jnp.zeros(weight.shape, jnp.float32) for weight in weights))
    totals, (outputs, input_grads) = lax.scan(group_step, zero_sums, (inputs, cotangent, members))
    return (outputs.reshape(tokens.shape), input_grads.reshape(tokens.shape), totals[0], totals[1], totals[2], totals[3], totals[4], totals[5], totals[6], totals[7], totals[8], totals[9], totals[10])
```

```python
import functools

import jax
import jax.numpy as jnp
from jax import lax
from jax.experimental import pallas as pl
from jax.experimental.pallas import tpu as pltpu
from jax.sharding import PartitionSpec as P

BLK = 32
PROMPT = 256
EPSILON = 1e-05
ROPE_BASE = 10000.0
MASK_FILL = -1e30
F32 = jnp.float32
BF16 = jnp.bfloat16
MESH = pl.DeviceIdType.MESH
ANY = pl.BlockSpec(memory_space=pl.ANY)
VMEM = pl.BlockSpec(memory_space=pltpu.VMEM)
NF = 4


def layout(member_row, block_len):
    count_blocks = member_row.shape[0]
    block_ids = jnp.arange(count_blocks, dtype=jnp.int32)
    same_run = (member_row[None, :] == member_row[:, None]) & (
        block_ids[None, :] < block_ids[:, None]
    )
    earlier = jnp.sum(same_run.astype(jnp.int32), axis=1)
    prompt_len = jnp.sum((member_row == 0).astype(jnp.int32)) * block_len
    labels = jnp.repeat(member_row, block_len)
    within = jnp.arange(count_blocks * block_len, dtype=jnp.int32) % block_len
    positions = (
        (labels > 0).astype(jnp.int32) * prompt_len
        + jnp.repeat(earlier, block_len) * block_len
        + within
    )
    return (labels, positions)


def rope_tables(positions, head_width):
    half_width = head_width // 2
    frequency = ROPE_BASE ** (-(jnp.arange(half_width, dtype=jnp.float32) * (2.0 / head_width)))
    angles = positions.astype(jnp.float32)[:, None] * frequency[None, :]
    return (jnp.cos(angles), jnp.sin(angles))


def al(x, n):
    return pl.multiple_of(x, n)


def mm(a, b):
    return lax.dot_general(a, b, (((1,), (0,)), ((), ())), preferred_element_type=F32)


def mm_nt(a, b):
    return lax.dot_general(a, b, (((1,), (1,)), ((), ())), preferred_element_type=F32)


def mm_tn(a, b):
    return lax.dot_general(a, b, (((0,), (0,)), ((), ())), preferred_element_type=F32)


class Place:
    def __init__(self, ndp):
        self.ndp = ndp
        self.nz = ndp // 2
        self.me = lax.axis_index("dp")
        self.f = lax.axis_index("fsdp")
        self.z = self.me // 2
        self.x = self.me % 2
        self.pair = self.z * 2 + 1 - self.x
        y, c = self.f // 2, self.f % 2
        self.f_core = y * 2 + 1 - c
        self.f_y = (1 - y) * 2 + c
        self.f_yc = (1 - y) * 2 + 1 - c
        self.to_pair = (self.pair, self.f)
        self.to_core = (self.me, self.f_core)
        self.to_y = (self.me, self.f_y)

    def zidx(self, k):
        return lax.rem(self.z + k + self.nz, self.nz)

    def to_z(self, k):
        return (self.zidx(k) * 2 + self.x, self.f)

    def barrier(self, fsdp=True):
        bar = pltpu.get_barrier_semaphore()
        count = self.nz
        devs = [self.to_pair] + [self.to_z(k) for k in range(1, self.nz)]
        if fsdp:
            devs += [self.to_core, self.to_y]
            count += 2
        for d in devs:
            pl.semaphore_signal(bar, inc=1, device_id=d, device_id_type=MESH)
        pl.semaphore_wait(bar, count)


def rcopy(src, dst, ss, rs, dev):
    return pltpu.make_async_remote_copy(
        src_ref=src, dst_ref=dst, send_sem=ss, recv_sem=rs, device_id=dev, device_id_type=MESH
    )


class DpGather:
    def __init__(self, pos, items, zs, zr, xs, xr):
        self.p, self.items = pos, items
        self.zs, self.zr, self.xs, self.xr = zs, zr, xs, xr

    def zcopy(self, i, k):
        src, dst = self.items[i]
        return rcopy(
            src, dst(self.p.me), self.zs.at[i, k - 1], self.zr.at[i, k - 1], self.p.to_z(k)
        )

    def zarrive(self, i, k):
        src, dst = self.items[i]
        j = self.p.zidx(-k) * 2 + self.p.x
        return rcopy(src, dst(j), self.zs.at[i, k - 1], self.zr.at[i, k - 1], self.p.to_z(-k))

    def xcopy(self, i, k):
        src, dst = self.items[i]
        j = self.p.zidx(-k) * 2 + self.p.x
        return rcopy(
            src if k == 0 else dst(j), dst(j), self.xs.at[i, k], self.xr.at[i, k], self.p.to_pair
        )

    def xarrive(self, i, k):
        src, dst = self.items[i]
        j = self.p.zidx(-k) * 2 + 1 - self.p.x
        return rcopy(src, dst(j), self.xs.at[i, k], self.xr.at[i, k], self.p.to_pair)

    def start_z(self, i):
        for k in range(1, self.p.nz):
            self.zcopy(i, k).start()

    def start_x(self, i):
        self.xcopy(i, 0).start()

    def forward(self, i, k):
        self.zarrive(i, k).wait_recv()
        self.xcopy(i, k).start()

    def wait_x(self, i):
        for k in range(self.p.nz):
            self.xarrive(i, k).wait_recv()

    def wait_sends(self, i):
        for k in range(self.p.nz):
            self.xcopy(i, k).wait_send()
        for k in range(1, self.p.nz):
            self.zcopy(i, k).wait_send()


class FsGather:
    def __init__(self, pos, blocks, ss, rs):
        self.p, self.b, self.ss, self.rs = pos, blocks, ss, rs

    def copy(self, n, fb, dev):
        return rcopy(self.b(fb), self.b(fb), self.ss.at[n], self.rs.at[n], dev)

    def start(self):
        self.copy(1, self.p.f, self.p.to_y).start()
        self.copy(0, self.p.f, self.p.to_core).start()

    def mid(self):
        self.copy(1, self.p.f_y, self.p.to_y).wait_recv()
        self.copy(2, self.p.f_y, self.p.to_core).start()

    def end(self):
        self.copy(0, self.p.f_core, self.p.to_core).wait_recv()
        self.copy(2, self.p.f_yc, self.p.to_core).wait_recv()

    def wait_sends(self):
        self.copy(1, self.p.f, self.p.to_y).wait_send()
        self.copy(0, self.p.f, self.p.to_core).wait_send()
        self.copy(2, self.p.f_y, self.p.to_core).wait_send()


class FsReduce:
    def __init__(self, pos, blocks, from_core, from_y, ss, rs):
        self.p, self.b, self.fc, self.fy, self.ss, self.rs = pos, blocks, from_core, from_y, ss, rs

    def c1(self):
        return rcopy(
            self.b(self.p.f_yc), self.fc.at[1], self.ss.at[1], self.rs.at[1], self.p.to_core
        )

    def c0(self):
        return rcopy(
            self.b(self.p.f_core), self.fc.at[0], self.ss.at[0], self.rs.at[0], self.p.to_core
        )

    def cy(self):
        return rcopy(self.fc.at[1], self.fy, self.ss.at[2], self.rs.at[2], self.p.to_y)

    def start(self):
        self.c1().start()
        self.c0().start()

    def mid(self, rows, tile=64):
        self.c1().wait_recv()
        mine = self.b(self.p.f_y)

        def add(t, _):
            r = pl.ds(al(t * tile, tile), tile)
            self.fc[1, r, :] = (self.fc[1, r, :].astype(F32) + mine[r, :].astype(F32)).astype(BF16)
            return 0

        lax.fori_loop(0, rows // tile, add, 0)
        self.cy().start()

    def end(self):
        self.c0().wait_recv()
        self.cy().wait_recv()

    def value(self, r):
        return (
            self.b(self.p.f)[r, :].astype(F32)
            + self.fc[0, r, :].astype(F32)
            + self.fy[r, :].astype(F32)
        )

    def wait_sends(self):
        self.c1().wait_send()
        self.c0().wait_send()
        self.cy().wait_send()


def softmax_parts(scores):
    top = jnp.max(scores, axis=-1, keepdims=True)
    lifted = jnp.exp(scores - top)
    return lifted / jnp.sum(lifted, axis=-1, keepdims=True)


def causal_bias(rows):
    r = lax.broadcasted_iota(jnp.int32, (rows, rows), 0)
    c = lax.broadcasted_iota(jnp.int32, (rows, rows), 1)
    return jnp.where(c <= r, 0.0, MASK_FILL).astype(F32)


def group_rows(ref, m, half, cols, own):
    t = own // 2
    first = ref[pl.ds((2 * half) * own + m * t, t), cols]
    second = ref[pl.ds((2 * half + 1) * own + m * t, t), cols]
    return jnp.concatenate([first, second], axis=0)


def put_rows(ref, m, half, cols, own, value):
    t = own // 2
    ref[pl.ds((2 * half) * own + m * t, t), cols] = value[:t]
    ref[pl.ds((2 * half + 1) * own + m * t, t), cols] = value[t:]


def forward_kernel(
    cfg,
    tok,
    dout,
    cos,
    sin,
    bias,
    seq_sh,
    gain_sh,
    qb_sh,
    out_sh,
    gate_sh,
    up_sh,
    down_sh,
    qb_all,
    out_all,
    gate_all,
    up_all,
    down_all,
    seq_all,
    gain_sum,
    lkv_o,
    q_o,
    mixed_o,
    latent_o,
    normed_o,
    middle_o,
    n2_o,
    d_o,
    seq_v,
    gain_v,
    qb_v,
    out_v,
    lkv_v,
    q_v,
    mixed_v,
    part_v,
    fcore_v,
    fy_v,
    n2_v,
    d_v,
    lat_v,
    zs,
    zr,
    xs,
    xr,
    fss,
    frs,
    sys_,
    syr,
    ls,
):
    ndp, own, dim, rank, hd, heads = cfg
    rows = NF * own
    p = Place(ndp)
    kvw = rank + 2 * hd
    sr = seq_sh.shape[0]
    items = []

    def add_item(src, dst):
        items.append((src, dst))
        return len(items) - 1

    i_seq = add_item(seq_sh, lambda j: seq_v.at[pl.ds(al((j * NF + p.f) * sr, sr), sr)])
    i_gain = add_item(gain_sh, lambda j: gain_v.at[j * NF + p.f])

    def weight_items(src, dst, pieces):
        n = src.shape[0]
        step = n // pieces
        return [
            add_item(
                src.at[pl.ds(c * step, step)],
                lambda j, c=c: dst.at[pl.ds(al(j * n + c * step, step), step)],
            )
            for c in range(pieces)
        ]

    i_qb = weight_items(qb_sh, qb_v, 1)
    i_out = weight_items(out_sh, out_v, 2)
    i_ffn = []
    for s, d in ((gate_sh, gate_all), (up_sh, up_all), (down_sh, down_all)):
        i_ffn += weight_items(s, d, 2)
    order = [i_seq, i_gain] + i_qb + i_out + i_ffn
    g = DpGather(p, items, zs, zr, xs, xr)
    fs_d = FsGather(p, lambda b: d_v.at[pl.ds(al(b * own, own), own)], fss.at[0], frs.at[0])
    fs_l = FsGather(p, lambda b: lkv_v.at[pl.ds(al(b * own, own), own)], fss.at[1], frs.at[1])
    fs_n = FsGather(p, lambda b: n2_v.at[pl.ds(al(b * own, own), own)], fss.at[2], frs.at[2])
    red = FsReduce(
        p, lambda b: part_v.at[pl.ds(al(b * own, own), own)], fcore_v, fy_v, fss.at[3], frs.at[3]
    )

    local = []

    def local_copy(src, dst):
        c = pltpu.make_async_copy(src, dst, ls.at[len(local)])
        c.start()
        local.append(c)
        return c

    own_copies = {}
    for i in order:
        src, dst = items[i]
        own_copies[i] = local_copy(src, dst(p.me))
    d_copies = [
        local_copy(dout.at[m], d_v.at[pl.ds(al(p.f * own + m * (own // 2), 128), own // 2)])
        for m in range(2)
    ]

    p.barrier()
    g.start_x(i_seq)
    g.start_x(i_gain)
    g.start_x(i_qb[0])
    for i in order:
        g.start_z(i)
    npiece = ndp

    def seq_piece(j, fb):
        return seq_v.at[pl.ds(al((j * NF + fb) * sr, sr), sr)]

    def seq_copy(t, j, fb, dev, which):
        b = seq_piece(j, fb) if which == 0 else gain_v.at[j * NF + fb]
        return rcopy(b, b, sys_.at[which, t, j], syr.at[which, t, j], dev)

    def spread(j):
        for which in (0, 1):
            seq_copy(1, j, p.f, p.to_y, which).start()
            seq_copy(0, j, p.f, p.to_core, which).start()

    for m in range(2):
        x = tok[m].astype(F32)
        inv = lax.rsqrt(jnp.mean(x * x, axis=-1, keepdims=True) + EPSILON)
        middle_o[pl.ds(m * (own // 2), own // 2), :] = x * inv
    own_copies[i_seq].wait()
    own_copies[i_gain].wait()
    spread(p.me)
    queue = order[2:]
    lead = [1]

    def more_x():
        if lead[0] < len(queue):
            g.start_x(queue[lead[0]])
            lead[0] += 1

    for k in range(1, p.nz):
        for i in (i_seq, i_gain):
            g.forward(i, k)
        spread(p.zidx(-k) * 2 + p.x)
    more_x()
    for k in range(p.nz):
        for i in (i_seq, i_gain):
            g.xarrive(i, k).wait_recv()
        spread(p.zidx(-k) * 2 + 1 - p.x)
    for c in d_copies:
        c.wait()

    def spread_forward(j, _):
        for which in (0, 1):
            seq_copy(1, j, p.f_y, p.to_y, which).wait_recv()
            seq_copy(2, j, p.f_y, p.to_core, which).start()
        return 0

    events = [(i, k) for i in queue for k in range(1, p.nz)]
    done = [0]

    def tick(n):
        for _ in range(n):
            if done[0] >= len(events):
                return
            i, k = events[done[0]]
            if k == 1:
                more_x()
            g.forward(i, k)
            done[0] += 1

    tick(p.nz - 1)
    lax.fori_loop(0, npiece, spread_forward, 0)
    fs_d.start()
    tick(p.nz - 1)

    def spread_end(j, _):
        for which in (0, 1):
            seq_copy(0, j, p.f_core, p.to_core, which).wait_recv()
            seq_copy(2, j, p.f_yc, p.to_core, which).wait_recv()
        return 0

    lax.fori_loop(0, npiece, spread_end, 0)

    def gain_add(j, acc):
        return acc + gain_v[j]

    gains = lax.fori_loop(0, ndp * NF, gain_add, jnp.zeros(gain_v.shape[1:], F32))
    gain_sum[...] = gains
    wide = dim // rank
    gain_one = jnp.concatenate([gains[r : r + 1] for r in range(wide)], axis=1)
    gain_two = jnp.concatenate([gains[wide + r : wide + r + 1] for r in range(wide)], axis=1)
    gain_lat = gains[2 * wide : 2 * wide + 1]
    normed_o[...] = (middle_o[...] * gain_one).astype(BF16)
    seq_out = local_copy(seq_v, seq_all)

    def project(j, _):
        cols = pl.ds(al(j * 256, 256), 256)
        lat_v[:, cols] = mm(normed_o[...], seq_v[:, cols])
        return 0

    lax.fori_loop(0, kvw // 256, project, 0)
    own_rows = pl.ds(al(p.f * own, own), own)
    lat = lat_v[:, :rank]
    latent_o[...] = lat
    inv_lat = lax.rsqrt(jnp.mean(lat * lat, axis=-1, keepdims=True) + EPSILON)
    lkv_v[own_rows, :rank] = (lat * inv_lat * gain_lat).astype(BF16)
    half = hd // 2
    co, si = cos[own_rows, :], sin[own_rows, :]
    ka, kb = lat_v[:, rank : rank + half], lat_v[:, rank + half : rank + hd]
    lkv_v[own_rows, rank : rank + half] = (ka * co - kb * si).astype(BF16)
    lkv_v[own_rows, rank + half : rank + hd] = (kb * co + ka * si).astype(BF16)
    lkv_v[own_rows, rank + hd :] = lat_v[:, rank + hd :].astype(BF16)
    fs_l.start()
    tick(p.nz - 1)
    fs_d.mid()
    fs_l.mid()
    tick(p.nz - 1)
    for i in i_qb:
        own_copies[i].wait()
        g.wait_x(i)
    fs_l.end()
    qb_out = local_copy(qb_v, qb_all)
    lkv_out = local_copy(lkv_v, lkv_o)

    def query(j, _):
        cols = pl.ds(al(j * hd, hd), hd)
        c0 = pl.ds(al(j * hd, half), half)
        c1 = pl.ds(al(j * hd + half, half), half)
        for r in range(rows // 512):
            rr = pl.ds(r * 512, 512)
            acc = mm(lkv_v[rr, :rank], qb_v[:, cols])
            a, b = acc[:, :half], acc[:, half:]
            c, s = cos[rr, :], sin[rr, :]
            q_v[rr, c0] = (a * c - b * s).astype(BF16)
            q_v[rr, c1] = (b * c + a * s).astype(BF16)
        return 0

    lax.fori_loop(0, heads, query, 0)
    q_out = local_copy(q_v, q_o)
    tick(1)
    scale = hd ** (-0.5)
    kcols, vcols = slice(rank, rank + hd), slice(rank + hd, rank + 2 * hd)
    causal = causal_bias(PROMPT)
    for m in range(2):
        k0, k1 = (group_rows(lkv_v, m, h2, kcols, own) for h2 in (0, 1))
        v0, v1 = (group_rows(lkv_v, m, h2, vcols, own) for h2 in (0, 1))
        low = bias[m]

        def attend(h, _):
            cols = pl.ds(al(h * hd, hd), hd)
            q0 = group_rows(q_v, m, 0, cols, own)
            pr = softmax_parts(mm_nt(q0, k0) * scale + causal).astype(BF16)
            put_rows(mixed_v, m, 0, cols, own, mm(pr, v0).astype(BF16))
            q1 = group_rows(q_v, m, 1, cols, own)
            s0 = mm_nt(q1, k0) * scale
            s1 = mm_nt(q1, k1) * scale + low
            top = jnp.maximum(
                jnp.max(s0, axis=-1, keepdims=True), jnp.max(s1, axis=-1, keepdims=True)
            )
            e0, e1 = jnp.exp(s0 - top), jnp.exp(s1 - top)
            total = jnp.sum(e0, axis=-1, keepdims=True) + jnp.sum(e1, axis=-1, keepdims=True)
            mix = mm((e0 / total).astype(BF16), v0) + mm((e1 / total).astype(BF16), v1)
            put_rows(mixed_v, m, 1, cols, own, mix.astype(BF16))
            return 0

        lax.fori_loop(0, heads, attend, 0)
        tick(2)
    fs_d.end()
    d_out = local_copy(d_v, d_o)
    mixed_out = local_copy(mixed_v, mixed_o)
    tick(1)
    for i in i_out:
        own_copies[i].wait()
        g.wait_x(i)
    out_out = local_copy(out_v, out_all)

    def project_out(fb):
        rr = pl.ds(al(fb * own, own), own)

        def one(j, _):
            wr = pl.ds(al(j * 256, 256), 256)
            part_v[rr, wr] = mm_nt(mixed_v[rr, :], out_v[wr, :]).astype(BF16)
            return 0

        lax.fori_loop(0, dim // 256, one, 0)

    project_out(p.f_yc)
    project_out(p.f_core)
    red.start()
    tick(1)
    project_out(p.f_y)
    red.mid(own)
    project_out(p.f)
    tick(2)
    red.end()
    for m in range(2):
        rr = pl.ds(m * (own // 2), own // 2)
        mid = tok[m].astype(F32) + red.value(rr)
        middle_o[rr, :] = mid
        inv = lax.rsqrt(jnp.mean(mid * mid, axis=-1, keepdims=True) + EPSILON)
        n2_v[pl.ds(al(p.f * own + m * (own // 2), 128), own // 2), :] = (
            mid * inv * gain_two
        ).astype(BF16)
    fs_n.start()
    tick(4)
    fs_n.mid()
    tick(1)
    fs_n.end()
    n2_out = local_copy(n2_v, n2_o)
    tick(len(events))
    for i in i_ffn:
        own_copies[i].wait()
        g.wait_x(i)
    for i in order:
        g.wait_sends(i)

    def spread_sends(j, _):
        for which in (0, 1):
            seq_copy(0, j, p.f, p.to_core, which).wait_send()
            seq_copy(1, j, p.f, p.to_y, which).wait_send()
            seq_copy(2, j, p.f_y, p.to_core, which).wait_send()
        return 0

    lax.fori_loop(0, npiece, spread_sends, 0)
    for t in (fs_d, fs_l, fs_n, red):
        t.wait_sends()
    for c in (seq_out, qb_out, lkv_out, q_out, d_out, mixed_out, out_out, n2_out):
        c.wait()


def forward_call(ndp, tok, dout, cos, sin, bias, seq_sh, gain_sh, qb, out, gate, up, down):
    own = tok.shape[0] * tok.shape[1]
    dim = tok.shape[2]
    rank = qb.shape[0] * ndp
    hd = (seq_sh.shape[1] - rank) // 2
    heads = qb.shape[1] // hd
    rows = NF * own
    kvw = seq_sh.shape[1]
    nz = ndp // 2
    n_items = 2 + 1 + 2 + 6

    def sds(shape, dtype=BF16):
        return jax.ShapeDtypeStruct(shape, dtype)

    full = lambda w: sds((w.shape[0] * ndp, w.shape[1]))
    out_shape = (
        full(qb),
        full(out),
        full(gate),
        full(up),
        full(down),
        sds((seq_sh.shape[0] * ndp * NF, kvw)),
        sds(gain_sh.shape, F32),
        sds((rows, kvw)),
        sds((rows, heads * hd)),
        sds((rows, heads * hd)),
        sds((own, rank), F32),
        sds((own, dim)),
        sds((own, dim), F32),
        sds((rows, dim)),
        sds((rows, dim)),
    )
    out_specs = (ANY,) * 6 + (VMEM,) + (ANY,) * 3 + (VMEM,) * 3 + (ANY,) * 2
    dma = pltpu.SemaphoreType.DMA
    scratch = [
        pltpu.VMEM((seq_sh.shape[0] * ndp * NF, kvw), BF16),
        pltpu.VMEM((ndp * NF,) + gain_sh.shape, F32),
        pltpu.VMEM((qb.shape[0] * ndp, qb.shape[1]), BF16),
        pltpu.VMEM((out.shape[0] * ndp, out.shape[1]), BF16),
        pltpu.VMEM((rows, kvw), BF16),
        pltpu.VMEM((rows, heads * hd), BF16),
        pltpu.VMEM((rows, heads * hd), BF16),
        pltpu.VMEM((rows, dim), BF16),
        pltpu.VMEM((2, own, dim), BF16),
        pltpu.VMEM((own, dim), BF16),
        pltpu.VMEM((rows, dim), BF16),
        pltpu.VMEM((rows, dim), BF16),
        pltpu.VMEM((own, kvw), F32),
        dma((n_items, nz - 1)),
        dma((n_items, nz - 1)),
        dma((n_items, nz)),
        dma((n_items, nz)),
        dma((4, 3)),
        dma((4, 3)),
        dma((2, 3, ndp)),
        dma((2, 3, ndp)),
        dma((n_items + 10,)),
    ]
    return pl.pallas_call(
        functools.partial(forward_kernel, (ndp, own, dim, rank, hd, heads)),
        out_shape=out_shape,
        in_specs=(VMEM,) * 5 + (ANY,) * 7,
        out_specs=out_specs,
        scratch_shapes=scratch,
        compiler_params=pltpu.CompilerParams(
            collective_id=0, has_side_effects=True, vmem_limit_bytes=60 * 2**20
        ),
        name="gather_forward",
    )(tok, dout, cos, sin, bias, seq_sh, gain_sh, qb, out, gate, up, down)


class DpScatter:
    def __init__(self, pos, xs, xr, zs, zr, ls):
        self.p = pos
        self.xs, self.xr, self.zs, self.zr, self.ls = xs, xr, zs, zr, ls
        self.items = []

    def add(self, src, own, xbuf, zbuf, out, r0, r):
        self.items.append((src, own, xbuf, zbuf, out, pl.ds(r0, r), r0, r))
        return len(self.items) - 1

    def xcopy(self, i):
        src, own, xbuf, zbuf, out, rr, r0, r = self.items[i]
        return rcopy(
            src.at[:, 1 - self.p.x, rr], xbuf.at[:, rr], self.xs.at[i], self.xr.at[i], self.p.to_pair
        )

    def owncopy(self, i):
        src, own, xbuf, zbuf, out, rr, r0, r = self.items[i]
        return pltpu.make_async_copy(src.at[:, self.p.x, rr], own.at[:, rr], self.ls.at[i])

    def start(self, i):
        self.xcopy(i).start()
        if self.items[i][1] is not None:
            self.owncopy(i).start()

    def zcopy(self, i, k):
        src, own, xbuf, zbuf, out, rr, r0, r = self.items[i]
        return rcopy(
            xbuf.at[self.p.zidx(k), rr],
            zbuf.at[k - 1, rr],
            self.zs.at[i, k - 1],
            self.zr.at[i, k - 1],
            self.p.to_z(k),
        )

    def combine(self, i):
        src, own, xbuf, zbuf, out, rr, r0, r = self.items[i]
        p = self.p
        self.xcopy(i).wait_recv()
        if own is not None:
            self.owncopy(i).wait()
        tile = 16

        def mine(j, t):
            if own is None:
                return src[j, p.x, t, :].astype(F32)
            return own[j, t, :].astype(F32)

        for k in range(1, p.nz):
            j = p.zidx(k)

            def add(t, _):
                t = pl.ds(al(r0 + t * tile, tile), tile)
                xbuf[j, t, :] = (xbuf[j, t, :].astype(F32) + mine(j, t)).astype(BF16)
                return 0

            lax.fori_loop(0, r // tile, add, 0)
            self.zcopy(i, k).start()

        def keep(t, _):
            t = pl.ds(al(r0 + t * tile, tile), tile)
            out[t, :] = xbuf[p.z, t, :].astype(F32) + mine(p.z, t)
            return 0

        lax.fori_loop(0, r // tile, keep, 0)

    def finish(self, i):
        src, own, xbuf, zbuf, out, rr, r0, r = self.items[i]
        for k in range(1, self.p.nz):
            self.zcopy(i, k).wait_recv()
        tile = 16

        def add(t, _):
            t = pl.ds(al(r0 + t * tile, tile), tile)
            total = out[t, :]
            for k in range(self.p.nz - 1):
                total = total + zbuf[k, t, :].astype(F32)
            out[t, :] = total
            return 0

        lax.fori_loop(0, r // tile, add, 0)

    def wait_sends(self, i):
        self.xcopy(i).wait_send()
        for k in range(1, self.p.nz):
            self.zcopy(i, k).wait_send()


def scatter_kernel(ndp, pieces, n, *refs):
    refs = list(refs)

    def take(c):
        out = refs[:c]
        del refs[:c]
        return out

    heads = take(n)
    seq, gain = take(2)
    outs = take(n)
    seq_o, gain_o = take(2)
    owns, xbufs, zbufs = take(n), take(n), take(n)
    seq_own, seq_core, seq_y, seq_x, seq_z, gain_rx, gain_acc = take(7)
    xs, xr, zs, zr, ls, gs, gr, qs, qr, qls = take(10)
    p = Place(ndp)
    sc = DpScatter(p, xs, xr, zs, zr, ls)
    head_items = []
    for w in range(n):
        rows = outs[w].shape[0]
        step = rows // pieces[w]
        for c in range(pieces[w]):
            head_items.append(
                sc.add(heads[w], owns[w], xbufs[w], zbufs[w], outs[w], c * step, step)
            )
    sr = seq_o.shape[0]
    seq_item = sc.add(seq_core.at[0], None, seq_x, seq_z, seq_o, 0, sr)
    own_f = pltpu.make_async_copy(seq.at[:, :, p.f], seq_own.at[0], qls.at[0])
    own_y = pltpu.make_async_copy(seq.at[:, :, p.f_y], seq_own.at[1], qls.at[1])
    own_y.start()
    own_f.start()
    p.barrier()
    c1 = rcopy(seq.at[:, :, p.f_yc], seq_core.at[1], qs.at[1], qr.at[1], p.to_core)
    c0 = rcopy(seq.at[:, :, p.f_core], seq_core.at[0], qs.at[0], qr.at[0], p.to_core)
    cy = rcopy(seq_core.at[1], seq_y, qs.at[2], qr.at[2], p.to_y)
    c1.start()
    c0.start()
    gains = [
        rcopy(gain, gain_rx.at[0], gs.at[0], gr.at[0], p.to_core),
        rcopy(gain_acc.at[0], gain_rx.at[1], gs.at[1], gr.at[1], p.to_y),
        rcopy(gain_acc.at[1], gain_rx.at[2], gs.at[2], gr.at[2], p.to_pair),
    ] + [
        rcopy(gain_acc.at[2], gain_rx.at[2 + k], gs.at[2 + k], gr.at[2 + k], p.to_z(k))
        for k in range(1, p.nz)
    ]
    gains[0].start()
    for i in head_items:
        sc.start(i)
    gains[0].wait_recv()
    gain_acc[0] = gain[...] + gain_rx[0]
    gains[1].start()
    gains[1].wait_recv()
    gain_acc[1] = gain_acc[0] + gain_rx[1]
    gains[2].start()
    own_y.wait()
    own_f.wait()
    c1.wait_recv()
    nz = p.nz

    def add_y(j, _):
        for x in range(2):
            seq_core[1, j, x] = (
                seq_core[1, j, x].astype(F32) + seq_own[1, j, x].astype(F32)
            ).astype(BF16)
        return 0

    lax.fori_loop(0, nz, add_y, 0)
    cy.start()
    gains[2].wait_recv()
    gain_acc[2] = gain_acc[1] + gain_rx[2]
    for k in range(1, nz):
        gains[2 + k].start()
    sc.combine(head_items[0])
    c0.wait_recv()
    cy.wait_recv()

    def add_f(j, _):
        for x in range(2):
            seq_core[0, j, x] = (
                seq_core[0, j, x].astype(F32)
                + seq_own[0, j, x].astype(F32)
                + seq_y[j, x].astype(F32)
            ).astype(BF16)
        return 0

    lax.fori_loop(0, nz, add_f, 0)
    sc.start(seq_item)
    todo = head_items[1:] + [seq_item]
    for i in todo:
        sc.combine(i)
    total = gain_acc[2]
    for k in range(1, nz):
        gains[2 + k].wait_recv()
        total = total + gain_rx[2 + k]
    gain_o[...] = total
    for i in head_items + [seq_item]:
        sc.finish(i)
    for i in head_items + [seq_item]:
        sc.wait_sends(i)
    for t in [c1, c0, cy] + gains:
        t.wait_send()


def scatter_call(ndp, heads, seq, gain):
    nz = ndp // 2
    n = len(heads)
    shards = [(w.shape[0] // ndp, w.shape[1]) for w in heads]
    pieces = [2 if s[0] % 32 == 0 else 1 for s in shards]
    n_items = sum(pieces) + 1
    sr, kvw = seq.shape[0] // (ndp * NF), seq.shape[1]
    dma = pltpu.SemaphoreType.DMA
    scratch = (
        [pltpu.VMEM((nz,) + s, BF16) for s in shards]
        + [pltpu.VMEM((nz,) + s, BF16) for s in shards]
        + [pltpu.VMEM((nz - 1,) + s, BF16) for s in shards]
        + [
            pltpu.VMEM((2, nz, 2, sr, kvw), BF16),
            pltpu.VMEM((2, nz, 2, sr, kvw), BF16),
            pltpu.VMEM((nz, 2, sr, kvw), BF16),
            pltpu.VMEM((nz, sr, kvw), BF16),
            pltpu.VMEM((nz - 1, sr, kvw), BF16),
            pltpu.VMEM((2 + nz,) + gain.shape, F32),
            pltpu.VMEM((3,) + gain.shape, F32),
            dma((n_items,)),
            dma((n_items,)),
            dma((n_items, nz - 1)),
            dma((n_items, nz - 1)),
            dma((n_items,)),
            dma((2 + nz,)),
            dma((2 + nz,)),
            dma((3,)),
            dma((3,)),
            dma((2,)),
        ]
    )
    return pl.pallas_call(
        functools.partial(scatter_kernel, ndp, pieces, n),
        out_shape=tuple(jax.ShapeDtypeStruct(s, F32) for s in shards)
        + (jax.ShapeDtypeStruct((sr, kvw), F32), jax.ShapeDtypeStruct(gain.shape, F32)),
        in_specs=(ANY,) * (n + 1) + (VMEM,),
        out_specs=(VMEM,) * (n + 2),
        scratch_shapes=scratch,
        compiler_params=pltpu.CompilerParams(
            collective_id=1, has_side_effects=True, vmem_limit_bytes=60 * 2**20
        ),
        name="scatter_grads",
    )(*[w.reshape((nz, 2) + s) for w, s in zip(heads, shards)], seq.reshape(nz, 2, NF, sr, kvw), gain)


def unrotate(vector, cos_tab, sin_tab):
    half_width = vector.shape[-1] // 2
    lower_half = vector[..., :half_width]
    upper_half = vector[..., half_width:]
    return jnp.concatenate(
        [lower_half * cos_tab + upper_half * sin_tab, upper_half * cos_tab - lower_half * sin_tab],
        axis=-1,
    )


def norm_back(grad_in, values, inverse, gain):
    scaled = grad_in * gain
    gain_term = jnp.sum(grad_in * values * inverse, axis=0)
    inner_sum = jnp.mean(scaled * values, axis=-1, keepdims=True)
    return (inverse * scaled - values * inverse * inverse * inverse * inner_sum, gain_term)


def inverse_rms(v):
    return lax.rsqrt(jnp.mean(v * v, axis=-1, keepdims=True) + EPSILON)


def per_device(
    ndp,
    tokens,
    membership,
    d_output,
    gain_attn,
    w_qa,
    gain_latent,
    w_qb,
    w_key,
    w_value,
    w_out,
    gain_ffn,
    w_gate,
    w_up,
    w_down,
):
    micro, tlen, dim = tokens.shape
    own = micro * tlen
    rank = w_qa.shape[1]
    hd = w_key.shape[1]
    heads = w_qb.shape[1] // hd
    rows = NF * own
    wide = dim // rank
    labels, positions = jax.vmap(lambda r: layout(r, BLK))(membership[0])
    pos_rows = positions.reshape(micro, NF, tlen).transpose(1, 0, 2).reshape(rows)
    cos, sin = rope_tables(pos_rows, hd)
    tail = labels[:, PROMPT:]
    idx = jnp.arange(tail.shape[1], dtype=jnp.int32)
    seen = (idx[None, None, :] <= idx[None, :, None]) & (tail[:, None, :] == tail[:, :, None])
    bias = jnp.where(seen, 0.0, MASK_FILL).astype(F32)
    block = lax.axis_index("dp") * NF + lax.axis_index("fsdp")

    def spot(gain):
        width = gain.shape[0]
        count = ndp * NF
        at = lax.broadcasted_iota(jnp.int32, (count, width), 0) == block
        placed = jnp.where(at, gain.astype(F32)[None, :], 0.0)
        return placed.reshape(count * width // rank, rank)

    gain_sh = jnp.concatenate([spot(gain_attn), spot(gain_ffn), spot(gain_latent)], axis=0)
    gain_sh = jnp.pad(gain_sh, ((0, 8 - gain_sh.shape[0]), (0, 0)))
    seq_sh = jnp.concatenate([w_qa, w_key, w_value], axis=1)
    (
        qb_all,
        out_all,
        gate_all,
        up_all,
        down_all,
        seq_all,
        gains,
        lkv,
        q_all,
        mixed,
        latent,
        normed,
        middle,
        n2,
        d_all,
    ) = forward_call(
        ndp, tokens, d_output, cos, sin, bias, seq_sh, gain_sh, w_qb, w_out, w_gate, w_up, w_down
    )
    gain_one = gains[:wide].reshape(1, dim)
    gain_two = gains[wide : 2 * wide].reshape(1, dim)
    gain_lat = gains[2 * wide].reshape(1, rank)

    gate = jnp.dot(n2, gate_all, preferred_element_type=F32)
    up = jnp.dot(n2, up_all, preferred_element_type=F32)
    sig = jax.nn.sigmoid(gate)
    hidden = (gate * sig * up).astype(BF16)
    grad_hidden = jnp.dot(d_all, down_all, preferred_element_type=F32)
    grad_gate = (grad_hidden * up * sig * (1.0 + gate * (1.0 - sig))).astype(BF16)
    grad_up = (grad_hidden * gate * sig).astype(BF16)
    ffn_part = mm_nt(hidden, down_all).astype(BF16)
    gnt_part = (mm_nt(grad_gate, gate_all) + mm_nt(grad_up, up_all)).astype(BF16)
    gw_down = mm_tn(d_all, hidden).astype(BF16)
    gw_gate = mm_tn(n2, grad_gate).astype(BF16)
    gw_up = mm_tn(n2, grad_up).astype(BF16)

    ffn_own = lax.psum_scatter(ffn_part, "fsdp", scatter_dimension=0, tiled=True).astype(F32)
    output = (middle + ffn_own).astype(BF16).reshape(tokens.shape)
    grad_n2 = lax.psum_scatter(gnt_part, "fsdp", scatter_dimension=0, tiled=True).astype(F32)
    grad_mid_norm, g_gain_two = norm_back(grad_n2, middle, inverse_rms(middle), gain_two)
    grad_middle = d_output.reshape(own, dim).astype(F32) + grad_mid_norm
    proj_all = lax.all_gather(grad_middle.astype(BF16), "fsdp", axis=0, tiled=True)
    gw_out = mm_tn(proj_all, mixed).astype(BF16)
    grad_mixed = mm(proj_all, out_all).astype(BF16)

    def by_group(v, *tail_shape):
        return (
            v.reshape((NF, micro, tlen) + tail_shape)
            .swapaxes(0, 1)
            .reshape((micro, NF * tlen) + tail_shape)
        )

    def by_block(v):
        tail_shape = v.shape[2:]
        return (
            v.reshape((micro, NF, tlen) + tail_shape)
            .swapaxes(0, 1)
            .reshape((rows,) + tail_shape)
        )

    scale = hd ** (-0.5)
    ki = jnp.arange(NF * tlen, dtype=jnp.int32)
    allowed = (ki[None, None, :] <= ki[None, :, None]) & (
        (labels[:, None, :] == 0) | (labels[:, None, :] == labels[:, :, None])
    )
    qg = by_group(q_all, heads, hd) if False else by_group(q_all.reshape(rows, heads, hd), heads, hd)
    gm = by_group(grad_mixed.reshape(rows, heads, hd), heads, hd)
    keys = by_group(lkv[:, rank : rank + hd], hd)
    values = by_group(lkv[:, rank + hd :], hd)
    scores = jnp.einsum("mqhd,mkd->mhqk", qg, keys, preferred_element_type=F32) * scale
    scores = jnp.where(allowed[:, None], scores, MASK_FILL)
    probs = jax.nn.softmax(scores, axis=-1)
    gp = jnp.einsum("mqhd,mkd->mhqk", gm, values, preferred_element_type=F32)
    gv = jnp.einsum("mhqk,mqhd->mkd", probs.astype(BF16), gm, preferred_element_type=F32)
    gs = (probs * (gp - jnp.sum(probs * gp, axis=-1, keepdims=True))).astype(BF16)
    gq = jnp.einsum("mhqk,mkd->mqhd", gs, keys, preferred_element_type=F32) * scale
    gk = jnp.einsum("mhqk,mqhd->mkd", gs, qg, preferred_element_type=F32) * scale
    gq = unrotate(by_block(gq), cos[:, None, :], sin[:, None, :]).astype(BF16)
    gq = gq.reshape(rows, heads * hd)
    gw_qb = mm_tn(lkv[:, :rank], gq).astype(BF16)
    glat_part = mm_nt(gq, qb_all).astype(BF16)
    packed = jnp.concatenate(
        [glat_part, by_block(gk).astype(BF16), by_block(gv).astype(BF16)], axis=1
    )
    back_own = lax.psum_scatter(packed, "fsdp", scatter_dimension=0, tiled=True).astype(F32)
    cos_own = lax.dynamic_slice_in_dim(cos, lax.axis_index("fsdp") * own, own, 0)
    sin_own = lax.dynamic_slice_in_dim(sin, lax.axis_index("fsdp") * own, own, 0)
    g_lat, g_gain_lat = norm_back(back_own[:, :rank], latent, inverse_rms(latent), gain_lat)
    g_key = unrotate(back_own[:, rank : rank + hd], cos_own, sin_own)
    g_all = jnp.concatenate([g_lat, g_key, back_own[:, rank + hd :]], axis=1).astype(BF16)
    gw_seq = mm_tn(normed, g_all).astype(BF16)
    grad_normed = mm_nt(g_all, seq_all)
    inputs = tokens.reshape(own, dim).astype(F32)
    grad_in, g_gain_one = norm_back(grad_normed, inputs, inverse_rms(inputs), gain_one)
    input_grad = (grad_middle + grad_in).astype(BF16).reshape(tokens.shape)
    gain_part = jnp.concatenate(
        [
            g_gain_one.reshape(wide, rank),
            g_gain_two.reshape(wide, rank),
            g_gain_lat.reshape(1, rank),
        ],
        axis=0,
    )
    gain_part = jnp.pad(gain_part, ((0, 8 - gain_part.shape[0]), (0, 0)))
    o_gate, o_up, o_down, o_out, o_qb, o_seq, o_gain = scatter_call(
        ndp, (gw_gate, gw_up, gw_down, gw_out, gw_qb), gw_seq, gain_part
    )

    def own_gain(flat, width):
        return lax.dynamic_slice_in_dim(flat.reshape(-1), block * width, width, 0)

    return (
        output,
        input_grad,
        own_gain(o_gain[:wide], gain_attn.shape[0]),
        o_seq[:, :rank],
        own_gain(o_gain[2 * wide], gain_latent.shape[0]),
        o_qb,
        o_seq[:, rank : rank + hd],
        o_seq[:, rank + hd :],
        o_out,
        own_gain(o_gain[wide : 2 * wide], gain_ffn.shape[0]),
        o_gate,
        o_up,
        o_down,
    )


def solution(mesh):
    both = ("dp", "fsdp")
    rowwise, vector = P(both, None), P(both)
    tok = P(None, both, None)
    head = P("dp", "fsdp")
    return jax.shard_map(
        functools.partial(per_device, mesh.shape["dp"]),
        mesh=mesh,
        in_specs=(
            tok,
            P("dp", None, None),
            tok,
            vector,
            rowwise,
            vector,
            head,
            rowwise,
            rowwise,
            head,
            vector,
            head,
            head,
            head,
        ),
        out_specs=(
            tok,
            tok,
            vector,
            rowwise,
            vector,
            head,
            rowwise,
            rowwise,
            head,
            vector,
            head,
            head,
            head,
        ),
        check_vma=False,
    )
```

```python
import functools

import jax
import jax.numpy as jnp
from jax import lax
from jax.experimental import pallas as pl
from jax.experimental.pallas import tpu as pltpu
from jax.sharding import PartitionSpec as P

BLK = 32
PROMPT = 256
EPSILON = 1e-05
ROPE_BASE = 10000.0
MASK_FILL = -1e30
F32 = jnp.float32
BF16 = jnp.bfloat16
MESH = pl.DeviceIdType.MESH
ANY = pl.BlockSpec(memory_space=pl.ANY)
VMEM = pl.BlockSpec(memory_space=pltpu.VMEM)
NF = 4


def layout(member_row, block_len):
    count_blocks = member_row.shape[0]
    block_ids = jnp.arange(count_blocks, dtype=jnp.int32)
    same_run = (member_row[None, :] == member_row[:, None]) & (
        block_ids[None, :] < block_ids[:, None]
    )
    earlier = jnp.sum(same_run.astype(jnp.int32), axis=1)
    prompt_len = jnp.sum((member_row == 0).astype(jnp.int32)) * block_len
    labels = jnp.repeat(member_row, block_len)
    within = jnp.arange(count_blocks * block_len, dtype=jnp.int32) % block_len
    positions = (
        (labels > 0).astype(jnp.int32) * prompt_len
        + jnp.repeat(earlier, block_len) * block_len
        + within
    )
    return (labels, positions)


def rope_tables(positions, head_width):
    half_width = head_width // 2
    frequency = ROPE_BASE ** (-(jnp.arange(half_width, dtype=jnp.float32) * (2.0 / head_width)))
    angles = positions.astype(jnp.float32)[:, None] * frequency[None, :]
    return (jnp.cos(angles), jnp.sin(angles))


def al(x, n):
    return pl.multiple_of(x, n)


def mm(a, b):
    return lax.dot_general(a, b, (((1,), (0,)), ((), ())), preferred_element_type=F32)


def mm_nt(a, b):
    return lax.dot_general(a, b, (((1,), (1,)), ((), ())), preferred_element_type=F32)


def mm_tn(a, b):
    return lax.dot_general(a, b, (((0,), (0,)), ((), ())), preferred_element_type=F32)


class Place:
    def __init__(self, ndp):
        self.ndp = ndp
        self.nz = ndp // 2
        self.me = lax.axis_index("dp")
        self.f = lax.axis_index("fsdp")
        self.z = self.me // 2
        self.x = self.me % 2
        self.pair = self.z * 2 + 1 - self.x
        y, c = self.f // 2, self.f % 2
        self.f_core = y * 2 + 1 - c
        self.f_y = (1 - y) * 2 + c
        self.f_yc = (1 - y) * 2 + 1 - c
        self.to_pair = (self.pair, self.f)
        self.to_core = (self.me, self.f_core)
        self.to_y = (self.me, self.f_y)

    def zidx(self, k):
        return lax.rem(self.z + k + self.nz, self.nz)

    def to_z(self, k):
        return (self.zidx(k) * 2 + self.x, self.f)

    def barrier(self, fsdp=True):
        bar = pltpu.get_barrier_semaphore()
        count = self.nz
        devs = [self.to_pair] + [self.to_z(k) for k in range(1, self.nz)]
        if fsdp:
            devs += [self.to_core, self.to_y]
            count += 2
        for d in devs:
            pl.semaphore_signal(bar, inc=1, device_id=d, device_id_type=MESH)
        pl.semaphore_wait(bar, count)


def rcopy(src, dst, ss, rs, dev):
    return pltpu.make_async_remote_copy(
        src_ref=src, dst_ref=dst, send_sem=ss, recv_sem=rs, device_id=dev, device_id_type=MESH
    )


class DpGather:
    def __init__(self, pos, items, zs, zr, xs, xr):
        self.p, self.items = pos, items
        self.zs, self.zr, self.xs, self.xr = zs, zr, xs, xr

    def zcopy(self, i, k):
        src, dst = self.items[i]
        return rcopy(
            src, dst(self.p.me), self.zs.at[i, k - 1], self.zr.at[i, k - 1], self.p.to_z(k)
        )

    def zarrive(self, i, k):
        src, dst = self.items[i]
        j = self.p.zidx(-k) * 2 + self.p.x
        return rcopy(src, dst(j), self.zs.at[i, k - 1], self.zr.at[i, k - 1], self.p.to_z(-k))

    def xcopy(self, i, k):
        src, dst = self.items[i]
        j = self.p.zidx(-k) * 2 + self.p.x
        return rcopy(
            src if k == 0 else dst(j), dst(j), self.xs.at[i, k], self.xr.at[i, k], self.p.to_pair
        )

    def xarrive(self, i, k):
        src, dst = self.items[i]
        j = self.p.zidx(-k) * 2 + 1 - self.p.x
        return rcopy(src, dst(j), self.xs.at[i, k], self.xr.at[i, k], self.p.to_pair)

    def start_z(self, i):
        for k in range(1, self.p.nz):
            self.zcopy(i, k).start()

    def start_x(self, i):
        self.xcopy(i, 0).start()

    def forward(self, i, k):
        self.zarrive(i, k).wait_recv()
        self.xcopy(i, k).start()

    def wait_x(self, i):
        for k in range(self.p.nz):
            self.xarrive(i, k).wait_recv()

    def wait_sends(self, i):
        for k in range(self.p.nz):
            self.xcopy(i, k).wait_send()
        for k in range(1, self.p.nz):
            self.zcopy(i, k).wait_send()


class FsGather:
    def __init__(self, pos, blocks, ss, rs):
        self.p, self.b, self.ss, self.rs = pos, blocks, ss, rs

    def copy(self, n, fb, dev):
        return rcopy(self.b(fb), self.b(fb), self.ss.at[n], self.rs.at[n], dev)

    def start(self):
        self.copy(1, self.p.f, self.p.to_y).start()
        self.copy(0, self.p.f, self.p.to_core).start()

    def mid(self):
        self.copy(1, self.p.f_y, self.p.to_y).wait_recv()
        self.copy(2, self.p.f_y, self.p.to_core).start()

    def end(self):
        self.copy(0, self.p.f_core, self.p.to_core).wait_recv()
        self.copy(2, self.p.f_yc, self.p.to_core).wait_recv()

    def wait_sends(self):
        self.copy(1, self.p.f, self.p.to_y).wait_send()
        self.copy(0, self.p.f, self.p.to_core).wait_send()
        self.copy(2, self.p.f_y, self.p.to_core).wait_send()


class FsReduce:
    def __init__(self, pos, blocks, from_core, from_y, ss, rs):
        self.p, self.b, self.fc, self.fy, self.ss, self.rs = pos, blocks, from_core, from_y, ss, rs

    def c1(self):
        return rcopy(
            self.b(self.p.f_yc), self.fc.at[1], self.ss.at[1], self.rs.at[1], self.p.to_core
        )

    def c0(self):
        return rcopy(
            self.b(self.p.f_core), self.fc.at[0], self.ss.at[0], self.rs.at[0], self.p.to_core
        )

    def cy(self):
        return rcopy(self.fc.at[1], self.fy, self.ss.at[2], self.rs.at[2], self.p.to_y)

    def start(self):
        self.c1().start()
        self.c0().start()

    def mid(self, rows, tile=64):
        self.c1().wait_recv()
        mine = self.b(self.p.f_y)

        def add(t, _):
            r = pl.ds(al(t * tile, tile), tile)
            self.fc[1, r, :] = (self.fc[1, r, :].astype(F32) + mine[r, :].astype(F32)).astype(BF16)
            return 0

        lax.fori_loop(0, rows // tile, add, 0)
        self.cy().start()

    def end(self):
        self.c0().wait_recv()
        self.cy().wait_recv()

    def value(self, r):
        return (
            self.b(self.p.f)[r, :].astype(F32)
            + self.fc[0, r, :].astype(F32)
            + self.fy[r, :].astype(F32)
        )

    def wait_sends(self):
        self.c1().wait_send()
        self.c0().wait_send()
        self.cy().wait_send()


def softmax_parts(scores):
    top = jnp.max(scores, axis=-1, keepdims=True)
    lifted = jnp.exp(scores - top)
    return lifted / jnp.sum(lifted, axis=-1, keepdims=True)


def causal_bias(rows):
    r = lax.broadcasted_iota(jnp.int32, (rows, rows), 0)
    c = lax.broadcasted_iota(jnp.int32, (rows, rows), 1)
    return jnp.where(c <= r, 0.0, MASK_FILL).astype(F32)


def group_rows(ref, m, half, cols, own):
    t = own // 2
    first = ref[pl.ds((2 * half) * own + m * t, t), cols]
    second = ref[pl.ds((2 * half + 1) * own + m * t, t), cols]
    return jnp.concatenate([first, second], axis=0)


def put_rows(ref, m, half, cols, own, value):
    t = own // 2
    ref[pl.ds((2 * half) * own + m * t, t), cols] = value[:t]
    ref[pl.ds((2 * half + 1) * own + m * t, t), cols] = value[t:]


def forward_kernel(
    cfg,
    tok,
    dout,
    cos,
    sin,
    bias,
    seq_sh,
    gain_sh,
    qb_sh,
    out_sh,
    gate_sh,
    up_sh,
    down_sh,
    qb_all,
    out_all,
    gate_all,
    up_all,
    down_all,
    seq_all,
    gain_sum,
    lkv_o,
    q_o,
    mixed_o,
    latent_o,
    normed_o,
    middle_o,
    n2_o,
    d_o,
    seq_v,
    gain_v,
    qb_v,
    out_v,
    lkv_v,
    q_v,
    mixed_v,
    part_v,
    fcore_v,
    fy_v,
    n2_v,
    d_v,
    lat_v,
    zs,
    zr,
    xs,
    xr,
    fss,
    frs,
    sys_,
    syr,
    ls,
):
    ndp, own, dim, rank, hd, heads = cfg
    rows = NF * own
    p = Place(ndp)
    kvw = rank + 2 * hd
    sr = seq_sh.shape[0]
    items = []

    def add_item(src, dst):
        items.append((src, dst))
        return len(items) - 1

    i_seq = add_item(seq_sh, lambda j: seq_v.at[pl.ds(al((j * NF + p.f) * sr, sr), sr)])
    i_gain = add_item(gain_sh, lambda j: gain_v.at[j * NF + p.f])

    def weight_items(src, dst, pieces):
        n = src.shape[0]
        step = n // pieces
        return [
            add_item(
                src.at[pl.ds(c * step, step)],
                lambda j, c=c: dst.at[pl.ds(al(j * n + c * step, step), step)],
            )
            for c in range(pieces)
        ]

    i_qb = weight_items(qb_sh, qb_v, 1)
    i_out = weight_items(out_sh, out_v, 2)
    i_ffn = []
    for s, d in ((gate_sh, gate_all), (up_sh, up_all), (down_sh, down_all)):
        i_ffn += weight_items(s, d, 2)
    order = [i_seq, i_gain] + i_qb + i_out + i_ffn
    g = DpGather(p, items, zs, zr, xs, xr)
    fs_d = FsGather(p, lambda b: d_v.at[pl.ds(al(b * own, own), own)], fss.at[0], frs.at[0])
    fs_l = FsGather(p, lambda b: lkv_v.at[pl.ds(al(b * own, own), own)], fss.at[1], frs.at[1])
    fs_n = FsGather(p, lambda b: n2_v.at[pl.ds(al(b * own, own), own)], fss.at[2], frs.at[2])
    red = FsReduce(
        p, lambda b: part_v.at[pl.ds(al(b * own, own), own)], fcore_v, fy_v, fss.at[3], frs.at[3]
    )

    local = []

    def local_copy(src, dst):
        c = pltpu.make_async_copy(src, dst, ls.at[len(local)])
        c.start()
        local.append(c)
        return c

    own_copies = {}
    for i in order:
        src, dst = items[i]
        own_copies[i] = local_copy(src, dst(p.me))
    d_copies = [
        local_copy(dout.at[m], d_v.at[pl.ds(al(p.f * own + m * (own // 2), 128), own // 2)])
        for m in range(2)
    ]

    p.barrier()
    g.start_x(i_seq)
    g.start_x(i_gain)
    g.start_x(i_qb[0])
    zahead = 4
    for i in order[:zahead]:
        g.start_z(i)
    zlead = [zahead]

    def more_z():
        if zlead[0] < len(order):
            g.start_z(order[zlead[0]])
            zlead[0] += 1

    npiece = ndp

    def seq_piece(j, fb):
        return seq_v.at[pl.ds(al((j * NF + fb) * sr, sr), sr)]

    def seq_copy(t, j, fb, dev, which):
        b = seq_piece(j, fb) if which == 0 else gain_v.at[j * NF + fb]
        return rcopy(b, b, sys_.at[which, t, j], syr.at[which, t, j], dev)

    def spread(j):
        for which in (0, 1):
            seq_copy(1, j, p.f, p.to_y, which).start()
            seq_copy(0, j, p.f, p.to_core, which).start()

    for m in range(2):
        x = tok[m].astype(F32)
        inv = lax.rsqrt(jnp.mean(x * x, axis=-1, keepdims=True) + EPSILON)
        middle_o[pl.ds(m * (own // 2), own // 2), :] = x * inv
    own_copies[i_seq].wait()
    own_copies[i_gain].wait()
    spread(p.me)
    queue = order[2:]
    lead = [1]

    def more_x():
        if lead[0] < len(queue):
            g.start_x(queue[lead[0]])
            lead[0] += 1

    for k in range(1, p.nz):
        for i in (i_seq, i_gain):
            g.forward(i, k)
        spread(p.zidx(-k) * 2 + p.x)
    more_x()
    for k in range(p.nz):
        for i in (i_seq, i_gain):
            g.xarrive(i, k).wait_recv()
        spread(p.zidx(-k) * 2 + 1 - p.x)
    for c in d_copies:
        c.wait()

    def spread_forward(j, _):
        for which in (0, 1):
            seq_copy(1, j, p.f_y, p.to_y, which).wait_recv()
            seq_copy(2, j, p.f_y, p.to_core, which).start()
        return 0

    events = [(i, k) for i in queue for k in range(1, p.nz)]
    done = [0]

    def tick(n):
        for _ in range(n):
            if done[0] >= len(events):
                return
            i, k = events[done[0]]
            if k == 1:
                more_x()
            g.forward(i, k)
            if k == p.nz - 1:
                more_z()
            done[0] += 1

    tick(p.nz - 1)
    lax.fori_loop(0, npiece, spread_forward, 0)
    fs_d.start()
    tick(p.nz - 1)

    def spread_end(j, _):
        for which in (0, 1):
            seq_copy(0, j, p.f_core, p.to_core, which).wait_recv()
            seq_copy(2, j, p.f_yc, p.to_core, which).wait_recv()
        return 0

    lax.fori_loop(0, npiece, spread_end, 0)

    def gain_add(j, acc):
        return acc + gain_v[j]

    gains = lax.fori_loop(0, ndp * NF, gain_add, jnp.zeros(gain_v.shape[1:], F32))
    gain_sum[...] = gains
    wide = dim // rank
    gain_one = jnp.concatenate([gains[r : r + 1] for r in range(wide)], axis=1)
    gain_two = jnp.concatenate([gains[wide + r : wide + r + 1] for r in range(wide)], axis=1)
    gain_lat = gains[2 * wide : 2 * wide + 1]
    normed_o[...] = (middle_o[...] * gain_one).astype(BF16)
    seq_out = local_copy(seq_v, seq_all)

    def project(j, _):
        cols = pl.ds(al(j * 256, 256), 256)
        lat_v[:, cols] = mm(normed_o[...], seq_v[:, cols])
        return 0

    lax.fori_loop(0, kvw // 256, project, 0)
    own_rows = pl.ds(al(p.f * own, own), own)
    lat = lat_v[:, :rank]
    latent_o[...] = lat
    inv_lat = lax.rsqrt(jnp.mean(lat * lat, axis=-1, keepdims=True) + EPSILON)
    lkv_v[own_rows, :rank] = (lat * inv_lat * gain_lat).astype(BF16)
    half = hd // 2
    co, si = cos[own_rows, :], sin[own_rows, :]
    ka, kb = lat_v[:, rank : rank + half], lat_v[:, rank + half : rank + hd]
    lkv_v[own_rows, rank : rank + half] = (ka * co - kb * si).astype(BF16)
    lkv_v[own_rows, rank + half : rank + hd] = (kb * co + ka * si).astype(BF16)
    lkv_v[own_rows, rank + hd :] = lat_v[:, rank + hd :].astype(BF16)
    fs_l.start()
    tick(p.nz - 1)
    fs_d.mid()
    fs_l.mid()
    tick(p.nz - 1)
    for i in i_qb:
        own_copies[i].wait()
        g.wait_x(i)
    fs_l.end()
    qb_out = local_copy(qb_v, qb_all)
    lkv_out = local_copy(lkv_v, lkv_o)

    def query(j, _):
        cols = pl.ds(al(j * hd, hd), hd)
        c0 = pl.ds(al(j * hd, half), half)
        c1 = pl.ds(al(j * hd + half, half), half)
        for r in range(rows // 512):
            rr = pl.ds(r * 512, 512)
            acc = mm(lkv_v[rr, :rank], qb_v[:, cols])
            a, b = acc[:, :half], acc[:, half:]
            c, s = cos[rr, :], sin[rr, :]
            q_v[rr, c0] = (a * c - b * s).astype(BF16)
            q_v[rr, c1] = (b * c + a * s).astype(BF16)
        return 0

    lax.fori_loop(0, heads, query, 0)
    q_out = local_copy(q_v, q_o)
    tick(1)
    scale = hd ** (-0.5)
    kcols, vcols = slice(rank, rank + hd), slice(rank + hd, rank + 2 * hd)
    causal = causal_bias(PROMPT)
    for m in range(2):
        k0, k1 = (group_rows(lkv_v, m, h2, kcols, own) for h2 in (0, 1))
        v0, v1 = (group_rows(lkv_v, m, h2, vcols, own) for h2 in (0, 1))
        low = bias[m]

        def attend(h, _):
            cols = pl.ds(al(h * hd, hd), hd)
            q0 = group_rows(q_v, m, 0, cols, own)
            pr = softmax_parts(mm_nt(q0, k0) * scale + causal).astype(BF16)
            put_rows(mixed_v, m, 0, cols, own, mm(pr, v0).astype(BF16))
            q1 = group_rows(q_v, m, 1, cols, own)
            s0 = mm_nt(q1, k0) * scale
            s1 = mm_nt(q1, k1) * scale + low
            top = jnp.maximum(
                jnp.max(s0, axis=-1, keepdims=True), jnp.max(s1, axis=-1, keepdims=True)
            )
            e0, e1 = jnp.exp(s0 - top), jnp.exp(s1 - top)
            total = jnp.sum(e0, axis=-1, keepdims=True) + jnp.sum(e1, axis=-1, keepdims=True)
            mix = mm((e0 / total).astype(BF16), v0) + mm((e1 / total).astype(BF16), v1)
            put_rows(mixed_v, m, 1, cols, own, mix.astype(BF16))
            return 0

        lax.fori_loop(0, heads, attend, 0)
        tick(2)
    fs_d.end()
    d_out = local_copy(d_v, d_o)
    mixed_out = local_copy(mixed_v, mixed_o)
    tick(1)
    for i in i_out:
        own_copies[i].wait()
        g.wait_x(i)
    out_out = local_copy(out_v, out_all)

    def project_out(fb):
        rr = pl.ds(al(fb * own, own), own)

        def one(j, _):
            wr = pl.ds(al(j * 256, 256), 256)
            part_v[rr, wr] = mm_nt(mixed_v[rr, :], out_v[wr, :]).astype(BF16)
            return 0

        lax.fori_loop(0, dim // 256, one, 0)

    project_out(p.f_yc)
    project_out(p.f_core)
    red.start()
    tick(1)
    project_out(p.f_y)
    red.mid(own)
    project_out(p.f)
    tick(2)
    red.end()
    for m in range(2):
        rr = pl.ds(m * (own // 2), own // 2)
        mid = tok[m].astype(F32) + red.value(rr)
        middle_o[rr, :] = mid
        inv = lax.rsqrt(jnp.mean(mid * mid, axis=-1, keepdims=True) + EPSILON)
        n2_v[pl.ds(al(p.f * own + m * (own // 2), 128), own // 2), :] = (
            mid * inv * gain_two
        ).astype(BF16)
    fs_n.start()
    tick(4)
    fs_n.mid()
    tick(1)
    fs_n.end()
    n2_out = local_copy(n2_v, n2_o)
    tick(len(events))
    for i in i_ffn:
        own_copies[i].wait()
        g.wait_x(i)
    for i in order:
        g.wait_sends(i)

    def spread_sends(j, _):
        for which in (0, 1):
            seq_copy(0, j, p.f, p.to_core, which).wait_send()
            seq_copy(1, j, p.f, p.to_y, which).wait_send()
            seq_copy(2, j, p.f_y, p.to_core, which).wait_send()
        return 0

    lax.fori_loop(0, npiece, spread_sends, 0)
    for t in (fs_d, fs_l, fs_n, red):
        t.wait_sends()
    for c in (seq_out, qb_out, lkv_out, q_out, d_out, mixed_out, out_out, n2_out):
        c.wait()


def forward_call(ndp, tok, dout, cos, sin, bias, seq_sh, gain_sh, qb, out, gate, up, down):
    own = tok.shape[0] * tok.shape[1]
    dim = tok.shape[2]
    rank = qb.shape[0] * ndp
    hd = (seq_sh.shape[1] - rank) // 2
    heads = qb.shape[1] // hd
    rows = NF * own
    kvw = seq_sh.shape[1]
    nz = ndp // 2
    n_items = 2 + 1 + 2 + 6

    def sds(shape, dtype=BF16):
        return jax.ShapeDtypeStruct(shape, dtype)

    full = lambda w: sds((w.shape[0] * ndp, w.shape[1]))
    out_shape = (
        full(qb),
        full(out),
        full(gate),
        full(up),
        full(down),
        sds((seq_sh.shape[0] * ndp * NF, kvw)),
        sds(gain_sh.shape, F32),
        sds((rows, kvw)),
        sds((rows, heads * hd)),
        sds((rows, heads * hd)),
        sds((own, rank), F32),
        sds((own, dim)),
        sds((own, dim), F32),
        sds((rows, dim)),
        sds((rows, dim)),
    )
    out_specs = (ANY,) * 6 + (VMEM,) + (ANY,) * 3 + (VMEM,) * 3 + (ANY,) * 2
    dma = pltpu.SemaphoreType.DMA
    scratch = [
        pltpu.VMEM((seq_sh.shape[0] * ndp * NF, kvw), BF16),
        pltpu.VMEM((ndp * NF,) + gain_sh.shape, F32),
        pltpu.VMEM((qb.shape[0] * ndp, qb.shape[1]), BF16),
        pltpu.VMEM((out.shape[0] * ndp, out.shape[1]), BF16),
        pltpu.VMEM((rows, kvw), BF16),
        pltpu.VMEM((rows, heads * hd), BF16),
        pltpu.VMEM((rows, heads * hd), BF16),
        pltpu.VMEM((rows, dim), BF16),
        pltpu.VMEM((2, own, dim), BF16),
        pltpu.VMEM((own, dim), BF16),
        pltpu.VMEM((rows, dim), BF16),
        pltpu.VMEM((rows, dim), BF16),
        pltpu.VMEM((own, kvw), F32),
        dma((n_items, nz - 1)),
        dma((n_items, nz - 1)),
        dma((n_items, nz)),
        dma((n_items, nz)),
        dma((4, 3)),
        dma((4, 3)),
        dma((2, 3, ndp)),
        dma((2, 3, ndp)),
        dma((n_items + 10,)),
    ]
    return pl.pallas_call(
        functools.partial(forward_kernel, (ndp, own, dim, rank, hd, heads)),
        out_shape=out_shape,
        in_specs=(VMEM,) * 5 + (ANY,) * 7,
        out_specs=out_specs,
        scratch_shapes=scratch,
        compiler_params=pltpu.CompilerParams(
            collective_id=0, has_side_effects=True, vmem_limit_bytes=60 * 2**20
        ),
        name="gather_forward",
    )(tok, dout, cos, sin, bias, seq_sh, gain_sh, qb, out, gate, up, down)


class DpScatter:
    SLOTS = 4
    AHEAD = 2

    def __init__(self, pos, count, xbuf, zbuf, own, acc, xs, xr, zs, zr, ls, xcredit, zcredit):
        self.p, self.count = pos, count
        self.xbuf, self.zbuf, self.own, self.acc = xbuf, zbuf, own, acc
        self.xs, self.xr, self.zs, self.zr, self.ls = xs, xr, zs, zr, ls
        self.xcredit, self.zcredit = xcredit, zcredit
        self.items = []
        self.started = self.stepped = 0

    def add(self, src, base, in_vmem, out, pieces):
        rows, cols = out.shape
        r = rows // pieces
        for c in range(pieces):
            self.items.append((src, base, in_vmem, out, rows, cols, c * r, r))
        self.pump()

    def block(self, n, j, x):
        src, base, in_vmem, out, rows, cols, r0, r = self.items[n]
        return src.at[pl.ds(al(base + (j * 2 + x) * rows + r0, r), r)]

    def slot(self, buf, n):
        src, base, in_vmem, out, rows, cols, r0, r = self.items[n]
        return buf.at[n % self.SLOTS, :, pl.ds(0, r), pl.ds(0, cols)]

    def xcopy(self, n, j):
        return rcopy(
            self.block(n, j, 1 - self.p.x),
            self.slot(self.xbuf, n).at[j],
            self.xs.at[n % self.SLOTS, j],
            self.xr.at[n % self.SLOTS, j],
            self.p.to_pair,
        )

    def owncopy(self, n, j):
        return pltpu.make_async_copy(
            self.block(n, j, self.p.x), self.slot(self.own, n).at[j], self.ls.at[n % self.SLOTS, j]
        )

    def zcopy(self, n, k):
        return rcopy(
            self.slot(self.xbuf, n).at[self.p.zidx(k)],
            self.slot(self.zbuf, n).at[k - 1],
            self.zs.at[n % self.SLOTS, k - 1],
            self.zr.at[n % self.SLOTS, k - 1],
            self.p.to_z(k),
        )

    def outcopy(self, n):
        src, base, in_vmem, out, rows, cols, r0, r = self.items[n]
        return pltpu.make_async_copy(
            self.acc.at[n % self.SLOTS, pl.ds(0, r), pl.ds(0, cols)],
            out.at[pl.ds(r0, r)],
            self.ls.at[n % self.SLOTS, self.p.nz],
        )

    def pump(self):
        while self.started < min(len(self.items), self.stepped + self.AHEAD):
            n = self.started
            if n >= self.SLOTS:
                pl.semaphore_wait(self.xcredit, 1)
                for j in range(self.p.nz):
                    self.xcopy(n - self.SLOTS, j).wait_send()
            for j in range(self.p.nz):
                self.xcopy(n, j).start()
            for j in range(self.p.nz):
                self.owncopy(n, j).start()
            self.started += 1

    def tick(self, steps=1):
        for _ in range(steps):
            n = self.stepped
            if n >= self.started:
                return
            self.combine(n)
            if n >= 1:
                for k in range(1, self.p.nz):
                    self.zcopy(n - 1, k).wait_send()
                if n - 1 + self.SLOTS < self.count:
                    pl.semaphore_signal(
                        self.xcredit, inc=1, device_id=self.p.to_pair, device_id_type=MESH
                    )
            self.stepped += 1
            self.pump()
            if n >= 2:
                self.finish(n - 2)

    def combine(self, n):
        src, base, in_vmem, out, rows, cols, r0, r = self.items[n]
        p, s = self.p, n % self.SLOTS
        tile = 16
        for j in range(p.nz):
            self.xcopy(n, j).wait_recv()
        for j in range(p.nz):
            self.owncopy(n, j).wait()
        for k in range(1, p.nz):
            j = p.zidx(k)

            def add(t, _):
                t = pl.ds(al(t * tile, tile), tile)
                self.xbuf[s, j, t, :cols] = self.xbuf[s, j, t, :cols] + self.own[s, j, t, :cols]
                return 0

            lax.fori_loop(0, r // tile, add, 0)
            if n >= self.SLOTS:
                pl.semaphore_wait(self.zcredit.at[k - 1], 1)
            self.zcopy(n, k).start()
        if n >= self.SLOTS:
            self.outcopy(n - self.SLOTS).wait()

        def keep(t, _):
            t = pl.ds(al(t * tile, tile), tile)
            self.acc[s, t, :cols] = self.xbuf[s, p.z, t, :cols].astype(F32) + self.own[
                s, p.z, t, :cols
            ].astype(F32)
            return 0

        lax.fori_loop(0, r // tile, keep, 0)

    def finish(self, n):
        src, base, in_vmem, out, rows, cols, r0, r = self.items[n]
        p, s = self.p, n % self.SLOTS
        for k in range(1, p.nz):
            self.zcopy(n, k).wait_recv()
        tile = 16

        def add(t, _):
            t = pl.ds(al(t * tile, tile), tile)
            total = self.acc[s, t, :cols]
            for k in range(p.nz - 1):
                total = total + self.zbuf[s, k, t, :cols].astype(F32)
            self.acc[s, t, :cols] = total
            return 0

        lax.fori_loop(0, r // tile, add, 0)
        self.outcopy(n).start()
        if n + self.SLOTS < self.count:
            for k in range(1, p.nz):
                pl.semaphore_signal(
                    self.zcredit.at[k - 1], inc=1, device_id=p.to_z(-k), device_id_type=MESH
                )

    def drain(self):
        self.tick(self.count)
        last = self.count - 1
        for k in range(1, self.p.nz):
            self.zcopy(last, k).wait_send()
        self.finish(last - 1)
        self.finish(last)
        for n in range(max(0, self.count - self.SLOTS), self.count):
            self.outcopy(n).wait()
        for n in range(max(0, self.count - self.SLOTS), self.count):
            for j in range(self.p.nz):
                self.xcopy(n, j).wait_send()


def piece_rows(rows, nz):
    return min(rows, max(16, 256 // nz))


def backward_kernel(
    cfg,
    tok,
    dout,
    middle,
    latent,
    normed,
    gains,
    cos,
    sin,
    bias,
    gw_gate,
    gw_up,
    gw_down,
    gnt,
    lkv_h,
    q_h,
    mixed_h,
    qb_h,
    out_h,
    seq_h,
    o_gate,
    o_up,
    o_down,
    o_out,
    o_qb,
    o_seq,
    o_gain,
    o_in,
    gnt_v,
    fcore_v,
    fy_v,
    proj_v,
    gmid_v,
    gnorm_v,
    lkv_v,
    q_v,
    mixed_v,
    gm_v,
    kv_acc,
    qb_v,
    out_v,
    seq_v,
    seqy_v,
    gall_v,
    gain_rx,
    gain_acc,
    xbuf,
    zbuf,
    own_b,
    acc_b,
    xs,
    xr,
    zs,
    zr,
    dls,
    xcredit,
    zcredit,
    fss,
    frs,
    gs,
    gr,
    ls,
):
    ndp, own, dim, rank, hd, heads, pieces = cfg
    rows = NF * own
    t2 = own // 2
    kvw = rank + 2 * hd
    wide = dim // rank
    p = Place(ndp)
    nz = p.nz
    sr = o_seq.shape[0]
    local = []

    def local_copy(src, dst):
        c = pltpu.make_async_copy(src, dst, ls.at[len(local)])
        c.start()
        local.append(c)
        return c

    gnt_own = local_copy(gnt.at[pl.ds(al(p.f * own, own), own)], gnt_v.at[0])
    gnt_y = local_copy(gnt.at[pl.ds(al(p.f_y * own, own), own)], gnt_v.at[1])
    out_in = local_copy(out_h, out_v)
    mixed_in = local_copy(mixed_h, mixed_v)
    q_in = local_copy(q_h, q_v)
    lkv_in = local_copy(lkv_h, lkv_v)
    qb_in = local_copy(qb_h, qb_v)
    seq_in = local_copy(seq_h, seq_v)
    sc = DpScatter(
        p, sum(pieces), xbuf, zbuf, own_b, acc_b, xs, xr, zs, zr, dls, xcredit, zcredit
    )
    p.barrier()

    def gnt_block(b):
        return gnt.at[pl.ds(al(b * own, own), own)]

    red1 = FsReduce(p, gnt_block, fcore_v, fy_v, fss.at[0], frs.at[0])
    red1.start()
    sc.add(gw_gate, 0, False, o_gate, pieces[0])
    sc.add(gw_up, 0, False, o_up, pieces[1])
    sc.add(gw_down, 0, False, o_down, pieces[2])
    gnt_y.wait()
    gnt_own.wait()
    red1.c1().wait_recv()

    def add_y(t, _):
        r = pl.ds(al(t * 64, 64), 64)
        fcore_v[1, r, :] = fcore_v[1, r, :] + gnt_v[1, r, :]
        return 0

    lax.fori_loop(0, own // 64, add_y, 0)
    red1.cy().start()
    sc.tick(1)
    red1.end()
    red1.wait_sends()
    gain_two = jnp.concatenate([gains[wide + r : wide + r + 1] for r in range(wide)], axis=1)
    gain_one = jnp.concatenate([gains[r : r + 1] for r in range(wide)], axis=1)
    gain_lat = gains[2 * wide : 2 * wide + 1]
    part_two = jnp.zeros((1, dim), F32)
    for m in range(2):
        rr = pl.ds(m * t2, t2)
        e = gnt_v[0, rr, :].astype(F32) + fcore_v[0, rr, :].astype(F32) + fy_v[rr, :].astype(F32)
        v = middle[rr, :]
        inv = lax.rsqrt(jnp.mean(v * v, axis=-1, keepdims=True) + EPSILON)
        part_two += jnp.sum(e * v * inv, axis=0, keepdims=True)
        scaled = e * gain_two
        inner = jnp.mean(scaled * v, axis=-1, keepdims=True)
        g = dout[m].astype(F32) + inv * scaled - v * (inv * inv * inv * inner)
        gmid_v[rr, :] = g
        proj_v[pl.ds(al(p.f * own + m * t2, t2), t2), :] = g.astype(BF16)
    gain_acc[0] = jnp.zeros(gain_acc.shape[1:], F32)
    for r in range(wide):
        gain_acc[0, pl.ds(wide + r, 1), :] = part_two[:, r * rank : (r + 1) * rank]
    ag = FsGather(p, lambda b: proj_v.at[pl.ds(al(b * own, own), own)], fss.at[1], frs.at[1])
    ag.start()
    sc.tick(1)
    ag.mid()
    sc.tick(1)
    out_in.wait()
    ag.end()
    ag.wait_sends()

    def back_out(j, _):
        cols = pl.ds(al(j * 256, 256), 256)
        for r in range(rows // 512):
            rr = pl.ds(r * 512, 512)
            gm_v[rr, cols] = mm(proj_v[rr, :], out_v[:, cols]).astype(BF16)
        return 0

    lax.fori_loop(0, heads * hd // 256, back_out, 0)
    sc.tick(1)
    mixed_in.wait()

    def grad_out(j, _):
        cols = pl.ds(al(j * 256, 256), 256)
        out_v[cols, :] = mm_tn(proj_v[:, cols], mixed_v[...]).astype(BF16)
        return 0

    lax.fori_loop(0, dim // 256, grad_out, 0)
    sc.tick(1)
    sc.add(out_v, 0, True, o_out, pieces[3])
    q_in.wait()
    lkv_in.wait()
    scale = hd ** (-0.5)
    half = hd // 2
    kcols, vcols = slice(rank, rank + hd), slice(rank + hd, rank + 2 * hd)
    causal = causal_bias(PROMPT)
    everything = slice(None)

    for m in range(2):
        k0, k1 = (group_rows(lkv_v, m, h2, kcols, own) for h2 in (0, 1))
        v0, v1 = (group_rows(lkv_v, m, h2, vcols, own) for h2 in (0, 1))
        low = bias[m]
        kv_acc[...] = jnp.zeros(kv_acc.shape, F32)

        def put_query(h, which, g):
            co = group_rows(cos, m, which, everything, own)
            si = group_rows(sin, m, which, everything, own)
            a, b = g[:, :half] * scale, g[:, half:] * scale
            c0 = pl.ds(al(h * hd, half), half)
            c1 = pl.ds(al(h * hd + half, half), half)
            put_rows(gm_v, m, which, c0, own, (a * co + b * si).astype(BF16))
            put_rows(gm_v, m, which, c1, own, (b * co - a * si).astype(BF16))

        def attend_back(h, _):
            cols = pl.ds(al(h * hd, hd), hd)
            q0 = group_rows(q_v, m, 0, cols, own)
            g0 = group_rows(gm_v, m, 0, cols, own)
            pr = softmax_parts(mm_nt(q0, k0) * scale + causal)
            gp = mm_nt(g0, v0)
            gsc = (pr * (gp - jnp.sum(pr * gp, axis=-1, keepdims=True))).astype(BF16)
            kv_acc[2] += mm_tn(pr.astype(BF16), g0)
            kv_acc[0] += mm_tn(gsc, q0)
            put_query(h, 0, mm(gsc, k0))
            q1 = group_rows(q_v, m, 1, cols, own)
            g1 = group_rows(gm_v, m, 1, cols, own)
            s0 = mm_nt(q1, k0) * scale
            s1 = mm_nt(q1, k1) * scale + low
            top = jnp.maximum(
                jnp.max(s0, axis=-1, keepdims=True), jnp.max(s1, axis=-1, keepdims=True)
            )
            e0, e1 = jnp.exp(s0 - top), jnp.exp(s1 - top)
            total = jnp.sum(e0, axis=-1, keepdims=True) + jnp.sum(e1, axis=-1, keepdims=True)
            p0, p1 = e0 / total, e1 / total
            gp0, gp1 = mm_nt(g1, v0), mm_nt(g1, v1)
            inner = jnp.sum(p0 * gp0, axis=-1, keepdims=True) + jnp.sum(
                p1 * gp1, axis=-1, keepdims=True
            )
            gs0 = (p0 * (gp0 - inner)).astype(BF16)
            gs1 = (p1 * (gp1 - inner)).astype(BF16)
            kv_acc[2] += mm_tn(p0.astype(BF16), g1)
            kv_acc[3] += mm_tn(p1.astype(BF16), g1)
            kv_acc[0] += mm_tn(gs0, q1)
            kv_acc[1] += mm_tn(gs1, q1)
            put_query(h, 1, mm(gs0, k0) + mm(gs1, k1))
            return 0

        lax.fori_loop(0, heads, attend_back, 0)
        for h2 in (0, 1):
            put_rows(proj_v, m, h2, kcols, own, (kv_acc[h2] * scale).astype(BF16))
            put_rows(proj_v, m, h2, vcols, own, kv_acc[2 + h2].astype(BF16))
        sc.tick(1)
    qb_in.wait()

    def back_latent(j, _):
        wr = pl.ds(al(j * 256, 256), 256)
        for r in range(rows // 512):
            rr = pl.ds(r * 512, 512)
            proj_v[rr, wr] = mm_nt(gm_v[rr, :], qb_v[wr, :]).astype(BF16)
        return 0

    lax.fori_loop(0, rank // 256, back_latent, 0)

    def grad_qb(j, _):
        cols = pl.ds(al(j * 256, 256), 256)
        qb_v[cols, :] = mm_tn(lkv_v[:, cols], gm_v[...]).astype(BF16)
        return 0

    lax.fori_loop(0, rank // 256, grad_qb, 0)
    narrow = pl.ds(0, kvw)
    red2 = FsReduce(
        p,
        lambda b: proj_v.at[pl.ds(al(b * own, own), own), narrow],
        fcore_v.at[:, :, narrow],
        fy_v.at[:, narrow],
        fss.at[2],
        frs.at[2],
    )
    red2.start()
    sc.tick(1)
    sc.add(qb_v, 0, True, o_qb, pieces[4])
    red2.mid(own)
    sc.tick(1)
    red2.end()
    own_rows = pl.ds(al(p.f * own, own), own)
    part_lat = jnp.zeros((1, rank), F32)
    for m in range(2):
        rr = pl.ds(m * t2, t2)
        gr_rows = pl.ds(al(p.f * own + m * t2, t2), t2)
        e = red2.value(rr)
        v = latent[rr, :]
        inv = lax.rsqrt(jnp.mean(v * v, axis=-1, keepdims=True) + EPSILON)
        el = e[:, :rank]
        part_lat += jnp.sum(el * v * inv, axis=0, keepdims=True)
        scaled = el * gain_lat
        inner = jnp.mean(scaled * v, axis=-1, keepdims=True)
        gall_v[rr, :rank] = (inv * scaled - v * (inv * inv * inv * inner)).astype(BF16)
        co, si = cos[gr_rows, :], sin[gr_rows, :]
        a, b = e[:, rank : rank + half], e[:, rank + half : rank + hd]
        gall_v[rr, rank : rank + half] = (a * co + b * si).astype(BF16)
        gall_v[rr, rank + half : rank + hd] = (b * co - a * si).astype(BF16)
        gall_v[rr, rank + hd :] = e[:, rank + hd :].astype(BF16)
    gain_acc[0, pl.ds(2 * wide, 1), :] = part_lat
    seq_in.wait()

    def back_seq(j, _):
        wr = pl.ds(al(j * 256, 256), 256)
        gnorm_v[:, wr] = mm_nt(gall_v[...], seq_v[wr, :])
        return 0

    lax.fori_loop(0, dim // 256, back_seq, 0)
    sc.tick(1)
    span = NF * sr

    def grad_seq(j, _):
        cols = pl.ds(al(j * 256, 256), 256)
        g = mm_tn(normed[:, cols], gall_v[...]).astype(BF16)
        for i in range(256 // span):
            for fb in range(NF):
                seq_v[pl.ds(al(fb * ndp * sr + (j * (256 // span) + i) * sr, sr), sr), :] = g[
                    i * span + fb * sr : i * span + (fb + 1) * sr
                ]
        return 0

    lax.fori_loop(0, dim // 256, grad_seq, 0)
    srows = ndp * sr
    core3 = [lkv_v.at[pl.ds(0, srows)], lkv_v.at[pl.ds(srows, srows)]]

    def sblock(b):
        return seq_v.at[pl.ds(al(b * srows, srows), srows)]

    c1 = rcopy(sblock(p.f_yc), core3[1], fss.at[3, 1], frs.at[3, 1], p.to_core)
    c0 = rcopy(sblock(p.f_core), core3[0], fss.at[3, 0], frs.at[3, 0], p.to_core)
    cy = rcopy(core3[1], seqy_v, fss.at[3, 2], frs.at[3, 2], p.to_y)
    c1.start()
    c0.start()
    part_one = jnp.zeros((1, dim), F32)
    for m in range(2):
        rr = pl.ds(m * t2, t2)
        e = gnorm_v[rr, :]
        v = tok[m].astype(F32)
        inv = lax.rsqrt(jnp.mean(v * v, axis=-1, keepdims=True) + EPSILON)
        part_one += jnp.sum(e * v * inv, axis=0, keepdims=True)
        scaled = e * gain_one
        inner = jnp.mean(scaled * v, axis=-1, keepdims=True)
        o_in[m] = (gmid_v[rr, :] + inv * scaled - v * (inv * inv * inv * inner)).astype(BF16)
    for r in range(wide):
        gain_acc[0, pl.ds(r, 1), :] = part_one[:, r * rank : (r + 1) * rank]
    gain_steps = [
        rcopy(gain_acc.at[0], gain_rx.at[0], gs.at[0], gr.at[0], p.to_core),
        rcopy(gain_acc.at[1], gain_rx.at[1], gs.at[1], gr.at[1], p.to_y),
        rcopy(gain_acc.at[2], gain_rx.at[2], gs.at[2], gr.at[2], p.to_pair),
    ] + [
        rcopy(gain_acc.at[3], gain_rx.at[2 + k], gs.at[2 + k], gr.at[2 + k], p.to_z(k))
        for k in range(1, nz)
    ]
    gain_steps[0].start()
    c1.wait_recv()

    def seq_y(t, _):
        t = al(t * 64, 64)
        a = pl.ds(srows + t, 64)
        b = pl.ds(al(p.f_y * srows + t, 64), 64)
        lkv_v[a, :] = lkv_v[a, :] + seq_v[b, :]
        return 0

    lax.fori_loop(0, srows // 64, seq_y, 0)
    cy.start()
    for n in range(3):
        gain_steps[n].wait_recv()
        gain_acc[n + 1] = gain_acc[n] + gain_rx[n]
        if n < 2:
            gain_steps[n + 1].start()
        else:
            for k in range(1, nz):
                gain_steps[2 + k].start()
        sc.tick(1)
    c0.wait_recv()
    cy.wait_recv()

    def seq_f(t, _):
        t = al(t * 64, 64)
        a = pl.ds(t, 64)
        b = pl.ds(al(p.f * srows + t, 64), 64)
        seq_v[b, :] = (
            lkv_v[a, :].astype(F32) + seq_v[b, :].astype(F32) + seqy_v[a, :].astype(F32)
        ).astype(BF16)
        return 0

    lax.fori_loop(0, srows // 64, seq_f, 0)
    sc.add(seq_v, p.f * srows, True, o_seq, pieces[5])
    total = gain_acc[3]
    for k in range(1, nz):
        gain_steps[2 + k].wait_recv()
        total = total + gain_rx[2 + k]
    o_gain[...] = total
    sc.drain()
    red2.wait_sends()
    for t in [c1, c0, cy] + gain_steps:
        t.wait_send()


def backward_call(ndp, tok, dout, middle, latent, normed, gains, cos, sin, bias, grads, gnt, saved):
    lkv, q, mixed, qb, out, seq = saved
    nz = ndp // 2
    own, dim = middle.shape
    rank = latent.shape[1]
    kvw = lkv.shape[1]
    hd = (kvw - rank) // 2
    heads = q.shape[1] // hd
    rows = NF * own
    sr = seq.shape[0] // (ndp * NF)
    shards = [(w.shape[0] // ndp, w.shape[1]) for w in grads] + [
        (out.shape[0] // ndp, out.shape[1]),
        (qb.shape[0] // ndp, qb.shape[1]),
        (sr, kvw),
    ]
    pieces = tuple(s[0] // piece_rows(s[0], nz) for s in shards)
    n = sum(pieces)
    slots = DpScatter.SLOTS
    pr = max(piece_rows(s[0], nz) for s in shards)
    width = max(s[1] for s in shards)
    dma = pltpu.SemaphoreType.DMA
    scratch = [
        pltpu.VMEM((2, own, dim), BF16),
        pltpu.VMEM((2, own, dim), BF16),
        pltpu.VMEM((own, dim), BF16),
        pltpu.VMEM((rows, dim), BF16),
        pltpu.VMEM((own, dim), F32),
        pltpu.VMEM((own, dim), F32),
        pltpu.VMEM(lkv.shape, BF16),
        pltpu.VMEM(q.shape, BF16),
        pltpu.VMEM(mixed.shape, BF16),
        pltpu.VMEM(q.shape, BF16),
        pltpu.VMEM((4, rows // 4, hd), F32),
        pltpu.VMEM(qb.shape, BF16),
        pltpu.VMEM(out.shape, BF16),
        pltpu.VMEM(seq.shape, BF16),
        pltpu.VMEM((ndp * sr, kvw), BF16),
        pltpu.VMEM((own, kvw), BF16),
        pltpu.VMEM((2 + nz,) + gains.shape, F32),
        pltpu.VMEM((4,) + gains.shape, F32),
        pltpu.VMEM((slots, nz, pr, width), BF16),
        pltpu.VMEM((slots, nz - 1, pr, width), BF16),
        pltpu.VMEM((slots, nz, pr, width), BF16),
        pltpu.VMEM((slots, pr, width), F32),
        dma((slots, nz)),
        dma((slots, nz)),
        dma((slots, nz - 1)),
        dma((slots, nz - 1)),
        dma((slots, nz + 1)),
        pltpu.SemaphoreType.REGULAR,
        pltpu.SemaphoreType.REGULAR((nz - 1,)),
        dma((4, 3)),
        dma((4, 3)),
        dma((2 + nz,)),
        dma((2 + nz,)),
        dma((8,)),
    ]
    return pl.pallas_call(
        functools.partial(backward_kernel, (ndp, own, dim, rank, hd, heads, pieces)),
        out_shape=tuple(jax.ShapeDtypeStruct(s, F32) for s in shards)
        + (jax.ShapeDtypeStruct(gains.shape, F32), jax.ShapeDtypeStruct(tok.shape, BF16)),
        in_specs=(VMEM,) * 9 + (ANY,) * 10,
        out_specs=(ANY,) * 6 + (VMEM,) * 2,
        scratch_shapes=scratch,
        compiler_params=pltpu.CompilerParams(
            collective_id=1, has_side_effects=True, vmem_limit_bytes=62 * 2**20
        ),
        name="backward_scatter",
    )(tok, dout, middle, latent, normed, gains, cos, sin, bias, *grads, gnt, lkv, q, mixed, qb, out, seq)


def per_device(
    ndp,
    tokens,
    membership,
    d_output,
    gain_attn,
    w_qa,
    gain_latent,
    w_qb,
    w_key,
    w_value,
    w_out,
    gain_ffn,
    w_gate,
    w_up,
    w_down,
):
    micro, tlen, dim = tokens.shape
    own = micro * tlen
    rank = w_qa.shape[1]
    hd = w_key.shape[1]
    heads = w_qb.shape[1] // hd
    rows = NF * own
    wide = dim // rank
    labels, positions = jax.vmap(lambda r: layout(r, BLK))(membership[0])
    pos_rows = positions.reshape(micro, NF, tlen).transpose(1, 0, 2).reshape(rows)
    cos, sin = rope_tables(pos_rows, hd)
    tail = labels[:, PROMPT:]
    idx = jnp.arange(tail.shape[1], dtype=jnp.int32)
    seen = (idx[None, None, :] <= idx[None, :, None]) & (tail[:, None, :] == tail[:, :, None])
    bias = jnp.where(seen, 0.0, MASK_FILL).astype(F32)
    block = lax.axis_index("dp") * NF + lax.axis_index("fsdp")

    def spot(gain):
        width = gain.shape[0]
        count = ndp * NF
        at = lax.broadcasted_iota(jnp.int32, (count, width), 0) == block
        placed = jnp.where(at, gain.astype(F32)[None, :], 0.0)
        return placed.reshape(count * width // rank, rank)

    gain_sh = jnp.concatenate([spot(gain_attn), spot(gain_ffn), spot(gain_latent)], axis=0)
    gain_sh = jnp.pad(gain_sh, ((0, 8 - gain_sh.shape[0]), (0, 0)))
    seq_sh = jnp.concatenate([w_qa, w_key, w_value], axis=1)
    (
        qb_all,
        out_all,
        gate_all,
        up_all,
        down_all,
        seq_all,
        gains,
        lkv,
        q_all,
        mixed,
        latent,
        normed,
        middle,
        n2,
        d_all,
    ) = forward_call(
        ndp, tokens, d_output, cos, sin, bias, seq_sh, gain_sh, w_qb, w_out, w_gate, w_up, w_down
    )
    gate = jnp.dot(n2, gate_all, preferred_element_type=F32)
    up = jnp.dot(n2, up_all, preferred_element_type=F32)
    sig = jax.nn.sigmoid(gate)
    hidden = (gate * sig * up).astype(BF16)
    grad_hidden = jnp.dot(d_all, down_all, preferred_element_type=F32)
    grad_gate = (grad_hidden * up * sig * (1.0 + gate * (1.0 - sig))).astype(BF16)
    grad_up = (grad_hidden * gate * sig).astype(BF16)
    ffn_part = mm_nt(hidden, down_all).astype(BF16)
    gnt_part = (mm_nt(grad_gate, gate_all) + mm_nt(grad_up, up_all)).astype(BF16)
    gw_down = mm_tn(d_all, hidden).astype(BF16)
    gw_gate = mm_tn(n2, grad_gate).astype(BF16)
    gw_up = mm_tn(n2, grad_up).astype(BF16)

    ffn_own = lax.psum_scatter(ffn_part, "fsdp", scatter_dimension=0, tiled=True).astype(F32)
    output = (middle + ffn_own).astype(BF16).reshape(tokens.shape)
    o_gate, o_up, o_down, o_out, o_qb, o_seq, o_gain, input_grad = backward_call(
        ndp,
        tokens,
        d_output,
        middle,
        latent,
        normed,
        gains,
        cos,
        sin,
        bias,
        (gw_gate, gw_up, gw_down),
        gnt_part,
        (lkv, q_all, mixed, qb_all, out_all, seq_all),
    )

    def own_gain(flat, width):
        return lax.dynamic_slice_in_dim(flat.reshape(-1), block * width, width, 0)

    return (
        output,
        input_grad,
        own_gain(o_gain[:wide], gain_attn.shape[0]),
        o_seq[:, :rank],
        own_gain(o_gain[2 * wide], gain_latent.shape[0]),
        o_qb,
        o_seq[:, rank : rank + hd],
        o_seq[:, rank + hd :],
        o_out,
        own_gain(o_gain[wide : 2 * wide], gain_ffn.shape[0]),
        o_gate,
        o_up,
        o_down,
    )


def solution(mesh):
    both = ("dp", "fsdp")
    rowwise, vector = P(both, None), P(both)
    tok = P(None, both, None)
    head = P("dp", "fsdp")
    return jax.shard_map(
        functools.partial(per_device, mesh.shape["dp"]),
        mesh=mesh,
        in_specs=(
            tok,
            P("dp", None, None),
            tok,
            vector,
            rowwise,
            vector,
            head,
            rowwise,
            rowwise,
            head,
            vector,
            head,
            head,
            head,
        ),
        out_specs=(
            tok,
            tok,
            vector,
            rowwise,
            vector,
            head,
            rowwise,
            rowwise,
            head,
            vector,
            head,
            head,
            head,
        ),
        check_vma=False,
    )
```

```python
import functools

import jax
import jax.numpy as jnp
from jax import lax
from jax.experimental import pallas as pl
from jax.experimental.pallas import tpu as pltpu
from jax.sharding import PartitionSpec as P

BLK = 32
PROMPT = 256
EPSILON = 1e-05
ROPE_BASE = 10000.0
MASK_FILL = -1e30
F32 = jnp.float32
BF16 = jnp.bfloat16
MESH = pl.DeviceIdType.MESH
ANY = pl.BlockSpec(memory_space=pl.ANY)
VMEM = pl.BlockSpec(memory_space=pltpu.VMEM)
NF = 4
GATHER_ROWS = 64
GATHER_AHEAD = 4
FFN_ROWS = 128
FFN_COLS = 512


def ffn_chunks(cols):
    return [(c, min(FFN_COLS, cols - c)) for c in range(0, cols, FFN_COLS)]


def layout(member_row, block_len):
    count_blocks = member_row.shape[0]
    block_ids = jnp.arange(count_blocks, dtype=jnp.int32)
    same_run = (member_row[None, :] == member_row[:, None]) & (
        block_ids[None, :] < block_ids[:, None]
    )
    earlier = jnp.sum(same_run.astype(jnp.int32), axis=1)
    prompt_len = jnp.sum((member_row == 0).astype(jnp.int32)) * block_len
    labels = jnp.repeat(member_row, block_len)
    within = jnp.arange(count_blocks * block_len, dtype=jnp.int32) % block_len
    positions = (
        (labels > 0).astype(jnp.int32) * prompt_len
        + jnp.repeat(earlier, block_len) * block_len
        + within
    )
    return (labels, positions)


def rope_tables(positions, head_width):
    half_width = head_width // 2
    frequency = ROPE_BASE ** (-(jnp.arange(half_width, dtype=jnp.float32) * (2.0 / head_width)))
    angles = positions.astype(jnp.float32)[:, None] * frequency[None, :]
    return (jnp.cos(angles), jnp.sin(angles))


def al(x, n):
    return pl.multiple_of(x, n)


def mm(a, b):
    return lax.dot_general(a, b, (((1,), (0,)), ((), ())), preferred_element_type=F32)


def mm_nt(a, b):
    return lax.dot_general(a, b, (((1,), (1,)), ((), ())), preferred_element_type=F32)


def mm_tn(a, b):
    return lax.dot_general(a, b, (((0,), (0,)), ((), ())), preferred_element_type=F32)


class Place:
    def __init__(self, ndp):
        self.ndp = ndp
        self.bits = [1 << b for b in range(ndp.bit_length() - 1)]
        self.me = lax.axis_index("dp")
        self.f = lax.axis_index("fsdp")
        y, c = self.f // 2, self.f % 2
        self.f_core = y * 2 + 1 - c
        self.f_y = (1 - y) * 2 + c
        self.f_yc = (1 - y) * 2 + 1 - c
        self.to_core = (self.me, self.f_core)
        self.to_y = (self.me, self.f_y)

    def at(self, mask):
        j = self.me
        for b in self.bits:
            if mask & b:
                j = j + b - 2 * b * ((self.me // b) % 2)
        return j

    def to_dp(self, mask):
        return (self.at(mask), self.f)

    def orders(self, swapped):
        o = list(self.bits)
        if swapped and len(o) > 1:
            o[0], o[1] = o[1], o[0]
        return o

    def barrier(self):
        bar = pltpu.get_barrier_semaphore()
        devs = [self.to_dp(b) for b in self.bits] + [self.to_core, self.to_y]
        for d in devs:
            pl.semaphore_signal(bar, inc=1, device_id=d, device_id_type=MESH)
        pl.semaphore_wait(bar, len(devs))


def rcopy(src, dst, ss, rs, dev):
    return pltpu.make_async_remote_copy(
        src_ref=src, dst_ref=dst, send_sem=ss, recv_sem=rs, device_id=dev, device_id_type=MESH
    )


class DpGather:
    def __init__(self, pos, ss, rs):
        self.p, self.ss, self.rs = pos, ss, rs
        self.items, self.events = [], []
        self.launched = self.seen = 0

    def add(self, src, dst, swapped=False):
        self.items.append((src, dst, self.p.orders(swapped)[::-1]))
        return len(self.items) - 1

    def copy(self, n, mask, stage):
        src, dst, order = self.items[n]
        j = self.p.at(mask)
        k = self.index(n, mask | order[stage])
        return rcopy(
            src if mask == 0 else dst(j),
            dst(j),
            self.ss.at[n, k],
            self.rs.at[n, k],
            self.p.to_dp(order[stage]),
        )

    def index(self, n, mask):
        return mask - 1

    def stage_of(self, n, mask):
        return max(i for i, b in enumerate(self.items[n][2]) if mask & b)

    def arrived(self, n, mask):
        src, dst, order = self.items[n]
        stage = self.stage_of(n, mask)
        j = self.p.at(mask)
        k = self.index(n, mask)
        rcopy(src, dst(j), self.ss.at[n, k], self.rs.at[n, k], self.p.to_dp(order[stage])).wait_recv()

    def launch(self):
        if self.launched < len(self.items):
            n = self.launched
            for stage in range(len(self.p.bits)):
                self.copy(n, 0, stage).start()
            self.launched += 1

    def masks(self, n):
        order = self.items[n][2]
        last = order[-1]
        out = [m for m in range(1, self.p.ndp) if not m & last]
        return sorted(out, key=lambda m: (self.stage_of(n, m), m))

    def forward(self, n):
        for m in self.masks(n):
            self.arrived(n, m)
            for stage in range(self.stage_of(n, m) + 1, len(self.p.bits)):
                self.copy(n, m, stage).start()

    def steps(self, count, ahead):
        for _ in range(count):
            if self.seen >= len(self.items):
                return
            while self.launched < min(len(self.items), self.seen + ahead):
                self.launch()
            self.forward(self.seen)
            self.seen += 1

    def wait_last(self, n):
        last = self.items[n][2][-1]
        for m in range(self.p.ndp):
            if m & last:
                self.arrived(n, m)

    def wait_sends(self, n):
        for m in range(self.p.ndp):
            first = 0 if m == 0 else self.stage_of(n, m) + 1
            for stage in range(first, len(self.p.bits)):
                self.copy(n, m, stage).wait_send()


class FsGather:
    def __init__(self, pos, blocks, ss, rs):
        self.p, self.b, self.ss, self.rs = pos, blocks, ss, rs

    def copy(self, n, fb, dev):
        return rcopy(self.b(fb), self.b(fb), self.ss.at[n], self.rs.at[n], dev)

    def start(self):
        self.copy(1, self.p.f, self.p.to_y).start()
        self.copy(0, self.p.f, self.p.to_core).start()

    def mid(self):
        self.copy(1, self.p.f_y, self.p.to_y).wait_recv()
        self.copy(2, self.p.f_y, self.p.to_core).start()

    def end(self):
        self.copy(0, self.p.f_core, self.p.to_core).wait_recv()
        self.copy(2, self.p.f_yc, self.p.to_core).wait_recv()

    def wait_sends(self):
        self.copy(1, self.p.f, self.p.to_y).wait_send()
        self.copy(0, self.p.f, self.p.to_core).wait_send()
        self.copy(2, self.p.f_y, self.p.to_core).wait_send()


class FsReduce:
    def __init__(self, pos, blocks, from_core, from_y, ss, rs):
        self.p, self.b, self.fc, self.fy, self.ss, self.rs = pos, blocks, from_core, from_y, ss, rs

    def c1(self):
        return rcopy(
            self.b(self.p.f_yc), self.fc.at[1], self.ss.at[1], self.rs.at[1], self.p.to_core
        )

    def c0(self):
        return rcopy(
            self.b(self.p.f_core), self.fc.at[0], self.ss.at[0], self.rs.at[0], self.p.to_core
        )

    def cy(self):
        return rcopy(self.fc.at[1], self.fy, self.ss.at[2], self.rs.at[2], self.p.to_y)

    def start(self):
        self.c1().start()
        self.c0().start()

    def mid(self, rows, tile=64):
        self.c1().wait_recv()
        mine = self.b(self.p.f_y)

        def add(t, _):
            r = pl.ds(al(t * tile, tile), tile)
            self.fc[1, r, :] = (self.fc[1, r, :].astype(F32) + mine[r, :].astype(F32)).astype(BF16)
            return 0

        lax.fori_loop(0, rows // tile, add, 0)
        self.cy().start()

    def end(self):
        self.c0().wait_recv()
        self.cy().wait_recv()

    def value(self, r):
        return (
            self.b(self.p.f)[r, :].astype(F32)
            + self.fc[0, r, :].astype(F32)
            + self.fy[r, :].astype(F32)
        )

    def wait_sends(self):
        self.c1().wait_send()
        self.c0().wait_send()
        self.cy().wait_send()


def softmax_parts(scores):
    top = jnp.max(scores, axis=-1, keepdims=True)
    lifted = jnp.exp(scores - top)
    return lifted / jnp.sum(lifted, axis=-1, keepdims=True)


def causal_bias(rows):
    r = lax.broadcasted_iota(jnp.int32, (rows, rows), 0)
    c = lax.broadcasted_iota(jnp.int32, (rows, rows), 1)
    return jnp.where(c <= r, 0.0, MASK_FILL).astype(F32)


def group_rows(ref, m, half, cols, own):
    t = own // 2
    first = ref[pl.ds((2 * half) * own + m * t, t), cols]
    second = ref[pl.ds((2 * half + 1) * own + m * t, t), cols]
    return jnp.concatenate([first, second], axis=0)


def put_rows(ref, m, half, cols, own, value):
    t = own // 2
    ref[pl.ds((2 * half) * own + m * t, t), cols] = value[:t]
    ref[pl.ds((2 * half + 1) * own + m * t, t), cols] = value[t:]


def forward_kernel(
    cfg,
    tok,
    dout,
    cos,
    sin,
    bias,
    seq_sh,
    gain_sh,
    qb_sh,
    out_sh,
    gate_sh,
    up_sh,
    down_sh,
    qb_all,
    out_all,
    gate_all,
    up_all,
    down_all,
    seq_all,
    gain_sum,
    lkv_o,
    q_o,
    mixed_o,
    latent_o,
    normed_o,
    middle_o,
    hid_o,
    gg_o,
    gu_o,
    gw_gate,
    gw_up,
    gw_down,
    seq_v,
    gain_v,
    qb_v,
    out_v,
    lkv_v,
    q_v,
    mixed_v,
    part_v,
    fcore_v,
    fy_v,
    n2_v,
    d_v,
    n2_t,
    d_t,
    lat_v,
    gss,
    grs,
    fss,
    frs,
    sys_,
    syr,
    ls,
    ffn_ls,
):
    ndp, own, dim, rank, hd, heads = cfg
    rows = NF * own
    p = Place(ndp)
    kvw = rank + 2 * hd
    sr = seq_sh.shape[0]
    g = DpGather(p, gss, grs)
    i_seq = g.add(seq_sh, lambda j: seq_v.at[pl.ds(al((j * NF + p.f) * sr, sr), sr)])
    i_gain = g.add(gain_sh, lambda j: gain_v.at[j * NF + p.f])
    turn = [0]

    def weight_items(src, dst, cols=slice(None), most=GATHER_ROWS):
        n = src.shape[0]
        step = min(n, most)
        out = []
        for c in range(n // step):
            turn[0] += 1
            out.append(
                g.add(
                    src.at[pl.ds(c * step, step), cols],
                    lambda j, c=c: dst.at[pl.ds(al(j * n + c * step, step), step), cols],
                    turn[0] % 4 == 0,
                )
            )
        return out

    i_qb = weight_items(qb_sh, qb_v)
    i_out = weight_items(out_sh, out_v)
    i_ffn = []
    for c0, cw in ffn_chunks(gate_sh.shape[1]):
        cols = pl.ds(c0, cw)
        some = []
        for s, d in ((gate_sh, gate_all), (up_sh, up_all), (down_sh, down_all)):
            some += weight_items(s, d, cols, FFN_ROWS)
        i_ffn.append(some)
    order = range(len(g.items))
    fs_d = FsGather(p, lambda b: d_v.at[pl.ds(al(b * own, own), own)], fss.at[0], frs.at[0])
    fs_l = FsGather(p, lambda b: lkv_v.at[pl.ds(al(b * own, own), own)], fss.at[1], frs.at[1])
    fs_n = FsGather(p, lambda b: n2_v.at[pl.ds(al(b * own, own), own)], fss.at[2], frs.at[2])
    red = FsReduce(
        p, lambda b: part_v.at[pl.ds(al(b * own, own), own)], fcore_v, fy_v, fss.at[3], frs.at[3]
    )

    local = []

    def local_copy(src, dst):
        c = pltpu.make_async_copy(src, dst, ls.at[len(local)])
        c.start()
        local.append(c)
        return c

    own_copies = {}
    for i in order:
        src, dst, _ = g.items[i]
        own_copies[i] = local_copy(src, dst(p.me))
    d_copies = [
        local_copy(dout.at[m], d_v.at[pl.ds(al(p.f * own + m * (own // 2), 128), own // 2)])
        for m in range(2)
    ]

    p.barrier()
    for _ in range(GATHER_AHEAD):
        g.launch()
    npiece = ndp

    def seq_piece(j, fb):
        return seq_v.at[pl.ds(al((j * NF + fb) * sr, sr), sr)]

    def seq_copy(t, j, fb, dev, which):
        b = seq_piece(j, fb) if which == 0 else gain_v.at[j * NF + fb]
        return rcopy(b, b, sys_.at[which, t, j], syr.at[which, t, j], dev)

    def spread(j):
        for which in (0, 1):
            seq_copy(1, j, p.f, p.to_y, which).start()
            seq_copy(0, j, p.f, p.to_core, which).start()

    for m in range(2):
        x = tok[m].astype(F32)
        inv = lax.rsqrt(jnp.mean(x * x, axis=-1, keepdims=True) + EPSILON)
        middle_o[pl.ds(m * (own // 2), own // 2), :] = x * inv
    own_copies[i_seq].wait()
    own_copies[i_gain].wait()
    spread(p.me)
    for m in sorted(range(1, ndp), key=lambda m: g.stage_of(i_seq, m)):
        for i in (i_seq, i_gain):
            g.arrived(i, m)
            for stage in range(g.stage_of(i, m) + 1, len(p.bits)):
                g.copy(i, m, stage).start()
        spread(p.at(m))
    g.seen = 2
    for c in d_copies:
        c.wait()

    def spread_forward(j, _):
        for which in (0, 1):
            seq_copy(1, j, p.f_y, p.to_y, which).wait_recv()
            seq_copy(2, j, p.f_y, p.to_core, which).start()
        return 0

    def tick(n):
        g.steps(n, GATHER_AHEAD)

    tick(1)
    lax.fori_loop(0, npiece, spread_forward, 0)
    fs_d.start()
    tick(1)

    def spread_end(j, _):
        for which in (0, 1):
            seq_copy(0, j, p.f_core, p.to_core, which).wait_recv()
            seq_copy(2, j, p.f_yc, p.to_core, which).wait_recv()
        return 0

    lax.fori_loop(0, npiece, spread_end, 0)

    def gain_add(j, acc):
        return acc + gain_v[j]

    gains = lax.fori_loop(0, ndp * NF, gain_add, jnp.zeros(gain_v.shape[1:], F32))
    gain_sum[...] = gains
    wide = dim // rank
    gain_one = jnp.concatenate([gains[r : r + 1] for r in range(wide)], axis=1)
    gain_two = jnp.concatenate([gains[wide + r : wide + r + 1] for r in range(wide)], axis=1)
    gain_lat = gains[2 * wide : 2 * wide + 1]
    normed_o[...] = (middle_o[...] * gain_one).astype(BF16)
    seq_out = local_copy(seq_v, seq_all)

    def project(j, _):
        cols = pl.ds(al(j * 256, 256), 256)
        lat_v[:, cols] = mm(normed_o[...], seq_v[:, cols])
        return 0

    lax.fori_loop(0, kvw // 256, project, 0)
    own_rows = pl.ds(al(p.f * own, own), own)
    lat = lat_v[:, :rank]
    latent_o[...] = lat
    inv_lat = lax.rsqrt(jnp.mean(lat * lat, axis=-1, keepdims=True) + EPSILON)
    lkv_v[own_rows, :rank] = (lat * inv_lat * gain_lat).astype(BF16)
    half = hd // 2
    co, si = cos[own_rows, :], sin[own_rows, :]
    ka, kb = lat_v[:, rank : rank + half], lat_v[:, rank + half : rank + hd]
    lkv_v[own_rows, rank : rank + half] = (ka * co - kb * si).astype(BF16)
    lkv_v[own_rows, rank + half : rank + hd] = (kb * co + ka * si).astype(BF16)
    lkv_v[own_rows, rank + hd :] = lat_v[:, rank + hd :].astype(BF16)
    fs_l.start()
    tick(1)
    fs_d.mid()
    fs_l.mid()
    tick(1)
    for i in i_qb:
        own_copies[i].wait()
        g.wait_last(i)
    fs_l.end()
    qb_out = local_copy(qb_v, qb_all)
    lkv_out = local_copy(lkv_v, lkv_o)

    def query(j, _):
        cols = pl.ds(al(j * hd, hd), hd)
        c0 = pl.ds(al(j * hd, half), half)
        c1 = pl.ds(al(j * hd + half, half), half)
        for r in range(rows // 512):
            rr = pl.ds(r * 512, 512)
            acc = mm(lkv_v[rr, :rank], qb_v[:, cols])
            a, b = acc[:, :half], acc[:, half:]
            c, s = cos[rr, :], sin[rr, :]
            q_v[rr, c0] = (a * c - b * s).astype(BF16)
            q_v[rr, c1] = (b * c + a * s).astype(BF16)
        return 0

    lax.fori_loop(0, heads, query, 0)
    q_out = local_copy(q_v, q_o)
    tick(1)
    scale = hd ** (-0.5)
    kcols, vcols = slice(rank, rank + hd), slice(rank + hd, rank + 2 * hd)
    causal = causal_bias(PROMPT)
    for m in range(2):
        k0, k1 = (group_rows(lkv_v, m, h2, kcols, own) for h2 in (0, 1))
        v0, v1 = (group_rows(lkv_v, m, h2, vcols, own) for h2 in (0, 1))
        low = bias[m]

        def attend(h, _):
            cols = pl.ds(al(h * hd, hd), hd)
            q0 = group_rows(q_v, m, 0, cols, own)
            pr = softmax_parts(mm_nt(q0, k0) * scale + causal).astype(BF16)
            put_rows(mixed_v, m, 0, cols, own, mm(pr, v0).astype(BF16))
            q1 = group_rows(q_v, m, 1, cols, own)
            s0 = mm_nt(q1, k0) * scale
            s1 = mm_nt(q1, k1) * scale + low
            top = jnp.maximum(
                jnp.max(s0, axis=-1, keepdims=True), jnp.max(s1, axis=-1, keepdims=True)
            )
            e0, e1 = jnp.exp(s0 - top), jnp.exp(s1 - top)
            total = jnp.sum(e0, axis=-1, keepdims=True) + jnp.sum(e1, axis=-1, keepdims=True)
            mix = mm((e0 / total).astype(BF16), v0) + mm((e1 / total).astype(BF16), v1)
            put_rows(mixed_v, m, 1, cols, own, mix.astype(BF16))
            return 0

        lax.fori_loop(0, heads, attend, 0)
        tick(2)
    fs_d.end()
    mixed_out = local_copy(mixed_v, mixed_o)
    tick(1)
    for i in i_out:
        own_copies[i].wait()
        g.wait_last(i)
    out_out = local_copy(out_v, out_all)

    def project_out(fb):
        rr = pl.ds(al(fb * own, own), own)

        def one(j, _):
            wr = pl.ds(al(j * 256, 256), 256)
            part_v[rr, wr] = mm_nt(mixed_v[rr, :], out_v[wr, :]).astype(BF16)
            return 0

        lax.fori_loop(0, dim // 256, one, 0)

    project_out(p.f_yc)
    project_out(p.f_core)
    red.start()
    tick(1)
    project_out(p.f_y)
    red.mid(own)
    project_out(p.f)
    tick(2)
    red.end()
    for m in range(2):
        rr = pl.ds(m * (own // 2), own // 2)
        mid = tok[m].astype(F32) + red.value(rr)
        middle_o[rr, :] = mid
        inv = lax.rsqrt(jnp.mean(mid * mid, axis=-1, keepdims=True) + EPSILON)
        n2_v[pl.ds(al(p.f * own + m * (own // 2), 128), own // 2), :] = (
            mid * inv * gain_two
        ).astype(BF16)
    fs_n.start()
    tick(1)

    def turn_d(j, _):
        cols = pl.ds(al(j * 256, 256), 256)
        d_t[cols, :] = d_v[:, cols].T
        return 0

    lax.fori_loop(0, dim // 256, turn_d, 0)
    tick(1)
    fs_n.mid()
    tick(1)
    fs_n.end()

    def turn_n2(j, _):
        cols = pl.ds(al(j * 256, 256), 256)
        n2_t[cols, :] = n2_v[:, cols].T
        return 0

    lax.fori_loop(0, dim // 256, turn_n2, 0)
    for c in (q_out, mixed_out, out_out, seq_out):
        c.wait()
    early = [i_seq, i_gain] + i_qb + i_out
    for i in early:
        g.wait_sends(i)

    def spread_sends(j, _):
        for which in (0, 1):
            seq_copy(0, j, p.f, p.to_core, which).wait_send()
            seq_copy(1, j, p.f, p.to_y, which).wait_send()
            seq_copy(2, j, p.f_y, p.to_core, which).wait_send()
        return 0

    lax.fori_loop(0, npiece, spread_sends, 0)
    red.wait_sends()
    pending = []
    width = FFN_COLS
    for (c0, cw), some in zip(ffn_chunks(gate_sh.shape[1]), i_ffn):
        tick(some[-1] + 1 - g.seen)
        for i in some:
            own_copies[i].wait()
            g.wait_last(i)
        cols = pl.ds(c0, cw)
        loads = [
            pltpu.make_async_copy(w.at[:, cols], seq_v.at[:, pl.ds(n * width, cw)], ffn_ls.at[n])
            for n, w in enumerate((gate_all, up_all, down_all))
        ]
        for c in loads:
            c.start()
        for c in pending:
            c.wait()
        for c in loads:
            c.wait()
        gate_c, up_c, down_c = (slice(n * width, n * width + cw) for n in range(3))

        def both(t, _):
            rr = pl.ds(al(t * 256, 256), 256)
            gate = mm(n2_v[rr, :], seq_v[:, gate_c])
            up = mm(n2_v[rr, :], seq_v[:, up_c])
            grad_hidden = mm(d_v[rr, :], seq_v[:, down_c])
            sig = 1.0 / (1.0 + jnp.exp(-gate))
            act = gate * sig
            mixed_v[rr, :cw] = (act * up).astype(BF16)
            q_v[rr, gate_c] = (grad_hidden * up * (sig * (1.0 + gate * (1.0 - sig)))).astype(BF16)
            q_v[rr, up_c] = (grad_hidden * act).astype(BF16)
            return 0

        lax.fori_loop(0, rows // 256, both, 0)
        pending = [
            pltpu.make_async_copy(src, dst.at[:, cols], ffn_ls.at[3 + n])
            for n, (src, dst) in enumerate(
                (
                    (mixed_v.at[:, pl.ds(0, cw)], hid_o),
                    (q_v.at[:, pl.ds(0, cw)], gg_o),
                    (q_v.at[:, pl.ds(width, cw)], gu_o),
                )
            )
        ]
        for c in pending:
            c.start()

        half_rows = part_v.shape[0] // 256
        for lo in range(0, dim // 256, half_rows):

            def weight_grads(j, _):
                rr = pl.ds(al(j * 256, 256), 256)
                pr = pl.ds(al((j - lo) * 256, 256), 256)
                pc = slice((lo // half_rows) * width, (lo // half_rows) * width + cw)
                out_v[rr, gate_c] = mm(n2_t[rr, :], q_v[:, gate_c]).astype(BF16)
                out_v[rr, up_c] = mm(n2_t[rr, :], q_v[:, up_c]).astype(BF16)
                part_v[pr, pc] = mm(d_t[rr, :], mixed_v[:, :cw]).astype(BF16)
                return 0

            lax.fori_loop(lo, min(dim // 256, lo + half_rows), weight_grads, 0)
        saves = [
            pltpu.make_async_copy(out_v.at[:, pl.ds(0, cw)], gw_gate.at[:, cols], ffn_ls.at[6]),
            pltpu.make_async_copy(out_v.at[:, pl.ds(width, cw)], gw_up.at[:, cols], ffn_ls.at[7]),
        ]
        prow = part_v.shape[0]
        for n in range(dim // prow):
            saves.append(
                pltpu.make_async_copy(
                    part_v.at[:, pl.ds(n * width, cw)],
                    gw_down.at[pl.ds(n * prow, prow), cols],
                    ffn_ls.at[8 + n],
                )
            )
        for c in saves:
            c.start()
        pending = pending + saves
    for c in pending:
        c.wait()
    tick(len(g.items))
    for i in order:
        if i not in early:
            g.wait_sends(i)
    for t in (fs_d, fs_l, fs_n):
        t.wait_sends()
    for c in (qb_out, lkv_out):
        c.wait()


def forward_call(ndp, tok, dout, cos, sin, bias, seq_sh, gain_sh, qb, out, gate, up, down):
    own = tok.shape[0] * tok.shape[1]
    dim = tok.shape[2]
    rank = qb.shape[0] * ndp
    hd = (seq_sh.shape[1] - rank) // 2
    heads = qb.shape[1] // hd
    rows = NF * own
    kvw = seq_sh.shape[1]
    n_items = 2 + sum(w.shape[0] // min(w.shape[0], GATHER_ROWS) for w in (qb, out))
    n_items += sum(w.shape[0] // min(w.shape[0], FFN_ROWS) for w in (gate, up, down)) * len(
        ffn_chunks(gate.shape[1])
    )

    def sds(shape, dtype=BF16):
        return jax.ShapeDtypeStruct(shape, dtype)

    full = lambda w: sds((w.shape[0] * ndp, w.shape[1]))
    out_shape = (
        full(qb),
        full(out),
        full(gate),
        full(up),
        full(down),
        sds((seq_sh.shape[0] * ndp * NF, kvw)),
        sds(gain_sh.shape, F32),
        sds((rows, kvw)),
        sds((rows, heads * hd)),
        sds((rows, heads * hd)),
        sds((own, rank), F32),
        sds((own, dim)),
        sds((own, dim), F32),
        sds((rows, gate.shape[1])),
        sds((rows, gate.shape[1])),
        sds((rows, gate.shape[1])),
        full(gate),
        full(up),
        full(down),
    )
    out_specs = (ANY,) * 6 + (VMEM,) + (ANY,) * 3 + (VMEM,) * 3 + (ANY,) * 6
    dma = pltpu.SemaphoreType.DMA
    scratch = [
        pltpu.VMEM((seq_sh.shape[0] * ndp * NF, kvw), BF16),
        pltpu.VMEM((ndp * NF,) + gain_sh.shape, F32),
        pltpu.VMEM((qb.shape[0] * ndp, qb.shape[1]), BF16),
        pltpu.VMEM((out.shape[0] * ndp, out.shape[1]), BF16),
        pltpu.VMEM((rows, kvw), BF16),
        pltpu.VMEM((rows, heads * hd), BF16),
        pltpu.VMEM((rows, heads * hd), BF16),
        pltpu.VMEM((rows, dim), BF16),
        pltpu.VMEM((2, own, dim), BF16),
        pltpu.VMEM((own, dim), BF16),
        pltpu.VMEM((rows, dim), BF16),
        pltpu.VMEM((rows, dim), BF16),
        pltpu.VMEM((dim, rows), BF16),
        pltpu.VMEM((dim, rows), BF16),
        pltpu.VMEM((own, kvw), F32),
        dma((n_items, ndp - 1)),
        dma((n_items, ndp - 1)),
        dma((4, 3)),
        dma((4, 3)),
        dma((2, 3, ndp)),
        dma((2, 3, ndp)),
        dma((n_items + 10,)),
        dma((10,)),
    ]
    return pl.pallas_call(
        functools.partial(forward_kernel, (ndp, own, dim, rank, hd, heads)),
        out_shape=out_shape,
        in_specs=(VMEM,) * 5 + (ANY,) * 7,
        out_specs=out_specs,
        scratch_shapes=scratch,
        compiler_params=pltpu.CompilerParams(
            collective_id=0, has_side_effects=True, vmem_limit_bytes=60 * 2**20
        ),
        name="gather_forward",
    )(tok, dout, cos, sin, bias, seq_sh, gain_sh, qb, out, gate, up, down)


class DpScatter:
    SLOTS = 5
    AHEAD = 2
    OWN = 3

    def __init__(self, pos, count, first, later, own, acc, ss, rs, ls, credit):
        self.p, self.count = pos, count
        self.n = len(pos.bits)
        self.first, self.later, self.own, self.acc = first, later, own, acc
        self.ss, self.rs, self.ls, self.credit = ss, rs, ls, credit
        self.items = []
        self.started = self.stepped = 0

    def order(self, n):
        return self.p.orders(n % 4 == 3)

    def width(self, stage):
        return 1 << (self.n - 1 - stage)

    def add(self, src, base, out, pieces):
        rows, cols = out.shape
        r = rows // pieces
        for c in range(pieces):
            self.items.append((src, base, out, rows, cols, c * r, r))
        self.pump()

    def mask(self, n, i):
        order = self.order(n)
        return sum(order[1 + t] for t in range(self.n - 1) if i >> (self.n - 2 - t) & 1)

    def block(self, n, mask):
        src, base, out, rows, cols, r0, r = self.items[n]
        return src.at[pl.ds(al(base + self.p.at(mask) * rows + r0, r), r)]

    def place(self, buf, n, lo, size):
        src, base, out, rows, cols, r0, r = self.items[n]
        return buf.at[n % self.SLOTS, pl.ds(lo, size), pl.ds(0, r), pl.ds(0, cols)]

    def copies(self, n, stage):
        bit = self.order(n)[stage]
        dev = self.p.to_dp(bit)
        s = n % self.SLOTS
        if stage == 0:
            return [
                rcopy(
                    self.block(n, bit | self.mask(n, i)),
                    self.place(self.first, n, i, 1).at[0],
                    self.ss.at[s, i],
                    self.rs.at[s, i],
                    dev,
                )
                for i in range(self.width(0))
            ]
        w = self.width(stage)
        k = self.width(0) + stage - 1
        return [
            rcopy(
                self.place(self.first, n, w, w),
                self.place(self.later, n, w - 1, w),
                self.ss.at[s, k],
                self.rs.at[s, k],
                dev,
            )
        ]

    def owncopy(self, n, i):
        src, base, out, rows, cols, r0, r = self.items[n]
        s = n % self.OWN
        return pltpu.make_async_copy(
            self.block(n, self.mask(n, i)),
            self.own.at[s, i, pl.ds(0, r), pl.ds(0, cols)],
            self.ls.at[s, i],
        )

    def outcopy(self, n):
        src, base, out, rows, cols, r0, r = self.items[n]
        s = n % self.SLOTS
        return pltpu.make_async_copy(
            self.acc.at[s, pl.ds(0, r), pl.ds(0, cols)],
            out.at[pl.ds(r0, r)],
            self.ls.at[s, self.width(0)],
        )

    def free(self, n, stage):
        m = n + self.SLOTS
        if m < self.count:
            bit = self.order(m)[stage]
            pl.semaphore_signal(
                self.credit.at[stage, self.p.bits.index(bit)],
                inc=1,
                device_id=self.p.to_dp(bit),
                device_id_type=MESH,
            )

    def send(self, n, stage):
        bit = self.order(n)[stage]
        if n >= self.SLOTS:
            pl.semaphore_wait(self.credit.at[stage, self.p.bits.index(bit)], 1)
        for c in self.copies(n, stage):
            c.start()

    def pump(self):
        while self.started < min(len(self.items), self.stepped + self.AHEAD):
            n = self.started
            self.send(n, 0)
            for i in range(self.width(0)):
                self.owncopy(n, i).start()
            self.started += 1

    def tick(self, steps=1):
        for _ in range(steps):
            n = self.stepped
            if n >= self.started:
                return
            self.combine(n, 0)
            self.stepped += 1
            self.pump()
            for stage in range(1, self.n):
                if n >= stage:
                    self.combine(n - stage, stage)

    def combine(self, n, stage):
        src, base, out, rows, cols, r0, r = self.items[n]
        s, tile = n % self.SLOTS, 16
        w = self.width(stage)
        for c in self.copies(n, stage):
            c.wait_recv()
        if stage == 0:
            for i in range(w):
                self.owncopy(n, i).wait()
        else:
            for c in self.copies(n, stage):
                c.wait_send()
        last = stage == self.n - 1

        def add(lo, size):
            def one(t, _):
                t = pl.ds(al(t * tile, tile), tile)
                for i in range(lo, lo + size):
                    a = self.first[s, i, t, :cols]
                    b = self.own[n % self.OWN, i, t, :cols] if stage == 0 else self.later[s, w - 1 + i, t, :cols]
                    if last:
                        self.acc[s, t, :cols] = a.astype(F32) + b.astype(F32)
                    else:
                        self.first[s, i, t, :cols] = a + b
                return 0

            lax.fori_loop(0, r // tile, one, 0)

        if last:
            if n >= self.SLOTS:
                self.outcopy(n - self.SLOTS).wait()
            for c in self.copies(n, 0):
                c.wait_send()
            add(0, 1)
            self.outcopy(n).start()
            for t in range(self.n):
                self.free(n, t)
        else:
            half = w // 2
            add(half, half)
            self.send(n, stage + 1)
            add(0, half)

    def drain(self):
        self.tick(self.count)
        for n in range(self.count, self.count + self.n - 1):
            for stage in range(1, self.n):
                if 0 <= n - stage < self.count:
                    self.combine(n - stage, stage)
        for n in range(max(0, self.count - self.SLOTS), self.count):
            self.outcopy(n).wait()


def piece_rows(rows, nz):
    return min(rows, max(16, 256 // nz))


def backward_kernel(
    cfg,
    tok,
    dout,
    middle,
    latent,
    normed,
    gains,
    cos,
    sin,
    bias,
    gw_gate,
    gw_up,
    gw_down,
    hid_h,
    gg_h,
    gu_h,
    gate_h,
    up_h,
    down_h,
    lkv_h,
    q_h,
    mixed_h,
    qb_h,
    out_h,
    seq_h,
    o_gate,
    o_up,
    o_down,
    o_out,
    o_qb,
    o_seq,
    o_gain,
    o_in,
    o_y,
    fcore_v,
    fy_v,
    proj_v,
    gmid_v,
    gnorm_v,
    lkv_v,
    q_v,
    mixed_v,
    gm_v,
    kv_acc,
    qb_v,
    out_v,
    seq_v,
    gall_v,
    gain_rx,
    gain_acc,
    first_b,
    later_b,
    own_b,
    acc_b,
    dss,
    drs,
    dls,
    credit,
    fss,
    frs,
    gs,
    gr,
    ls,
    tls,
):
    ndp, own, dim, rank, hd, heads, pieces = cfg
    rows = NF * own
    t2 = own // 2
    kvw = rank + 2 * hd
    wide = dim // rank
    p = Place(ndp)
    sr = o_seq.shape[0]
    local = []

    def local_copy(src, dst):
        c = pltpu.make_async_copy(src, dst, ls.at[len(local)])
        c.start()
        local.append(c)
        return c

    ff = gg_h.shape[1]
    ffc = pl.ds(0, ff)
    gg_in = local_copy(gg_h, lkv_v.at[:, ffc])
    gu_in = local_copy(gu_h, seq_v.at[pl.ds(0, rows), ffc])
    mixed_in = local_copy(mixed_h, mixed_v)
    q_in = local_copy(q_h, q_v)
    qb_in = local_copy(qb_h, qb_v)
    hh = out_v.shape[1]

    def tile_load(t, which):
        src = gate_h if which == 0 else up_h
        s = lax.rem(t, 2) * 2 + which
        return pltpu.make_async_copy(
            src.at[pl.ds(al(t * 256, 256), 256)],
            seq_v.at[pl.ds(al(rows + s * 256, 256), 256), ffc],
            tls.at[s],
        )

    for which in (0, 1):
        tile_load(0, which).start()
    sc = DpScatter(p, sum(pieces), first_b, later_b, own_b, acc_b, dss, drs, dls, credit)
    p.barrier()
    sc.add(gw_gate, 0, o_gate, pieces[0])
    sc.add(gw_up, 0, o_up, pieces[1])
    sc.add(gw_down, 0, o_down, pieces[2])
    gg_in.wait()
    gu_in.wait()
    n_tiles = dim // 256
    per_half = hh // 256

    def norm_grad(t, _):
        for which in (0, 1):
            tile_load(t, which).wait()

        @pl.when(t + 1 < n_tiles)
        def _():
            for which in (0, 1):
                tile_load(t + 1, which).start()

        s = lax.rem(t, 2) * 2
        wg = seq_v[pl.ds(al(rows + s * 256, 256), 256), ffc]
        wu = seq_v[pl.ds(al(rows + s * 256 + 256, 256), 256), ffc]
        cols = pl.ds(al(lax.rem(t, per_half) * 256, 256), 256)
        for r in range(rows // 256):
            rr = pl.ds(r * 256, 256)
            to = pl.ds(al((t // per_half) * rows + r * 256, 256), 256)
            out_v[to, cols] = (
                mm_nt(lkv_v[rr, ffc], wg) + mm_nt(seq_v[rr, ffc], wu)
            ).astype(BF16)
        return 0

    halves = []
    for h in range(dim // hh):
        wide_cols = pl.ds(h * hh, hh)
        lax.fori_loop(h * per_half, (h + 1) * per_half, norm_grad, 0)
        red = FsReduce(
            p,
            lambda b, h=h: out_v.at[pl.ds(al(h * rows + b * own, own), own)],
            fcore_v.at[:, :, wide_cols],
            fy_v.at[:, wide_cols],
            fss.at[4 * h],
            frs.at[4 * h],
        )
        red.start()
        if h > 0:
            halves[-1].mid(own)
        sc.tick(1)
        halves.append(red)
    lkv_in = local_copy(lkv_h, lkv_v)
    seq_in = local_copy(seq_h, seq_v)
    halves[-1].mid(own)
    sc.tick(1)
    for red in halves:
        red.end()
        red.wait_sends()
    gain_two = jnp.concatenate([gains[wide + r : wide + r + 1] for r in range(wide)], axis=1)
    gain_one = jnp.concatenate([gains[r : r + 1] for r in range(wide)], axis=1)
    gain_lat = gains[2 * wide : 2 * wide + 1]
    part_two = jnp.zeros((1, dim), F32)
    for m in range(2):
        rr = pl.ds(m * t2, t2)
        e = jnp.concatenate([red.value(rr) for red in halves], axis=1)
        v = middle[rr, :]
        inv = lax.rsqrt(jnp.mean(v * v, axis=-1, keepdims=True) + EPSILON)
        part_two += jnp.sum(e * v * inv, axis=0, keepdims=True)
        scaled = e * gain_two
        inner = jnp.mean(scaled * v, axis=-1, keepdims=True)
        g = dout[m].astype(F32) + inv * scaled - v * (inv * inv * inv * inner)
        gmid_v[rr, :] = g
        proj_v[pl.ds(al(p.f * own + m * t2, t2), t2), :] = g.astype(BF16)
    out_in = local_copy(out_h, out_v)
    gain_acc[0] = jnp.zeros(gain_acc.shape[1:], F32)
    for r in range(wide):
        gain_acc[0, pl.ds(wide + r, 1), :] = part_two[:, r * rank : (r + 1) * rank]
    ag = FsGather(p, lambda b: proj_v.at[pl.ds(al(b * own, own), own)], fss.at[1], frs.at[1])
    ag.start()
    sc.tick(1)
    ag.mid()
    sc.tick(1)
    out_in.wait()
    ag.end()
    ag.wait_sends()

    def back_out(j, _):
        cols = pl.ds(al(j * 256, 256), 256)
        for r in range(rows // 512):
            rr = pl.ds(r * 512, 512)
            gm_v[rr, cols] = mm(proj_v[rr, :], out_v[:, cols]).astype(BF16)
        return 0

    lax.fori_loop(0, heads * hd // 256, back_out, 0)
    sc.tick(1)
    mixed_in.wait()

    def grad_out(j, _):
        cols = pl.ds(al(j * 256, 256), 256)
        out_v[cols, :] = mm_tn(proj_v[:, cols], mixed_v[...]).astype(BF16)
        return 0

    lax.fori_loop(0, dim // 256, grad_out, 0)
    sc.tick(1)
    sc.add(out_v, 0, o_out, pieces[3])
    q_in.wait()
    lkv_in.wait()
    scale = hd ** (-0.5)
    half = hd // 2
    kcols, vcols = slice(rank, rank + hd), slice(rank + hd, rank + 2 * hd)
    causal = causal_bias(PROMPT)
    everything = slice(None)

    for m in range(2):
        k0, k1 = (group_rows(lkv_v, m, h2, kcols, own) for h2 in (0, 1))
        v0, v1 = (group_rows(lkv_v, m, h2, vcols, own) for h2 in (0, 1))
        low = bias[m]
        kv_acc[...] = jnp.zeros(kv_acc.shape, F32)

        def put_query(h, which, g):
            co = group_rows(cos, m, which, everything, own)
            si = group_rows(sin, m, which, everything, own)
            a, b = g[:, :half] * scale, g[:, half:] * scale
            c0 = pl.ds(al(h * hd, half), half)
            c1 = pl.ds(al(h * hd + half, half), half)
            put_rows(gm_v, m, which, c0, own, (a * co + b * si).astype(BF16))
            put_rows(gm_v, m, which, c1, own, (b * co - a * si).astype(BF16))

        def attend_back(h, _):
            cols = pl.ds(al(h * hd, hd), hd)
            q0 = group_rows(q_v, m, 0, cols, own)
            g0 = group_rows(gm_v, m, 0, cols, own)
            pr = softmax_parts(mm_nt(q0, k0) * scale + causal)
            gp = mm_nt(g0, v0)
            gsc = (pr * (gp - jnp.sum(pr * gp, axis=-1, keepdims=True))).astype(BF16)
            kv_acc[2] += mm_tn(pr.astype(BF16), g0)
            kv_acc[0] += mm_tn(gsc, q0)
            put_query(h, 0, mm(gsc, k0))
            q1 = group_rows(q_v, m, 1, cols, own)
            g1 = group_rows(gm_v, m, 1, cols, own)
            s0 = mm_nt(q1, k0) * scale
            s1 = mm_nt(q1, k1) * scale + low
            top = jnp.maximum(
                jnp.max(s0, axis=-1, keepdims=True), jnp.max(s1, axis=-1, keepdims=True)
            )
            e0, e1 = jnp.exp(s0 - top), jnp.exp(s1 - top)
            total = jnp.sum(e0, axis=-1, keepdims=True) + jnp.sum(e1, axis=-1, keepdims=True)
            p0, p1 = e0 / total, e1 / total
            gp0, gp1 = mm_nt(g1, v0), mm_nt(g1, v1)
            inner = jnp.sum(p0 * gp0, axis=-1, keepdims=True) + jnp.sum(
                p1 * gp1, axis=-1, keepdims=True
            )
            gs0 = (p0 * (gp0 - inner)).astype(BF16)
            gs1 = (p1 * (gp1 - inner)).astype(BF16)
            kv_acc[2] += mm_tn(p0.astype(BF16), g1)
            kv_acc[3] += mm_tn(p1.astype(BF16), g1)
            kv_acc[0] += mm_tn(gs0, q1)
            kv_acc[1] += mm_tn(gs1, q1)
            put_query(h, 1, mm(gs0, k0) + mm(gs1, k1))
            return 0

        lax.fori_loop(0, heads, attend_back, 0)
        for h2 in (0, 1):
            put_rows(proj_v, m, h2, kcols, own, (kv_acc[h2] * scale).astype(BF16))
            put_rows(proj_v, m, h2, vcols, own, kv_acc[2 + h2].astype(BF16))
        sc.tick(1)
    qb_in.wait()

    def back_latent(j, _):
        wr = pl.ds(al(j * 256, 256), 256)
        for r in range(rows // 512):
            rr = pl.ds(r * 512, 512)
            proj_v[rr, wr] = mm_nt(gm_v[rr, :], qb_v[wr, :]).astype(BF16)
        return 0

    lax.fori_loop(0, rank // 256, back_latent, 0)

    def grad_qb(j, _):
        cols = pl.ds(al(j * 256, 256), 256)
        qb_v[cols, :] = mm_tn(lkv_v[:, cols], gm_v[...]).astype(BF16)
        return 0

    lax.fori_loop(0, rank // 256, grad_qb, 0)
    narrow = pl.ds(0, kvw)
    red2 = FsReduce(
        p,
        lambda b: proj_v.at[pl.ds(al(b * own, own), own), narrow],
        fcore_v.at[:, :, narrow],
        fy_v.at[:, narrow],
        fss.at[2],
        frs.at[2],
    )
    red2.start()
    sc.tick(1)
    sc.add(qb_v, 0, o_qb, pieces[4])
    red2.mid(own)
    sc.tick(1)
    red2.end()
    red2.wait_sends()
    own_rows = pl.ds(al(p.f * own, own), own)
    part_lat = jnp.zeros((1, rank), F32)
    for m in range(2):
        rr = pl.ds(m * t2, t2)
        gr_rows = pl.ds(al(p.f * own + m * t2, t2), t2)
        e = red2.value(rr)
        v = latent[rr, :]
        inv = lax.rsqrt(jnp.mean(v * v, axis=-1, keepdims=True) + EPSILON)
        el = e[:, :rank]
        part_lat += jnp.sum(el * v * inv, axis=0, keepdims=True)
        scaled = el * gain_lat
        inner = jnp.mean(scaled * v, axis=-1, keepdims=True)
        gall_v[rr, :rank] = (inv * scaled - v * (inv * inv * inv * inner)).astype(BF16)
        co, si = cos[gr_rows, :], sin[gr_rows, :]
        a, b = e[:, rank : rank + half], e[:, rank + half : rank + hd]
        gall_v[rr, rank : rank + half] = (a * co + b * si).astype(BF16)
        gall_v[rr, rank + half : rank + hd] = (b * co - a * si).astype(BF16)
        gall_v[rr, rank + hd :] = e[:, rank + hd :].astype(BF16)
    gain_acc[0, pl.ds(2 * wide, 1), :] = part_lat
    seq_in.wait()

    def back_seq(j, _):
        wr = pl.ds(al(j * 256, 256), 256)
        gnorm_v[:, wr] = mm_nt(gall_v[...], seq_v[wr, :])
        return 0

    lax.fori_loop(0, dim // 256, back_seq, 0)
    sc.tick(1)
    span = NF * sr

    def grad_seq(j, _):
        cols = pl.ds(al(j * 256, 256), 256)
        g = mm_tn(normed[:, cols], gall_v[...]).astype(BF16)
        for i in range(256 // span):
            for fb in range(NF):
                seq_v[pl.ds(al(fb * ndp * sr + (j * (256 // span) + i) * sr, sr), sr), :] = g[
                    i * span + fb * sr : i * span + (fb + 1) * sr
                ]
        return 0

    lax.fori_loop(0, dim // 256, grad_seq, 0)
    srows = ndp * sr
    core3 = [lkv_v.at[pl.ds(0, srows)], lkv_v.at[pl.ds(srows, srows)]]

    def sblock(b):
        return seq_v.at[pl.ds(al(b * srows, srows), srows)]

    c1 = rcopy(sblock(p.f_yc), core3[1], fss.at[3, 1], frs.at[3, 1], p.to_core)
    c0 = rcopy(sblock(p.f_core), core3[0], fss.at[3, 0], frs.at[3, 0], p.to_core)
    mw = mixed_v.shape[1]
    cys = [
        rcopy(
            lkv_v.at[pl.ds(srows, srows), pl.ds(0, mw)],
            mixed_v.at[pl.ds(0, srows)],
            fss.at[3, 2],
            frs.at[3, 2],
            p.to_y,
        ),
        rcopy(
            lkv_v.at[pl.ds(srows, srows), pl.ds(mw, kvw - mw)],
            mixed_v.at[pl.ds(srows, srows), pl.ds(0, kvw - mw)],
            fss.at[3, 3],
            frs.at[3, 3],
            p.to_y,
        ),
    ]
    c1.start()
    c0.start()
    part_one = jnp.zeros((1, dim), F32)
    for m in range(2):
        rr = pl.ds(m * t2, t2)
        e = gnorm_v[rr, :]
        v = tok[m].astype(F32)
        inv = lax.rsqrt(jnp.mean(v * v, axis=-1, keepdims=True) + EPSILON)
        part_one += jnp.sum(e * v * inv, axis=0, keepdims=True)
        scaled = e * gain_one
        inner = jnp.mean(scaled * v, axis=-1, keepdims=True)
        o_in[m] = (gmid_v[rr, :] + inv * scaled - v * (inv * inv * inv * inner)).astype(BF16)
    for r in range(wide):
        gain_acc[0, pl.ds(r, 1), :] = part_one[:, r * rank : (r + 1) * rank]
    gain_steps = [
        rcopy(gain_acc.at[0], gain_rx.at[0], gs.at[0], gr.at[0], p.to_core),
        rcopy(gain_acc.at[1], gain_rx.at[1], gs.at[1], gr.at[1], p.to_y),
    ] + [
        rcopy(gain_acc.at[2 + b], gain_rx.at[2 + b], gs.at[2 + b], gr.at[2 + b], p.to_dp(bit))
        for b, bit in enumerate(p.bits)
    ]
    gain_steps[0].start()
    c1.wait_recv()

    def seq_y(t, _):
        t = al(t * 64, 64)
        a = pl.ds(srows + t, 64)
        b = pl.ds(al(p.f_y * srows + t, 64), 64)
        lkv_v[a, :] = lkv_v[a, :] + seq_v[b, :]
        return 0

    lax.fori_loop(0, srows // 64, seq_y, 0)
    for c in cys:
        c.start()
    for n in range(len(gain_steps)):
        gain_steps[n].wait_recv()
        gain_acc[n + 1] = gain_acc[n] + gain_rx[n]
        if n + 1 < len(gain_steps):
            gain_steps[n + 1].start()
        if n % 2 == 0:
            sc.tick(1)
    c0.wait_recv()
    for c in cys:
        c.wait_recv()

    def seq_f(t, _):
        t = al(t * 64, 64)
        a = pl.ds(t, 64)
        b = pl.ds(al(p.f * srows + t, 64), 64)
        a2 = pl.ds(srows + t, 64)
        seq_v[b, :mw] = (
            lkv_v[a, :mw].astype(F32) + seq_v[b, :mw].astype(F32) + mixed_v[a, :].astype(F32)
        ).astype(BF16)
        seq_v[b, mw:] = (
            lkv_v[a, mw:].astype(F32)
            + seq_v[b, mw:].astype(F32)
            + mixed_v[a2, : kvw - mw].astype(F32)
        ).astype(BF16)
        return 0

    lax.fori_loop(0, srows // 64, seq_f, 0)
    sc.add(seq_v, p.f * srows, o_seq, pieces[5])
    o_gain[...] = gain_acc[len(gain_steps)]
    for t in [c1, c0] + cys:
        t.wait_send()
    hid_in = local_copy(hid_h, lkv_v.at[:, ffc])

    def down_load(t):
        s = lax.rem(t, 2)
        return pltpu.make_async_copy(
            down_h.at[pl.ds(al(t * 256, 256), 256)],
            seq_v.at[pl.ds(al(p.f_core * srows + s * 256, 256), 256), ffc],
            tls.at[s],
        )

    down_load(0).start()
    sc.tick(1)
    hid_in.wait()

    def ffn_out(t, _):
        down_load(t).wait()

        @pl.when(t + 1 < n_tiles)
        def _():
            down_load(t + 1).start()

        w = seq_v[pl.ds(al(p.f_core * srows + lax.rem(t, 2) * 256, 256), 256), ffc]
        cols = pl.ds(al(t * 256, 256), 256)
        for r in range(rows // 256):
            rr = pl.ds(r * 256, 256)
            proj_v[rr, cols] = mm_nt(lkv_v[rr, ffc], w).astype(BF16)
        return 0

    lax.fori_loop(0, n_tiles, ffn_out, 0)
    red3 = FsReduce(
        p,
        lambda b: proj_v.at[pl.ds(al(b * own, own), own)],
        fcore_v,
        fy_v,
        fss.at[5],
        frs.at[5],
    )
    red3.start()
    sc.tick(1)
    red3.mid(own)
    sc.tick(2)
    red3.end()
    for m in range(2):
        rr = pl.ds(m * t2, t2)
        o_y[m] = (middle[rr, :] + red3.value(rr)).astype(BF16)
    sc.drain()
    red3.wait_sends()
    for t in gain_steps:
        t.wait_send()


def backward_call(ndp, tok, dout, middle, latent, normed, gains, cos, sin, bias, grads, ffn, saved):
    lkv, q, mixed, qb, out, seq = saved
    nz = ndp // 2
    own, dim = middle.shape
    rank = latent.shape[1]
    kvw = lkv.shape[1]
    hd = (kvw - rank) // 2
    heads = q.shape[1] // hd
    rows = NF * own
    sr = seq.shape[0] // (ndp * NF)
    shards = [(w.shape[0] // ndp, w.shape[1]) for w in grads] + [
        (out.shape[0] // ndp, out.shape[1]),
        (qb.shape[0] // ndp, qb.shape[1]),
        (sr, kvw),
    ]
    pieces = tuple(s[0] // piece_rows(s[0], nz) for s in shards)
    n = sum(pieces)
    slots = DpScatter.SLOTS
    nb = ndp.bit_length() - 1
    pr = max(piece_rows(s[0], nz) for s in shards)
    width = max(s[1] for s in shards)
    dma = pltpu.SemaphoreType.DMA
    scratch = [
        pltpu.VMEM((2, own, dim), BF16),
        pltpu.VMEM((own, dim), BF16),
        pltpu.VMEM((rows, dim), BF16),
        pltpu.VMEM((own, dim), F32),
        pltpu.VMEM((own, dim), F32),
        pltpu.VMEM(lkv.shape, BF16),
        pltpu.VMEM(q.shape, BF16),
        pltpu.VMEM(mixed.shape, BF16),
        pltpu.VMEM(q.shape, BF16),
        pltpu.VMEM((4, rows // 4, hd), F32),
        pltpu.VMEM(qb.shape, BF16),
        pltpu.VMEM(out.shape, BF16),
        pltpu.VMEM(seq.shape, BF16),
        pltpu.VMEM((own, kvw), BF16),
        pltpu.VMEM((2 + nb,) + gains.shape, F32),
        pltpu.VMEM((3 + nb,) + gains.shape, F32),
        pltpu.VMEM((slots, nz, pr, width), BF16),
        pltpu.VMEM((slots, nz - 1, pr, width), BF16),
        pltpu.VMEM((DpScatter.OWN, nz, pr, width), BF16),
        pltpu.VMEM((slots, pr, width), F32),
        dma((slots, nz + nb - 1)),
        dma((slots, nz + nb - 1)),
        dma((slots, nz + 1)),
        pltpu.SemaphoreType.REGULAR((nb, nb)),
        dma((6, 4)),
        dma((6, 4)),
        dma((2 + nb,)),
        dma((2 + nb,)),
        dma((9,)),
        dma((4,)),
    ]
    return pl.pallas_call(
        functools.partial(backward_kernel, (ndp, own, dim, rank, hd, heads, pieces)),
        out_shape=tuple(jax.ShapeDtypeStruct(s, F32) for s in shards)
        + (
            jax.ShapeDtypeStruct(gains.shape, F32),
            jax.ShapeDtypeStruct(tok.shape, BF16),
            jax.ShapeDtypeStruct(tok.shape, BF16),
        ),
        in_specs=(VMEM,) * 9 + (ANY,) * 15,
        out_specs=(ANY,) * 6 + (VMEM,) * 3,
        scratch_shapes=scratch,
        compiler_params=pltpu.CompilerParams(
            collective_id=1, has_side_effects=True, vmem_limit_bytes=62 * 2**20
        ),
        name="backward_scatter",
    )(tok, dout, middle, latent, normed, gains, cos, sin, bias, *grads, *ffn, lkv, q, mixed, qb, out, seq)


def per_device(
    ndp,
    tokens,
    membership,
    d_output,
    gain_attn,
    w_qa,
    gain_latent,
    w_qb,
    w_key,
    w_value,
    w_out,
    gain_ffn,
    w_gate,
    w_up,
    w_down,
):
    micro, tlen, dim = tokens.shape
    own = micro * tlen
    rank = w_qa.shape[1]
    hd = w_key.shape[1]
    heads = w_qb.shape[1] // hd
    rows = NF * own
    wide = dim // rank
    labels, positions = jax.vmap(lambda r: layout(r, BLK))(membership[0])
    pos_rows = positions.reshape(micro, NF, tlen).transpose(1, 0, 2).reshape(rows)
    cos, sin = rope_tables(pos_rows, hd)
    tail = labels[:, PROMPT:]
    idx = jnp.arange(tail.shape[1], dtype=jnp.int32)
    seen = (idx[None, None, :] <= idx[None, :, None]) & (tail[:, None, :] == tail[:, :, None])
    bias = jnp.where(seen, 0.0, MASK_FILL).astype(F32)
    block = lax.axis_index("dp") * NF + lax.axis_index("fsdp")

    def spot(gain):
        width = gain.shape[0]
        count = ndp * NF
        at = lax.broadcasted_iota(jnp.int32, (count, width), 0) == block
        placed = jnp.where(at, gain.astype(F32)[None, :], 0.0)
        return placed.reshape(count * width // rank, rank)

    gain_sh = jnp.concatenate([spot(gain_attn), spot(gain_ffn), spot(gain_latent)], axis=0)
    gain_sh = jnp.pad(gain_sh, ((0, 8 - gain_sh.shape[0]), (0, 0)))
    seq_sh = jnp.concatenate([w_qa, w_key, w_value], axis=1)
    (
        qb_all,
        out_all,
        gate_all,
        up_all,
        down_all,
        seq_all,
        gains,
        lkv,
        q_all,
        mixed,
        latent,
        normed,
        middle,
        hidden,
        grad_gate,
        grad_up,
        gw_gate,
        gw_up,
        gw_down,
    ) = forward_call(
        ndp, tokens, d_output, cos, sin, bias, seq_sh, gain_sh, w_qb, w_out, w_gate, w_up, w_down
    )
    o_gate, o_up, o_down, o_out, o_qb, o_seq, o_gain, input_grad, output = backward_call(
        ndp,
        tokens,
        d_output,
        middle,
        latent,
        normed,
        gains,
        cos,
        sin,
        bias,
        (gw_gate, gw_up, gw_down),
        (hidden, grad_gate, grad_up, gate_all, up_all, down_all),
        (lkv, q_all, mixed, qb_all, out_all, seq_all),
    )

    def own_gain(flat, width):
        return lax.dynamic_slice_in_dim(flat.reshape(-1), block * width, width, 0)

    return (
        output,
        input_grad,
        own_gain(o_gain[:wide], gain_attn.shape[0]),
        o_seq[:, :rank],
        own_gain(o_gain[2 * wide], gain_latent.shape[0]),
        o_qb,
        o_seq[:, rank : rank + hd],
        o_seq[:, rank + hd :],
        o_out,
        own_gain(o_gain[wide : 2 * wide], gain_ffn.shape[0]),
        o_gate,
        o_up,
        o_down,
    )


def solution(mesh):
    both = ("dp", "fsdp")
    rowwise, vector = P(both, None), P(both)
    tok = P(None, both, None)
    head = P("dp", "fsdp")
    return jax.shard_map(
        functools.partial(per_device, mesh.shape["dp"]),
        mesh=mesh,
        in_specs=(
            tok,
            P("dp", None, None),
            tok,
            vector,
            rowwise,
            vector,
            head,
            rowwise,
            rowwise,
            head,
            vector,
            head,
            head,
            head,
        ),
        out_specs=(
            tok,
            tok,
            vector,
            rowwise,
            vector,
            head,
            rowwise,
            rowwise,
            head,
            vector,
            head,
            head,
            head,
        ),
        check_vma=False,
    )
```

```python
import functools

import jax
import jax.numpy as jnp
from jax import lax
from jax.experimental import pallas as pl
from jax.experimental.pallas import tpu as pltpu
from jax.sharding import PartitionSpec as P

BLK = 32
PROMPT = 256
EPSILON = 1e-05
ROPE_BASE = 10000.0
MASK_FILL = -1e30
F32 = jnp.float32
BF16 = jnp.bfloat16
MESH = pl.DeviceIdType.MESH
ANY = pl.BlockSpec(memory_space=pl.ANY)
VMEM = pl.BlockSpec(memory_space=pltpu.VMEM)
NF = 4
GATHER_ROWS = 64
GATHER_AHEAD = 4
FFN_ROWS = 128
FFN_COLS = 512


def ffn_chunks(cols):
    return [(c, min(FFN_COLS, cols - c)) for c in range(0, cols, FFN_COLS)]


def layout(member_row, block_len):
    count_blocks = member_row.shape[0]
    block_ids = jnp.arange(count_blocks, dtype=jnp.int32)
    same_run = (member_row[None, :] == member_row[:, None]) & (
        block_ids[None, :] < block_ids[:, None]
    )
    earlier = jnp.sum(same_run.astype(jnp.int32), axis=1)
    prompt_len = jnp.sum((member_row == 0).astype(jnp.int32)) * block_len
    labels = jnp.repeat(member_row, block_len)
    within = jnp.arange(count_blocks * block_len, dtype=jnp.int32) % block_len
    positions = (
        (labels > 0).astype(jnp.int32) * prompt_len
        + jnp.repeat(earlier, block_len) * block_len
        + within
    )
    return (labels, positions)


def rope_tables(positions, head_width):
    half_width = head_width // 2
    frequency = ROPE_BASE ** (-(jnp.arange(half_width, dtype=jnp.float32) * (2.0 / head_width)))
    angles = positions.astype(jnp.float32)[:, None] * frequency[None, :]
    return (jnp.cos(angles), jnp.sin(angles))


def al(x, n):
    return pl.multiple_of(x, n)


def mm(a, b):
    return lax.dot_general(a, b, (((1,), (0,)), ((), ())), preferred_element_type=F32)


def mm_nt(a, b):
    return lax.dot_general(a, b, (((1,), (1,)), ((), ())), preferred_element_type=F32)


def mm_tn(a, b):
    return lax.dot_general(a, b, (((0,), (0,)), ((), ())), preferred_element_type=F32)


class Place:
    def __init__(self, ndp):
        self.ndp = ndp
        self.bits = [1 << b for b in range(ndp.bit_length() - 1)]
        self.me = lax.axis_index("dp")
        self.f = lax.axis_index("fsdp")
        y, c = self.f // 2, self.f % 2
        self.f_core = y * 2 + 1 - c
        self.f_y = (1 - y) * 2 + c
        self.f_yc = (1 - y) * 2 + 1 - c
        self.to_core = (self.me, self.f_core)
        self.to_y = (self.me, self.f_y)

    def at(self, mask):
        j = self.me
        for b in self.bits:
            if mask & b:
                j = j + b - 2 * b * ((self.me // b) % 2)
        return j

    def to_dp(self, mask):
        return (self.at(mask), self.f)

    def orders(self, swapped):
        o = list(self.bits)
        if swapped and len(o) > 1:
            o[0], o[1] = o[1], o[0]
        return o

    def barrier(self):
        bar = pltpu.get_barrier_semaphore()
        devs = [self.to_dp(b) for b in self.bits] + [self.to_core, self.to_y]
        for d in devs:
            pl.semaphore_signal(bar, inc=1, device_id=d, device_id_type=MESH)
        pl.semaphore_wait(bar, len(devs))


def rcopy(src, dst, ss, rs, dev):
    return pltpu.make_async_remote_copy(
        src_ref=src, dst_ref=dst, send_sem=ss, recv_sem=rs, device_id=dev, device_id_type=MESH
    )


class DpGather:
    def __init__(self, pos, ss, rs):
        self.p, self.ss, self.rs = pos, ss, rs
        self.items, self.events = [], []
        self.launched = self.seen = self.first = 0

    def add(self, src, dst, swapped=False):
        self.items.append((src, dst, self.p.orders(swapped)[::-1]))
        return len(self.items) - 1

    def copy(self, n, mask, stage):
        src, dst, order = self.items[n]
        j = self.p.at(mask)
        k = self.index(n, mask | order[stage])
        return rcopy(
            src if mask == 0 else dst(j),
            dst(j),
            self.ss.at[n, k],
            self.rs.at[n, k],
            self.p.to_dp(order[stage]),
        )

    def index(self, n, mask):
        return mask - 1

    def stage_of(self, n, mask):
        return max(i for i, b in enumerate(self.items[n][2]) if mask & b)

    def arrived(self, n, mask):
        src, dst, order = self.items[n]
        stage = self.stage_of(n, mask)
        j = self.p.at(mask)
        k = self.index(n, mask)
        rcopy(src, dst(j), self.ss.at[n, k], self.rs.at[n, k], self.p.to_dp(order[stage])).wait_recv()

    def launch(self):
        if self.launched < len(self.items):
            n = self.launched
            for stage in range(len(self.p.bits)):
                self.copy(n, 0, stage).start()
            self.launched += 1

    def masks(self, n):
        order = self.items[n][2]
        last = order[-1]
        out = [m for m in range(1, self.p.ndp) if not m & last]
        return sorted(out, key=lambda m: (self.stage_of(n, m), m))

    def forward(self, n, stage):
        for m in self.masks(n):
            if self.stage_of(n, m) == stage:
                self.arrived(n, m)
                for later in range(stage + 1, len(self.p.bits)):
                    self.copy(n, m, later).start()

    def steps(self, count, ahead):
        lag = len(self.p.bits) - 1
        for _ in range(count):
            if self.seen >= len(self.items) + lag - 1:
                return
            while self.launched < min(len(self.items), self.seen + ahead):
                self.launch()
            for stage in range(lag):
                n = self.seen - stage
                if self.first <= n < len(self.items):
                    self.forward(n, stage)
            self.seen += 1

    def need(self, n, ahead):
        self.steps(n + len(self.p.bits) - 1 - self.seen, ahead)

    def wait_last(self, n):
        last = self.items[n][2][-1]
        for m in range(self.p.ndp):
            if m & last:
                self.arrived(n, m)

    def wait_sends(self, n):
        for m in range(self.p.ndp):
            first = 0 if m == 0 else self.stage_of(n, m) + 1
            for stage in range(first, len(self.p.bits)):
                self.copy(n, m, stage).wait_send()


class FsGather:
    def __init__(self, pos, blocks, ss, rs):
        self.p, self.b, self.ss, self.rs = pos, blocks, ss, rs

    def copy(self, n, fb, dev):
        return rcopy(self.b(fb), self.b(fb), self.ss.at[n], self.rs.at[n], dev)

    def start(self):
        self.copy(1, self.p.f, self.p.to_y).start()
        self.copy(0, self.p.f, self.p.to_core).start()

    def mid(self):
        self.copy(1, self.p.f_y, self.p.to_y).wait_recv()
        self.copy(2, self.p.f_y, self.p.to_core).start()

    def end(self):
        self.copy(0, self.p.f_core, self.p.to_core).wait_recv()
        self.copy(2, self.p.f_yc, self.p.to_core).wait_recv()

    def wait_sends(self):
        self.copy(1, self.p.f, self.p.to_y).wait_send()
        self.copy(0, self.p.f, self.p.to_core).wait_send()
        self.copy(2, self.p.f_y, self.p.to_core).wait_send()


class FsReduce:
    def __init__(self, pos, blocks, from_core, from_y, ss, rs):
        self.p, self.b, self.fc, self.fy, self.ss, self.rs = pos, blocks, from_core, from_y, ss, rs

    def c1(self):
        return rcopy(
            self.b(self.p.f_yc), self.fc.at[1], self.ss.at[1], self.rs.at[1], self.p.to_core
        )

    def c0(self):
        return rcopy(
            self.b(self.p.f_core), self.fc.at[0], self.ss.at[0], self.rs.at[0], self.p.to_core
        )

    def cy(self):
        return rcopy(self.fc.at[1], self.fy, self.ss.at[2], self.rs.at[2], self.p.to_y)

    def start(self):
        self.c1().start()
        self.c0().start()

    def mid(self, rows, tile=64):
        self.c1().wait_recv()
        mine = self.b(self.p.f_y)

        def add(t, _):
            r = pl.ds(al(t * tile, tile), tile)
            self.fc[1, r, :] = (self.fc[1, r, :].astype(F32) + mine[r, :].astype(F32)).astype(BF16)
            return 0

        lax.fori_loop(0, rows // tile, add, 0)
        self.cy().start()

    def end(self):
        self.c0().wait_recv()
        self.cy().wait_recv()

    def value(self, r):
        return (
            self.b(self.p.f)[r, :].astype(F32)
            + self.fc[0, r, :].astype(F32)
            + self.fy[r, :].astype(F32)
        )

    def wait_sends(self):
        self.c1().wait_send()
        self.c0().wait_send()
        self.cy().wait_send()


def softmax_parts(scores):
    top = jnp.max(scores, axis=-1, keepdims=True)
    lifted = jnp.exp(scores - top)
    return lifted / jnp.sum(lifted, axis=-1, keepdims=True)


def causal_bias(rows):
    r = lax.broadcasted_iota(jnp.int32, (rows, rows), 0)
    c = lax.broadcasted_iota(jnp.int32, (rows, rows), 1)
    return jnp.where(c <= r, 0.0, MASK_FILL).astype(F32)


def group_rows(ref, m, half, cols, own):
    t = own // 2
    first = ref[pl.ds((2 * half) * own + m * t, t), cols]
    second = ref[pl.ds((2 * half + 1) * own + m * t, t), cols]
    return jnp.concatenate([first, second], axis=0)


def put_rows(ref, m, half, cols, own, value):
    t = own // 2
    ref[pl.ds((2 * half) * own + m * t, t), cols] = value[:t]
    ref[pl.ds((2 * half + 1) * own + m * t, t), cols] = value[t:]


def forward_kernel(
    cfg,
    tok,
    dout,
    cos,
    sin,
    bias,
    seq_sh,
    gain_sh,
    qb_sh,
    out_sh,
    gate_sh,
    up_sh,
    down_sh,
    qb_all,
    out_all,
    gate_all,
    up_all,
    down_all,
    seq_all,
    gain_sum,
    lkv_o,
    q_o,
    mixed_o,
    latent_o,
    normed_o,
    middle_o,
    hid_o,
    gg_o,
    gu_o,
    gw_gate,
    gw_up,
    gw_down,
    seq_v,
    gain_v,
    qb_v,
    out_v,
    lkv_v,
    q_v,
    mixed_v,
    part_v,
    fcore_v,
    fy_v,
    n2_v,
    d_v,
    n2_t,
    d_t,
    lat_v,
    gss,
    grs,
    fss,
    frs,
    sys_,
    syr,
    ls,
    ffn_ls,
):
    ndp, own, dim, rank, hd, heads = cfg
    rows = NF * own
    p = Place(ndp)
    kvw = rank + 2 * hd
    sr = seq_sh.shape[0]
    g = DpGather(p, gss, grs)
    i_seq = g.add(seq_sh, lambda j: seq_v.at[pl.ds(al((j * NF + p.f) * sr, sr), sr)])
    i_gain = g.add(gain_sh, lambda j: gain_v.at[j * NF + p.f])
    turn = [0]

    def weight_items(src, dst, cols=slice(None), most=GATHER_ROWS):
        n = src.shape[0]
        step = min(n, most)
        out = []
        for c in range(n // step):
            turn[0] += 1
            out.append(
                g.add(
                    src.at[pl.ds(c * step, step), cols],
                    lambda j, c=c: dst.at[pl.ds(al(j * n + c * step, step), step), cols],
                    turn[0] % 4 == 0,
                )
            )
        return out

    i_qb = weight_items(qb_sh, qb_v)
    i_out = weight_items(out_sh, out_v)
    i_ffn = []
    for c0, cw in ffn_chunks(gate_sh.shape[1]):
        cols = pl.ds(c0, cw)
        some = []
        for s, d in ((gate_sh, gate_all), (up_sh, up_all), (down_sh, down_all)):
            some += weight_items(s, d, cols, FFN_ROWS)
        i_ffn.append(some)
    order = range(len(g.items))
    fs_d = FsGather(p, lambda b: d_v.at[pl.ds(al(b * own, own), own)], fss.at[0], frs.at[0])
    fs_l = FsGather(p, lambda b: lkv_v.at[pl.ds(al(b * own, own), own)], fss.at[1], frs.at[1])
    fs_n = FsGather(p, lambda b: n2_v.at[pl.ds(al(b * own, own), own)], fss.at[2], frs.at[2])
    red = FsReduce(
        p, lambda b: part_v.at[pl.ds(al(b * own, own), own)], fcore_v, fy_v, fss.at[3], frs.at[3]
    )

    local = []

    def local_copy(src, dst):
        c = pltpu.make_async_copy(src, dst, ls.at[len(local)])
        c.start()
        local.append(c)
        return c

    own_copies = {}
    for i in order:
        src, dst, _ = g.items[i]
        own_copies[i] = local_copy(src, dst(p.me))
    d_copies = [
        local_copy(dout.at[m], d_v.at[pl.ds(al(p.f * own + m * (own // 2), 128), own // 2)])
        for m in range(2)
    ]

    p.barrier()
    for _ in range(GATHER_AHEAD):
        g.launch()
    npiece = ndp

    def seq_piece(j, fb):
        return seq_v.at[pl.ds(al((j * NF + fb) * sr, sr), sr)]

    def seq_copy(t, j, fb, dev, which):
        b = seq_piece(j, fb) if which == 0 else gain_v.at[j * NF + fb]
        return rcopy(b, b, sys_.at[which, t, j], syr.at[which, t, j], dev)

    def spread(j):
        for which in (0, 1):
            seq_copy(1, j, p.f, p.to_y, which).start()
            seq_copy(0, j, p.f, p.to_core, which).start()

    for m in range(2):
        x = tok[m].astype(F32)
        inv = lax.rsqrt(jnp.mean(x * x, axis=-1, keepdims=True) + EPSILON)
        middle_o[pl.ds(m * (own // 2), own // 2), :] = x * inv
    own_copies[i_seq].wait()
    own_copies[i_gain].wait()
    spread(p.me)
    for m in sorted(range(1, ndp), key=lambda m: g.stage_of(i_seq, m)):
        for i in (i_seq, i_gain):
            g.arrived(i, m)
            for stage in range(g.stage_of(i, m) + 1, len(p.bits)):
                g.copy(i, m, stage).start()
        spread(p.at(m))
    g.seen = g.first = 2
    for c in d_copies:
        c.wait()

    def spread_forward(j, _):
        for which in (0, 1):
            seq_copy(1, j, p.f_y, p.to_y, which).wait_recv()
            seq_copy(2, j, p.f_y, p.to_core, which).start()
        return 0

    def tick(n):
        g.steps(n, GATHER_AHEAD)

    tick(1)
    lax.fori_loop(0, npiece, spread_forward, 0)
    fs_d.start()
    tick(1)

    def spread_end(j, _):
        for which in (0, 1):
            seq_copy(0, j, p.f_core, p.to_core, which).wait_recv()
            seq_copy(2, j, p.f_yc, p.to_core, which).wait_recv()
        return 0

    lax.fori_loop(0, npiece, spread_end, 0)

    def gain_add(j, acc):
        return acc + gain_v[j]

    gains = lax.fori_loop(0, ndp * NF, gain_add, jnp.zeros(gain_v.shape[1:], F32))
    gain_sum[...] = gains
    wide = dim // rank
    gain_one = jnp.concatenate([gains[r : r + 1] for r in range(wide)], axis=1)
    gain_two = jnp.concatenate([gains[wide + r : wide + r + 1] for r in range(wide)], axis=1)
    gain_lat = gains[2 * wide : 2 * wide + 1]
    normed_o[...] = (middle_o[...] * gain_one).astype(BF16)
    seq_out = local_copy(seq_v, seq_all)

    def project(j, _):
        cols = pl.ds(al(j * 256, 256), 256)
        lat_v[:, cols] = mm(normed_o[...], seq_v[:, cols])
        return 0

    lax.fori_loop(0, kvw // 256, project, 0)
    own_rows = pl.ds(al(p.f * own, own), own)
    lat = lat_v[:, :rank]
    latent_o[...] = lat
    inv_lat = lax.rsqrt(jnp.mean(lat * lat, axis=-1, keepdims=True) + EPSILON)
    lkv_v[own_rows, :rank] = (lat * inv_lat * gain_lat).astype(BF16)
    half = hd // 2
    co, si = cos[own_rows, :], sin[own_rows, :]
    ka, kb = lat_v[:, rank : rank + half], lat_v[:, rank + half : rank + hd]
    lkv_v[own_rows, rank : rank + half] = (ka * co - kb * si).astype(BF16)
    lkv_v[own_rows, rank + half : rank + hd] = (kb * co + ka * si).astype(BF16)
    lkv_v[own_rows, rank + hd :] = lat_v[:, rank + hd :].astype(BF16)
    fs_l.start()
    tick(1)
    fs_d.mid()
    fs_l.mid()
    tick(1)
    for i in i_qb:
        g.need(i, GATHER_AHEAD)
        own_copies[i].wait()
        g.wait_last(i)
    fs_l.end()
    qb_out = local_copy(qb_v, qb_all)
    lkv_out = local_copy(lkv_v, lkv_o)

    def query(j, _):
        cols = pl.ds(al(j * hd, hd), hd)
        c0 = pl.ds(al(j * hd, half), half)
        c1 = pl.ds(al(j * hd + half, half), half)
        for r in range(rows // 512):
            rr = pl.ds(r * 512, 512)
            acc = mm(lkv_v[rr, :rank], qb_v[:, cols])
            a, b = acc[:, :half], acc[:, half:]
            c, s = cos[rr, :], sin[rr, :]
            q_v[rr, c0] = (a * c - b * s).astype(BF16)
            q_v[rr, c1] = (b * c + a * s).astype(BF16)
        return 0

    lax.fori_loop(0, heads, query, 0)
    q_out = local_copy(q_v, q_o)
    tick(1)
    scale = hd ** (-0.5)
    kcols, vcols = slice(rank, rank + hd), slice(rank + hd, rank + 2 * hd)
    causal = causal_bias(PROMPT)
    for m in range(2):
        k0, k1 = (group_rows(lkv_v, m, h2, kcols, own) for h2 in (0, 1))
        v0, v1 = (group_rows(lkv_v, m, h2, vcols, own) for h2 in (0, 1))
        low = bias[m]

        def attend(h, _):
            cols = pl.ds(al(h * hd, hd), hd)
            q0 = group_rows(q_v, m, 0, cols, own)
            pr = softmax_parts(mm_nt(q0, k0) * scale + causal).astype(BF16)
            put_rows(mixed_v, m, 0, cols, own, mm(pr, v0).astype(BF16))
            q1 = group_rows(q_v, m, 1, cols, own)
            s0 = mm_nt(q1, k0) * scale
            s1 = mm_nt(q1, k1) * scale + low
            top = jnp.maximum(
                jnp.max(s0, axis=-1, keepdims=True), jnp.max(s1, axis=-1, keepdims=True)
            )
            e0, e1 = jnp.exp(s0 - top), jnp.exp(s1 - top)
            total = jnp.sum(e0, axis=-1, keepdims=True) + jnp.sum(e1, axis=-1, keepdims=True)
            mix = mm((e0 / total).astype(BF16), v0) + mm((e1 / total).astype(BF16), v1)
            put_rows(mixed_v, m, 1, cols, own, mix.astype(BF16))
            return 0

        lax.fori_loop(0, heads, attend, 0)
        tick(2)
    fs_d.end()
    mixed_out = local_copy(mixed_v, mixed_o)
    tick(1)
    for i in i_out:
        g.need(i, GATHER_AHEAD)
        own_copies[i].wait()
        g.wait_last(i)
    out_out = local_copy(out_v, out_all)

    def project_out(fb):
        rr = pl.ds(al(fb * own, own), own)

        def one(j, _):
            wr = pl.ds(al(j * 256, 256), 256)
            part_v[rr, wr] = mm_nt(mixed_v[rr, :], out_v[wr, :]).astype(BF16)
            return 0

        lax.fori_loop(0, dim // 256, one, 0)

    project_out(p.f_yc)
    project_out(p.f_core)
    red.start()
    tick(1)
    project_out(p.f_y)
    red.mid(own)
    project_out(p.f)
    tick(2)
    red.end()
    for m in range(2):
        rr = pl.ds(m * (own // 2), own // 2)
        mid = tok[m].astype(F32) + red.value(rr)
        middle_o[rr, :] = mid
        inv = lax.rsqrt(jnp.mean(mid * mid, axis=-1, keepdims=True) + EPSILON)
        n2_v[pl.ds(al(p.f * own + m * (own // 2), 128), own // 2), :] = (
            mid * inv * gain_two
        ).astype(BF16)
    fs_n.start()
    tick(1)

    def turn_d(j, _):
        cols = pl.ds(al(j * 256, 256), 256)
        d_t[cols, :] = d_v[:, cols].T
        return 0

    lax.fori_loop(0, dim // 256, turn_d, 0)
    tick(1)
    fs_n.mid()
    tick(1)
    fs_n.end()

    def turn_n2(j, _):
        cols = pl.ds(al(j * 256, 256), 256)
        n2_t[cols, :] = n2_v[:, cols].T
        return 0

    lax.fori_loop(0, dim // 256, turn_n2, 0)
    for c in (q_out, mixed_out, out_out, seq_out):
        c.wait()
    early = [i_seq, i_gain] + i_qb + i_out
    for i in early:
        g.wait_sends(i)

    def spread_sends(j, _):
        for which in (0, 1):
            seq_copy(0, j, p.f, p.to_core, which).wait_send()
            seq_copy(1, j, p.f, p.to_y, which).wait_send()
            seq_copy(2, j, p.f_y, p.to_core, which).wait_send()
        return 0

    lax.fori_loop(0, npiece, spread_sends, 0)
    red.wait_sends()
    pending = []
    width = FFN_COLS
    for (c0, cw), some in zip(ffn_chunks(gate_sh.shape[1]), i_ffn):
        g.need(some[-1], GATHER_AHEAD)
        for i in some:
            own_copies[i].wait()
            g.wait_last(i)
        cols = pl.ds(c0, cw)
        loads = [
            pltpu.make_async_copy(w.at[:, cols], seq_v.at[:, pl.ds(n * width, cw)], ffn_ls.at[n])
            for n, w in enumerate((gate_all, up_all, down_all))
        ]
        for c in loads:
            c.start()
        for c in pending:
            c.wait()
        for c in loads:
            c.wait()
        gate_c, up_c, down_c = (slice(n * width, n * width + cw) for n in range(3))

        def both(t, _):
            rr = pl.ds(al(t * 256, 256), 256)
            gate = mm(n2_v[rr, :], seq_v[:, gate_c])
            up = mm(n2_v[rr, :], seq_v[:, up_c])
            grad_hidden = mm(d_v[rr, :], seq_v[:, down_c])
            sig = 1.0 / (1.0 + jnp.exp(-gate))
            act = gate * sig
            mixed_v[rr, :cw] = (act * up).astype(BF16)
            q_v[rr, gate_c] = (grad_hidden * up * (sig * (1.0 + gate * (1.0 - sig)))).astype(BF16)
            q_v[rr, up_c] = (grad_hidden * act).astype(BF16)
            return 0

        lax.fori_loop(0, rows // 256, both, 0)
        pending = [
            pltpu.make_async_copy(src, dst.at[:, cols], ffn_ls.at[3 + n])
            for n, (src, dst) in enumerate(
                (
                    (mixed_v.at[:, pl.ds(0, cw)], hid_o),
                    (q_v.at[:, pl.ds(0, cw)], gg_o),
                    (q_v.at[:, pl.ds(width, cw)], gu_o),
                )
            )
        ]
        for c in pending:
            c.start()

        half_rows = part_v.shape[0] // 256
        for lo in range(0, dim // 256, half_rows):

            def weight_grads(j, _):
                rr = pl.ds(al(j * 256, 256), 256)
                pr = pl.ds(al((j - lo) * 256, 256), 256)
                pc = slice((lo // half_rows) * width, (lo // half_rows) * width + cw)
                out_v[rr, gate_c] = mm(n2_t[rr, :], q_v[:, gate_c]).astype(BF16)
                out_v[rr, up_c] = mm(n2_t[rr, :], q_v[:, up_c]).astype(BF16)
                part_v[pr, pc] = mm(d_t[rr, :], mixed_v[:, :cw]).astype(BF16)
                return 0

            lax.fori_loop(lo, min(dim // 256, lo + half_rows), weight_grads, 0)
        saves = [
            pltpu.make_async_copy(out_v.at[:, pl.ds(0, cw)], gw_gate.at[:, cols], ffn_ls.at[6]),
            pltpu.make_async_copy(out_v.at[:, pl.ds(width, cw)], gw_up.at[:, cols], ffn_ls.at[7]),
        ]
        prow = part_v.shape[0]
        for n in range(dim // prow):
            saves.append(
                pltpu.make_async_copy(
                    part_v.at[:, pl.ds(n * width, cw)],
                    gw_down.at[pl.ds(n * prow, prow), cols],
                    ffn_ls.at[8 + n],
                )
            )
        for c in saves:
            c.start()
        pending = pending + saves
    for c in pending:
        c.wait()
    tick(2 * len(g.items))
    for i in order:
        if i not in early:
            g.wait_sends(i)
    for t in (fs_d, fs_l, fs_n):
        t.wait_sends()
    for c in (qb_out, lkv_out):
        c.wait()


def forward_call(ndp, tok, dout, cos, sin, bias, seq_sh, gain_sh, qb, out, gate, up, down):
    own = tok.shape[0] * tok.shape[1]
    dim = tok.shape[2]
    rank = qb.shape[0] * ndp
    hd = (seq_sh.shape[1] - rank) // 2
    heads = qb.shape[1] // hd
    rows = NF * own
    kvw = seq_sh.shape[1]
    n_items = 2 + sum(w.shape[0] // min(w.shape[0], GATHER_ROWS) for w in (qb, out))
    n_items += sum(w.shape[0] // min(w.shape[0], FFN_ROWS) for w in (gate, up, down)) * len(
        ffn_chunks(gate.shape[1])
    )

    def sds(shape, dtype=BF16):
        return jax.ShapeDtypeStruct(shape, dtype)

    full = lambda w: sds((w.shape[0] * ndp, w.shape[1]))
    out_shape = (
        full(qb),
        full(out),
        full(gate),
        full(up),
        full(down),
        sds((seq_sh.shape[0] * ndp * NF, kvw)),
        sds(gain_sh.shape, F32),
        sds((rows, kvw)),
        sds((rows, heads * hd)),
        sds((rows, heads * hd)),
        sds((own, rank), F32),
        sds((own, dim)),
        sds((own, dim), F32),
        sds((rows, gate.shape[1])),
        sds((rows, gate.shape[1])),
        sds((rows, gate.shape[1])),
        full(gate),
        full(up),
        full(down),
    )
    out_specs = (ANY,) * 6 + (VMEM,) + (ANY,) * 3 + (VMEM,) * 3 + (ANY,) * 6
    dma = pltpu.SemaphoreType.DMA
    scratch = [
        pltpu.VMEM((seq_sh.shape[0] * ndp * NF, kvw), BF16),
        pltpu.VMEM((ndp * NF,) + gain_sh.shape, F32),
        pltpu.VMEM((qb.shape[0] * ndp, qb.shape[1]), BF16),
        pltpu.VMEM((out.shape[0] * ndp, out.shape[1]), BF16),
        pltpu.VMEM((rows, kvw), BF16),
        pltpu.VMEM((rows, heads * hd), BF16),
        pltpu.VMEM((rows, heads * hd), BF16),
        pltpu.VMEM((rows, dim), BF16),
        pltpu.VMEM((2, own, dim), BF16),
        pltpu.VMEM((own, dim), BF16),
        pltpu.VMEM((rows, dim), BF16),
        pltpu.VMEM((rows, dim), BF16),
        pltpu.VMEM((dim, rows), BF16),
        pltpu.VMEM((dim, rows), BF16),
        pltpu.VMEM((own, kvw), F32),
        dma((n_items, ndp - 1)),
        dma((n_items, ndp - 1)),
        dma((4, 3)),
        dma((4, 3)),
        dma((2, 3, ndp)),
        dma((2, 3, ndp)),
        dma((n_items + 10,)),
        dma((10,)),
    ]
    return pl.pallas_call(
        functools.partial(forward_kernel, (ndp, own, dim, rank, hd, heads)),
        out_shape=out_shape,
        in_specs=(VMEM,) * 5 + (ANY,) * 7,
        out_specs=out_specs,
        scratch_shapes=scratch,
        compiler_params=pltpu.CompilerParams(
            collective_id=0, has_side_effects=True, vmem_limit_bytes=60 * 2**20
        ),
        name="gather_forward",
    )(tok, dout, cos, sin, bias, seq_sh, gain_sh, qb, out, gate, up, down)


class DpScatter:
    PER_TICK = 2

    def __init__(self, pos, count, first, later, own, acc, ss, rs, ls, credit):
        self.p, self.count = pos, count
        self.n = len(pos.bits)
        self.SLOTS, self.AHEAD, self.OWN = scatter_ring(pos.ndp // 2)
        self.first, self.later, self.own, self.acc = first, later, own, acc
        self.ss, self.rs, self.ls, self.credit = ss, rs, ls, credit
        self.items = []
        self.started = self.stepped = 0

    def order(self, n):
        return self.p.orders(False)

    def width(self, stage):
        return 1 << (self.n - 1 - stage)

    def add(self, src, base, out, pieces):
        rows, cols = out.shape
        r = rows // pieces
        for c in range(pieces):
            self.items.append((src, base, out, rows, cols, c * r, r))
        self.pump()

    def mask(self, n, i):
        order = self.order(n)
        return sum(order[1 + t] for t in range(self.n - 1) if i >> (self.n - 2 - t) & 1)

    def block(self, n, mask):
        src, base, out, rows, cols, r0, r = self.items[n]
        return src.at[pl.ds(al(base + self.p.at(mask) * rows + r0, r), r)]

    def place(self, buf, n, lo, size):
        src, base, out, rows, cols, r0, r = self.items[n]
        return buf.at[n % self.SLOTS, pl.ds(lo, size), pl.ds(0, r), pl.ds(0, cols)]

    def copies(self, n, stage):
        bit = self.order(n)[stage]
        dev = self.p.to_dp(bit)
        s = n % self.SLOTS
        if stage == 0:
            return [
                rcopy(
                    self.block(n, bit | self.mask(n, i)),
                    self.place(self.first, n, i, 1).at[0],
                    self.ss.at[s, i],
                    self.rs.at[s, i],
                    dev,
                )
                for i in range(self.width(0))
            ]
        w = self.width(stage)
        k = self.width(0) + stage - 1
        return [
            rcopy(
                self.place(self.first, n, w, w),
                self.place(self.later, n, w - 1, w),
                self.ss.at[s, k],
                self.rs.at[s, k],
                dev,
            )
        ]

    def owncopy(self, n, i):
        src, base, out, rows, cols, r0, r = self.items[n]
        s = n % self.OWN
        return pltpu.make_async_copy(
            self.block(n, self.mask(n, i)),
            self.own.at[s, i, pl.ds(0, r), pl.ds(0, cols)],
            self.ls.at[s, i],
        )

    def outcopy(self, n):
        src, base, out, rows, cols, r0, r = self.items[n]
        s = n % self.SLOTS
        return pltpu.make_async_copy(
            self.acc.at[s, pl.ds(0, r), pl.ds(0, cols)],
            out.at[pl.ds(r0, r)],
            self.ls.at[s, self.width(0)],
        )

    def free(self, n, stage):
        m = n + self.SLOTS
        if m < self.count:
            bit = self.order(m)[stage]
            pl.semaphore_signal(
                self.credit.at[stage, self.p.bits.index(bit)],
                inc=1,
                device_id=self.p.to_dp(bit),
                device_id_type=MESH,
            )

    def send(self, n, stage):
        bit = self.order(n)[stage]
        if n >= self.SLOTS:
            pl.semaphore_wait(self.credit.at[stage, self.p.bits.index(bit)], 1)
        for c in self.copies(n, stage):
            c.start()

    def pump(self):
        while self.started < min(len(self.items), self.stepped + self.AHEAD):
            n = self.started
            self.send(n, 0)
            for i in range(self.width(0)):
                self.owncopy(n, i).start()
            self.started += 1

    def tick(self, steps=1):
        for _ in range(self.PER_TICK * steps):
            n = self.stepped
            if n >= self.started:
                return
            self.combine(n, 0)
            self.stepped += 1
            self.pump()
            for stage in range(1, self.n):
                if n >= stage:
                    self.combine(n - stage, stage)

    def combine(self, n, stage):
        src, base, out, rows, cols, r0, r = self.items[n]
        s, tile = n % self.SLOTS, 16
        w = self.width(stage)
        for c in self.copies(n, stage):
            c.wait_recv()
        if stage == 0:
            for i in range(w):
                self.owncopy(n, i).wait()
        else:
            for c in self.copies(n, stage):
                c.wait_send()
        last = stage == self.n - 1

        def add(lo, size):
            def one(t, _):
                t = pl.ds(al(t * tile, tile), tile)
                for i in range(lo, lo + size):
                    a = self.first[s, i, t, :cols]
                    b = self.own[n % self.OWN, i, t, :cols] if stage == 0 else self.later[s, w - 1 + i, t, :cols]
                    if last:
                        self.acc[s, t, :cols] = a.astype(F32) + b.astype(F32)
                    else:
                        self.first[s, i, t, :cols] = a + b
                return 0

            lax.fori_loop(0, r // tile, one, 0)

        if last:
            if n >= self.SLOTS:
                self.outcopy(n - self.SLOTS).wait()
            for c in self.copies(n, 0):
                c.wait_send()
            add(0, 1)
            self.outcopy(n).start()
            for t in range(self.n):
                self.free(n, t)
        else:
            half = w // 2
            add(half, half)
            self.send(n, stage + 1)
            add(0, half)

    def drain(self):
        self.tick(self.count)
        for n in range(self.count, self.count + self.n - 1):
            for stage in range(1, self.n):
                if 0 <= n - stage < self.count:
                    self.combine(n - stage, stage)
        for n in range(max(0, self.count - self.SLOTS), self.count):
            self.outcopy(n).wait()


def scatter_ring(nz):
    return (10, 6, 7) if nz * max(16, 128 // nz) <= 128 else (5, 2, 3)


def piece_rows(rows, nz):
    return min(rows, max(16, 128 // nz))


def backward_kernel(
    cfg,
    tok,
    dout,
    middle,
    latent,
    normed,
    gains,
    cos,
    sin,
    bias,
    gw_gate,
    gw_up,
    gw_down,
    hid_h,
    gg_h,
    gu_h,
    gate_h,
    up_h,
    down_h,
    lkv_h,
    q_h,
    mixed_h,
    qb_h,
    out_h,
    seq_h,
    o_gate,
    o_up,
    o_down,
    o_out,
    o_qb,
    o_seq,
    o_gain,
    o_in,
    o_y,
    fcore_v,
    fy_v,
    proj_v,
    gmid_v,
    gnorm_v,
    lkv_v,
    q_v,
    mixed_v,
    gm_v,
    kv_acc,
    qb_v,
    out_v,
    seq_v,
    gall_v,
    gain_rx,
    gain_acc,
    first_b,
    later_b,
    own_b,
    acc_b,
    dss,
    drs,
    dls,
    credit,
    fss,
    frs,
    gs,
    gr,
    ls,
    tls,
):
    ndp, own, dim, rank, hd, heads, pieces = cfg
    rows = NF * own
    t2 = own // 2
    kvw = rank + 2 * hd
    wide = dim // rank
    p = Place(ndp)
    sr = o_seq.shape[0]
    local = []

    def local_copy(src, dst):
        c = pltpu.make_async_copy(src, dst, ls.at[len(local)])
        c.start()
        local.append(c)
        return c

    ff = gg_h.shape[1]
    ffc = pl.ds(0, ff)
    gg_in = local_copy(gg_h, lkv_v.at[:, ffc])
    gu_in = local_copy(gu_h, seq_v.at[pl.ds(0, rows), ffc])
    mixed_in = local_copy(mixed_h, mixed_v)
    q_in = local_copy(q_h, q_v)
    qb_in = local_copy(qb_h, qb_v)
    hh = out_v.shape[1]

    def tile_load(t, which):
        src = gate_h if which == 0 else up_h
        s = lax.rem(t, 2) * 2 + which
        return pltpu.make_async_copy(
            src.at[pl.ds(al(t * 256, 256), 256)],
            seq_v.at[pl.ds(al(rows + s * 256, 256), 256), ffc],
            tls.at[s],
        )

    for which in (0, 1):
        tile_load(0, which).start()
    sc = DpScatter(p, sum(pieces), first_b, later_b, own_b, acc_b, dss, drs, dls, credit)
    p.barrier()
    sc.add(gw_gate, 0, o_gate, pieces[0])
    sc.add(gw_up, 0, o_up, pieces[1])
    sc.add(gw_down, 0, o_down, pieces[2])
    gg_in.wait()
    gu_in.wait()
    n_tiles = dim // 256
    per_half = hh // 256

    def norm_grad(t, _):
        for which in (0, 1):
            tile_load(t, which).wait()

        @pl.when(t + 1 < n_tiles)
        def _():
            for which in (0, 1):
                tile_load(t + 1, which).start()

        s = lax.rem(t, 2) * 2
        wg = seq_v[pl.ds(al(rows + s * 256, 256), 256), ffc]
        wu = seq_v[pl.ds(al(rows + s * 256 + 256, 256), 256), ffc]
        cols = pl.ds(al(lax.rem(t, per_half) * 256, 256), 256)
        for r in range(rows // 256):
            rr = pl.ds(r * 256, 256)
            to = pl.ds(al((t // per_half) * rows + r * 256, 256), 256)
            out_v[to, cols] = (
                mm_nt(lkv_v[rr, ffc], wg) + mm_nt(seq_v[rr, ffc], wu)
            ).astype(BF16)
        return 0

    halves = []
    for h in range(dim // hh):
        wide_cols = pl.ds(h * hh, hh)
        lax.fori_loop(h * per_half, (h + 1) * per_half, norm_grad, 0)
        red = FsReduce(
            p,
            lambda b, h=h: out_v.at[pl.ds(al(h * rows + b * own, own), own)],
            fcore_v.at[:, :, wide_cols],
            fy_v.at[:, wide_cols],
            fss.at[4 * h],
            frs.at[4 * h],
        )
        red.start()
        if h > 0:
            halves[-1].mid(own)
        sc.tick(1)
        halves.append(red)
    lkv_in = local_copy(lkv_h, lkv_v)
    seq_in = local_copy(seq_h, seq_v)
    halves[-1].mid(own)
    sc.tick(1)
    for red in halves:
        red.end()
        red.wait_sends()
    gain_two = jnp.concatenate([gains[wide + r : wide + r + 1] for r in range(wide)], axis=1)
    gain_one = jnp.concatenate([gains[r : r + 1] for r in range(wide)], axis=1)
    gain_lat = gains[2 * wide : 2 * wide + 1]
    part_two = jnp.zeros((1, dim), F32)
    for m in range(2):
        rr = pl.ds(m * t2, t2)
        e = jnp.concatenate([red.value(rr) for red in halves], axis=1)
        v = middle[rr, :]
        inv = lax.rsqrt(jnp.mean(v * v, axis=-1, keepdims=True) + EPSILON)
        part_two += jnp.sum(e * v * inv, axis=0, keepdims=True)
        scaled = e * gain_two
        inner = jnp.mean(scaled * v, axis=-1, keepdims=True)
        g = dout[m].astype(F32) + inv * scaled - v * (inv * inv * inv * inner)
        gmid_v[rr, :] = g
        proj_v[pl.ds(al(p.f * own + m * t2, t2), t2), :] = g.astype(BF16)
    out_in = local_copy(out_h, out_v)
    gain_acc[0] = jnp.zeros(gain_acc.shape[1:], F32)
    for r in range(wide):
        gain_acc[0, pl.ds(wide + r, 1), :] = part_two[:, r * rank : (r + 1) * rank]
    ag = FsGather(p, lambda b: proj_v.at[pl.ds(al(b * own, own), own)], fss.at[1], frs.at[1])
    ag.start()
    sc.tick(1)
    ag.mid()
    sc.tick(1)
    out_in.wait()
    ag.end()
    ag.wait_sends()

    def back_out(j, _):
        cols = pl.ds(al(j * 256, 256), 256)
        for r in range(rows // 512):
            rr = pl.ds(r * 512, 512)
            gm_v[rr, cols] = mm(proj_v[rr, :], out_v[:, cols]).astype(BF16)
        return 0

    lax.fori_loop(0, heads * hd // 256, back_out, 0)
    sc.tick(1)
    mixed_in.wait()

    def grad_out(j, _):
        cols = pl.ds(al(j * 256, 256), 256)
        out_v[cols, :] = mm_tn(proj_v[:, cols], mixed_v[...]).astype(BF16)
        return 0

    lax.fori_loop(0, dim // 256, grad_out, 0)
    sc.tick(1)
    sc.add(out_v, 0, o_out, pieces[3])
    q_in.wait()
    lkv_in.wait()
    scale = hd ** (-0.5)
    half = hd // 2
    kcols, vcols = slice(rank, rank + hd), slice(rank + hd, rank + 2 * hd)
    causal = causal_bias(PROMPT)
    everything = slice(None)

    for m in range(2):
        k0, k1 = (group_rows(lkv_v, m, h2, kcols, own) for h2 in (0, 1))
        v0, v1 = (group_rows(lkv_v, m, h2, vcols, own) for h2 in (0, 1))
        low = bias[m]
        kv_acc[...] = jnp.zeros(kv_acc.shape, F32)

        def put_query(h, which, g):
            co = group_rows(cos, m, which, everything, own)
            si = group_rows(sin, m, which, everything, own)
            a, b = g[:, :half] * scale, g[:, half:] * scale
            c0 = pl.ds(al(h * hd, half), half)
            c1 = pl.ds(al(h * hd + half, half), half)
            put_rows(gm_v, m, which, c0, own, (a * co + b * si).astype(BF16))
            put_rows(gm_v, m, which, c1, own, (b * co - a * si).astype(BF16))

        def attend_back(h, _):
            cols = pl.ds(al(h * hd, hd), hd)
            q0 = group_rows(q_v, m, 0, cols, own)
            g0 = group_rows(gm_v, m, 0, cols, own)
            pr = softmax_parts(mm_nt(q0, k0) * scale + causal)
            gp = mm_nt(g0, v0)
            gsc = (pr * (gp - jnp.sum(pr * gp, axis=-1, keepdims=True))).astype(BF16)
            kv_acc[2] += mm_tn(pr.astype(BF16), g0)
            kv_acc[0] += mm_tn(gsc, q0)
            put_query(h, 0, mm(gsc, k0))
            q1 = group_rows(q_v, m, 1, cols, own)
            g1 = group_rows(gm_v, m, 1, cols, own)
            s0 = mm_nt(q1, k0) * scale
            s1 = mm_nt(q1, k1) * scale + low
            top = jnp.maximum(
                jnp.max(s0, axis=-1, keepdims=True), jnp.max(s1, axis=-1, keepdims=True)
            )
            e0, e1 = jnp.exp(s0 - top), jnp.exp(s1 - top)
            total = jnp.sum(e0, axis=-1, keepdims=True) + jnp.sum(e1, axis=-1, keepdims=True)
            p0, p1 = e0 / total, e1 / total
            gp0, gp1 = mm_nt(g1, v0), mm_nt(g1, v1)
            inner = jnp.sum(p0 * gp0, axis=-1, keepdims=True) + jnp.sum(
                p1 * gp1, axis=-1, keepdims=True
            )
            gs0 = (p0 * (gp0 - inner)).astype(BF16)
            gs1 = (p1 * (gp1 - inner)).astype(BF16)
            kv_acc[2] += mm_tn(p0.astype(BF16), g1)
            kv_acc[3] += mm_tn(p1.astype(BF16), g1)
            kv_acc[0] += mm_tn(gs0, q1)
            kv_acc[1] += mm_tn(gs1, q1)
            put_query(h, 1, mm(gs0, k0) + mm(gs1, k1))
            return 0

        lax.fori_loop(0, heads, attend_back, 0)
        for h2 in (0, 1):
            put_rows(proj_v, m, h2, kcols, own, (kv_acc[h2] * scale).astype(BF16))
            put_rows(proj_v, m, h2, vcols, own, kv_acc[2 + h2].astype(BF16))
        sc.tick(1)
    qb_in.wait()

    def back_latent(j, _):
        wr = pl.ds(al(j * 256, 256), 256)
        for r in range(rows // 512):
            rr = pl.ds(r * 512, 512)
            proj_v[rr, wr] = mm_nt(gm_v[rr, :], qb_v[wr, :]).astype(BF16)
        return 0

    lax.fori_loop(0, rank // 256, back_latent, 0)

    def grad_qb(j, _):
        cols = pl.ds(al(j * 256, 256), 256)
        qb_v[cols, :] = mm_tn(lkv_v[:, cols], gm_v[...]).astype(BF16)
        return 0

    lax.fori_loop(0, rank // 256, grad_qb, 0)
    narrow = pl.ds(0, kvw)
    red2 = FsReduce(
        p,
        lambda b: proj_v.at[pl.ds(al(b * own, own), own), narrow],
        fcore_v.at[:, :, narrow],
        fy_v.at[:, narrow],
        fss.at[2],
        frs.at[2],
    )
    red2.start()
    sc.tick(1)
    sc.add(qb_v, 0, o_qb, pieces[4])
    red2.mid(own)
    sc.tick(1)
    red2.end()
    red2.wait_sends()
    own_rows = pl.ds(al(p.f * own, own), own)
    part_lat = jnp.zeros((1, rank), F32)
    for m in range(2):
        rr = pl.ds(m * t2, t2)
        gr_rows = pl.ds(al(p.f * own + m * t2, t2), t2)
        e = red2.value(rr)
        v = latent[rr, :]
        inv = lax.rsqrt(jnp.mean(v * v, axis=-1, keepdims=True) + EPSILON)
        el = e[:, :rank]
        part_lat += jnp.sum(el * v * inv, axis=0, keepdims=True)
        scaled = el * gain_lat
        inner = jnp.mean(scaled * v, axis=-1, keepdims=True)
        gall_v[rr, :rank] = (inv * scaled - v * (inv * inv * inv * inner)).astype(BF16)
        co, si = cos[gr_rows, :], sin[gr_rows, :]
        a, b = e[:, rank : rank + half], e[:, rank + half : rank + hd]
        gall_v[rr, rank : rank + half] = (a * co + b * si).astype(BF16)
        gall_v[rr, rank + half : rank + hd] = (b * co - a * si).astype(BF16)
        gall_v[rr, rank + hd :] = e[:, rank + hd :].astype(BF16)
    gain_acc[0, pl.ds(2 * wide, 1), :] = part_lat
    seq_in.wait()

    def back_seq(j, _):
        wr = pl.ds(al(j * 256, 256), 256)
        gnorm_v[:, wr] = mm_nt(gall_v[...], seq_v[wr, :])
        return 0

    lax.fori_loop(0, dim // 256, back_seq, 0)
    sc.tick(1)
    span = NF * sr

    def grad_seq(j, _):
        cols = pl.ds(al(j * 256, 256), 256)
        g = mm_tn(normed[:, cols], gall_v[...]).astype(BF16)
        for i in range(256 // span):
            for fb in range(NF):
                seq_v[pl.ds(al(fb * ndp * sr + (j * (256 // span) + i) * sr, sr), sr), :] = g[
                    i * span + fb * sr : i * span + (fb + 1) * sr
                ]
        return 0

    lax.fori_loop(0, dim // 256, grad_seq, 0)
    srows = ndp * sr
    core3 = [lkv_v.at[pl.ds(0, srows)], lkv_v.at[pl.ds(srows, srows)]]

    def sblock(b):
        return seq_v.at[pl.ds(al(b * srows, srows), srows)]

    c1 = rcopy(sblock(p.f_yc), core3[1], fss.at[3, 1], frs.at[3, 1], p.to_core)
    c0 = rcopy(sblock(p.f_core), core3[0], fss.at[3, 0], frs.at[3, 0], p.to_core)
    mw = mixed_v.shape[1]
    cys = [
        rcopy(
            lkv_v.at[pl.ds(srows, srows), pl.ds(0, mw)],
            mixed_v.at[pl.ds(0, srows)],
            fss.at[3, 2],
            frs.at[3, 2],
            p.to_y,
        ),
        rcopy(
            lkv_v.at[pl.ds(srows, srows), pl.ds(mw, kvw - mw)],
            mixed_v.at[pl.ds(srows, srows), pl.ds(0, kvw - mw)],
            fss.at[3, 3],
            frs.at[3, 3],
            p.to_y,
        ),
    ]
    c1.start()
    c0.start()
    part_one = jnp.zeros((1, dim), F32)
    for m in range(2):
        rr = pl.ds(m * t2, t2)
        e = gnorm_v[rr, :]
        v = tok[m].astype(F32)
        inv = lax.rsqrt(jnp.mean(v * v, axis=-1, keepdims=True) + EPSILON)
        part_one += jnp.sum(e * v * inv, axis=0, keepdims=True)
        scaled = e * gain_one
        inner = jnp.mean(scaled * v, axis=-1, keepdims=True)
        o_in[m] = (gmid_v[rr, :] + inv * scaled - v * (inv * inv * inv * inner)).astype(BF16)
    for r in range(wide):
        gain_acc[0, pl.ds(r, 1), :] = part_one[:, r * rank : (r + 1) * rank]
    gain_steps = [
        rcopy(gain_acc.at[0], gain_rx.at[0], gs.at[0], gr.at[0], p.to_core),
        rcopy(gain_acc.at[1], gain_rx.at[1], gs.at[1], gr.at[1], p.to_y),
    ] + [
        rcopy(gain_acc.at[2 + b], gain_rx.at[2 + b], gs.at[2 + b], gr.at[2 + b], p.to_dp(bit))
        for b, bit in enumerate(p.bits)
    ]
    gain_steps[0].start()
    c1.wait_recv()

    def seq_y(t, _):
        t = al(t * 64, 64)
        a = pl.ds(srows + t, 64)
        b = pl.ds(al(p.f_y * srows + t, 64), 64)
        lkv_v[a, :] = lkv_v[a, :] + seq_v[b, :]
        return 0

    lax.fori_loop(0, srows // 64, seq_y, 0)
    for c in cys:
        c.start()
    for n in range(len(gain_steps)):
        gain_steps[n].wait_recv()
        gain_acc[n + 1] = gain_acc[n] + gain_rx[n]
        if n + 1 < len(gain_steps):
            gain_steps[n + 1].start()
        if n % 2 == 0:
            sc.tick(1)
    c0.wait_recv()
    for c in cys:
        c.wait_recv()

    def seq_f(t, _):
        t = al(t * 64, 64)
        a = pl.ds(t, 64)
        b = pl.ds(al(p.f * srows + t, 64), 64)
        a2 = pl.ds(srows + t, 64)
        seq_v[b, :mw] = (
            lkv_v[a, :mw].astype(F32) + seq_v[b, :mw].astype(F32) + mixed_v[a, :].astype(F32)
        ).astype(BF16)
        seq_v[b, mw:] = (
            lkv_v[a, mw:].astype(F32)
            + seq_v[b, mw:].astype(F32)
            + mixed_v[a2, : kvw - mw].astype(F32)
        ).astype(BF16)
        return 0

    lax.fori_loop(0, srows // 64, seq_f, 0)
    sc.add(seq_v, p.f * srows, o_seq, pieces[5])
    o_gain[...] = gain_acc[len(gain_steps)]
    for t in [c1, c0] + cys:
        t.wait_send()
    hid_in = local_copy(hid_h, lkv_v.at[:, ffc])

    def down_load(t):
        s = lax.rem(t, 2)
        return pltpu.make_async_copy(
            down_h.at[pl.ds(al(t * 256, 256), 256)],
            seq_v.at[pl.ds(al(p.f_core * srows + s * 256, 256), 256), ffc],
            tls.at[s],
        )

    down_load(0).start()
    sc.tick(1)
    hid_in.wait()

    def ffn_out(t, _):
        down_load(t).wait()

        @pl.when(t + 1 < n_tiles)
        def _():
            down_load(t + 1).start()

        w = seq_v[pl.ds(al(p.f_core * srows + lax.rem(t, 2) * 256, 256), 256), ffc]
        cols = pl.ds(al(t * 256, 256), 256)
        for r in range(rows // 256):
            rr = pl.ds(r * 256, 256)
            proj_v[rr, cols] = mm_nt(lkv_v[rr, ffc], w).astype(BF16)
        return 0

    lax.fori_loop(0, n_tiles, ffn_out, 0)
    red3 = FsReduce(
        p,
        lambda b: proj_v.at[pl.ds(al(b * own, own), own)],
        fcore_v,
        fy_v,
        fss.at[5],
        frs.at[5],
    )
    red3.start()
    sc.tick(1)
    red3.mid(own)
    sc.tick(2)
    red3.end()
    for m in range(2):
        rr = pl.ds(m * t2, t2)
        o_y[m] = (middle[rr, :] + red3.value(rr)).astype(BF16)
    sc.drain()
    red3.wait_sends()
    for t in gain_steps:
        t.wait_send()


def backward_call(ndp, tok, dout, middle, latent, normed, gains, cos, sin, bias, grads, ffn, saved):
    lkv, q, mixed, qb, out, seq = saved
    nz = ndp // 2
    own, dim = middle.shape
    rank = latent.shape[1]
    kvw = lkv.shape[1]
    hd = (kvw - rank) // 2
    heads = q.shape[1] // hd
    rows = NF * own
    sr = seq.shape[0] // (ndp * NF)
    shards = [(w.shape[0] // ndp, w.shape[1]) for w in grads] + [
        (out.shape[0] // ndp, out.shape[1]),
        (qb.shape[0] // ndp, qb.shape[1]),
        (sr, kvw),
    ]
    pieces = tuple(s[0] // piece_rows(s[0], nz) for s in shards)
    n = sum(pieces)
    slots, _, own_slots = scatter_ring(nz)
    nb = ndp.bit_length() - 1
    pr = max(piece_rows(s[0], nz) for s in shards)
    width = max(s[1] for s in shards)
    dma = pltpu.SemaphoreType.DMA
    scratch = [
        pltpu.VMEM((2, own, dim), BF16),
        pltpu.VMEM((own, dim), BF16),
        pltpu.VMEM((rows, dim), BF16),
        pltpu.VMEM((own, dim), F32),
        pltpu.VMEM((own, dim), F32),
        pltpu.VMEM(lkv.shape, BF16),
        pltpu.VMEM(q.shape, BF16),
        pltpu.VMEM(mixed.shape, BF16),
        pltpu.VMEM(q.shape, BF16),
        pltpu.VMEM((4, rows // 4, hd), F32),
        pltpu.VMEM(qb.shape, BF16),
        pltpu.VMEM(out.shape, BF16),
        pltpu.VMEM(seq.shape, BF16),
        pltpu.VMEM((own, kvw), BF16),
        pltpu.VMEM((2 + nb,) + gains.shape, F32),
        pltpu.VMEM((3 + nb,) + gains.shape, F32),
        pltpu.VMEM((slots, nz, pr, width), BF16),
        pltpu.VMEM((slots, nz - 1, pr, width), BF16),
        pltpu.VMEM((own_slots, nz, pr, width), BF16),
        pltpu.VMEM((slots, pr, width), F32),
        dma((slots, nz + nb - 1)),
        dma((slots, nz + nb - 1)),
        dma((slots, nz + 1)),
        pltpu.SemaphoreType.REGULAR((nb, nb)),
        dma((6, 4)),
        dma((6, 4)),
        dma((2 + nb,)),
        dma((2 + nb,)),
        dma((9,)),
        dma((4,)),
    ]
    return pl.pallas_call(
        functools.partial(backward_kernel, (ndp, own, dim, rank, hd, heads, pieces)),
        out_shape=tuple(jax.ShapeDtypeStruct(s, F32) for s in shards)
        + (
            jax.ShapeDtypeStruct(gains.shape, F32),
            jax.ShapeDtypeStruct(tok.shape, BF16),
            jax.ShapeDtypeStruct(tok.shape, BF16),
        ),
        in_specs=(VMEM,) * 9 + (ANY,) * 15,
        out_specs=(ANY,) * 6 + (VMEM,) * 3,
        scratch_shapes=scratch,
        compiler_params=pltpu.CompilerParams(
            collective_id=1, has_side_effects=True, vmem_limit_bytes=62 * 2**20
        ),
        name="backward_scatter",
    )(tok, dout, middle, latent, normed, gains, cos, sin, bias, *grads, *ffn, lkv, q, mixed, qb, out, seq)


def per_device(
    ndp,
    tokens,
    membership,
    d_output,
    gain_attn,
    w_qa,
    gain_latent,
    w_qb,
    w_key,
    w_value,
    w_out,
    gain_ffn,
    w_gate,
    w_up,
    w_down,
):
    micro, tlen, dim = tokens.shape
    own = micro * tlen
    rank = w_qa.shape[1]
    hd = w_key.shape[1]
    heads = w_qb.shape[1] // hd
    rows = NF * own
    wide = dim // rank
    labels, positions = jax.vmap(lambda r: layout(r, BLK))(membership[0])
    pos_rows = positions.reshape(micro, NF, tlen).transpose(1, 0, 2).reshape(rows)
    cos, sin = rope_tables(pos_rows, hd)
    tail = labels[:, PROMPT:]
    idx = jnp.arange(tail.shape[1], dtype=jnp.int32)
    seen = (idx[None, None, :] <= idx[None, :, None]) & (tail[:, None, :] == tail[:, :, None])
    bias = jnp.where(seen, 0.0, MASK_FILL).astype(F32)
    block = lax.axis_index("dp") * NF + lax.axis_index("fsdp")

    def spot(gain):
        width = gain.shape[0]
        count = ndp * NF
        at = lax.broadcasted_iota(jnp.int32, (count, width), 0) == block
        placed = jnp.where(at, gain.astype(F32)[None, :], 0.0)
        return placed.reshape(count * width // rank, rank)

    gain_sh = jnp.concatenate([spot(gain_attn), spot(gain_ffn), spot(gain_latent)], axis=0)
    gain_sh = jnp.pad(gain_sh, ((0, 8 - gain_sh.shape[0]), (0, 0)))
    seq_sh = jnp.concatenate([w_qa, w_key, w_value], axis=1)
    (
        qb_all,
        out_all,
        gate_all,
        up_all,
        down_all,
        seq_all,
        gains,
        lkv,
        q_all,
        mixed,
        latent,
        normed,
        middle,
        hidden,
        grad_gate,
        grad_up,
        gw_gate,
        gw_up,
        gw_down,
    ) = forward_call(
        ndp, tokens, d_output, cos, sin, bias, seq_sh, gain_sh, w_qb, w_out, w_gate, w_up, w_down
    )
    o_gate, o_up, o_down, o_out, o_qb, o_seq, o_gain, input_grad, output = backward_call(
        ndp,
        tokens,
        d_output,
        middle,
        latent,
        normed,
        gains,
        cos,
        sin,
        bias,
        (gw_gate, gw_up, gw_down),
        (hidden, grad_gate, grad_up, gate_all, up_all, down_all),
        (lkv, q_all, mixed, qb_all, out_all, seq_all),
    )

    def own_gain(flat, width):
        return lax.dynamic_slice_in_dim(flat.reshape(-1), block * width, width, 0)

    return (
        output,
        input_grad,
        own_gain(o_gain[:wide], gain_attn.shape[0]),
        o_seq[:, :rank],
        own_gain(o_gain[2 * wide], gain_latent.shape[0]),
        o_qb,
        o_seq[:, rank : rank + hd],
        o_seq[:, rank + hd :],
        o_out,
        own_gain(o_gain[wide : 2 * wide], gain_ffn.shape[0]),
        o_gate,
        o_up,
        o_down,
    )


def solution(mesh):
    both = ("dp", "fsdp")
    rowwise, vector = P(both, None), P(both)
    tok = P(None, both, None)
    head = P("dp", "fsdp")
    return jax.shard_map(
        functools.partial(per_device, mesh.shape["dp"]),
        mesh=mesh,
        in_specs=(
            tok,
            P("dp", None, None),
            tok,
            vector,
            rowwise,
            vector,
            head,
            rowwise,
            rowwise,
            head,
            vector,
            head,
            head,
            head,
        ),
        out_specs=(
            tok,
            tok,
            vector,
            rowwise,
            vector,
            head,
            rowwise,
            rowwise,
            head,
            vector,
            head,
            head,
            head,
        ),
        check_vma=False,
    )
```

```python
import functools

import jax
import jax.numpy as jnp
from jax import lax
from jax.experimental import pallas as pl
from jax.experimental.pallas import tpu as pltpu
from jax.sharding import PartitionSpec as P

BLK = 32
PROMPT = 256
EPSILON = 1e-05
ROPE_BASE = 10000.0
MASK_FILL = -1e30
F32 = jnp.float32
BF16 = jnp.bfloat16
MESH = pl.DeviceIdType.MESH
ANY = pl.BlockSpec(memory_space=pl.ANY)
VMEM = pl.BlockSpec(memory_space=pltpu.VMEM)
NF = 4
GATHER_ROWS = 64
GATHER_AHEAD = 5
GATHER_FIRST = 4
FFN_ROWS = 128
FFN_COLS = 512


def ffn_chunks(cols):
    return [(c, min(FFN_COLS, cols - c)) for c in range(0, cols, FFN_COLS)]


def layout(member_row, block_len):
    count_blocks = member_row.shape[0]
    block_ids = jnp.arange(count_blocks, dtype=jnp.int32)
    same_run = (member_row[None, :] == member_row[:, None]) & (
        block_ids[None, :] < block_ids[:, None]
    )
    earlier = jnp.sum(same_run.astype(jnp.int32), axis=1)
    prompt_len = jnp.sum((member_row == 0).astype(jnp.int32)) * block_len
    labels = jnp.repeat(member_row, block_len)
    within = jnp.arange(count_blocks * block_len, dtype=jnp.int32) % block_len
    positions = (
        (labels > 0).astype(jnp.int32) * prompt_len
        + jnp.repeat(earlier, block_len) * block_len
        + within
    )
    return (labels, positions)


def rope_tables(positions, head_width):
    half_width = head_width // 2
    frequency = ROPE_BASE ** (-(jnp.arange(half_width, dtype=jnp.float32) * (2.0 / head_width)))
    angles = positions.astype(jnp.float32)[:, None] * frequency[None, :]
    return (jnp.cos(angles), jnp.sin(angles))


def al(x, n):
    return pl.multiple_of(x, n)


def mm(a, b):
    return lax.dot_general(a, b, (((1,), (0,)), ((), ())), preferred_element_type=F32)


def mm_nt(a, b):
    return lax.dot_general(a, b, (((1,), (1,)), ((), ())), preferred_element_type=F32)


def mm_tn(a, b):
    return lax.dot_general(a, b, (((0,), (0,)), ((), ())), preferred_element_type=F32)


class Place:
    def __init__(self, ndp):
        self.ndp = ndp
        self.bits = [1 << b for b in range(ndp.bit_length() - 1)]
        self.me = lax.axis_index("dp")
        self.f = lax.axis_index("fsdp")
        y, c = self.f // 2, self.f % 2
        self.f_core = y * 2 + 1 - c
        self.f_y = (1 - y) * 2 + c
        self.f_yc = (1 - y) * 2 + 1 - c
        self.to_core = (self.me, self.f_core)
        self.to_y = (self.me, self.f_y)

    def at(self, mask):
        j = self.me
        for b in self.bits:
            if mask & b:
                j = j + b - 2 * b * ((self.me // b) % 2)
        return j

    def to_dp(self, mask):
        return (self.at(mask), self.f)

    def orders(self, swapped):
        o = list(self.bits)
        if swapped and len(o) > 1:
            o[0], o[1] = o[1], o[0]
        return o

    def barrier(self):
        bar = pltpu.get_barrier_semaphore()
        devs = [self.to_dp(b) for b in self.bits] + [self.to_core, self.to_y]
        for d in devs:
            pl.semaphore_signal(bar, inc=1, device_id=d, device_id_type=MESH)
        pl.semaphore_wait(bar, len(devs))


def rcopy(src, dst, ss, rs, dev):
    return pltpu.make_async_remote_copy(
        src_ref=src, dst_ref=dst, send_sem=ss, recv_sem=rs, device_id=dev, device_id_type=MESH
    )


class DpGather:
    def __init__(self, pos, ss, rs):
        self.p, self.ss, self.rs = pos, ss, rs
        self.items, self.events = [], []
        self.launched = self.seen = self.first = 0

    def add(self, src, dst, swapped=False):
        self.items.append((src, dst, self.p.orders(swapped)[::-1]))
        return len(self.items) - 1

    def copy(self, n, mask, stage):
        src, dst, order = self.items[n]
        j = self.p.at(mask)
        k = self.index(n, mask | order[stage])
        return rcopy(
            src if mask == 0 else dst(j),
            dst(j),
            self.ss.at[n, k],
            self.rs.at[n, k],
            self.p.to_dp(order[stage]),
        )

    def index(self, n, mask):
        return mask - 1

    def stage_of(self, n, mask):
        return max(i for i, b in enumerate(self.items[n][2]) if mask & b)

    def arrived(self, n, mask):
        src, dst, order = self.items[n]
        stage = self.stage_of(n, mask)
        j = self.p.at(mask)
        k = self.index(n, mask)
        rcopy(src, dst(j), self.ss.at[n, k], self.rs.at[n, k], self.p.to_dp(order[stage])).wait_recv()

    def launch(self):
        if self.launched < len(self.items):
            n = self.launched
            for stage in range(len(self.p.bits)):
                self.copy(n, 0, stage).start()
            self.launched += 1

    def masks(self, n):
        order = self.items[n][2]
        last = order[-1]
        out = [m for m in range(1, self.p.ndp) if not m & last]
        return sorted(out, key=lambda m: (self.stage_of(n, m), m))

    def forward(self, n, stage):
        for m in self.masks(n):
            if self.stage_of(n, m) == stage:
                self.arrived(n, m)
                for later in range(stage + 1, len(self.p.bits)):
                    self.copy(n, m, later).start()

    def steps(self, count, ahead):
        lag = len(self.p.bits) - 1
        for _ in range(count):
            if self.seen >= len(self.items) + lag - 1:
                return
            while self.launched < min(len(self.items), self.seen + ahead):
                self.launch()
            for stage in range(lag):
                n = self.seen - stage
                if self.first <= n < len(self.items):
                    self.forward(n, stage)
            self.seen += 1

    def need(self, n, ahead):
        self.steps(n + len(self.p.bits) - 1 - self.seen, ahead)

    def wait_last(self, n):
        last = self.items[n][2][-1]
        for m in range(self.p.ndp):
            if m & last:
                self.arrived(n, m)

    def wait_sends(self, n):
        for m in range(self.p.ndp):
            first = 0 if m == 0 else self.stage_of(n, m) + 1
            for stage in range(first, len(self.p.bits)):
                self.copy(n, m, stage).wait_send()


class FsGather:
    def __init__(self, pos, blocks, ss, rs):
        self.p, self.b, self.ss, self.rs = pos, blocks, ss, rs

    def copy(self, n, fb, dev):
        return rcopy(self.b(fb), self.b(fb), self.ss.at[n], self.rs.at[n], dev)

    def start(self):
        self.copy(1, self.p.f, self.p.to_y).start()
        self.copy(0, self.p.f, self.p.to_core).start()

    def mid(self):
        self.copy(1, self.p.f_y, self.p.to_y).wait_recv()
        self.copy(2, self.p.f_y, self.p.to_core).start()

    def end(self):
        self.copy(0, self.p.f_core, self.p.to_core).wait_recv()
        self.copy(2, self.p.f_yc, self.p.to_core).wait_recv()

    def wait_sends(self):
        self.copy(1, self.p.f, self.p.to_y).wait_send()
        self.copy(0, self.p.f, self.p.to_core).wait_send()
        self.copy(2, self.p.f_y, self.p.to_core).wait_send()


class FsReduce:
    def __init__(self, pos, blocks, from_core, from_y, ss, rs):
        self.p, self.b, self.fc, self.fy, self.ss, self.rs = pos, blocks, from_core, from_y, ss, rs

    def c1(self):
        return rcopy(
            self.b(self.p.f_yc), self.fc.at[1], self.ss.at[1], self.rs.at[1], self.p.to_core
        )

    def c0(self):
        return rcopy(
            self.b(self.p.f_core), self.fc.at[0], self.ss.at[0], self.rs.at[0], self.p.to_core
        )

    def cy(self):
        return rcopy(self.fc.at[1], self.fy, self.ss.at[2], self.rs.at[2], self.p.to_y)

    def start(self):
        self.c1().start()
        self.c0().start()

    def mid(self, rows, tile=64):
        self.c1().wait_recv()
        mine = self.b(self.p.f_y)

        def add(t, _):
            r = pl.ds(al(t * tile, tile), tile)
            self.fc[1, r, :] = (self.fc[1, r, :].astype(F32) + mine[r, :].astype(F32)).astype(BF16)
            return 0

        lax.fori_loop(0, rows // tile, add, 0)
        self.cy().start()

    def end(self):
        self.c0().wait_recv()
        self.cy().wait_recv()

    def value(self, r):
        return (
            self.b(self.p.f)[r, :].astype(F32)
            + self.fc[0, r, :].astype(F32)
            + self.fy[r, :].astype(F32)
        )

    def wait_sends(self):
        self.c1().wait_send()
        self.c0().wait_send()
        self.cy().wait_send()


def softmax_parts(scores):
    top = jnp.max(scores, axis=-1, keepdims=True)
    lifted = jnp.exp(scores - top)
    return lifted / jnp.sum(lifted, axis=-1, keepdims=True)


def causal_bias(rows):
    r = lax.broadcasted_iota(jnp.int32, (rows, rows), 0)
    c = lax.broadcasted_iota(jnp.int32, (rows, rows), 1)
    return jnp.where(c <= r, 0.0, MASK_FILL).astype(F32)


def group_rows(ref, m, half, cols, own):
    t = own // 2
    first = ref[pl.ds((2 * half) * own + m * t, t), cols]
    second = ref[pl.ds((2 * half + 1) * own + m * t, t), cols]
    return jnp.concatenate([first, second], axis=0)


def put_rows(ref, m, half, cols, own, value):
    t = own // 2
    ref[pl.ds((2 * half) * own + m * t, t), cols] = value[:t]
    ref[pl.ds((2 * half + 1) * own + m * t, t), cols] = value[t:]


def forward_kernel(
    cfg,
    tok,
    dout,
    cos,
    sin,
    bias,
    seq_sh,
    gain_sh,
    qb_sh,
    out_sh,
    gate_sh,
    up_sh,
    down_sh,
    qb_all,
    out_all,
    gate_all,
    up_all,
    down_all,
    seq_all,
    gain_sum,
    lkv_o,
    q_o,
    mixed_o,
    latent_o,
    normed_o,
    middle_o,
    hid_o,
    gg_o,
    gu_o,
    gw_gate,
    gw_up,
    gw_down,
    seq_v,
    gain_v,
    qb_v,
    out_v,
    lkv_v,
    q_v,
    mixed_v,
    part_v,
    fcore_v,
    fy_v,
    n2_v,
    d_v,
    n2_t,
    d_t,
    lat_v,
    gss,
    grs,
    fss,
    frs,
    sys_,
    syr,
    ls,
    ffn_ls,
):
    ndp, own, dim, rank, hd, heads = cfg
    rows = NF * own
    p = Place(ndp)
    kvw = rank + 2 * hd
    sr = seq_sh.shape[0]
    g = DpGather(p, gss, grs)
    i_seq = g.add(seq_sh, lambda j: seq_v.at[pl.ds(al((j * NF + p.f) * sr, sr), sr)])
    i_gain = g.add(gain_sh, lambda j: gain_v.at[j * NF + p.f])
    turn = [0]

    def weight_items(src, dst, cols=slice(None), most=GATHER_ROWS):
        n = src.shape[0]
        step = min(n, most)
        out = []
        for c in range(n // step):
            turn[0] += 1
            out.append(
                g.add(
                    src.at[pl.ds(c * step, step), cols],
                    lambda j, c=c: dst.at[pl.ds(al(j * n + c * step, step), step), cols],
                    turn[0] % 8 == 0,
                )
            )
        return out

    i_qb = weight_items(qb_sh, qb_v)
    i_out = weight_items(out_sh, out_v)
    i_ffn = []
    for c0, cw in ffn_chunks(gate_sh.shape[1]):
        cols = pl.ds(c0, cw)
        some = []
        for s, d in ((gate_sh, gate_all), (up_sh, up_all), (down_sh, down_all)):
            some += weight_items(s, d, cols, FFN_ROWS)
        i_ffn.append(some)
    order = range(len(g.items))
    fs_d = FsGather(p, lambda b: d_v.at[pl.ds(al(b * own, own), own)], fss.at[0], frs.at[0])
    fs_l = FsGather(p, lambda b: lkv_v.at[pl.ds(al(b * own, own), own)], fss.at[1], frs.at[1])
    fs_n = FsGather(p, lambda b: n2_v.at[pl.ds(al(b * own, own), own)], fss.at[2], frs.at[2])
    red = FsReduce(
        p, lambda b: part_v.at[pl.ds(al(b * own, own), own)], fcore_v, fy_v, fss.at[3], frs.at[3]
    )

    local = []

    def local_copy(src, dst):
        c = pltpu.make_async_copy(src, dst, ls.at[len(local)])
        c.start()
        local.append(c)
        return c

    own_copies = {}
    for i in order:
        src, dst, _ = g.items[i]
        own_copies[i] = local_copy(src, dst(p.me))
    d_copies = [
        local_copy(dout.at[m], d_v.at[pl.ds(al(p.f * own + m * (own // 2), 128), own // 2)])
        for m in range(2)
    ]

    p.barrier()
    for _ in range(GATHER_FIRST):
        g.launch()
    npiece = ndp

    def seq_piece(j, fb):
        return seq_v.at[pl.ds(al((j * NF + fb) * sr, sr), sr)]

    def seq_copy(t, j, fb, dev, which):
        b = seq_piece(j, fb) if which == 0 else gain_v.at[j * NF + fb]
        return rcopy(b, b, sys_.at[which, t, j], syr.at[which, t, j], dev)

    def spread(j):
        for which in (0, 1):
            seq_copy(1, j, p.f, p.to_y, which).start()
            seq_copy(0, j, p.f, p.to_core, which).start()

    for m in range(2):
        x = tok[m].astype(F32)
        inv = lax.rsqrt(jnp.mean(x * x, axis=-1, keepdims=True) + EPSILON)
        middle_o[pl.ds(m * (own // 2), own // 2), :] = x * inv
    own_copies[i_seq].wait()
    own_copies[i_gain].wait()
    spread(p.me)
    for m in sorted(range(1, ndp), key=lambda m: g.stage_of(i_seq, m)):
        for i in (i_seq, i_gain):
            g.arrived(i, m)
            for stage in range(g.stage_of(i, m) + 1, len(p.bits)):
                g.copy(i, m, stage).start()
        spread(p.at(m))
    g.seen = g.first = 2
    for c in d_copies:
        c.wait()

    def spread_forward(j, _):
        for which in (0, 1):
            seq_copy(1, j, p.f_y, p.to_y, which).wait_recv()
            seq_copy(2, j, p.f_y, p.to_core, which).start()
        return 0

    def tick(n):
        g.steps(n, GATHER_AHEAD)

    tick(1)
    lax.fori_loop(0, npiece, spread_forward, 0)
    fs_d.start()
    tick(1)

    def spread_end(j, _):
        for which in (0, 1):
            seq_copy(0, j, p.f_core, p.to_core, which).wait_recv()
            seq_copy(2, j, p.f_yc, p.to_core, which).wait_recv()
        return 0

    lax.fori_loop(0, npiece, spread_end, 0)

    def gain_add(j, acc):
        return acc + gain_v[j]

    gains = lax.fori_loop(0, ndp * NF, gain_add, jnp.zeros(gain_v.shape[1:], F32))
    gain_sum[...] = gains
    wide = dim // rank
    gain_one = jnp.concatenate([gains[r : r + 1] for r in range(wide)], axis=1)
    gain_two = jnp.concatenate([gains[wide + r : wide + r + 1] for r in range(wide)], axis=1)
    gain_lat = gains[2 * wide : 2 * wide + 1]
    normed_o[...] = (middle_o[...] * gain_one).astype(BF16)
    seq_out = local_copy(seq_v, seq_all)

    def project(j, _):
        cols = pl.ds(al(j * 256, 256), 256)
        lat_v[:, cols] = mm(normed_o[...], seq_v[:, cols])
        return 0

    lax.fori_loop(0, kvw // 256, project, 0)
    own_rows = pl.ds(al(p.f * own, own), own)
    lat = lat_v[:, :rank]
    latent_o[...] = lat
    inv_lat = lax.rsqrt(jnp.mean(lat * lat, axis=-1, keepdims=True) + EPSILON)
    lkv_v[own_rows, :rank] = (lat * inv_lat * gain_lat).astype(BF16)
    half = hd // 2
    co, si = cos[own_rows, :], sin[own_rows, :]
    ka, kb = lat_v[:, rank : rank + half], lat_v[:, rank + half : rank + hd]
    lkv_v[own_rows, rank : rank + half] = (ka * co - kb * si).astype(BF16)
    lkv_v[own_rows, rank + half : rank + hd] = (kb * co + ka * si).astype(BF16)
    lkv_v[own_rows, rank + hd :] = lat_v[:, rank + hd :].astype(BF16)
    fs_l.start()
    tick(1)
    fs_d.mid()
    fs_l.mid()
    tick(1)
    for i in i_qb:
        g.need(i, GATHER_AHEAD)
        own_copies[i].wait()
        g.wait_last(i)
    fs_l.end()
    qb_out = local_copy(qb_v, qb_all)
    lkv_out = local_copy(lkv_v, lkv_o)

    def query(j, _):
        cols = pl.ds(al(j * hd, hd), hd)
        c0 = pl.ds(al(j * hd, half), half)
        c1 = pl.ds(al(j * hd + half, half), half)
        for r in range(rows // 512):
            rr = pl.ds(r * 512, 512)
            acc = mm(lkv_v[rr, :rank], qb_v[:, cols])
            a, b = acc[:, :half], acc[:, half:]
            c, s = cos[rr, :], sin[rr, :]
            q_v[rr, c0] = (a * c - b * s).astype(BF16)
            q_v[rr, c1] = (b * c + a * s).astype(BF16)
        return 0

    lax.fori_loop(0, heads, query, 0)
    q_out = local_copy(q_v, q_o)
    tick(1)
    scale = hd ** (-0.5)
    kcols, vcols = slice(rank, rank + hd), slice(rank + hd, rank + 2 * hd)
    causal = causal_bias(PROMPT)
    for m in range(2):
        k0, k1 = (group_rows(lkv_v, m, h2, kcols, own) for h2 in (0, 1))
        v0, v1 = (group_rows(lkv_v, m, h2, vcols, own) for h2 in (0, 1))
        low = bias[m]

        def attend(h, _):
            cols = pl.ds(al(h * hd, hd), hd)
            q0 = group_rows(q_v, m, 0, cols, own)
            pr = softmax_parts(mm_nt(q0, k0) * scale + causal).astype(BF16)
            put_rows(mixed_v, m, 0, cols, own, mm(pr, v0).astype(BF16))
            q1 = group_rows(q_v, m, 1, cols, own)
            s0 = mm_nt(q1, k0) * scale
            s1 = mm_nt(q1, k1) * scale + low
            top = jnp.maximum(
                jnp.max(s0, axis=-1, keepdims=True), jnp.max(s1, axis=-1, keepdims=True)
            )
            e0, e1 = jnp.exp(s0 - top), jnp.exp(s1 - top)
            total = jnp.sum(e0, axis=-1, keepdims=True) + jnp.sum(e1, axis=-1, keepdims=True)
            mix = mm((e0 / total).astype(BF16), v0) + mm((e1 / total).astype(BF16), v1)
            put_rows(mixed_v, m, 1, cols, own, mix.astype(BF16))
            return 0

        lax.fori_loop(0, heads, attend, 0)
        tick(2)
    fs_d.end()
    mixed_out = local_copy(mixed_v, mixed_o)
    tick(1)
    for i in i_out:
        g.need(i, GATHER_AHEAD)
        own_copies[i].wait()
        g.wait_last(i)
    out_out = local_copy(out_v, out_all)

    def project_out(fb):
        rr = pl.ds(al(fb * own, own), own)

        def one(j, _):
            wr = pl.ds(al(j * 256, 256), 256)
            part_v[rr, wr] = mm_nt(mixed_v[rr, :], out_v[wr, :]).astype(BF16)
            return 0

        lax.fori_loop(0, dim // 256, one, 0)

    project_out(p.f_yc)
    project_out(p.f_core)
    red.start()
    tick(1)
    project_out(p.f_y)
    red.mid(own)
    project_out(p.f)
    tick(2)
    red.end()
    for m in range(2):
        rr = pl.ds(m * (own // 2), own // 2)
        mid = tok[m].astype(F32) + red.value(rr)
        middle_o[rr, :] = mid
        inv = lax.rsqrt(jnp.mean(mid * mid, axis=-1, keepdims=True) + EPSILON)
        n2_v[pl.ds(al(p.f * own + m * (own // 2), 128), own // 2), :] = (
            mid * inv * gain_two
        ).astype(BF16)
    fs_n.start()
    tick(1)

    def turn_d(j, _):
        cols = pl.ds(al(j * 256, 256), 256)
        d_t[cols, :] = d_v[:, cols].T
        return 0

    lax.fori_loop(0, dim // 256, turn_d, 0)
    tick(1)
    fs_n.mid()
    tick(1)
    fs_n.end()

    def turn_n2(j, _):
        cols = pl.ds(al(j * 256, 256), 256)
        n2_t[cols, :] = n2_v[:, cols].T
        return 0

    lax.fori_loop(0, dim // 256, turn_n2, 0)
    for c in (q_out, mixed_out, out_out, seq_out):
        c.wait()
    early = [i_seq, i_gain] + i_qb + i_out
    for i in early:
        g.wait_sends(i)

    def spread_sends(j, _):
        for which in (0, 1):
            seq_copy(0, j, p.f, p.to_core, which).wait_send()
            seq_copy(1, j, p.f, p.to_y, which).wait_send()
            seq_copy(2, j, p.f_y, p.to_core, which).wait_send()
        return 0

    lax.fori_loop(0, npiece, spread_sends, 0)
    red.wait_sends()
    pending = []
    width = FFN_COLS
    for (c0, cw), some in zip(ffn_chunks(gate_sh.shape[1]), i_ffn):
        g.need(some[-1], GATHER_AHEAD)
        for i in some:
            own_copies[i].wait()
            g.wait_last(i)
        cols = pl.ds(c0, cw)
        loads = [
            pltpu.make_async_copy(w.at[:, cols], seq_v.at[:, pl.ds(n * width, cw)], ffn_ls.at[n])
            for n, w in enumerate((gate_all, up_all, down_all))
        ]
        for c in loads:
            c.start()
        for c in pending:
            c.wait()
        for c in loads:
            c.wait()
        gate_c, up_c, down_c = (slice(n * width, n * width + cw) for n in range(3))

        def both(t, _):
            rr = pl.ds(al(t * 256, 256), 256)
            gate = mm(n2_v[rr, :], seq_v[:, gate_c])
            up = mm(n2_v[rr, :], seq_v[:, up_c])
            grad_hidden = mm(d_v[rr, :], seq_v[:, down_c])
            sig = 1.0 / (1.0 + jnp.exp(-gate))
            act = gate * sig
            mixed_v[rr, :cw] = (act * up).astype(BF16)
            q_v[rr, gate_c] = (grad_hidden * up * (sig * (1.0 + gate * (1.0 - sig)))).astype(BF16)
            q_v[rr, up_c] = (grad_hidden * act).astype(BF16)
            return 0

        for lo in range(0, rows // 256, 2):
            lax.fori_loop(lo, lo + 2, both, 0)
            tick(1)
        pending = [
            pltpu.make_async_copy(src, dst.at[:, cols], ffn_ls.at[3 + n])
            for n, (src, dst) in enumerate(
                (
                    (mixed_v.at[:, pl.ds(0, cw)], hid_o),
                    (q_v.at[:, pl.ds(0, cw)], gg_o),
                    (q_v.at[:, pl.ds(width, cw)], gu_o),
                )
            )
        ]
        for c in pending:
            c.start()

        half_rows = part_v.shape[0] // 256
        for lo in range(0, dim // 256, half_rows):

            def weight_grads(j, _):
                rr = pl.ds(al(j * 256, 256), 256)
                pr = pl.ds(al((j - lo) * 256, 256), 256)
                pc = slice((lo // half_rows) * width, (lo // half_rows) * width + cw)
                out_v[rr, gate_c] = mm(n2_t[rr, :], q_v[:, gate_c]).astype(BF16)
                out_v[rr, up_c] = mm(n2_t[rr, :], q_v[:, up_c]).astype(BF16)
                part_v[pr, pc] = mm(d_t[rr, :], mixed_v[:, :cw]).astype(BF16)
                return 0

            lax.fori_loop(lo, min(dim // 256, lo + half_rows), weight_grads, 0)
            tick(1)
        saves = [
            pltpu.make_async_copy(out_v.at[:, pl.ds(0, cw)], gw_gate.at[:, cols], ffn_ls.at[6]),
            pltpu.make_async_copy(out_v.at[:, pl.ds(width, cw)], gw_up.at[:, cols], ffn_ls.at[7]),
        ]
        prow = part_v.shape[0]
        for n in range(dim // prow):
            saves.append(
                pltpu.make_async_copy(
                    part_v.at[:, pl.ds(n * width, cw)],
                    gw_down.at[pl.ds(n * prow, prow), cols],
                    ffn_ls.at[8 + n],
                )
            )
        for c in saves:
            c.start()
        pending = pending + saves
    for c in pending:
        c.wait()
    tick(2 * len(g.items))
    for i in order:
        if i not in early:
            g.wait_sends(i)
    for t in (fs_d, fs_l, fs_n):
        t.wait_sends()
    for c in (qb_out, lkv_out):
        c.wait()


def forward_call(ndp, tok, dout, cos, sin, bias, seq_sh, gain_sh, qb, out, gate, up, down):
    own = tok.shape[0] * tok.shape[1]
    dim = tok.shape[2]
    rank = qb.shape[0] * ndp
    hd = (seq_sh.shape[1] - rank) // 2
    heads = qb.shape[1] // hd
    rows = NF * own
    kvw = seq_sh.shape[1]
    n_items = 2 + sum(w.shape[0] // min(w.shape[0], GATHER_ROWS) for w in (qb, out))
    n_items += sum(w.shape[0] // min(w.shape[0], FFN_ROWS) for w in (gate, up, down)) * len(
        ffn_chunks(gate.shape[1])
    )

    def sds(shape, dtype=BF16):
        return jax.ShapeDtypeStruct(shape, dtype)

    full = lambda w: sds((w.shape[0] * ndp, w.shape[1]))
    out_shape = (
        full(qb),
        full(out),
        full(gate),
        full(up),
        full(down),
        sds((seq_sh.shape[0] * ndp * NF, kvw)),
        sds(gain_sh.shape, F32),
        sds((rows, kvw)),
        sds((rows, heads * hd)),
        sds((rows, heads * hd)),
        sds((own, rank), F32),
        sds((own, dim)),
        sds((own, dim), F32),
        sds((rows, gate.shape[1])),
        sds((rows, gate.shape[1])),
        sds((rows, gate.shape[1])),
        full(gate),
        full(up),
        full(down),
    )
    out_specs = (ANY,) * 6 + (VMEM,) + (ANY,) * 3 + (VMEM,) * 3 + (ANY,) * 6
    dma = pltpu.SemaphoreType.DMA
    scratch = [
        pltpu.VMEM((seq_sh.shape[0] * ndp * NF, kvw), BF16),
        pltpu.VMEM((ndp * NF,) + gain_sh.shape, F32),
        pltpu.VMEM((qb.shape[0] * ndp, qb.shape[1]), BF16),
        pltpu.VMEM((out.shape[0] * ndp, out.shape[1]), BF16),
        pltpu.VMEM((rows, kvw), BF16),
        pltpu.VMEM((rows, heads * hd), BF16),
        pltpu.VMEM((rows, heads * hd), BF16),
        pltpu.VMEM((rows, dim), BF16),
        pltpu.VMEM((2, own, dim), BF16),
        pltpu.VMEM((own, dim), BF16),
        pltpu.VMEM((rows, dim), BF16),
        pltpu.VMEM((rows, dim), BF16),
        pltpu.VMEM((dim, rows), BF16),
        pltpu.VMEM((dim, rows), BF16),
        pltpu.VMEM((own, kvw), F32),
        dma((n_items, ndp - 1)),
        dma((n_items, ndp - 1)),
        dma((4, 3)),
        dma((4, 3)),
        dma((2, 3, ndp)),
        dma((2, 3, ndp)),
        dma((n_items + 10,)),
        dma((10,)),
    ]
    return pl.pallas_call(
        functools.partial(forward_kernel, (ndp, own, dim, rank, hd, heads)),
        out_shape=out_shape,
        in_specs=(VMEM,) * 5 + (ANY,) * 7,
        out_specs=out_specs,
        scratch_shapes=scratch,
        compiler_params=pltpu.CompilerParams(
            collective_id=0, has_side_effects=True, vmem_limit_bytes=60 * 2**20
        ),
        name="gather_forward",
    )(tok, dout, cos, sin, bias, seq_sh, gain_sh, qb, out, gate, up, down)


class DpScatter:
    PER_TICK = 2

    def __init__(self, pos, count, first, later, own, acc, ss, rs, ls, credit):
        self.p, self.count = pos, count
        self.n = len(pos.bits)
        self.SLOTS, self.AHEAD, self.OWN = scatter_ring(pos.ndp // 2)
        self.first, self.later, self.own, self.acc = first, later, own, acc
        self.ss, self.rs, self.ls, self.credit = ss, rs, ls, credit
        self.items = []
        self.started = self.stepped = 0

    def order(self, n):
        return self.p.orders(False)

    def width(self, stage):
        return 1 << (self.n - 1 - stage)

    def add(self, src, base, out, pieces):
        rows, cols = out.shape
        r = rows // pieces
        for c in range(pieces):
            self.items.append((src, base, out, rows, cols, c * r, r))
        self.pump()

    def mask(self, n, i):
        order = self.order(n)
        return sum(order[1 + t] for t in range(self.n - 1) if i >> (self.n - 2 - t) & 1)

    def block(self, n, mask):
        src, base, out, rows, cols, r0, r = self.items[n]
        return src.at[pl.ds(al(base + self.p.at(mask) * rows + r0, r), r)]

    def place(self, buf, n, lo, size):
        src, base, out, rows, cols, r0, r = self.items[n]
        return buf.at[n % self.SLOTS, pl.ds(lo, size), pl.ds(0, r), pl.ds(0, cols)]

    def copies(self, n, stage):
        bit = self.order(n)[stage]
        dev = self.p.to_dp(bit)
        s = n % self.SLOTS
        if stage == 0:
            return [
                rcopy(
                    self.block(n, bit | self.mask(n, i)),
                    self.place(self.first, n, i, 1).at[0],
                    self.ss.at[s, i],
                    self.rs.at[s, i],
                    dev,
                )
                for i in range(self.width(0))
            ]
        w = self.width(stage)
        k = self.width(0) + stage - 1
        return [
            rcopy(
                self.place(self.first, n, w, w),
                self.place(self.later, n, w - 1, w),
                self.ss.at[s, k],
                self.rs.at[s, k],
                dev,
            )
        ]

    def owncopy(self, n, i):
        src, base, out, rows, cols, r0, r = self.items[n]
        s = n % self.OWN
        return pltpu.make_async_copy(
            self.block(n, self.mask(n, i)),
            self.own.at[s, i, pl.ds(0, r), pl.ds(0, cols)],
            self.ls.at[s, i],
        )

    def outcopy(self, n):
        src, base, out, rows, cols, r0, r = self.items[n]
        s = n % self.SLOTS
        return pltpu.make_async_copy(
            self.acc.at[s, pl.ds(0, r), pl.ds(0, cols)],
            out.at[pl.ds(r0, r)],
            self.ls.at[s, self.width(0)],
        )

    def free(self, n, stage):
        m = n + self.SLOTS
        if m < self.count:
            bit = self.order(m)[stage]
            pl.semaphore_signal(
                self.credit.at[stage, self.p.bits.index(bit)],
                inc=1,
                device_id=self.p.to_dp(bit),
                device_id_type=MESH,
            )

    def send(self, n, stage):
        bit = self.order(n)[stage]
        if n >= self.SLOTS:
            pl.semaphore_wait(self.credit.at[stage, self.p.bits.index(bit)], 1)
        for c in self.copies(n, stage):
            c.start()

    def pump(self):
        while self.started < min(len(self.items), self.stepped + self.AHEAD):
            n = self.started
            self.send(n, 0)
            for i in range(self.width(0)):
                self.owncopy(n, i).start()
            self.started += 1

    def tick(self, steps=1):
        for _ in range(self.PER_TICK * steps):
            n = self.stepped
            if n >= self.started:
                return
            self.combine(n, 0)
            self.stepped += 1
            self.pump()
            for stage in range(1, self.n):
                if n >= stage:
                    self.combine(n - stage, stage)

    def combine(self, n, stage):
        src, base, out, rows, cols, r0, r = self.items[n]
        s, tile = n % self.SLOTS, 16
        w = self.width(stage)
        for c in self.copies(n, stage):
            c.wait_recv()
        if stage == 0:
            for i in range(w):
                self.owncopy(n, i).wait()
        else:
            for c in self.copies(n, stage):
                c.wait_send()
        last = stage == self.n - 1

        def add(lo, size):
            def one(t, _):
                t = pl.ds(al(t * tile, tile), tile)
                for i in range(lo, lo + size):
                    a = self.first[s, i, t, :cols]
                    b = self.own[n % self.OWN, i, t, :cols] if stage == 0 else self.later[s, w - 1 + i, t, :cols]
                    if last:
                        self.acc[s, t, :cols] = a.astype(F32) + b.astype(F32)
                    else:
                        self.first[s, i, t, :cols] = a + b
                return 0

            lax.fori_loop(0, r // tile, one, 0)

        if last:
            if n >= self.SLOTS:
                self.outcopy(n - self.SLOTS).wait()
            for c in self.copies(n, 0):
                c.wait_send()
            add(0, 1)
            self.outcopy(n).start()
            for t in range(self.n):
                self.free(n, t)
        else:
            half = w // 2
            add(half, half)
            self.send(n, stage + 1)
            add(0, half)

    def drain(self):
        self.tick(self.count)
        for n in range(self.count, self.count + self.n - 1):
            for stage in range(1, self.n):
                if 0 <= n - stage < self.count:
                    self.combine(n - stage, stage)
        for n in range(max(0, self.count - self.SLOTS), self.count):
            self.outcopy(n).wait()


def scatter_ring(nz):
    return (10, 6, 7) if nz * max(16, 128 // nz) <= 128 else (5, 2, 3)


def piece_rows(rows, nz):
    return min(rows, max(16, 128 // nz))


def backward_kernel(
    cfg,
    tok,
    dout,
    middle,
    latent,
    normed,
    gains,
    cos,
    sin,
    bias,
    gw_gate,
    gw_up,
    gw_down,
    hid_h,
    gg_h,
    gu_h,
    gate_h,
    up_h,
    down_h,
    lkv_h,
    q_h,
    mixed_h,
    qb_h,
    out_h,
    seq_h,
    o_gate,
    o_up,
    o_down,
    o_out,
    o_qb,
    o_seq,
    o_gain,
    o_in,
    o_y,
    fcore_v,
    fy_v,
    proj_v,
    gmid_v,
    gnorm_v,
    lkv_v,
    q_v,
    mixed_v,
    gm_v,
    kv_acc,
    qb_v,
    out_v,
    seq_v,
    gall_v,
    gain_rx,
    gain_acc,
    first_b,
    later_b,
    own_b,
    acc_b,
    dss,
    drs,
    dls,
    credit,
    fss,
    frs,
    gs,
    gr,
    ls,
    tls,
):
    ndp, own, dim, rank, hd, heads, pieces = cfg
    rows = NF * own
    t2 = own // 2
    kvw = rank + 2 * hd
    wide = dim // rank
    p = Place(ndp)
    sr = o_seq.shape[0]
    local = []

    def local_copy(src, dst):
        c = pltpu.make_async_copy(src, dst, ls.at[len(local)])
        c.start()
        local.append(c)
        return c

    ff = gg_h.shape[1]
    ffc = pl.ds(0, ff)
    gg_in = local_copy(gg_h, lkv_v.at[:, ffc])
    gu_in = local_copy(gu_h, seq_v.at[pl.ds(0, rows), ffc])
    mixed_in = local_copy(mixed_h, mixed_v)
    q_in = local_copy(q_h, q_v)
    qb_in = local_copy(qb_h, qb_v)
    hh = out_v.shape[1]

    def tile_load(t, which):
        src = gate_h if which == 0 else up_h
        s = lax.rem(t, 2) * 2 + which
        return pltpu.make_async_copy(
            src.at[pl.ds(al(t * 256, 256), 256)],
            seq_v.at[pl.ds(al(rows + s * 256, 256), 256), ffc],
            tls.at[s],
        )

    for which in (0, 1):
        tile_load(0, which).start()
    sc = DpScatter(p, sum(pieces), first_b, later_b, own_b, acc_b, dss, drs, dls, credit)
    p.barrier()
    sc.add(gw_gate, 0, o_gate, pieces[0])
    sc.add(gw_up, 0, o_up, pieces[1])
    sc.add(gw_down, 0, o_down, pieces[2])
    gg_in.wait()
    gu_in.wait()
    n_tiles = dim // 256
    per_half = hh // 256

    def norm_grad(t, _):
        for which in (0, 1):
            tile_load(t, which).wait()

        @pl.when(t + 1 < n_tiles)
        def _():
            for which in (0, 1):
                tile_load(t + 1, which).start()

        s = lax.rem(t, 2) * 2
        wg = seq_v[pl.ds(al(rows + s * 256, 256), 256), ffc]
        wu = seq_v[pl.ds(al(rows + s * 256 + 256, 256), 256), ffc]
        cols = pl.ds(al(lax.rem(t, per_half) * 256, 256), 256)
        for r in range(rows // 256):
            rr = pl.ds(r * 256, 256)
            to = pl.ds(al((t // per_half) * rows + r * 256, 256), 256)
            out_v[to, cols] = (
                mm_nt(lkv_v[rr, ffc], wg) + mm_nt(seq_v[rr, ffc], wu)
            ).astype(BF16)
        return 0

    halves = []
    for h in range(dim // hh):
        wide_cols = pl.ds(h * hh, hh)
        lax.fori_loop(h * per_half, (h + 1) * per_half, norm_grad, 0)
        red = FsReduce(
            p,
            lambda b, h=h: out_v.at[pl.ds(al(h * rows + b * own, own), own)],
            fcore_v.at[:, :, wide_cols],
            fy_v.at[:, wide_cols],
            fss.at[4 * h],
            frs.at[4 * h],
        )
        red.start()
        if h > 0:
            halves[-1].mid(own)
        sc.tick(1)
        halves.append(red)
    lkv_in = local_copy(lkv_h, lkv_v)
    seq_in = local_copy(seq_h, seq_v)
    halves[-1].mid(own)
    sc.tick(1)
    for red in halves:
        red.end()
        red.wait_sends()
    gain_two = jnp.concatenate([gains[wide + r : wide + r + 1] for r in range(wide)], axis=1)
    gain_one = jnp.concatenate([gains[r : r + 1] for r in range(wide)], axis=1)
    gain_lat = gains[2 * wide : 2 * wide + 1]
    part_two = jnp.zeros((1, dim), F32)
    for m in range(2):
        rr = pl.ds(m * t2, t2)
        e = jnp.concatenate([red.value(rr) for red in halves], axis=1)
        v = middle[rr, :]
        inv = lax.rsqrt(jnp.mean(v * v, axis=-1, keepdims=True) + EPSILON)
        part_two += jnp.sum(e * v * inv, axis=0, keepdims=True)
        scaled = e * gain_two
        inner = jnp.mean(scaled * v, axis=-1, keepdims=True)
        g = dout[m].astype(F32) + inv * scaled - v * (inv * inv * inv * inner)
        gmid_v[rr, :] = g
        proj_v[pl.ds(al(p.f * own + m * t2, t2), t2), :] = g.astype(BF16)
    out_in = local_copy(out_h, out_v)
    gain_acc[0] = jnp.zeros(gain_acc.shape[1:], F32)
    for r in range(wide):
        gain_acc[0, pl.ds(wide + r, 1), :] = part_two[:, r * rank : (r + 1) * rank]
    ag = FsGather(p, lambda b: proj_v.at[pl.ds(al(b * own, own), own)], fss.at[1], frs.at[1])
    ag.start()
    sc.tick(1)
    ag.mid()
    sc.tick(1)
    out_in.wait()
    ag.end()
    ag.wait_sends()

    def back_out(j, _):
        cols = pl.ds(al(j * 256, 256), 256)
        for r in range(rows // 512):
            rr = pl.ds(r * 512, 512)
            gm_v[rr, cols] = mm(proj_v[rr, :], out_v[:, cols]).astype(BF16)
        return 0

    lax.fori_loop(0, heads * hd // 256, back_out, 0)
    sc.tick(1)
    mixed_in.wait()

    def grad_out(j, _):
        cols = pl.ds(al(j * 256, 256), 256)
        out_v[cols, :] = mm_tn(proj_v[:, cols], mixed_v[...]).astype(BF16)
        return 0

    lax.fori_loop(0, dim // 256, grad_out, 0)
    sc.tick(1)
    sc.add(out_v, 0, o_out, pieces[3])
    q_in.wait()
    lkv_in.wait()
    scale = hd ** (-0.5)
    half = hd // 2
    kcols, vcols = slice(rank, rank + hd), slice(rank + hd, rank + 2 * hd)
    causal = causal_bias(PROMPT)
    everything = slice(None)

    for m in range(2):
        k0, k1 = (group_rows(lkv_v, m, h2, kcols, own) for h2 in (0, 1))
        v0, v1 = (group_rows(lkv_v, m, h2, vcols, own) for h2 in (0, 1))
        low = bias[m]
        kv_acc[...] = jnp.zeros(kv_acc.shape, F32)

        def put_query(h, which, g):
            co = group_rows(cos, m, which, everything, own)
            si = group_rows(sin, m, which, everything, own)
            a, b = g[:, :half] * scale, g[:, half:] * scale
            c0 = pl.ds(al(h * hd, half), half)
            c1 = pl.ds(al(h * hd + half, half), half)
            put_rows(gm_v, m, which, c0, own, (a * co + b * si).astype(BF16))
            put_rows(gm_v, m, which, c1, own, (b * co - a * si).astype(BF16))

        def attend_back(h, _):
            cols = pl.ds(al(h * hd, hd), hd)
            q0 = group_rows(q_v, m, 0, cols, own)
            g0 = group_rows(gm_v, m, 0, cols, own)
            pr = softmax_parts(mm_nt(q0, k0) * scale + causal)
            gp = mm_nt(g0, v0)
            gsc = (pr * (gp - jnp.sum(pr * gp, axis=-1, keepdims=True))).astype(BF16)
            kv_acc[2] += mm_tn(pr.astype(BF16), g0)
            kv_acc[0] += mm_tn(gsc, q0)
            put_query(h, 0, mm(gsc, k0))
            q1 = group_rows(q_v, m, 1, cols, own)
            g1 = group_rows(gm_v, m, 1, cols, own)
            s0 = mm_nt(q1, k0) * scale
            s1 = mm_nt(q1, k1) * scale + low
            top = jnp.maximum(
                jnp.max(s0, axis=-1, keepdims=True), jnp.max(s1, axis=-1, keepdims=True)
            )
            e0, e1 = jnp.exp(s0 - top), jnp.exp(s1 - top)
            total = jnp.sum(e0, axis=-1, keepdims=True) + jnp.sum(e1, axis=-1, keepdims=True)
            p0, p1 = e0 / total, e1 / total
            gp0, gp1 = mm_nt(g1, v0), mm_nt(g1, v1)
            inner = jnp.sum(p0 * gp0, axis=-1, keepdims=True) + jnp.sum(
                p1 * gp1, axis=-1, keepdims=True
            )
            gs0 = (p0 * (gp0 - inner)).astype(BF16)
            gs1 = (p1 * (gp1 - inner)).astype(BF16)
            kv_acc[2] += mm_tn(p0.astype(BF16), g1)
            kv_acc[3] += mm_tn(p1.astype(BF16), g1)
            kv_acc[0] += mm_tn(gs0, q1)
            kv_acc[1] += mm_tn(gs1, q1)
            put_query(h, 1, mm(gs0, k0) + mm(gs1, k1))
            return 0

        lax.fori_loop(0, heads, attend_back, 0)
        for h2 in (0, 1):
            put_rows(proj_v, m, h2, kcols, own, (kv_acc[h2] * scale).astype(BF16))
            put_rows(proj_v, m, h2, vcols, own, kv_acc[2 + h2].astype(BF16))
        sc.tick(1)
    qb_in.wait()

    def back_latent(j, _):
        wr = pl.ds(al(j * 256, 256), 256)
        for r in range(rows // 512):
            rr = pl.ds(r * 512, 512)
            proj_v[rr, wr] = mm_nt(gm_v[rr, :], qb_v[wr, :]).astype(BF16)
        return 0

    lax.fori_loop(0, rank // 256, back_latent, 0)

    def grad_qb(j, _):
        cols = pl.ds(al(j * 256, 256), 256)
        qb_v[cols, :] = mm_tn(lkv_v[:, cols], gm_v[...]).astype(BF16)
        return 0

    lax.fori_loop(0, rank // 256, grad_qb, 0)
    narrow = pl.ds(0, kvw)
    red2 = FsReduce(
        p,
        lambda b: proj_v.at[pl.ds(al(b * own, own), own), narrow],
        fcore_v.at[:, :, narrow],
        fy_v.at[:, narrow],
        fss.at[2],
        frs.at[2],
    )
    red2.start()
    sc.tick(1)
    sc.add(qb_v, 0, o_qb, pieces[4])
    red2.mid(own)
    sc.tick(1)
    red2.end()
    red2.wait_sends()
    own_rows = pl.ds(al(p.f * own, own), own)
    part_lat = jnp.zeros((1, rank), F32)
    for m in range(2):
        rr = pl.ds(m * t2, t2)
        gr_rows = pl.ds(al(p.f * own + m * t2, t2), t2)
        e = red2.value(rr)
        v = latent[rr, :]
        inv = lax.rsqrt(jnp.mean(v * v, axis=-1, keepdims=True) + EPSILON)
        el = e[:, :rank]
        part_lat += jnp.sum(el * v * inv, axis=0, keepdims=True)
        scaled = el * gain_lat
        inner = jnp.mean(scaled * v, axis=-1, keepdims=True)
        gall_v[rr, :rank] = (inv * scaled - v * (inv * inv * inv * inner)).astype(BF16)
        co, si = cos[gr_rows, :], sin[gr_rows, :]
        a, b = e[:, rank : rank + half], e[:, rank + half : rank + hd]
        gall_v[rr, rank : rank + half] = (a * co + b * si).astype(BF16)
        gall_v[rr, rank + half : rank + hd] = (b * co - a * si).astype(BF16)
        gall_v[rr, rank + hd :] = e[:, rank + hd :].astype(BF16)
    gain_acc[0, pl.ds(2 * wide, 1), :] = part_lat
    seq_in.wait()

    def back_seq(j, _):
        wr = pl.ds(al(j * 256, 256), 256)
        gnorm_v[:, wr] = mm_nt(gall_v[...], seq_v[wr, :])
        return 0

    lax.fori_loop(0, dim // 256, back_seq, 0)
    sc.tick(1)
    span = NF * sr

    def grad_seq(j, _):
        cols = pl.ds(al(j * 256, 256), 256)
        g = mm_tn(normed[:, cols], gall_v[...]).astype(BF16)
        for i in range(256 // span):
            for fb in range(NF):
                seq_v[pl.ds(al(fb * ndp * sr + (j * (256 // span) + i) * sr, sr), sr), :] = g[
                    i * span + fb * sr : i * span + (fb + 1) * sr
                ]
        return 0

    lax.fori_loop(0, dim // 256, grad_seq, 0)
    srows = ndp * sr
    core3 = [lkv_v.at[pl.ds(0, srows)], lkv_v.at[pl.ds(srows, srows)]]

    def sblock(b):
        return seq_v.at[pl.ds(al(b * srows, srows), srows)]

    c1 = rcopy(sblock(p.f_yc), core3[1], fss.at[3, 1], frs.at[3, 1], p.to_core)
    c0 = rcopy(sblock(p.f_core), core3[0], fss.at[3, 0], frs.at[3, 0], p.to_core)
    mw = mixed_v.shape[1]
    cys = [
        rcopy(
            lkv_v.at[pl.ds(srows, srows), pl.ds(0, mw)],
            mixed_v.at[pl.ds(0, srows)],
            fss.at[3, 2],
            frs.at[3, 2],
            p.to_y,
        ),
        rcopy(
            lkv_v.at[pl.ds(srows, srows), pl.ds(mw, kvw - mw)],
            mixed_v.at[pl.ds(srows, srows), pl.ds(0, kvw - mw)],
            fss.at[3, 3],
            frs.at[3, 3],
            p.to_y,
        ),
    ]
    c1.start()
    c0.start()
    part_one = jnp.zeros((1, dim), F32)
    for m in range(2):
        rr = pl.ds(m * t2, t2)
        e = gnorm_v[rr, :]
        v = tok[m].astype(F32)
        inv = lax.rsqrt(jnp.mean(v * v, axis=-1, keepdims=True) + EPSILON)
        part_one += jnp.sum(e * v * inv, axis=0, keepdims=True)
        scaled = e * gain_one
        inner = jnp.mean(scaled * v, axis=-1, keepdims=True)
        o_in[m] = (gmid_v[rr, :] + inv * scaled - v * (inv * inv * inv * inner)).astype(BF16)
    for r in range(wide):
        gain_acc[0, pl.ds(r, 1), :] = part_one[:, r * rank : (r + 1) * rank]
    gain_steps = [
        rcopy(gain_acc.at[0], gain_rx.at[0], gs.at[0], gr.at[0], p.to_core),
        rcopy(gain_acc.at[1], gain_rx.at[1], gs.at[1], gr.at[1], p.to_y),
    ] + [
        rcopy(gain_acc.at[2 + b], gain_rx.at[2 + b], gs.at[2 + b], gr.at[2 + b], p.to_dp(bit))
        for b, bit in enumerate(p.bits)
    ]
    gain_steps[0].start()
    c1.wait_recv()

    def seq_y(t, _):
        t = al(t * 64, 64)
        a = pl.ds(srows + t, 64)
        b = pl.ds(al(p.f_y * srows + t, 64), 64)
        lkv_v[a, :] = lkv_v[a, :] + seq_v[b, :]
        return 0

    lax.fori_loop(0, srows // 64, seq_y, 0)
    for c in cys:
        c.start()
    for n in range(len(gain_steps)):
        gain_steps[n].wait_recv()
        gain_acc[n + 1] = gain_acc[n] + gain_rx[n]
        if n + 1 < len(gain_steps):
            gain_steps[n + 1].start()
        if n % 2 == 0:
            sc.tick(1)
    c0.wait_recv()
    for c in cys:
        c.wait_recv()

    def seq_f(t, _):
        t = al(t * 64, 64)
        a = pl.ds(t, 64)
        b = pl.ds(al(p.f * srows + t, 64), 64)
        a2 = pl.ds(srows + t, 64)
        seq_v[b, :mw] = (
            lkv_v[a, :mw].astype(F32) + seq_v[b, :mw].astype(F32) + mixed_v[a, :].astype(F32)
        ).astype(BF16)
        seq_v[b, mw:] = (
            lkv_v[a, mw:].astype(F32)
            + seq_v[b, mw:].astype(F32)
            + mixed_v[a2, : kvw - mw].astype(F32)
        ).astype(BF16)
        return 0

    lax.fori_loop(0, srows // 64, seq_f, 0)
    sc.add(seq_v, p.f * srows, o_seq, pieces[5])
    o_gain[...] = gain_acc[len(gain_steps)]
    for t in [c1, c0] + cys:
        t.wait_send()
    hid_in = local_copy(hid_h, lkv_v.at[:, ffc])

    def down_load(t):
        s = lax.rem(t, 2)
        return pltpu.make_async_copy(
            down_h.at[pl.ds(al(t * 256, 256), 256)],
            seq_v.at[pl.ds(al(p.f_core * srows + s * 256, 256), 256), ffc],
            tls.at[s],
        )

    down_load(0).start()
    sc.tick(1)
    hid_in.wait()

    def ffn_out(t, _):
        down_load(t).wait()

        @pl.when(t + 1 < n_tiles)
        def _():
            down_load(t + 1).start()

        w = seq_v[pl.ds(al(p.f_core * srows + lax.rem(t, 2) * 256, 256), 256), ffc]
        cols = pl.ds(al(t * 256, 256), 256)
        for r in range(rows // 256):
            rr = pl.ds(r * 256, 256)
            proj_v[rr, cols] = mm_nt(lkv_v[rr, ffc], w).astype(BF16)
        return 0

    lax.fori_loop(0, n_tiles, ffn_out, 0)
    red3 = FsReduce(
        p,
        lambda b: proj_v.at[pl.ds(al(b * own, own), own)],
        fcore_v,
        fy_v,
        fss.at[5],
        frs.at[5],
    )
    red3.start()
    sc.tick(1)
    red3.mid(own)
    sc.tick(2)
    red3.end()
    for m in range(2):
        rr = pl.ds(m * t2, t2)
        o_y[m] = (middle[rr, :] + red3.value(rr)).astype(BF16)
    sc.drain()
    red3.wait_sends()
    for t in gain_steps:
        t.wait_send()


def backward_call(ndp, tok, dout, middle, latent, normed, gains, cos, sin, bias, grads, ffn, saved):
    lkv, q, mixed, qb, out, seq = saved
    nz = ndp // 2
    own, dim = middle.shape
    rank = latent.shape[1]
    kvw = lkv.shape[1]
    hd = (kvw - rank) // 2
    heads = q.shape[1] // hd
    rows = NF * own
    sr = seq.shape[0] // (ndp * NF)
    shards = [(w.shape[0] // ndp, w.shape[1]) for w in grads] + [
        (out.shape[0] // ndp, out.shape[1]),
        (qb.shape[0] // ndp, qb.shape[1]),
        (sr, kvw),
    ]
    pieces = tuple(s[0] // piece_rows(s[0], nz) for s in shards)
    n = sum(pieces)
    slots, _, own_slots = scatter_ring(nz)
    nb = ndp.bit_length() - 1
    pr = max(piece_rows(s[0], nz) for s in shards)
    width = max(s[1] for s in shards)
    dma = pltpu.SemaphoreType.DMA
    scratch = [
        pltpu.VMEM((2, own, dim), BF16),
        pltpu.VMEM((own, dim), BF16),
        pltpu.VMEM((rows, dim), BF16),
        pltpu.VMEM((own, dim), F32),
        pltpu.VMEM((own, dim), F32),
        pltpu.VMEM(lkv.shape, BF16),
        pltpu.VMEM(q.shape, BF16),
        pltpu.VMEM(mixed.shape, BF16),
        pltpu.VMEM(q.shape, BF16),
        pltpu.VMEM((4, rows // 4, hd), F32),
        pltpu.VMEM(qb.shape, BF16),
        pltpu.VMEM(out.shape, BF16),
        pltpu.VMEM(seq.shape, BF16),
        pltpu.VMEM((own, kvw), BF16),
        pltpu.VMEM((2 + nb,) + gains.shape, F32),
        pltpu.VMEM((3 + nb,) + gains.shape, F32),
        pltpu.VMEM((slots, nz, pr, width), BF16),
        pltpu.VMEM((slots, nz - 1, pr, width), BF16),
        pltpu.VMEM((own_slots, nz, pr, width), BF16),
        pltpu.VMEM((slots, pr, width), F32),
        dma((slots, nz + nb - 1)),
        dma((slots, nz + nb - 1)),
        dma((slots, nz + 1)),
        pltpu.SemaphoreType.REGULAR((nb, nb)),
        dma((6, 4)),
        dma((6, 4)),
        dma((2 + nb,)),
        dma((2 + nb,)),
        dma((9,)),
        dma((4,)),
    ]
    return pl.pallas_call(
        functools.partial(backward_kernel, (ndp, own, dim, rank, hd, heads, pieces)),
        out_shape=tuple(jax.ShapeDtypeStruct(s, F32) for s in shards)
        + (
            jax.ShapeDtypeStruct(gains.shape, F32),
            jax.ShapeDtypeStruct(tok.shape, BF16),
            jax.ShapeDtypeStruct(tok.shape, BF16),
        ),
        in_specs=(VMEM,) * 9 + (ANY,) * 15,
        out_specs=(ANY,) * 6 + (VMEM,) * 3,
        scratch_shapes=scratch,
        compiler_params=pltpu.CompilerParams(
            collective_id=1, has_side_effects=True, vmem_limit_bytes=62 * 2**20
        ),
        name="backward_scatter",
    )(tok, dout, middle, latent, normed, gains, cos, sin, bias, *grads, *ffn, lkv, q, mixed, qb, out, seq)


def per_device(
    ndp,
    tokens,
    membership,
    d_output,
    gain_attn,
    w_qa,
    gain_latent,
    w_qb,
    w_key,
    w_value,
    w_out,
    gain_ffn,
    w_gate,
    w_up,
    w_down,
):
    micro, tlen, dim = tokens.shape
    own = micro * tlen
    rank = w_qa.shape[1]
    hd = w_key.shape[1]
    heads = w_qb.shape[1] // hd
    rows = NF * own
    wide = dim // rank
    labels, positions = jax.vmap(lambda r: layout(r, BLK))(membership[0])
    pos_rows = positions.reshape(micro, NF, tlen).transpose(1, 0, 2).reshape(rows)
    cos, sin = rope_tables(pos_rows, hd)
    tail = labels[:, PROMPT:]
    idx = jnp.arange(tail.shape[1], dtype=jnp.int32)
    seen = (idx[None, None, :] <= idx[None, :, None]) & (tail[:, None, :] == tail[:, :, None])
    bias = jnp.where(seen, 0.0, MASK_FILL).astype(F32)
    block = lax.axis_index("dp") * NF + lax.axis_index("fsdp")

    def spot(gain):
        width = gain.shape[0]
        count = ndp * NF
        at = lax.broadcasted_iota(jnp.int32, (count, width), 0) == block
        placed = jnp.where(at, gain.astype(F32)[None, :], 0.0)
        return placed.reshape(count * width // rank, rank)

    gain_sh = jnp.concatenate([spot(gain_attn), spot(gain_ffn), spot(gain_latent)], axis=0)
    gain_sh = jnp.pad(gain_sh, ((0, 8 - gain_sh.shape[0]), (0, 0)))
    seq_sh = jnp.concatenate([w_qa, w_key, w_value], axis=1)
    (
        qb_all,
        out_all,
        gate_all,
        up_all,
        down_all,
        seq_all,
        gains,
        lkv,
        q_all,
        mixed,
        latent,
        normed,
        middle,
        hidden,
        grad_gate,
        grad_up,
        gw_gate,
        gw_up,
        gw_down,
    ) = forward_call(
        ndp, tokens, d_output, cos, sin, bias, seq_sh, gain_sh, w_qb, w_out, w_gate, w_up, w_down
    )
    o_gate, o_up, o_down, o_out, o_qb, o_seq, o_gain, input_grad, output = backward_call(
        ndp,
        tokens,
        d_output,
        middle,
        latent,
        normed,
        gains,
        cos,
        sin,
        bias,
        (gw_gate, gw_up, gw_down),
        (hidden, grad_gate, grad_up, gate_all, up_all, down_all),
        (lkv, q_all, mixed, qb_all, out_all, seq_all),
    )

    def own_gain(flat, width):
        return lax.dynamic_slice_in_dim(flat.reshape(-1), block * width, width, 0)

    return (
        output,
        input_grad,
        own_gain(o_gain[:wide], gain_attn.shape[0]),
        o_seq[:, :rank],
        own_gain(o_gain[2 * wide], gain_latent.shape[0]),
        o_qb,
        o_seq[:, rank : rank + hd],
        o_seq[:, rank + hd :],
        o_out,
        own_gain(o_gain[wide : 2 * wide], gain_ffn.shape[0]),
        o_gate,
        o_up,
        o_down,
    )


def solution(mesh):
    both = ("dp", "fsdp")
    rowwise, vector = P(both, None), P(both)
    tok = P(None, both, None)
    head = P("dp", "fsdp")
    return jax.shard_map(
        functools.partial(per_device, mesh.shape["dp"]),
        mesh=mesh,
        in_specs=(
            tok,
            P("dp", None, None),
            tok,
            vector,
            rowwise,
            vector,
            head,
            rowwise,
            rowwise,
            head,
            vector,
            head,
            head,
            head,
        ),
        out_specs=(
            tok,
            tok,
            vector,
            rowwise,
            vector,
            head,
            rowwise,
            rowwise,
            head,
            vector,
            head,
            head,
            head,
        ),
        check_vma=False,
    )
```

```python
import functools

import jax
import jax.numpy as jnp
from jax import lax
from jax.experimental import pallas as pl
from jax.experimental.pallas import tpu as pltpu
from jax.sharding import PartitionSpec as P

BLK = 32
PROMPT = 256
EPSILON = 1e-05
ROPE_BASE = 10000.0
MASK_FILL = -1e30
F32 = jnp.float32
BF16 = jnp.bfloat16
MESH = pl.DeviceIdType.MESH
ANY = pl.BlockSpec(memory_space=pl.ANY)
VMEM = pl.BlockSpec(memory_space=pltpu.VMEM)
NF = 4
GATHER_ROWS = 64
GATHER_AHEAD = 5
GATHER_FIRST = 4
FFN_ROWS = 128
FFN_COLS = 512


def ffn_chunks(cols):
    return [(c, min(FFN_COLS, cols - c)) for c in range(0, cols, FFN_COLS)]


def layout(member_row, block_len):
    count_blocks = member_row.shape[0]
    block_ids = jnp.arange(count_blocks, dtype=jnp.int32)
    same_run = (member_row[None, :] == member_row[:, None]) & (
        block_ids[None, :] < block_ids[:, None]
    )
    earlier = jnp.sum(same_run.astype(jnp.int32), axis=1)
    prompt_len = jnp.sum((member_row == 0).astype(jnp.int32)) * block_len
    labels = jnp.repeat(member_row, block_len)
    within = jnp.arange(count_blocks * block_len, dtype=jnp.int32) % block_len
    positions = (
        (labels > 0).astype(jnp.int32) * prompt_len
        + jnp.repeat(earlier, block_len) * block_len
        + within
    )
    return (labels, positions)


def rope_tables(positions, head_width):
    half_width = head_width // 2
    frequency = ROPE_BASE ** (-(jnp.arange(half_width, dtype=jnp.float32) * (2.0 / head_width)))
    angles = positions.astype(jnp.float32)[:, None] * frequency[None, :]
    return (jnp.cos(angles), jnp.sin(angles))


def al(x, n):
    return pl.multiple_of(x, n)


def mm(a, b):
    return lax.dot_general(a, b, (((1,), (0,)), ((), ())), preferred_element_type=F32)


def mm_nt(a, b):
    return lax.dot_general(a, b, (((1,), (1,)), ((), ())), preferred_element_type=F32)


def mm_tn(a, b):
    return lax.dot_general(a, b, (((0,), (0,)), ((), ())), preferred_element_type=F32)


class Place:
    def __init__(self, ndp):
        self.ndp = ndp
        self.bits = [1 << b for b in range(ndp.bit_length() - 1)]
        self.me = lax.axis_index("dp")
        self.f = lax.axis_index("fsdp")
        y, c = self.f // 2, self.f % 2
        self.f_core = y * 2 + 1 - c
        self.f_y = (1 - y) * 2 + c
        self.f_yc = (1 - y) * 2 + 1 - c
        self.to_core = (self.me, self.f_core)
        self.to_y = (self.me, self.f_y)

    def at(self, mask):
        j = self.me
        for b in self.bits:
            if mask & b:
                j = j + b - 2 * b * ((self.me // b) % 2)
        return j

    def to_dp(self, mask):
        return (self.at(mask), self.f)

    def orders(self, swapped):
        o = list(self.bits)
        if swapped and len(o) > 1:
            o[0], o[1] = o[1], o[0]
        return o

    def barrier(self):
        bar = pltpu.get_barrier_semaphore()
        devs = [self.to_dp(b) for b in self.bits] + [self.to_core, self.to_y]
        for d in devs:
            pl.semaphore_signal(bar, inc=1, device_id=d, device_id_type=MESH)
        pl.semaphore_wait(bar, len(devs))


def rcopy(src, dst, ss, rs, dev):
    return pltpu.make_async_remote_copy(
        src_ref=src, dst_ref=dst, send_sem=ss, recv_sem=rs, device_id=dev, device_id_type=MESH
    )


class DpGather:
    def __init__(self, pos, ss, rs):
        self.p, self.ss, self.rs = pos, ss, rs
        self.items, self.events = [], []
        self.launched = self.seen = self.first = 0

    def add(self, src, dst, swapped=False):
        self.items.append((src, dst, self.p.orders(swapped)[::-1]))
        return len(self.items) - 1

    def copy(self, n, mask, stage):
        src, dst, order = self.items[n]
        j = self.p.at(mask)
        k = self.index(n, mask | order[stage])
        return rcopy(
            src if mask == 0 else dst(j),
            dst(j),
            self.ss.at[n, k],
            self.rs.at[n, k],
            self.p.to_dp(order[stage]),
        )

    def index(self, n, mask):
        return mask - 1

    def stage_of(self, n, mask):
        return max(i for i, b in enumerate(self.items[n][2]) if mask & b)

    def arrived(self, n, mask):
        src, dst, order = self.items[n]
        stage = self.stage_of(n, mask)
        j = self.p.at(mask)
        k = self.index(n, mask)
        rcopy(src, dst(j), self.ss.at[n, k], self.rs.at[n, k], self.p.to_dp(order[stage])).wait_recv()

    def launch(self):
        if self.launched < len(self.items):
            n = self.launched
            for stage in range(len(self.p.bits)):
                self.copy(n, 0, stage).start()
            self.launched += 1

    def masks(self, n):
        order = self.items[n][2]
        last = order[-1]
        out = [m for m in range(1, self.p.ndp) if not m & last]
        return sorted(out, key=lambda m: (self.stage_of(n, m), m))

    def forward(self, n, stage):
        for m in self.masks(n):
            if self.stage_of(n, m) == stage:
                self.arrived(n, m)
                for later in range(stage + 1, len(self.p.bits)):
                    self.copy(n, m, later).start()

    def steps(self, count, ahead):
        lag = len(self.p.bits) - 1
        for _ in range(count):
            if self.seen >= len(self.items) + lag - 1:
                return
            while self.launched < min(len(self.items), self.seen + ahead):
                self.launch()
            for stage in range(lag):
                n = self.seen - stage
                if self.first <= n < len(self.items):
                    self.forward(n, stage)
            self.seen += 1

    def need(self, n, ahead):
        self.steps(n + len(self.p.bits) - 1 - self.seen, ahead)

    def wait_last(self, n):
        last = self.items[n][2][-1]
        for m in range(self.p.ndp):
            if m & last:
                self.arrived(n, m)

    def wait_sends(self, n):
        for m in range(self.p.ndp):
            first = 0 if m == 0 else self.stage_of(n, m) + 1
            for stage in range(first, len(self.p.bits)):
                self.copy(n, m, stage).wait_send()


class FsGather:
    def __init__(self, pos, blocks, ss, rs):
        self.p, self.b, self.ss, self.rs = pos, blocks, ss, rs

    def copy(self, n, fb, dev):
        return rcopy(self.b(fb), self.b(fb), self.ss.at[n], self.rs.at[n], dev)

    def start(self):
        self.copy(1, self.p.f, self.p.to_y).start()
        self.copy(0, self.p.f, self.p.to_core).start()

    def mid(self):
        self.copy(1, self.p.f_y, self.p.to_y).wait_recv()
        self.copy(2, self.p.f_y, self.p.to_core).start()

    def end(self):
        self.copy(0, self.p.f_core, self.p.to_core).wait_recv()
        self.copy(2, self.p.f_yc, self.p.to_core).wait_recv()

    def wait_sends(self):
        self.copy(1, self.p.f, self.p.to_y).wait_send()
        self.copy(0, self.p.f, self.p.to_core).wait_send()
        self.copy(2, self.p.f_y, self.p.to_core).wait_send()


class FsReduce:
    def __init__(self, pos, blocks, from_core, from_y, ss, rs):
        self.p, self.b, self.fc, self.fy, self.ss, self.rs = pos, blocks, from_core, from_y, ss, rs

    def c1(self):
        return rcopy(
            self.b(self.p.f_yc), self.fc.at[1], self.ss.at[1], self.rs.at[1], self.p.to_core
        )

    def c0(self):
        return rcopy(
            self.b(self.p.f_core), self.fc.at[0], self.ss.at[0], self.rs.at[0], self.p.to_core
        )

    def cy(self):
        return rcopy(self.fc.at[1], self.fy, self.ss.at[2], self.rs.at[2], self.p.to_y)

    def start(self):
        self.c1().start()
        self.c0().start()

    def mid(self, rows, tile=64):
        self.c1().wait_recv()
        mine = self.b(self.p.f_y)

        def add(t, _):
            r = pl.ds(al(t * tile, tile), tile)
            self.fc[1, r, :] = (self.fc[1, r, :].astype(F32) + mine[r, :].astype(F32)).astype(BF16)
            return 0

        lax.fori_loop(0, rows // tile, add, 0)
        self.cy().start()

    def end(self):
        self.c0().wait_recv()
        self.cy().wait_recv()

    def value(self, r):
        return (
            self.b(self.p.f)[r, :].astype(F32)
            + self.fc[0, r, :].astype(F32)
            + self.fy[r, :].astype(F32)
        )

    def wait_sends(self):
        self.c1().wait_send()
        self.c0().wait_send()
        self.cy().wait_send()


def softmax_parts(scores):
    top = jnp.max(scores, axis=-1, keepdims=True)
    lifted = jnp.exp(scores - top)
    return lifted / jnp.sum(lifted, axis=-1, keepdims=True)


def causal_bias(rows):
    r = lax.broadcasted_iota(jnp.int32, (rows, rows), 0)
    c = lax.broadcasted_iota(jnp.int32, (rows, rows), 1)
    return jnp.where(c <= r, 0.0, MASK_FILL).astype(F32)


def group_rows(ref, m, half, cols, own):
    t = own // 2
    first = ref[pl.ds((2 * half) * own + m * t, t), cols]
    second = ref[pl.ds((2 * half + 1) * own + m * t, t), cols]
    return jnp.concatenate([first, second], axis=0)


def put_rows(ref, m, half, cols, own, value):
    t = own // 2
    ref[pl.ds((2 * half) * own + m * t, t), cols] = value[:t]
    ref[pl.ds((2 * half + 1) * own + m * t, t), cols] = value[t:]


def forward_kernel(
    cfg,
    tok,
    dout,
    cos,
    sin,
    bias,
    seq_sh,
    gain_sh,
    qb_sh,
    out_sh,
    gate_sh,
    up_sh,
    down_sh,
    qb_all,
    out_all,
    gate_all,
    up_all,
    down_all,
    seq_all,
    gain_sum,
    lkv_o,
    q_o,
    mixed_o,
    latent_o,
    normed_o,
    middle_o,
    hid_o,
    gg_o,
    gu_o,
    gw_gate,
    gw_up,
    gw_down,
    rx_o,
    seq_v,
    gain_v,
    qb_v,
    out_v,
    lkv_v,
    q_v,
    mixed_v,
    part_v,
    fcore_v,
    fy_v,
    n2_v,
    d_v,
    n2_t,
    d_t,
    lat_v,
    gss,
    grs,
    fss,
    frs,
    sys_,
    syr,
    ls,
    ffn_ls,
    pss,
    prs,
):
    ndp, own, dim, rank, hd, heads = cfg
    rows = NF * own
    p = Place(ndp)
    kvw = rank + 2 * hd
    sr = seq_sh.shape[0]
    g = DpGather(p, gss, grs)
    i_seq = g.add(seq_sh, lambda j: seq_v.at[pl.ds(al((j * NF + p.f) * sr, sr), sr)])
    i_gain = g.add(gain_sh, lambda j: gain_v.at[j * NF + p.f])
    turn = [0]

    def weight_items(src, dst, cols=slice(None), most=GATHER_ROWS):
        n = src.shape[0]
        step = min(n, most)
        out = []
        for c in range(n // step):
            turn[0] += 1
            out.append(
                g.add(
                    src.at[pl.ds(c * step, step), cols],
                    lambda j, c=c: dst.at[pl.ds(al(j * n + c * step, step), step), cols],
                    turn[0] % 8 == 0,
                )
            )
        return out

    i_qb = weight_items(qb_sh, qb_v)
    i_out = weight_items(out_sh, out_v)
    i_ffn = []
    for c0, cw in ffn_chunks(gate_sh.shape[1]):
        cols = pl.ds(c0, cw)
        some = []
        for s, d in ((gate_sh, gate_all), (up_sh, up_all), (down_sh, down_all)):
            some += weight_items(s, d, cols, FFN_ROWS)
        i_ffn.append(some)
    order = range(len(g.items))
    fs_d = FsGather(p, lambda b: d_v.at[pl.ds(al(b * own, own), own)], fss.at[0], frs.at[0])
    fs_l = FsGather(p, lambda b: lkv_v.at[pl.ds(al(b * own, own), own)], fss.at[1], frs.at[1])
    fs_n = FsGather(p, lambda b: n2_v.at[pl.ds(al(b * own, own), own)], fss.at[2], frs.at[2])
    red = FsReduce(
        p, lambda b: part_v.at[pl.ds(al(b * own, own), own)], fcore_v, fy_v, fss.at[3], frs.at[3]
    )

    local = []

    def local_copy(src, dst):
        c = pltpu.make_async_copy(src, dst, ls.at[len(local)])
        c.start()
        local.append(c)
        return c

    own_copies = {}
    for i in order:
        src, dst, _ = g.items[i]
        own_copies[i] = local_copy(src, dst(p.me))
    d_copies = [
        local_copy(dout.at[m], d_v.at[pl.ds(al(p.f * own + m * (own // 2), 128), own // 2)])
        for m in range(2)
    ]

    p.barrier()
    for _ in range(GATHER_FIRST):
        g.launch()
    npiece = ndp

    def seq_piece(j, fb):
        return seq_v.at[pl.ds(al((j * NF + fb) * sr, sr), sr)]

    def seq_copy(t, j, fb, dev, which):
        b = seq_piece(j, fb) if which == 0 else gain_v.at[j * NF + fb]
        return rcopy(b, b, sys_.at[which, t, j], syr.at[which, t, j], dev)

    def spread(j):
        for which in (0, 1):
            seq_copy(1, j, p.f, p.to_y, which).start()
            seq_copy(0, j, p.f, p.to_core, which).start()

    for m in range(2):
        x = tok[m].astype(F32)
        inv = lax.rsqrt(jnp.mean(x * x, axis=-1, keepdims=True) + EPSILON)
        middle_o[pl.ds(m * (own // 2), own // 2), :] = x * inv
    own_copies[i_seq].wait()
    own_copies[i_gain].wait()
    spread(p.me)
    for m in sorted(range(1, ndp), key=lambda m: g.stage_of(i_seq, m)):
        for i in (i_seq, i_gain):
            g.arrived(i, m)
            for stage in range(g.stage_of(i, m) + 1, len(p.bits)):
                g.copy(i, m, stage).start()
        spread(p.at(m))
    g.seen = g.first = 2
    for c in d_copies:
        c.wait()

    def spread_forward(j, _):
        for which in (0, 1):
            seq_copy(1, j, p.f_y, p.to_y, which).wait_recv()
            seq_copy(2, j, p.f_y, p.to_core, which).start()
        return 0

    def tick(n):
        g.steps(n, GATHER_AHEAD)

    tick(1)
    lax.fori_loop(0, npiece, spread_forward, 0)
    fs_d.start()
    tick(1)

    def spread_end(j, _):
        for which in (0, 1):
            seq_copy(0, j, p.f_core, p.to_core, which).wait_recv()
            seq_copy(2, j, p.f_yc, p.to_core, which).wait_recv()
        return 0

    lax.fori_loop(0, npiece, spread_end, 0)

    def gain_add(j, acc):
        return acc + gain_v[j]

    gains = lax.fori_loop(0, ndp * NF, gain_add, jnp.zeros(gain_v.shape[1:], F32))
    gain_sum[...] = gains
    wide = dim // rank
    gain_one = jnp.concatenate([gains[r : r + 1] for r in range(wide)], axis=1)
    gain_two = jnp.concatenate([gains[wide + r : wide + r + 1] for r in range(wide)], axis=1)
    gain_lat = gains[2 * wide : 2 * wide + 1]
    normed_o[...] = (middle_o[...] * gain_one).astype(BF16)
    seq_out = local_copy(seq_v, seq_all)

    def project(j, _):
        cols = pl.ds(al(j * 256, 256), 256)
        lat_v[:, cols] = mm(normed_o[...], seq_v[:, cols])
        return 0

    lax.fori_loop(0, kvw // 256, project, 0)
    own_rows = pl.ds(al(p.f * own, own), own)
    lat = lat_v[:, :rank]
    latent_o[...] = lat
    inv_lat = lax.rsqrt(jnp.mean(lat * lat, axis=-1, keepdims=True) + EPSILON)
    lkv_v[own_rows, :rank] = (lat * inv_lat * gain_lat).astype(BF16)
    half = hd // 2
    co, si = cos[own_rows, :], sin[own_rows, :]
    ka, kb = lat_v[:, rank : rank + half], lat_v[:, rank + half : rank + hd]
    lkv_v[own_rows, rank : rank + half] = (ka * co - kb * si).astype(BF16)
    lkv_v[own_rows, rank + half : rank + hd] = (kb * co + ka * si).astype(BF16)
    lkv_v[own_rows, rank + hd :] = lat_v[:, rank + hd :].astype(BF16)
    fs_l.start()
    tick(1)
    fs_d.mid()
    fs_l.mid()
    tick(1)
    for i in i_qb:
        g.need(i, GATHER_AHEAD)
        own_copies[i].wait()
        g.wait_last(i)
    fs_l.end()
    qb_out = local_copy(qb_v, qb_all)
    lkv_out = local_copy(lkv_v, lkv_o)

    def query(j, _):
        cols = pl.ds(al(j * hd, hd), hd)
        c0 = pl.ds(al(j * hd, half), half)
        c1 = pl.ds(al(j * hd + half, half), half)
        for r in range(rows // 512):
            rr = pl.ds(r * 512, 512)
            acc = mm(lkv_v[rr, :rank], qb_v[:, cols])
            a, b = acc[:, :half], acc[:, half:]
            c, s = cos[rr, :], sin[rr, :]
            q_v[rr, c0] = (a * c - b * s).astype(BF16)
            q_v[rr, c1] = (b * c + a * s).astype(BF16)
        return 0

    lax.fori_loop(0, heads, query, 0)
    q_out = local_copy(q_v, q_o)
    tick(1)
    scale = hd ** (-0.5)
    kcols, vcols = slice(rank, rank + hd), slice(rank + hd, rank + 2 * hd)
    causal = causal_bias(PROMPT)
    for m in range(2):
        k0, k1 = (group_rows(lkv_v, m, h2, kcols, own) for h2 in (0, 1))
        v0, v1 = (group_rows(lkv_v, m, h2, vcols, own) for h2 in (0, 1))
        low = bias[m]

        def attend(h, _):
            cols = pl.ds(al(h * hd, hd), hd)
            q0 = group_rows(q_v, m, 0, cols, own)
            pr = softmax_parts(mm_nt(q0, k0) * scale + causal).astype(BF16)
            put_rows(mixed_v, m, 0, cols, own, mm(pr, v0).astype(BF16))
            q1 = group_rows(q_v, m, 1, cols, own)
            s0 = mm_nt(q1, k0) * scale
            s1 = mm_nt(q1, k1) * scale + low
            top = jnp.maximum(
                jnp.max(s0, axis=-1, keepdims=True), jnp.max(s1, axis=-1, keepdims=True)
            )
            e0, e1 = jnp.exp(s0 - top), jnp.exp(s1 - top)
            total = jnp.sum(e0, axis=-1, keepdims=True) + jnp.sum(e1, axis=-1, keepdims=True)
            mix = mm((e0 / total).astype(BF16), v0) + mm((e1 / total).astype(BF16), v1)
            put_rows(mixed_v, m, 1, cols, own, mix.astype(BF16))
            return 0

        lax.fori_loop(0, heads, attend, 0)
        tick(2)
    fs_d.end()
    mixed_out = local_copy(mixed_v, mixed_o)
    tick(1)
    for i in i_out:
        g.need(i, GATHER_AHEAD)
        own_copies[i].wait()
        g.wait_last(i)
    out_out = local_copy(out_v, out_all)

    def project_out(fb):
        rr = pl.ds(al(fb * own, own), own)

        def one(j, _):
            wr = pl.ds(al(j * 256, 256), 256)
            part_v[rr, wr] = mm_nt(mixed_v[rr, :], out_v[wr, :]).astype(BF16)
            return 0

        lax.fori_loop(0, dim // 256, one, 0)

    project_out(p.f_yc)
    project_out(p.f_core)
    red.start()
    tick(1)
    project_out(p.f_y)
    red.mid(own)
    project_out(p.f)
    tick(2)
    red.end()
    for m in range(2):
        rr = pl.ds(m * (own // 2), own // 2)
        mid = tok[m].astype(F32) + red.value(rr)
        middle_o[rr, :] = mid
        inv = lax.rsqrt(jnp.mean(mid * mid, axis=-1, keepdims=True) + EPSILON)
        n2_v[pl.ds(al(p.f * own + m * (own // 2), 128), own // 2), :] = (
            mid * inv * gain_two
        ).astype(BF16)
    fs_n.start()
    tick(1)

    def turn_d(j, _):
        cols = pl.ds(al(j * 256, 256), 256)
        d_t[cols, :] = d_v[:, cols].T
        return 0

    lax.fori_loop(0, dim // 256, turn_d, 0)
    tick(1)
    fs_n.mid()
    tick(1)
    fs_n.end()

    def turn_n2(j, _):
        cols = pl.ds(al(j * 256, 256), 256)
        n2_t[cols, :] = n2_v[:, cols].T
        return 0

    lax.fori_loop(0, dim // 256, turn_n2, 0)
    for c in (q_out, mixed_out, out_out, seq_out):
        c.wait()
    early = [i_seq, i_gain] + i_qb + i_out
    for i in early:
        g.wait_sends(i)

    def spread_sends(j, _):
        for which in (0, 1):
            seq_copy(0, j, p.f, p.to_core, which).wait_send()
            seq_copy(1, j, p.f, p.to_y, which).wait_send()
            seq_copy(2, j, p.f_y, p.to_core, which).wait_send()
        return 0

    lax.fori_loop(0, npiece, spread_sends, 0)
    red.wait_sends()
    pending = []
    width = FFN_COLS
    chunks = ffn_chunks(gate_sh.shape[1])
    nb = len(p.bits)
    blk = gate_sh.shape[0]

    def early_copy(i):
        mask = 1 + sum(p.bits[1 + t] for t in range(nb - 1) if i >> (nb - 2 - t) & 1)
        return rcopy(
            gw_gate.at[pl.ds(al(p.at(mask) * blk, blk), blk), pl.ds(0, width)],
            rx_o.at[i],
            pss.at[i],
            prs.at[i],
            p.to_dp(1),
        )

    for n_chunk, ((c0, cw), some) in enumerate(zip(chunks, i_ffn)):
        g.need(some[-1], GATHER_AHEAD)
        for i in some:
            own_copies[i].wait()
            g.wait_last(i)
        cols = pl.ds(c0, cw)
        loads = [
            pltpu.make_async_copy(w.at[:, cols], seq_v.at[:, pl.ds(n * width, cw)], ffn_ls.at[n])
            for n, w in enumerate((gate_all, up_all, down_all))
        ]
        for c in loads:
            c.start()
        for c in pending:
            c.wait()
        if n_chunk == len(chunks) - 1:
            for i in range(ndp // 2):
                early_copy(i).start()
        for c in loads:
            c.wait()
        gate_c, up_c, down_c = (slice(n * width, n * width + cw) for n in range(3))

        def both(t, _):
            rr = pl.ds(al(t * 256, 256), 256)
            gate = mm(n2_v[rr, :], seq_v[:, gate_c])
            up = mm(n2_v[rr, :], seq_v[:, up_c])
            grad_hidden = mm(d_v[rr, :], seq_v[:, down_c])
            sig = 1.0 / (1.0 + jnp.exp(-gate))
            act = gate * sig
            mixed_v[rr, :cw] = (act * up).astype(BF16)
            q_v[rr, gate_c] = (grad_hidden * up * (sig * (1.0 + gate * (1.0 - sig)))).astype(BF16)
            q_v[rr, up_c] = (grad_hidden * act).astype(BF16)
            return 0

        for lo in range(0, rows // 256, 2):
            lax.fori_loop(lo, lo + 2, both, 0)
            tick(1)
        pending = [
            pltpu.make_async_copy(src, dst.at[:, cols], ffn_ls.at[3 + n])
            for n, (src, dst) in enumerate(
                (
                    (mixed_v.at[:, pl.ds(0, cw)], hid_o),
                    (q_v.at[:, pl.ds(0, cw)], gg_o),
                    (q_v.at[:, pl.ds(width, cw)], gu_o),
                )
            )
        ]
        for c in pending:
            c.start()

        half_rows = part_v.shape[0] // 256
        for lo in range(0, dim // 256, half_rows):

            def weight_grads(j, _):
                rr = pl.ds(al(j * 256, 256), 256)
                pr = pl.ds(al((j - lo) * 256, 256), 256)
                pc = slice((lo // half_rows) * width, (lo // half_rows) * width + cw)
                out_v[rr, gate_c] = mm(n2_t[rr, :], q_v[:, gate_c]).astype(BF16)
                out_v[rr, up_c] = mm(n2_t[rr, :], q_v[:, up_c]).astype(BF16)
                part_v[pr, pc] = mm(d_t[rr, :], mixed_v[:, :cw]).astype(BF16)
                return 0

            lax.fori_loop(lo, min(dim // 256, lo + half_rows), weight_grads, 0)
            tick(1)
        saves = [
            pltpu.make_async_copy(out_v.at[:, pl.ds(0, cw)], gw_gate.at[:, cols], ffn_ls.at[6]),
            pltpu.make_async_copy(out_v.at[:, pl.ds(width, cw)], gw_up.at[:, cols], ffn_ls.at[7]),
        ]
        prow = part_v.shape[0]
        for n in range(dim // prow):
            saves.append(
                pltpu.make_async_copy(
                    part_v.at[:, pl.ds(n * width, cw)],
                    gw_down.at[pl.ds(n * prow, prow), cols],
                    ffn_ls.at[8 + n],
                )
            )
        for c in saves:
            c.start()
        pending = pending + saves
    for c in pending:
        c.wait()
    tick(2 * len(g.items))
    for i in range(ndp // 2):
        early_copy(i).wait_recv()
        early_copy(i).wait_send()
    for i in order:
        if i not in early:
            g.wait_sends(i)
    for t in (fs_d, fs_l, fs_n):
        t.wait_sends()
    for c in (qb_out, lkv_out):
        c.wait()


def forward_call(ndp, tok, dout, cos, sin, bias, seq_sh, gain_sh, qb, out, gate, up, down):
    own = tok.shape[0] * tok.shape[1]
    dim = tok.shape[2]
    rank = qb.shape[0] * ndp
    hd = (seq_sh.shape[1] - rank) // 2
    heads = qb.shape[1] // hd
    rows = NF * own
    kvw = seq_sh.shape[1]
    n_items = 2 + sum(w.shape[0] // min(w.shape[0], GATHER_ROWS) for w in (qb, out))
    n_items += sum(w.shape[0] // min(w.shape[0], FFN_ROWS) for w in (gate, up, down)) * len(
        ffn_chunks(gate.shape[1])
    )

    def sds(shape, dtype=BF16):
        return jax.ShapeDtypeStruct(shape, dtype)

    full = lambda w: sds((w.shape[0] * ndp, w.shape[1]))
    out_shape = (
        full(qb),
        full(out),
        full(gate),
        full(up),
        full(down),
        sds((seq_sh.shape[0] * ndp * NF, kvw)),
        sds(gain_sh.shape, F32),
        sds((rows, kvw)),
        sds((rows, heads * hd)),
        sds((rows, heads * hd)),
        sds((own, rank), F32),
        sds((own, dim)),
        sds((own, dim), F32),
        sds((rows, gate.shape[1])),
        sds((rows, gate.shape[1])),
        sds((rows, gate.shape[1])),
        full(gate),
        full(up),
        full(down),
        sds((ndp // 2, gate.shape[0], FFN_COLS)),
    )
    out_specs = (ANY,) * 6 + (VMEM,) + (ANY,) * 3 + (VMEM,) * 3 + (ANY,) * 7
    dma = pltpu.SemaphoreType.DMA
    scratch = [
        pltpu.VMEM((seq_sh.shape[0] * ndp * NF, kvw), BF16),
        pltpu.VMEM((ndp * NF,) + gain_sh.shape, F32),
        pltpu.VMEM((qb.shape[0] * ndp, qb.shape[1]), BF16),
        pltpu.VMEM((out.shape[0] * ndp, out.shape[1]), BF16),
        pltpu.VMEM((rows, kvw), BF16),
        pltpu.VMEM((rows, heads * hd), BF16),
        pltpu.VMEM((rows, heads * hd), BF16),
        pltpu.VMEM((rows, dim), BF16),
        pltpu.VMEM((2, own, dim), BF16),
        pltpu.VMEM((own, dim), BF16),
        pltpu.VMEM((rows, dim), BF16),
        pltpu.VMEM((rows, dim), BF16),
        pltpu.VMEM((dim, rows), BF16),
        pltpu.VMEM((dim, rows), BF16),
        pltpu.VMEM((own, kvw), F32),
        dma((n_items, ndp - 1)),
        dma((n_items, ndp - 1)),
        dma((4, 3)),
        dma((4, 3)),
        dma((2, 3, ndp)),
        dma((2, 3, ndp)),
        dma((n_items + 10,)),
        dma((10,)),
        dma((ndp // 2,)),
        dma((ndp // 2,)),
    ]
    return pl.pallas_call(
        functools.partial(forward_kernel, (ndp, own, dim, rank, hd, heads)),
        out_shape=out_shape,
        in_specs=(VMEM,) * 5 + (ANY,) * 7,
        out_specs=out_specs,
        scratch_shapes=scratch,
        compiler_params=pltpu.CompilerParams(
            collective_id=0, has_side_effects=True, vmem_limit_bytes=60 * 2**20
        ),
        name="gather_forward",
    )(tok, dout, cos, sin, bias, seq_sh, gain_sh, qb, out, gate, up, down)


class DpScatter:
    PER_TICK = 1

    def __init__(self, pos, count, first, later, own, acc, ss, rs, ls, credit, pls):
        self.p, self.count = pos, count
        self.n = len(pos.bits)
        self.SLOTS, self.AHEAD, self.OWN = scatter_ring(pos.ndp // 2)
        self.first, self.later, self.own, self.acc = first, later, own, acc
        self.ss, self.rs, self.ls, self.credit, self.pls = ss, rs, ls, credit, pls
        self.items = []
        self.started = self.stepped = 0

    def order(self, n):
        return self.p.orders(False)

    def width(self, stage):
        return 1 << (self.n - 1 - stage)

    def make(self, src, base, out, pieces, c0=0, cols=None, pre=None):
        rows = out.shape[0]
        cols = out.shape[1] if cols is None else cols
        r = rows // pieces
        return [(src, base, out, rows, cols, c * r, r, c0, pre) for c in range(pieces)]

    def add(self, *args):
        self.items += self.make(*args)
        self.pump()

    def mask(self, n, i):
        order = self.order(n)
        return sum(order[1 + t] for t in range(self.n - 1) if i >> (self.n - 2 - t) & 1)

    def block(self, n, mask):
        src, base, out, rows, cols, r0, r, c0, pre = self.items[n]
        return src.at[pl.ds(al(base + self.p.at(mask) * rows + r0, r), r), pl.ds(c0, cols)]

    def place(self, buf, n, lo, size):
        src, base, out, rows, cols, r0, r, c0, pre = self.items[n]
        return buf.at[n % self.SLOTS, pl.ds(lo, size), pl.ds(0, r), pl.ds(0, cols)]

    def copies(self, n, stage):
        bit = self.order(n)[stage]
        dev = self.p.to_dp(bit)
        s = n % self.SLOTS
        if stage == 0:
            return [
                rcopy(
                    self.block(n, bit | self.mask(n, i)),
                    self.place(self.first, n, i, 1).at[0],
                    self.ss.at[s, i],
                    self.rs.at[s, i],
                    dev,
                )
                for i in range(self.width(0))
            ]
        w = self.width(stage)
        k = self.width(0) + stage - 1
        return [
            rcopy(
                self.place(self.first, n, w, w),
                self.place(self.later, n, w - 1, w),
                self.ss.at[s, k],
                self.rs.at[s, k],
                dev,
            )
        ]

    def owncopy(self, n, i):
        src, base, out, rows, cols, r0, r, c0, pre = self.items[n]
        s = n % self.OWN
        return pltpu.make_async_copy(
            self.block(n, self.mask(n, i)),
            self.own.at[s, i, pl.ds(0, r), pl.ds(0, cols)],
            self.ls.at[s, i],
        )

    def outcopy(self, n):
        src, base, out, rows, cols, r0, r, c0, pre = self.items[n]
        s = n % self.SLOTS
        return pltpu.make_async_copy(
            self.acc.at[s, pl.ds(0, r), pl.ds(0, cols)],
            out.at[pl.ds(r0, r), pl.ds(c0, cols)],
            self.ls.at[s, self.width(0)],
        )

    def free(self, n, stage):
        m = n + self.SLOTS
        if m < self.count and not (stage == 0 and self.given(m)):
            bit = self.order(m)[stage]
            pl.semaphore_signal(
                self.credit.at[stage, self.p.bits.index(bit)],
                inc=1,
                device_id=self.p.to_dp(bit),
                device_id_type=MESH,
            )

    def given(self, n):
        return n < len(self.items) and self.items[n][-1] is not None

    def precopy(self, n, i):
        src, base, out, rows, cols, r0, r, c0, pre = self.items[n]
        s = n % self.SLOTS
        return pltpu.make_async_copy(
            pre.at[i, pl.ds(r0, r)], self.place(self.first, n, i, 1).at[0], self.pls.at[s, i]
        )

    def send(self, n, stage):
        if stage == 0 and self.given(n):
            for i in range(self.width(0)):
                self.precopy(n, i).start()
            return
        bit = self.order(n)[stage]
        if n >= self.SLOTS:
            pl.semaphore_wait(self.credit.at[stage, self.p.bits.index(bit)], 1)
        for c in self.copies(n, stage):
            c.start()

    def pump(self):
        while self.started < min(len(self.items), self.stepped + self.AHEAD):
            n = self.started
            self.send(n, 0)
            for i in range(self.width(0)):
                self.owncopy(n, i).start()
            self.started += 1

    def tick(self, steps=1):
        for _ in range(self.PER_TICK * steps):
            n = self.stepped
            if n >= self.started:
                return
            self.combine(n, 0)
            self.stepped += 1
            self.pump()
            for stage in range(1, self.n):
                if n >= stage:
                    self.combine(n - stage, stage)

    def combine(self, n, stage):
        src, base, out, rows, cols, r0, r, c0, pre = self.items[n]
        s, tile = n % self.SLOTS, 16
        w = self.width(stage)
        if stage == 0 and pre is not None:
            for i in range(w):
                self.precopy(n, i).wait()
        else:
            for c in self.copies(n, stage):
                c.wait_recv()
        if stage == 0:
            for i in range(w):
                self.owncopy(n, i).wait()
        else:
            for c in self.copies(n, stage):
                c.wait_send()
        last = stage == self.n - 1

        def add(lo, size):
            def one(t, _):
                t = pl.ds(al(t * tile, tile), tile)
                for i in range(lo, lo + size):
                    a = self.first[s, i, t, :cols]
                    b = self.own[n % self.OWN, i, t, :cols] if stage == 0 else self.later[s, w - 1 + i, t, :cols]
                    if last:
                        self.acc[s, t, :cols] = a.astype(F32) + b.astype(F32)
                    else:
                        self.first[s, i, t, :cols] = a + b
                return 0

            lax.fori_loop(0, r // tile, one, 0)

        if last:
            if n >= self.SLOTS:
                self.outcopy(n - self.SLOTS).wait()
            if pre is None:
                for c in self.copies(n, 0):
                    c.wait_send()
            add(0, 1)
            self.outcopy(n).start()
            for t in range(self.n):
                self.free(n, t)
        else:
            half = w // 2
            add(half, half)
            self.send(n, stage + 1)
            add(0, half)

    def drain(self):
        self.tick(self.count)
        for n in range(self.count, self.count + self.n - 1):
            for stage in range(1, self.n):
                if 0 <= n - stage < self.count:
                    self.combine(n - stage, stage)
        for n in range(max(0, self.count - self.SLOTS), self.count):
            self.outcopy(n).wait()


def scatter_ring(nz):
    return (10, 6, 7) if nz * max(16, 128 // nz) <= 128 else (5, 2, 3)


def piece_rows(rows, nz):
    return min(rows, max(16, 128 // nz))


def backward_kernel(
    cfg,
    tok,
    dout,
    middle,
    latent,
    normed,
    gains,
    cos,
    sin,
    bias,
    gw_gate,
    gw_up,
    gw_down,
    hid_h,
    gg_h,
    gu_h,
    gate_h,
    up_h,
    down_h,
    rx_h,
    lkv_h,
    q_h,
    mixed_h,
    qb_h,
    out_h,
    seq_h,
    o_gate,
    o_up,
    o_down,
    o_out,
    o_qb,
    o_seq,
    o_gain,
    o_in,
    o_y,
    fcore_v,
    fy_v,
    proj_v,
    gmid_v,
    gnorm_v,
    lkv_v,
    q_v,
    mixed_v,
    gm_v,
    kv_acc,
    qb_v,
    out_v,
    seq_v,
    gall_v,
    gain_rx,
    gain_acc,
    first_b,
    later_b,
    own_b,
    acc_b,
    dss,
    drs,
    dls,
    credit,
    pls,
    fss,
    frs,
    gs,
    gr,
    ls,
    tls,
):
    ndp, own, dim, rank, hd, heads, pieces = cfg
    rows = NF * own
    t2 = own // 2
    kvw = rank + 2 * hd
    wide = dim // rank
    p = Place(ndp)
    sr = o_seq.shape[0]
    local = []

    def local_copy(src, dst):
        c = pltpu.make_async_copy(src, dst, ls.at[len(local)])
        c.start()
        local.append(c)
        return c

    ff = gg_h.shape[1]
    ffc = pl.ds(0, ff)
    gg_in = local_copy(gg_h, lkv_v.at[:, ffc])
    gu_in = local_copy(gu_h, seq_v.at[pl.ds(0, rows), ffc])
    mixed_in = local_copy(mixed_h, mixed_v)
    q_in = local_copy(q_h, q_v)
    qb_in = local_copy(qb_h, qb_v)
    hh = out_v.shape[1]

    def tile_load(t, which):
        src = gate_h if which == 0 else up_h
        s = lax.rem(t, 2) * 2 + which
        return pltpu.make_async_copy(
            src.at[pl.ds(al(t * 256, 256), 256)],
            seq_v.at[pl.ds(al(rows + s * 256, 256), 256), ffc],
            tls.at[s],
        )

    for which in (0, 1):
        tile_load(0, which).start()
    sc = DpScatter(p, sum(pieces) + pieces[0], first_b, later_b, own_b, acc_b, dss, drs, dls, credit, pls)
    p.barrier()
    cut = rx_h.shape[2]
    ready = sc.make(gw_gate, 0, o_gate, pieces[0], 0, cut, rx_h)
    fresh = sc.make(gw_up, 0, o_up, pieces[1])
    for a, b in zip(fresh, ready):
        sc.items += [a, b]
    sc.add(gw_gate, 0, o_gate, pieces[0], cut, o_gate.shape[1] - cut)
    sc.add(gw_down, 0, o_down, pieces[2])
    gg_in.wait()
    gu_in.wait()
    n_tiles = dim // 256
    per_half = hh // 256

    def norm_grad(t, _):
        for which in (0, 1):
            tile_load(t, which).wait()

        @pl.when(t + 1 < n_tiles)
        def _():
            for which in (0, 1):
                tile_load(t + 1, which).start()

        s = lax.rem(t, 2) * 2
        wg = seq_v[pl.ds(al(rows + s * 256, 256), 256), ffc]
        wu = seq_v[pl.ds(al(rows + s * 256 + 256, 256), 256), ffc]
        cols = pl.ds(al(lax.rem(t, per_half) * 256, 256), 256)
        for r in range(rows // 256):
            rr = pl.ds(r * 256, 256)
            to = pl.ds(al((t // per_half) * rows + r * 256, 256), 256)
            out_v[to, cols] = (
                mm_nt(lkv_v[rr, ffc], wg) + mm_nt(seq_v[rr, ffc], wu)
            ).astype(BF16)
        return 0

    halves = []
    for h in range(dim // hh):
        wide_cols = pl.ds(h * hh, hh)
        lax.fori_loop(h * per_half, (h + 1) * per_half, norm_grad, 0)
        red = FsReduce(
            p,
            lambda b, h=h: out_v.at[pl.ds(al(h * rows + b * own, own), own)],
            fcore_v.at[:, :, wide_cols],
            fy_v.at[:, wide_cols],
            fss.at[4 * h],
            frs.at[4 * h],
        )
        red.start()
        if h > 0:
            halves[-1].mid(own)
        sc.tick(2)
        halves.append(red)
    lkv_in = local_copy(lkv_h, lkv_v)
    seq_in = local_copy(seq_h, seq_v)
    halves[-1].mid(own)
    sc.tick(4)
    for red in halves:
        red.end()
        red.wait_sends()
    gain_two = jnp.concatenate([gains[wide + r : wide + r + 1] for r in range(wide)], axis=1)
    gain_one = jnp.concatenate([gains[r : r + 1] for r in range(wide)], axis=1)
    gain_lat = gains[2 * wide : 2 * wide + 1]
    part_two = jnp.zeros((1, dim), F32)
    for m in range(2):
        rr = pl.ds(m * t2, t2)
        e = jnp.concatenate([red.value(rr) for red in halves], axis=1)
        v = middle[rr, :]
        inv = lax.rsqrt(jnp.mean(v * v, axis=-1, keepdims=True) + EPSILON)
        part_two += jnp.sum(e * v * inv, axis=0, keepdims=True)
        scaled = e * gain_two
        inner = jnp.mean(scaled * v, axis=-1, keepdims=True)
        g = dout[m].astype(F32) + inv * scaled - v * (inv * inv * inv * inner)
        gmid_v[rr, :] = g
        proj_v[pl.ds(al(p.f * own + m * t2, t2), t2), :] = g.astype(BF16)
    out_in = local_copy(out_h, out_v)
    gain_acc[0] = jnp.zeros(gain_acc.shape[1:], F32)
    for r in range(wide):
        gain_acc[0, pl.ds(wide + r, 1), :] = part_two[:, r * rank : (r + 1) * rank]
    ag = FsGather(p, lambda b: proj_v.at[pl.ds(al(b * own, own), own)], fss.at[1], frs.at[1])
    ag.start()
    sc.tick(4)
    ag.mid()
    sc.tick(2)
    out_in.wait()
    ag.end()
    ag.wait_sends()

    def back_out(j, _):
        cols = pl.ds(al(j * 256, 256), 256)
        for r in range(rows // 512):
            rr = pl.ds(r * 512, 512)
            gm_v[rr, cols] = mm(proj_v[rr, :], out_v[:, cols]).astype(BF16)
        return 0

    lax.fori_loop(0, heads * hd // 256, back_out, 0)
    sc.tick(2)
    mixed_in.wait()

    def grad_out(j, _):
        cols = pl.ds(al(j * 256, 256), 256)
        out_v[cols, :] = mm_tn(proj_v[:, cols], mixed_v[...]).astype(BF16)
        return 0

    lax.fori_loop(0, dim // 256, grad_out, 0)
    sc.tick(2)
    sc.add(out_v, 0, o_out, pieces[3])
    q_in.wait()
    lkv_in.wait()
    scale = hd ** (-0.5)
    half = hd // 2
    kcols, vcols = slice(rank, rank + hd), slice(rank + hd, rank + 2 * hd)
    causal = causal_bias(PROMPT)
    everything = slice(None)

    for m in range(2):
        k0, k1 = (group_rows(lkv_v, m, h2, kcols, own) for h2 in (0, 1))
        v0, v1 = (group_rows(lkv_v, m, h2, vcols, own) for h2 in (0, 1))
        low = bias[m]
        kv_acc[...] = jnp.zeros(kv_acc.shape, F32)

        def put_query(h, which, g):
            co = group_rows(cos, m, which, everything, own)
            si = group_rows(sin, m, which, everything, own)
            a, b = g[:, :half] * scale, g[:, half:] * scale
            c0 = pl.ds(al(h * hd, half), half)
            c1 = pl.ds(al(h * hd + half, half), half)
            put_rows(gm_v, m, which, c0, own, (a * co + b * si).astype(BF16))
            put_rows(gm_v, m, which, c1, own, (b * co - a * si).astype(BF16))

        def attend_back(h, _):
            cols = pl.ds(al(h * hd, hd), hd)
            q0 = group_rows(q_v, m, 0, cols, own)
            g0 = group_rows(gm_v, m, 0, cols, own)
            pr = softmax_parts(mm_nt(q0, k0) * scale + causal)
            gp = mm_nt(g0, v0)
            gsc = (pr * (gp - jnp.sum(pr * gp, axis=-1, keepdims=True))).astype(BF16)
            kv_acc[2] += mm_tn(pr.astype(BF16), g0)
            kv_acc[0] += mm_tn(gsc, q0)
            put_query(h, 0, mm(gsc, k0))
            q1 = group_rows(q_v, m, 1, cols, own)
            g1 = group_rows(gm_v, m, 1, cols, own)
            s0 = mm_nt(q1, k0) * scale
            s1 = mm_nt(q1, k1) * scale + low
            top = jnp.maximum(
                jnp.max(s0, axis=-1, keepdims=True), jnp.max(s1, axis=-1, keepdims=True)
            )
            e0, e1 = jnp.exp(s0 - top), jnp.exp(s1 - top)
            total = jnp.sum(e0, axis=-1, keepdims=True) + jnp.sum(e1, axis=-1, keepdims=True)
            p0, p1 = e0 / total, e1 / total
            gp0, gp1 = mm_nt(g1, v0), mm_nt(g1, v1)
            inner = jnp.sum(p0 * gp0, axis=-1, keepdims=True) + jnp.sum(
                p1 * gp1, axis=-1, keepdims=True
            )
            gs0 = (p0 * (gp0 - inner)).astype(BF16)
            gs1 = (p1 * (gp1 - inner)).astype(BF16)
            kv_acc[2] += mm_tn(p0.astype(BF16), g1)
            kv_acc[3] += mm_tn(p1.astype(BF16), g1)
            kv_acc[0] += mm_tn(gs0, q1)
            kv_acc[1] += mm_tn(gs1, q1)
            put_query(h, 1, mm(gs0, k0) + mm(gs1, k1))
            return 0

        lax.fori_loop(0, heads, attend_back, 0)
        for h2 in (0, 1):
            put_rows(proj_v, m, h2, kcols, own, (kv_acc[h2] * scale).astype(BF16))
            put_rows(proj_v, m, h2, vcols, own, kv_acc[2 + h2].astype(BF16))
        sc.tick(3)
    qb_in.wait()

    def back_latent(j, _):
        wr = pl.ds(al(j * 256, 256), 256)
        for r in range(rows // 512):
            rr = pl.ds(r * 512, 512)
            proj_v[rr, wr] = mm_nt(gm_v[rr, :], qb_v[wr, :]).astype(BF16)
        return 0

    lax.fori_loop(0, rank // 256, back_latent, 0)

    def grad_qb(j, _):
        cols = pl.ds(al(j * 256, 256), 256)
        qb_v[cols, :] = mm_tn(lkv_v[:, cols], gm_v[...]).astype(BF16)
        return 0

    lax.fori_loop(0, rank // 256, grad_qb, 0)
    narrow = pl.ds(0, kvw)
    red2 = FsReduce(
        p,
        lambda b: proj_v.at[pl.ds(al(b * own, own), own), narrow],
        fcore_v.at[:, :, narrow],
        fy_v.at[:, narrow],
        fss.at[2],
        frs.at[2],
    )
    red2.start()
    sc.tick(2)
    sc.add(qb_v, 0, o_qb, pieces[4])
    red2.mid(own)
    sc.tick(5)
    red2.end()
    red2.wait_sends()
    own_rows = pl.ds(al(p.f * own, own), own)
    part_lat = jnp.zeros((1, rank), F32)
    for m in range(2):
        rr = pl.ds(m * t2, t2)
        gr_rows = pl.ds(al(p.f * own + m * t2, t2), t2)
        e = red2.value(rr)
        v = latent[rr, :]
        inv = lax.rsqrt(jnp.mean(v * v, axis=-1, keepdims=True) + EPSILON)
        el = e[:, :rank]
        part_lat += jnp.sum(el * v * inv, axis=0, keepdims=True)
        scaled = el * gain_lat
        inner = jnp.mean(scaled * v, axis=-1, keepdims=True)
        gall_v[rr, :rank] = (inv * scaled - v * (inv * inv * inv * inner)).astype(BF16)
        co, si = cos[gr_rows, :], sin[gr_rows, :]
        a, b = e[:, rank : rank + half], e[:, rank + half : rank + hd]
        gall_v[rr, rank : rank + half] = (a * co + b * si).astype(BF16)
        gall_v[rr, rank + half : rank + hd] = (b * co - a * si).astype(BF16)
        gall_v[rr, rank + hd :] = e[:, rank + hd :].astype(BF16)
    gain_acc[0, pl.ds(2 * wide, 1), :] = part_lat
    seq_in.wait()

    def back_seq(j, _):
        wr = pl.ds(al(j * 256, 256), 256)
        gnorm_v[:, wr] = mm_nt(gall_v[...], seq_v[wr, :])
        return 0

    lax.fori_loop(0, dim // 256, back_seq, 0)
    sc.tick(2)
    span = NF * sr

    def grad_seq(j, _):
        cols = pl.ds(al(j * 256, 256), 256)
        g = mm_tn(normed[:, cols], gall_v[...]).astype(BF16)
        for i in range(256 // span):
            for fb in range(NF):
                seq_v[pl.ds(al(fb * ndp * sr + (j * (256 // span) + i) * sr, sr), sr), :] = g[
                    i * span + fb * sr : i * span + (fb + 1) * sr
                ]
        return 0

    lax.fori_loop(0, dim // 256, grad_seq, 0)
    srows = ndp * sr
    core3 = [lkv_v.at[pl.ds(0, srows)], lkv_v.at[pl.ds(srows, srows)]]

    def sblock(b):
        return seq_v.at[pl.ds(al(b * srows, srows), srows)]

    c1 = rcopy(sblock(p.f_yc), core3[1], fss.at[3, 1], frs.at[3, 1], p.to_core)
    c0 = rcopy(sblock(p.f_core), core3[0], fss.at[3, 0], frs.at[3, 0], p.to_core)
    mw = mixed_v.shape[1]
    cys = [
        rcopy(
            lkv_v.at[pl.ds(srows, srows), pl.ds(0, mw)],
            mixed_v.at[pl.ds(0, srows)],
            fss.at[3, 2],
            frs.at[3, 2],
            p.to_y,
        ),
        rcopy(
            lkv_v.at[pl.ds(srows, srows), pl.ds(mw, kvw - mw)],
            mixed_v.at[pl.ds(srows, srows), pl.ds(0, kvw - mw)],
            fss.at[3, 3],
            frs.at[3, 3],
            p.to_y,
        ),
    ]
    c1.start()
    c0.start()
    part_one = jnp.zeros((1, dim), F32)
    for m in range(2):
        rr = pl.ds(m * t2, t2)
        e = gnorm_v[rr, :]
        v = tok[m].astype(F32)
        inv = lax.rsqrt(jnp.mean(v * v, axis=-1, keepdims=True) + EPSILON)
        part_one += jnp.sum(e * v * inv, axis=0, keepdims=True)
        scaled = e * gain_one
        inner = jnp.mean(scaled * v, axis=-1, keepdims=True)
        o_in[m] = (gmid_v[rr, :] + inv * scaled - v * (inv * inv * inv * inner)).astype(BF16)
    for r in range(wide):
        gain_acc[0, pl.ds(r, 1), :] = part_one[:, r * rank : (r + 1) * rank]
    gain_steps = [
        rcopy(gain_acc.at[0], gain_rx.at[0], gs.at[0], gr.at[0], p.to_core),
        rcopy(gain_acc.at[1], gain_rx.at[1], gs.at[1], gr.at[1], p.to_y),
    ] + [
        rcopy(gain_acc.at[2 + b], gain_rx.at[2 + b], gs.at[2 + b], gr.at[2 + b], p.to_dp(bit))
        for b, bit in enumerate(p.bits)
    ]
    gain_steps[0].start()
    c1.wait_recv()

    def seq_y(t, _):
        t = al(t * 64, 64)
        a = pl.ds(srows + t, 64)
        b = pl.ds(al(p.f_y * srows + t, 64), 64)
        lkv_v[a, :] = lkv_v[a, :] + seq_v[b, :]
        return 0

    lax.fori_loop(0, srows // 64, seq_y, 0)
    for c in cys:
        c.start()
    for n in range(len(gain_steps)):
        gain_steps[n].wait_recv()
        gain_acc[n + 1] = gain_acc[n] + gain_rx[n]
        if n + 1 < len(gain_steps):
            gain_steps[n + 1].start()
        sc.tick(1)
    c0.wait_recv()
    for c in cys:
        c.wait_recv()

    def seq_f(t, _):
        t = al(t * 64, 64)
        a = pl.ds(t, 64)
        b = pl.ds(al(p.f * srows + t, 64), 64)
        a2 = pl.ds(srows + t, 64)
        seq_v[b, :mw] = (
            lkv_v[a, :mw].astype(F32) + seq_v[b, :mw].astype(F32) + mixed_v[a, :].astype(F32)
        ).astype(BF16)
        seq_v[b, mw:] = (
            lkv_v[a, mw:].astype(F32)
            + seq_v[b, mw:].astype(F32)
            + mixed_v[a2, : kvw - mw].astype(F32)
        ).astype(BF16)
        return 0

    lax.fori_loop(0, srows // 64, seq_f, 0)
    sc.add(seq_v, p.f * srows, o_seq, pieces[5])
    o_gain[...] = gain_acc[len(gain_steps)]
    for t in [c1, c0] + cys:
        t.wait_send()
    hid_in = local_copy(hid_h, lkv_v.at[:, ffc])

    def down_load(t):
        s = lax.rem(t, 2)
        return pltpu.make_async_copy(
            down_h.at[pl.ds(al(t * 256, 256), 256)],
            seq_v.at[pl.ds(al(p.f_core * srows + s * 256, 256), 256), ffc],
            tls.at[s],
        )

    down_load(0).start()
    sc.tick(2)
    hid_in.wait()

    def ffn_out(t, _):
        down_load(t).wait()

        @pl.when(t + 1 < n_tiles)
        def _():
            down_load(t + 1).start()

        w = seq_v[pl.ds(al(p.f_core * srows + lax.rem(t, 2) * 256, 256), 256), ffc]
        cols = pl.ds(al(t * 256, 256), 256)
        for r in range(rows // 256):
            rr = pl.ds(r * 256, 256)
            proj_v[rr, cols] = mm_nt(lkv_v[rr, ffc], w).astype(BF16)
        return 0

    lax.fori_loop(0, n_tiles, ffn_out, 0)
    red3 = FsReduce(
        p,
        lambda b: proj_v.at[pl.ds(al(b * own, own), own)],
        fcore_v,
        fy_v,
        fss.at[5],
        frs.at[5],
    )
    red3.start()
    sc.tick(2)
    red3.mid(own)
    sc.tick(5)
    red3.end()
    for m in range(2):
        rr = pl.ds(m * t2, t2)
        o_y[m] = (middle[rr, :] + red3.value(rr)).astype(BF16)
    sc.drain()
    red3.wait_sends()
    for t in gain_steps:
        t.wait_send()


def backward_call(ndp, tok, dout, middle, latent, normed, gains, cos, sin, bias, grads, ffn, saved):
    lkv, q, mixed, qb, out, seq = saved
    nz = ndp // 2
    own, dim = middle.shape
    rank = latent.shape[1]
    kvw = lkv.shape[1]
    hd = (kvw - rank) // 2
    heads = q.shape[1] // hd
    rows = NF * own
    sr = seq.shape[0] // (ndp * NF)
    shards = [(w.shape[0] // ndp, w.shape[1]) for w in grads] + [
        (out.shape[0] // ndp, out.shape[1]),
        (qb.shape[0] // ndp, qb.shape[1]),
        (sr, kvw),
    ]
    pieces = tuple(s[0] // piece_rows(s[0], nz) for s in shards)
    n = sum(pieces)
    slots, _, own_slots = scatter_ring(nz)
    nb = ndp.bit_length() - 1
    pr = max(piece_rows(s[0], nz) for s in shards)
    width = max(s[1] for s in shards)
    dma = pltpu.SemaphoreType.DMA
    scratch = [
        pltpu.VMEM((2, own, dim), BF16),
        pltpu.VMEM((own, dim), BF16),
        pltpu.VMEM((rows, dim), BF16),
        pltpu.VMEM((own, dim), F32),
        pltpu.VMEM((own, dim), F32),
        pltpu.VMEM(lkv.shape, BF16),
        pltpu.VMEM(q.shape, BF16),
        pltpu.VMEM(mixed.shape, BF16),
        pltpu.VMEM(q.shape, BF16),
        pltpu.VMEM((4, rows // 4, hd), F32),
        pltpu.VMEM(qb.shape, BF16),
        pltpu.VMEM(out.shape, BF16),
        pltpu.VMEM(seq.shape, BF16),
        pltpu.VMEM((own, kvw), BF16),
        pltpu.VMEM((2 + nb,) + gains.shape, F32),
        pltpu.VMEM((3 + nb,) + gains.shape, F32),
        pltpu.VMEM((slots, nz, pr, width), BF16),
        pltpu.VMEM((slots, nz - 1, pr, width), BF16),
        pltpu.VMEM((own_slots, nz, pr, width), BF16),
        pltpu.VMEM((slots, pr, width), F32),
        dma((slots, nz + nb - 1)),
        dma((slots, nz + nb - 1)),
        dma((slots, nz + 1)),
        pltpu.SemaphoreType.REGULAR((nb, nb)),
        dma((slots, nz)),
        dma((6, 4)),
        dma((6, 4)),
        dma((2 + nb,)),
        dma((2 + nb,)),
        dma((9,)),
        dma((4,)),
    ]
    return pl.pallas_call(
        functools.partial(backward_kernel, (ndp, own, dim, rank, hd, heads, pieces)),
        out_shape=tuple(jax.ShapeDtypeStruct(s, F32) for s in shards)
        + (
            jax.ShapeDtypeStruct(gains.shape, F32),
            jax.ShapeDtypeStruct(tok.shape, BF16),
            jax.ShapeDtypeStruct(tok.shape, BF16),
        ),
        in_specs=(VMEM,) * 9 + (ANY,) * 16,
        out_specs=(ANY,) * 6 + (VMEM,) * 3,
        scratch_shapes=scratch,
        compiler_params=pltpu.CompilerParams(
            collective_id=1, has_side_effects=True, vmem_limit_bytes=62 * 2**20
        ),
        name="backward_scatter",
    )(tok, dout, middle, latent, normed, gains, cos, sin, bias, *grads, *ffn, lkv, q, mixed, qb, out, seq)


def per_device(
    ndp,
    tokens,
    membership,
    d_output,
    gain_attn,
    w_qa,
    gain_latent,
    w_qb,
    w_key,
    w_value,
    w_out,
    gain_ffn,
    w_gate,
    w_up,
    w_down,
):
    micro, tlen, dim = tokens.shape
    own = micro * tlen
    rank = w_qa.shape[1]
    hd = w_key.shape[1]
    heads = w_qb.shape[1] // hd
    rows = NF * own
    wide = dim // rank
    labels, positions = jax.vmap(lambda r: layout(r, BLK))(membership[0])
    pos_rows = positions.reshape(micro, NF, tlen).transpose(1, 0, 2).reshape(rows)
    cos, sin = rope_tables(pos_rows, hd)
    tail = labels[:, PROMPT:]
    idx = jnp.arange(tail.shape[1], dtype=jnp.int32)
    seen = (idx[None, None, :] <= idx[None, :, None]) & (tail[:, None, :] == tail[:, :, None])
    bias = jnp.where(seen, 0.0, MASK_FILL).astype(F32)
    block = lax.axis_index("dp") * NF + lax.axis_index("fsdp")

    def spot(gain):
        width = gain.shape[0]
        count = ndp * NF
        at = lax.broadcasted_iota(jnp.int32, (count, width), 0) == block
        placed = jnp.where(at, gain.astype(F32)[None, :], 0.0)
        return placed.reshape(count * width // rank, rank)

    gain_sh = jnp.concatenate([spot(gain_attn), spot(gain_ffn), spot(gain_latent)], axis=0)
    gain_sh = jnp.pad(gain_sh, ((0, 8 - gain_sh.shape[0]), (0, 0)))
    seq_sh = jnp.concatenate([w_qa, w_key, w_value], axis=1)
    (
        qb_all,
        out_all,
        gate_all,
        up_all,
        down_all,
        seq_all,
        gains,
        lkv,
        q_all,
        mixed,
        latent,
        normed,
        middle,
        hidden,
        grad_gate,
        grad_up,
        gw_gate,
        gw_up,
        gw_down,
        early_gate,
    ) = forward_call(
        ndp, tokens, d_output, cos, sin, bias, seq_sh, gain_sh, w_qb, w_out, w_gate, w_up, w_down
    )
    o_gate, o_up, o_down, o_out, o_qb, o_seq, o_gain, input_grad, output = backward_call(
        ndp,
        tokens,
        d_output,
        middle,
        latent,
        normed,
        gains,
        cos,
        sin,
        bias,
        (gw_gate, gw_up, gw_down),
        (hidden, grad_gate, grad_up, gate_all, up_all, down_all, early_gate),
        (lkv, q_all, mixed, qb_all, out_all, seq_all),
    )

    def own_gain(flat, width):
        return lax.dynamic_slice_in_dim(flat.reshape(-1), block * width, width, 0)

    return (
        output,
        input_grad,
        own_gain(o_gain[:wide], gain_attn.shape[0]),
        o_seq[:, :rank],
        own_gain(o_gain[2 * wide], gain_latent.shape[0]),
        o_qb,
        o_seq[:, rank : rank + hd],
        o_seq[:, rank + hd :],
        o_out,
        own_gain(o_gain[wide : 2 * wide], gain_ffn.shape[0]),
        o_gate,
        o_up,
        o_down,
    )


def solution(mesh):
    both = ("dp", "fsdp")
    rowwise, vector = P(both, None), P(both)
    tok = P(None, both, None)
    head = P("dp", "fsdp")
    return jax.shard_map(
        functools.partial(per_device, mesh.shape["dp"]),
        mesh=mesh,
        in_specs=(
            tok,
            P("dp", None, None),
            tok,
            vector,
            rowwise,
            vector,
            head,
            rowwise,
            rowwise,
            head,
            vector,
            head,
            head,
            head,
        ),
        out_specs=(
            tok,
            tok,
            vector,
            rowwise,
            vector,
            head,
            rowwise,
            rowwise,
            head,
            vector,
            head,
            head,
            head,
        ),
        check_vma=False,
    )
```

```python
import functools

import jax
import jax.numpy as jnp
from jax import lax
from jax.experimental import pallas as pl
from jax.experimental.pallas import tpu as pltpu
from jax.sharding import PartitionSpec as P

BLK = 32
PROMPT = 256
EPSILON = 1e-05
ROPE_BASE = 10000.0
MASK_FILL = -1e30
F32 = jnp.float32
BF16 = jnp.bfloat16
MESH = pl.DeviceIdType.MESH
ANY = pl.BlockSpec(memory_space=pl.ANY)
VMEM = pl.BlockSpec(memory_space=pltpu.VMEM)
NF = 4
GATHER_ROWS = 64
GATHER_AHEAD = 5
GATHER_FIRST = 4
FFN_ROWS = 128
FFN_COLS = 512


def ffn_chunks(cols):
    return [(c, min(FFN_COLS, cols - c)) for c in range(0, cols, FFN_COLS)]


def layout(member_row, block_len):
    count_blocks = member_row.shape[0]
    block_ids = jnp.arange(count_blocks, dtype=jnp.int32)
    same_run = (member_row[None, :] == member_row[:, None]) & (
        block_ids[None, :] < block_ids[:, None]
    )
    earlier = jnp.sum(same_run.astype(jnp.int32), axis=1)
    prompt_len = jnp.sum((member_row == 0).astype(jnp.int32)) * block_len
    labels = jnp.repeat(member_row, block_len)
    within = jnp.arange(count_blocks * block_len, dtype=jnp.int32) % block_len
    positions = (
        (labels > 0).astype(jnp.int32) * prompt_len
        + jnp.repeat(earlier, block_len) * block_len
        + within
    )
    return (labels, positions)


def rope_tables(positions, head_width):
    half_width = head_width // 2
    frequency = ROPE_BASE ** (-(jnp.arange(half_width, dtype=jnp.float32) * (2.0 / head_width)))
    angles = positions.astype(jnp.float32)[:, None] * frequency[None, :]
    return (jnp.cos(angles), jnp.sin(angles))


def al(x, n):
    return pl.multiple_of(x, n)


def mm(a, b):
    return lax.dot_general(a, b, (((1,), (0,)), ((), ())), preferred_element_type=F32)


def mm_nt(a, b):
    return lax.dot_general(a, b, (((1,), (1,)), ((), ())), preferred_element_type=F32)


def mm_tn(a, b):
    return lax.dot_general(a, b, (((0,), (0,)), ((), ())), preferred_element_type=F32)


class Place:
    def __init__(self, ndp):
        self.ndp = ndp
        self.bits = [1 << b for b in range(ndp.bit_length() - 1)]
        self.me = lax.axis_index("dp")
        self.f = lax.axis_index("fsdp")
        y, c = self.f // 2, self.f % 2
        self.f_core = y * 2 + 1 - c
        self.f_y = (1 - y) * 2 + c
        self.f_yc = (1 - y) * 2 + 1 - c
        self.to_core = (self.me, self.f_core)
        self.to_y = (self.me, self.f_y)

    def at(self, mask):
        j = self.me
        for b in self.bits:
            if mask & b:
                j = j + b - 2 * b * ((self.me // b) % 2)
        return j

    def to_dp(self, mask):
        return (self.at(mask), self.f)

    def orders(self, swapped):
        o = list(self.bits)
        if swapped and len(o) > 1:
            o[0], o[1] = o[1], o[0]
        return o

    def barrier(self):
        bar = pltpu.get_barrier_semaphore()
        devs = [self.to_dp(b) for b in self.bits] + [self.to_core, self.to_y]
        for d in devs:
            pl.semaphore_signal(bar, inc=1, device_id=d, device_id_type=MESH)
        pl.semaphore_wait(bar, len(devs))


def rcopy(src, dst, ss, rs, dev):
    return pltpu.make_async_remote_copy(
        src_ref=src, dst_ref=dst, send_sem=ss, recv_sem=rs, device_id=dev, device_id_type=MESH
    )


class DpGather:
    def __init__(self, pos, ss, rs):
        self.p, self.ss, self.rs = pos, ss, rs
        self.items, self.events = [], []
        self.launched = self.seen = self.first = 0

    def add(self, src, dst, swapped=False):
        self.items.append((src, dst, self.p.orders(swapped)[::-1]))
        return len(self.items) - 1

    def copy(self, n, mask, stage):
        src, dst, order = self.items[n]
        j = self.p.at(mask)
        k = self.index(n, mask | order[stage])
        return rcopy(
            src if mask == 0 else dst(j),
            dst(j),
            self.ss.at[n, k],
            self.rs.at[n, k],
            self.p.to_dp(order[stage]),
        )

    def index(self, n, mask):
        return mask - 1

    def stage_of(self, n, mask):
        return max(i for i, b in enumerate(self.items[n][2]) if mask & b)

    def arrived(self, n, mask):
        src, dst, order = self.items[n]
        stage = self.stage_of(n, mask)
        j = self.p.at(mask)
        k = self.index(n, mask)
        rcopy(src, dst(j), self.ss.at[n, k], self.rs.at[n, k], self.p.to_dp(order[stage])).wait_recv()

    def launch(self):
        if self.launched < len(self.items):
            n = self.launched
            for stage in range(len(self.p.bits)):
                self.copy(n, 0, stage).start()
            self.launched += 1

    def masks(self, n):
        order = self.items[n][2]
        last = order[-1]
        out = [m for m in range(1, self.p.ndp) if not m & last]
        return sorted(out, key=lambda m: (self.stage_of(n, m), m))

    def forward(self, n, stage):
        for m in self.masks(n):
            if self.stage_of(n, m) == stage:
                self.arrived(n, m)
                for later in range(stage + 1, len(self.p.bits)):
                    self.copy(n, m, later).start()

    def steps(self, count, ahead):
        lag = len(self.p.bits) - 1
        for _ in range(count):
            if self.seen >= len(self.items) + lag - 1:
                return
            while self.launched < min(len(self.items), self.seen + ahead):
                self.launch()
            for stage in range(lag):
                n = self.seen - stage
                if self.first <= n < len(self.items):
                    self.forward(n, stage)
            self.seen += 1

    def need(self, n, ahead):
        self.steps(n + len(self.p.bits) - 1 - self.seen, ahead)

    def wait_last(self, n):
        last = self.items[n][2][-1]
        for m in range(self.p.ndp):
            if m & last:
                self.arrived(n, m)

    def wait_sends(self, n):
        for m in range(self.p.ndp):
            first = 0 if m == 0 else self.stage_of(n, m) + 1
            for stage in range(first, len(self.p.bits)):
                self.copy(n, m, stage).wait_send()


class FsGather:
    def __init__(self, pos, blocks, ss, rs):
        self.p, self.b, self.ss, self.rs = pos, blocks, ss, rs

    def copy(self, n, fb, dev):
        return rcopy(self.b(fb), self.b(fb), self.ss.at[n], self.rs.at[n], dev)

    def start(self):
        self.copy(1, self.p.f, self.p.to_y).start()
        self.copy(0, self.p.f, self.p.to_core).start()

    def mid(self):
        self.copy(1, self.p.f_y, self.p.to_y).wait_recv()
        self.copy(2, self.p.f_y, self.p.to_core).start()

    def end(self):
        self.copy(0, self.p.f_core, self.p.to_core).wait_recv()
        self.copy(2, self.p.f_yc, self.p.to_core).wait_recv()

    def wait_sends(self):
        self.copy(1, self.p.f, self.p.to_y).wait_send()
        self.copy(0, self.p.f, self.p.to_core).wait_send()
        self.copy(2, self.p.f_y, self.p.to_core).wait_send()


class FsReduce:
    def __init__(self, pos, blocks, from_core, from_y, ss, rs):
        self.p, self.b, self.fc, self.fy, self.ss, self.rs = pos, blocks, from_core, from_y, ss, rs

    def c1(self):
        return rcopy(
            self.b(self.p.f_yc), self.fc.at[1], self.ss.at[1], self.rs.at[1], self.p.to_core
        )

    def c0(self):
        return rcopy(
            self.b(self.p.f_core), self.fc.at[0], self.ss.at[0], self.rs.at[0], self.p.to_core
        )

    def cy(self):
        return rcopy(self.fc.at[1], self.fy, self.ss.at[2], self.rs.at[2], self.p.to_y)

    def start(self):
        self.c1().start()
        self.c0().start()

    def mid(self, rows, tile=64):
        self.c1().wait_recv()
        mine = self.b(self.p.f_y)

        def add(t, _):
            r = pl.ds(al(t * tile, tile), tile)
            self.fc[1, r, :] = (self.fc[1, r, :].astype(F32) + mine[r, :].astype(F32)).astype(BF16)
            return 0

        lax.fori_loop(0, rows // tile, add, 0)
        self.cy().start()

    def end(self):
        self.c0().wait_recv()
        self.cy().wait_recv()

    def value(self, r):
        return (
            self.b(self.p.f)[r, :].astype(F32)
            + self.fc[0, r, :].astype(F32)
            + self.fy[r, :].astype(F32)
        )

    def wait_sends(self):
        self.c1().wait_send()
        self.c0().wait_send()
        self.cy().wait_send()


def softmax_parts(scores):
    top = jnp.max(scores, axis=-1, keepdims=True)
    lifted = jnp.exp(scores - top)
    return lifted / jnp.sum(lifted, axis=-1, keepdims=True)


def causal_bias(rows):
    r = lax.broadcasted_iota(jnp.int32, (rows, rows), 0)
    c = lax.broadcasted_iota(jnp.int32, (rows, rows), 1)
    return jnp.where(c <= r, 0.0, MASK_FILL).astype(F32)


def group_rows(ref, m, half, cols, own):
    t = own // 2
    first = ref[pl.ds((2 * half) * own + m * t, t), cols]
    second = ref[pl.ds((2 * half + 1) * own + m * t, t), cols]
    return jnp.concatenate([first, second], axis=0)


def put_rows(ref, m, half, cols, own, value):
    t = own // 2
    ref[pl.ds((2 * half) * own + m * t, t), cols] = value[:t]
    ref[pl.ds((2 * half + 1) * own + m * t, t), cols] = value[t:]


def forward_kernel(
    cfg,
    tok,
    dout,
    cos,
    sin,
    bias,
    seq_sh,
    gain_sh,
    qb_sh,
    out_sh,
    gate_sh,
    up_sh,
    down_sh,
    qb_all,
    out_all,
    gate_all,
    up_all,
    down_all,
    seq_all,
    gain_sum,
    lkv_o,
    q_o,
    mixed_o,
    latent_o,
    normed_o,
    middle_o,
    hid_o,
    gg_o,
    gu_o,
    gw_gate,
    gw_up,
    gw_down,
    rx_o,
    seq_v,
    gain_v,
    qb_v,
    out_v,
    lkv_v,
    q_v,
    mixed_v,
    part_v,
    fcore_v,
    fy_v,
    n2_v,
    d_v,
    n2_t,
    d_t,
    lat_v,
    gss,
    grs,
    fss,
    frs,
    sys_,
    syr,
    ls,
    ffn_ls,
    pss,
    prs,
):
    ndp, own, dim, rank, hd, heads = cfg
    rows = NF * own
    p = Place(ndp)
    kvw = rank + 2 * hd
    sr = seq_sh.shape[0]
    g = DpGather(p, gss, grs)
    i_seq = g.add(seq_sh, lambda j: seq_v.at[pl.ds(al((j * NF + p.f) * sr, sr), sr)])
    i_gain = g.add(gain_sh, lambda j: gain_v.at[j * NF + p.f])
    turn = [0]

    def weight_items(src, dst, cols=slice(None), most=GATHER_ROWS):
        n = src.shape[0]
        step = min(n, most)
        out = []
        for c in range(n // step):
            turn[0] += 1
            out.append(
                g.add(
                    src.at[pl.ds(c * step, step), cols],
                    lambda j, c=c: dst.at[pl.ds(al(j * n + c * step, step), step), cols],
                    turn[0] % 8 == 0,
                )
            )
        return out

    i_qb = weight_items(qb_sh, qb_v)
    i_out = weight_items(out_sh, out_v)
    i_ffn = []
    for c0, cw in ffn_chunks(gate_sh.shape[1]):
        cols = pl.ds(c0, cw)
        some = []
        for s, d in ((gate_sh, gate_all), (up_sh, up_all), (down_sh, down_all)):
            some += weight_items(s, d, cols, FFN_ROWS)
        i_ffn.append(some)
    order = range(len(g.items))
    fs_d = FsGather(p, lambda b: d_v.at[pl.ds(al(b * own, own), own)], fss.at[0], frs.at[0])
    fs_l = FsGather(p, lambda b: lkv_v.at[pl.ds(al(b * own, own), own)], fss.at[1], frs.at[1])
    fs_n = FsGather(p, lambda b: n2_v.at[pl.ds(al(b * own, own), own)], fss.at[2], frs.at[2])
    red = FsReduce(
        p, lambda b: part_v.at[pl.ds(al(b * own, own), own)], fcore_v, fy_v, fss.at[3], frs.at[3]
    )

    local = []

    def local_copy(src, dst):
        c = pltpu.make_async_copy(src, dst, ls.at[len(local)])
        c.start()
        local.append(c)
        return c

    own_copies = {}
    for i in order:
        src, dst, _ = g.items[i]
        own_copies[i] = local_copy(src, dst(p.me))
    d_copies = [
        local_copy(dout.at[m], d_v.at[pl.ds(al(p.f * own + m * (own // 2), 128), own // 2)])
        for m in range(2)
    ]

    p.barrier()
    for _ in range(GATHER_FIRST):
        g.launch()
    npiece = ndp

    def seq_piece(j, fb):
        return seq_v.at[pl.ds(al((j * NF + fb) * sr, sr), sr)]

    def seq_copy(t, j, fb, dev, which):
        b = seq_piece(j, fb) if which == 0 else gain_v.at[j * NF + fb]
        return rcopy(b, b, sys_.at[which, t, j], syr.at[which, t, j], dev)

    def spread(j):
        for which in (0, 1):
            seq_copy(1, j, p.f, p.to_y, which).start()
            seq_copy(0, j, p.f, p.to_core, which).start()

    for m in range(2):
        x = tok[m].astype(F32)
        inv = lax.rsqrt(jnp.mean(x * x, axis=-1, keepdims=True) + EPSILON)
        middle_o[pl.ds(m * (own // 2), own // 2), :] = x * inv
    own_copies[i_seq].wait()
    own_copies[i_gain].wait()
    spread(p.me)
    for m in sorted(range(1, ndp), key=lambda m: g.stage_of(i_seq, m)):
        for i in (i_seq, i_gain):
            g.arrived(i, m)
            for stage in range(g.stage_of(i, m) + 1, len(p.bits)):
                g.copy(i, m, stage).start()
        spread(p.at(m))
    g.seen = g.first = 2
    for c in d_copies:
        c.wait()

    def spread_forward(j, _):
        for which in (0, 1):
            seq_copy(1, j, p.f_y, p.to_y, which).wait_recv()
            seq_copy(2, j, p.f_y, p.to_core, which).start()
        return 0

    def tick(n):
        g.steps(n, GATHER_AHEAD)

    tick(1)
    lax.fori_loop(0, npiece, spread_forward, 0)
    fs_d.start()
    tick(1)

    def spread_end(j, _):
        for which in (0, 1):
            seq_copy(0, j, p.f_core, p.to_core, which).wait_recv()
            seq_copy(2, j, p.f_yc, p.to_core, which).wait_recv()
        return 0

    lax.fori_loop(0, npiece, spread_end, 0)

    def gain_add(j, acc):
        return acc + gain_v[j]

    gains = lax.fori_loop(0, ndp * NF, gain_add, jnp.zeros(gain_v.shape[1:], F32))
    gain_sum[...] = gains
    wide = dim // rank
    gain_one = jnp.concatenate([gains[r : r + 1] for r in range(wide)], axis=1)
    gain_two = jnp.concatenate([gains[wide + r : wide + r + 1] for r in range(wide)], axis=1)
    gain_lat = gains[2 * wide : 2 * wide + 1]
    normed_o[...] = (middle_o[...] * gain_one).astype(BF16)
    seq_out = local_copy(seq_v, seq_all)

    def project(j, _):
        cols = pl.ds(al(j * 256, 256), 256)
        lat_v[:, cols] = mm(normed_o[...], seq_v[:, cols])
        return 0

    lax.fori_loop(0, kvw // 256, project, 0)
    own_rows = pl.ds(al(p.f * own, own), own)
    lat = lat_v[:, :rank]
    latent_o[...] = lat
    inv_lat = lax.rsqrt(jnp.mean(lat * lat, axis=-1, keepdims=True) + EPSILON)
    lkv_v[own_rows, :rank] = (lat * inv_lat * gain_lat).astype(BF16)
    half = hd // 2
    co, si = cos[own_rows, :], sin[own_rows, :]
    ka, kb = lat_v[:, rank : rank + half], lat_v[:, rank + half : rank + hd]
    lkv_v[own_rows, rank : rank + half] = (ka * co - kb * si).astype(BF16)
    lkv_v[own_rows, rank + half : rank + hd] = (kb * co + ka * si).astype(BF16)
    lkv_v[own_rows, rank + hd :] = lat_v[:, rank + hd :].astype(BF16)
    fs_l.start()
    tick(1)
    fs_d.mid()
    fs_l.mid()
    tick(1)
    for i in i_qb:
        g.need(i, GATHER_AHEAD)
        own_copies[i].wait()
        g.wait_last(i)
    fs_l.end()
    qb_out = local_copy(qb_v, qb_all)
    lkv_out = local_copy(lkv_v, lkv_o)

    def query(j, _):
        cols = pl.ds(al(j * hd, hd), hd)
        c0 = pl.ds(al(j * hd, half), half)
        c1 = pl.ds(al(j * hd + half, half), half)
        for r in range(rows // 512):
            rr = pl.ds(r * 512, 512)
            acc = mm(lkv_v[rr, :rank], qb_v[:, cols])
            a, b = acc[:, :half], acc[:, half:]
            c, s = cos[rr, :], sin[rr, :]
            q_v[rr, c0] = (a * c - b * s).astype(BF16)
            q_v[rr, c1] = (b * c + a * s).astype(BF16)
        return 0

    lax.fori_loop(0, heads, query, 0)
    q_out = local_copy(q_v, q_o)
    tick(1)
    scale = hd ** (-0.5)
    kcols, vcols = slice(rank, rank + hd), slice(rank + hd, rank + 2 * hd)
    causal = causal_bias(PROMPT)
    for m in range(2):
        k0, k1 = (group_rows(lkv_v, m, h2, kcols, own) for h2 in (0, 1))
        v0, v1 = (group_rows(lkv_v, m, h2, vcols, own) for h2 in (0, 1))
        low = bias[m]

        def attend(h, _):
            cols = pl.ds(al(h * hd, hd), hd)
            q0 = group_rows(q_v, m, 0, cols, own)
            pr = softmax_parts(mm_nt(q0, k0) * scale + causal).astype(BF16)
            put_rows(mixed_v, m, 0, cols, own, mm(pr, v0).astype(BF16))
            q1 = group_rows(q_v, m, 1, cols, own)
            s0 = mm_nt(q1, k0) * scale
            s1 = mm_nt(q1, k1) * scale + low
            top = jnp.maximum(
                jnp.max(s0, axis=-1, keepdims=True), jnp.max(s1, axis=-1, keepdims=True)
            )
            e0, e1 = jnp.exp(s0 - top), jnp.exp(s1 - top)
            total = jnp.sum(e0, axis=-1, keepdims=True) + jnp.sum(e1, axis=-1, keepdims=True)
            mix = mm((e0 / total).astype(BF16), v0) + mm((e1 / total).astype(BF16), v1)
            put_rows(mixed_v, m, 1, cols, own, mix.astype(BF16))
            return 0

        lax.fori_loop(0, heads, attend, 0)
        tick(2)
    fs_d.end()
    mixed_out = local_copy(mixed_v, mixed_o)
    tick(1)
    for i in i_out:
        g.need(i, GATHER_AHEAD)
        own_copies[i].wait()
        g.wait_last(i)
    out_out = local_copy(out_v, out_all)

    def project_out(fb):
        rr = pl.ds(al(fb * own, own), own)

        def one(j, _):
            wr = pl.ds(al(j * 256, 256), 256)
            part_v[rr, wr] = mm_nt(mixed_v[rr, :], out_v[wr, :]).astype(BF16)
            return 0

        lax.fori_loop(0, dim // 256, one, 0)

    project_out(p.f_yc)
    project_out(p.f_core)
    red.start()
    tick(1)
    project_out(p.f_y)
    red.mid(own)
    project_out(p.f)
    tick(2)
    red.end()
    for m in range(2):
        rr = pl.ds(m * (own // 2), own // 2)
        mid = tok[m].astype(F32) + red.value(rr)
        middle_o[rr, :] = mid
        inv = lax.rsqrt(jnp.mean(mid * mid, axis=-1, keepdims=True) + EPSILON)
        n2_v[pl.ds(al(p.f * own + m * (own // 2), 128), own // 2), :] = (
            mid * inv * gain_two
        ).astype(BF16)
    fs_n.start()
    tick(1)

    def turn_d(j, _):
        cols = pl.ds(al(j * 256, 256), 256)
        d_t[cols, :] = d_v[:, cols].T
        return 0

    lax.fori_loop(0, dim // 256, turn_d, 0)
    tick(1)
    fs_n.mid()
    tick(1)
    fs_n.end()

    def turn_n2(j, _):
        cols = pl.ds(al(j * 256, 256), 256)
        n2_t[cols, :] = n2_v[:, cols].T
        return 0

    lax.fori_loop(0, dim // 256, turn_n2, 0)
    for c in (q_out, mixed_out, out_out, seq_out):
        c.wait()
    early = [i_seq, i_gain] + i_qb + i_out
    for i in early:
        g.wait_sends(i)

    def spread_sends(j, _):
        for which in (0, 1):
            seq_copy(0, j, p.f, p.to_core, which).wait_send()
            seq_copy(1, j, p.f, p.to_y, which).wait_send()
            seq_copy(2, j, p.f_y, p.to_core, which).wait_send()
        return 0

    lax.fori_loop(0, npiece, spread_sends, 0)
    red.wait_sends()
    pending = []
    width = FFN_COLS
    chunks = ffn_chunks(gate_sh.shape[1])
    nb = len(p.bits)
    blk = gate_sh.shape[0]

    def early_copy(i):
        mask = 1 + sum(p.bits[1 + t] for t in range(nb - 1) if i >> (nb - 2 - t) & 1)
        return rcopy(
            gw_gate.at[pl.ds(al(p.at(mask) * blk, blk), blk), pl.ds(0, width)],
            rx_o.at[i],
            pss.at[i],
            prs.at[i],
            p.to_dp(1),
        )

    for n_chunk, ((c0, cw), some) in enumerate(zip(chunks, i_ffn)):
        g.need(some[-1], GATHER_AHEAD)
        for i in some:
            own_copies[i].wait()
            g.wait_last(i)
        cols = pl.ds(c0, cw)
        loads = [
            pltpu.make_async_copy(w.at[:, cols], seq_v.at[:, pl.ds(n * width, cw)], ffn_ls.at[n])
            for n, w in enumerate((gate_all, up_all, down_all))
        ]
        for c in loads:
            c.start()
        for c in pending:
            c.wait()
        if n_chunk == len(chunks) - 1:
            for i in range(ndp // 2):
                early_copy(i).start()
        for c in loads:
            c.wait()
        gate_c, up_c, down_c = (slice(n * width, n * width + cw) for n in range(3))

        def both(t, _):
            rr = pl.ds(al(t * 256, 256), 256)
            gate = mm(n2_v[rr, :], seq_v[:, gate_c])
            up = mm(n2_v[rr, :], seq_v[:, up_c])
            grad_hidden = mm(d_v[rr, :], seq_v[:, down_c])
            sig = 1.0 / (1.0 + jnp.exp(-gate))
            act = gate * sig
            mixed_v[rr, :cw] = (act * up).astype(BF16)
            q_v[rr, gate_c] = (grad_hidden * up * (sig * (1.0 + gate * (1.0 - sig)))).astype(BF16)
            q_v[rr, up_c] = (grad_hidden * act).astype(BF16)
            return 0

        for lo in range(0, rows // 256, 2):
            lax.fori_loop(lo, lo + 2, both, 0)
            tick(1)
        pending = [
            pltpu.make_async_copy(src, dst.at[:, cols], ffn_ls.at[3 + n])
            for n, (src, dst) in enumerate(
                (
                    (mixed_v.at[:, pl.ds(0, cw)], hid_o),
                    (q_v.at[:, pl.ds(0, cw)], gg_o),
                    (q_v.at[:, pl.ds(width, cw)], gu_o),
                )
            )
        ]
        for c in pending:
            c.start()

        half_rows = part_v.shape[0] // 256
        for lo in range(0, dim // 256, half_rows):

            def weight_grads(j, _):
                rr = pl.ds(al(j * 256, 256), 256)
                pr = pl.ds(al((j - lo) * 256, 256), 256)
                pc = slice((lo // half_rows) * width, (lo // half_rows) * width + cw)
                out_v[rr, gate_c] = mm(n2_t[rr, :], q_v[:, gate_c]).astype(BF16)
                out_v[rr, up_c] = mm(n2_t[rr, :], q_v[:, up_c]).astype(BF16)
                part_v[pr, pc] = mm(d_t[rr, :], mixed_v[:, :cw]).astype(BF16)
                return 0

            lax.fori_loop(lo, min(dim // 256, lo + half_rows), weight_grads, 0)
            tick(1)
        saves = [
            pltpu.make_async_copy(out_v.at[:, pl.ds(0, cw)], gw_gate.at[:, cols], ffn_ls.at[6]),
            pltpu.make_async_copy(out_v.at[:, pl.ds(width, cw)], gw_up.at[:, cols], ffn_ls.at[7]),
        ]
        prow = part_v.shape[0]
        for n in range(dim // prow):
            saves.append(
                pltpu.make_async_copy(
                    part_v.at[:, pl.ds(n * width, cw)],
                    gw_down.at[pl.ds(n * prow, prow), cols],
                    ffn_ls.at[8 + n],
                )
            )
        for c in saves:
            c.start()
        pending = pending + saves
    for c in pending:
        c.wait()
    tick(2 * len(g.items))
    for i in range(ndp // 2):
        early_copy(i).wait_recv()
        early_copy(i).wait_send()
    for i in order:
        if i not in early:
            g.wait_sends(i)
    for t in (fs_d, fs_l, fs_n):
        t.wait_sends()
    for c in (qb_out, lkv_out):
        c.wait()


def forward_call(ndp, tok, dout, cos, sin, bias, seq_sh, gain_sh, qb, out, gate, up, down):
    own = tok.shape[0] * tok.shape[1]
    dim = tok.shape[2]
    rank = qb.shape[0] * ndp
    hd = (seq_sh.shape[1] - rank) // 2
    heads = qb.shape[1] // hd
    rows = NF * own
    kvw = seq_sh.shape[1]
    n_items = 2 + sum(w.shape[0] // min(w.shape[0], GATHER_ROWS) for w in (qb, out))
    n_items += sum(w.shape[0] // min(w.shape[0], FFN_ROWS) for w in (gate, up, down)) * len(
        ffn_chunks(gate.shape[1])
    )

    def sds(shape, dtype=BF16):
        return jax.ShapeDtypeStruct(shape, dtype)

    full = lambda w: sds((w.shape[0] * ndp, w.shape[1]))
    out_shape = (
        full(qb),
        full(out),
        full(gate),
        full(up),
        full(down),
        sds((seq_sh.shape[0] * ndp * NF, kvw)),
        sds(gain_sh.shape, F32),
        sds((rows, kvw)),
        sds((rows, heads * hd)),
        sds((rows, heads * hd)),
        sds((own, rank), F32),
        sds((own, dim)),
        sds((own, dim), F32),
        sds((rows, gate.shape[1])),
        sds((rows, gate.shape[1])),
        sds((rows, gate.shape[1])),
        full(gate),
        full(up),
        full(down),
        sds((ndp // 2, gate.shape[0], FFN_COLS)),
    )
    out_specs = (ANY,) * 6 + (VMEM,) + (ANY,) * 3 + (VMEM,) * 3 + (ANY,) * 7
    dma = pltpu.SemaphoreType.DMA
    scratch = [
        pltpu.VMEM((seq_sh.shape[0] * ndp * NF, kvw), BF16),
        pltpu.VMEM((ndp * NF,) + gain_sh.shape, F32),
        pltpu.VMEM((qb.shape[0] * ndp, qb.shape[1]), BF16),
        pltpu.VMEM((out.shape[0] * ndp, out.shape[1]), BF16),
        pltpu.VMEM((rows, kvw), BF16),
        pltpu.VMEM((rows, heads * hd), BF16),
        pltpu.VMEM((rows, heads * hd), BF16),
        pltpu.VMEM((rows, dim), BF16),
        pltpu.VMEM((2, own, dim), BF16),
        pltpu.VMEM((own, dim), BF16),
        pltpu.VMEM((rows, dim), BF16),
        pltpu.VMEM((rows, dim), BF16),
        pltpu.VMEM((dim, rows), BF16),
        pltpu.VMEM((dim, rows), BF16),
        pltpu.VMEM((own, kvw), F32),
        dma((n_items, ndp - 1)),
        dma((n_items, ndp - 1)),
        dma((4, 3)),
        dma((4, 3)),
        dma((2, 3, ndp)),
        dma((2, 3, ndp)),
        dma((n_items + 10,)),
        dma((10,)),
        dma((ndp // 2,)),
        dma((ndp // 2,)),
    ]
    return pl.pallas_call(
        functools.partial(forward_kernel, (ndp, own, dim, rank, hd, heads)),
        out_shape=out_shape,
        in_specs=(VMEM,) * 5 + (ANY,) * 7,
        out_specs=out_specs,
        scratch_shapes=scratch,
        compiler_params=pltpu.CompilerParams(
            collective_id=0, has_side_effects=True, vmem_limit_bytes=60 * 2**20
        ),
        name="gather_forward",
    )(tok, dout, cos, sin, bias, seq_sh, gain_sh, qb, out, gate, up, down)


class DpScatter:
    PER_TICK = 1

    def __init__(self, pos, count, first, later, own, acc, ss, rs, ls, credit, pls):
        self.p, self.count = pos, count
        self.n = len(pos.bits)
        self.SLOTS, self.AHEAD, self.OWN = scatter_ring(pos.ndp // 2)
        self.first, self.later, self.own, self.acc = first, later, own, acc
        self.ss, self.rs, self.ls, self.credit, self.pls = ss, rs, ls, credit, pls
        self.items = []
        self.started = self.stepped = 0

    def order(self, n):
        return self.p.orders(False)

    def width(self, stage):
        return 1 << (self.n - 1 - stage)

    def make(self, src, base, out, pieces, c0=0, cols=None, pre=None):
        rows = out.shape[0]
        cols = out.shape[1] if cols is None else cols
        r = rows // pieces
        return [(src, base, out, rows, cols, c * r, r, c0, pre) for c in range(pieces)]

    def add(self, *args):
        self.items += self.make(*args)
        self.pump()

    def mask(self, n, i):
        order = self.order(n)
        return sum(order[1 + t] for t in range(self.n - 1) if i >> (self.n - 2 - t) & 1)

    def block(self, n, mask):
        src, base, out, rows, cols, r0, r, c0, pre = self.items[n]
        return src.at[pl.ds(al(base + self.p.at(mask) * rows + r0, r), r), pl.ds(c0, cols)]

    def place(self, buf, n, lo, size):
        src, base, out, rows, cols, r0, r, c0, pre = self.items[n]
        return buf.at[n % self.SLOTS, pl.ds(lo, size), pl.ds(0, r), pl.ds(0, cols)]

    def copies(self, n, stage):
        bit = self.order(n)[stage]
        dev = self.p.to_dp(bit)
        s = n % self.SLOTS
        if stage == 0:
            return [
                rcopy(
                    self.block(n, bit | self.mask(n, i)),
                    self.place(self.first, n, i, 1).at[0],
                    self.ss.at[s, i],
                    self.rs.at[s, i],
                    dev,
                )
                for i in range(self.width(0))
            ]
        w = self.width(stage)
        k = self.width(0) + stage - 1
        return [
            rcopy(
                self.place(self.first, n, w, w),
                self.place(self.later, n, w - 1, w),
                self.ss.at[s, k],
                self.rs.at[s, k],
                dev,
            )
        ]

    def owncopy(self, n, i):
        src, base, out, rows, cols, r0, r, c0, pre = self.items[n]
        s = n % self.OWN
        return pltpu.make_async_copy(
            self.block(n, self.mask(n, i)),
            self.own.at[s, i, pl.ds(0, r), pl.ds(0, cols)],
            self.ls.at[s, i],
        )

    def outcopy(self, n):
        src, base, out, rows, cols, r0, r, c0, pre = self.items[n]
        s = n % self.SLOTS
        return pltpu.make_async_copy(
            self.acc.at[s, pl.ds(0, r), pl.ds(0, cols)],
            out.at[pl.ds(r0, r), pl.ds(c0, cols)],
            self.ls.at[s, self.width(0)],
        )

    def free(self, n, stage):
        m = n + self.SLOTS
        if m < self.count and not (stage == 0 and self.given(m)):
            bit = self.order(m)[stage]
            pl.semaphore_signal(
                self.credit.at[stage, self.p.bits.index(bit)],
                inc=1,
                device_id=self.p.to_dp(bit),
                device_id_type=MESH,
            )

    def given(self, n):
        return n < len(self.items) and self.items[n][-1] is not None

    def precopy(self, n, i):
        src, base, out, rows, cols, r0, r, c0, pre = self.items[n]
        s = n % self.SLOTS
        return pltpu.make_async_copy(
            pre.at[i, pl.ds(r0, r)], self.place(self.first, n, i, 1).at[0], self.pls.at[s, i]
        )

    def send(self, n, stage):
        if stage == 0 and self.given(n):
            for i in range(self.width(0)):
                self.precopy(n, i).start()
            return
        bit = self.order(n)[stage]
        if n >= self.SLOTS:
            pl.semaphore_wait(self.credit.at[stage, self.p.bits.index(bit)], 1)
        for c in self.copies(n, stage):
            c.start()

    def pump(self):
        while self.started < min(len(self.items), self.stepped + self.AHEAD):
            n = self.started
            self.send(n, 0)
            for i in range(self.width(0)):
                self.owncopy(n, i).start()
            self.started += 1

    def tick(self, steps=1):
        for _ in range(self.PER_TICK * steps):
            n = self.stepped
            if n >= self.started:
                return
            self.combine(n, 0)
            self.stepped += 1
            self.pump()
            for stage in range(1, self.n):
                if n >= stage:
                    self.combine(n - stage, stage)

    def combine(self, n, stage):
        src, base, out, rows, cols, r0, r, c0, pre = self.items[n]
        s, tile = n % self.SLOTS, 16
        w = self.width(stage)
        if stage == 0 and pre is not None:
            for i in range(w):
                self.precopy(n, i).wait()
        else:
            for c in self.copies(n, stage):
                c.wait_recv()
        if stage == 0:
            for i in range(w):
                self.owncopy(n, i).wait()
        else:
            for c in self.copies(n, stage):
                c.wait_send()
        last = stage == self.n - 1

        def add(lo, size):
            def one(t, _):
                t = pl.ds(al(t * tile, tile), tile)
                for i in range(lo, lo + size):
                    a = self.first[s, i, t, :cols]
                    b = self.own[n % self.OWN, i, t, :cols] if stage == 0 else self.later[s, w - 1 + i, t, :cols]
                    if last:
                        self.acc[s, t, :cols] = a.astype(F32) + b.astype(F32)
                    else:
                        self.first[s, i, t, :cols] = a + b
                return 0

            lax.fori_loop(0, r // tile, one, 0)

        if last:
            if n >= self.SLOTS:
                self.outcopy(n - self.SLOTS).wait()
            if pre is None:
                for c in self.copies(n, 0):
                    c.wait_send()
            add(0, 1)
            self.outcopy(n).start()
            for t in range(self.n):
                self.free(n, t)
        else:
            half = w // 2
            add(half, half)
            self.send(n, stage + 1)
            add(0, half)

    def drain(self):
        self.tick(self.count)
        for n in range(self.count, self.count + self.n - 1):
            for stage in range(1, self.n):
                if 0 <= n - stage < self.count:
                    self.combine(n - stage, stage)
        for n in range(max(0, self.count - self.SLOTS), self.count):
            self.outcopy(n).wait()


def scatter_ring(nz):
    return (10, 6, 7) if nz * max(16, 128 // nz) <= 128 else (5, 2, 3)


def piece_rows(rows, nz):
    return min(rows, max(16, 128 // nz))


def backward_kernel(
    cfg,
    tok,
    dout,
    middle,
    latent,
    normed,
    gains,
    cos,
    sin,
    bias,
    gw_gate,
    gw_up,
    gw_down,
    hid_h,
    gg_h,
    gu_h,
    gate_h,
    up_h,
    down_h,
    rx_h,
    lkv_h,
    q_h,
    mixed_h,
    qb_h,
    out_h,
    seq_h,
    o_gate,
    o_up,
    o_down,
    o_out,
    o_qb,
    o_seq,
    o_gain,
    o_in,
    o_y,
    fcore_v,
    fy_v,
    proj_v,
    gmid_v,
    gnorm_v,
    lkv_v,
    q_v,
    mixed_v,
    gm_v,
    kv_acc,
    qb_v,
    out_v,
    seq_v,
    gall_v,
    gain_rx,
    gain_acc,
    first_b,
    later_b,
    own_b,
    acc_b,
    dss,
    drs,
    dls,
    credit,
    pls,
    fss,
    frs,
    gs,
    gr,
    ls,
    tls,
):
    ndp, own, dim, rank, hd, heads, pieces = cfg
    rows = NF * own
    t2 = own // 2
    kvw = rank + 2 * hd
    wide = dim // rank
    p = Place(ndp)
    sr = o_seq.shape[0]
    local = []

    def local_copy(src, dst):
        c = pltpu.make_async_copy(src, dst, ls.at[len(local)])
        c.start()
        local.append(c)
        return c

    ff = gg_h.shape[1]
    ffc = pl.ds(0, ff)
    gg_in = local_copy(gg_h, lkv_v.at[:, ffc])
    gu_in = local_copy(gu_h, seq_v.at[pl.ds(0, rows), ffc])
    mixed_in = local_copy(mixed_h, mixed_v)
    q_in = local_copy(q_h, q_v)
    qb_in = local_copy(qb_h, qb_v)
    hh = out_v.shape[1]

    def tile_load(t, which):
        src = gate_h if which == 0 else up_h
        s = lax.rem(t, 2) * 2 + which
        return pltpu.make_async_copy(
            src.at[pl.ds(al(t * 256, 256), 256)],
            seq_v.at[pl.ds(al(rows + s * 256, 256), 256), ffc],
            tls.at[s],
        )

    for which in (0, 1):
        tile_load(0, which).start()
    sc = DpScatter(p, sum(pieces) + pieces[0], first_b, later_b, own_b, acc_b, dss, drs, dls, credit, pls)
    p.barrier()
    cut = rx_h.shape[2]
    ready = sc.make(gw_gate, 0, o_gate, pieces[0], 0, cut, rx_h)
    fresh = sc.make(gw_up, 0, o_up, pieces[1])
    for a, b in zip(fresh, ready):
        sc.items += [a, b]
    sc.add(gw_gate, 0, o_gate, pieces[0], cut, o_gate.shape[1] - cut)
    sc.add(gw_down, 0, o_down, pieces[2])
    gg_in.wait()
    gu_in.wait()
    n_tiles = dim // 256
    per_half = hh // 256

    def norm_grad(t, _):
        for which in (0, 1):
            tile_load(t, which).wait()

        @pl.when(t + 1 < n_tiles)
        def _():
            for which in (0, 1):
                tile_load(t + 1, which).start()

        s = lax.rem(t, 2) * 2
        wg = seq_v[pl.ds(al(rows + s * 256, 256), 256), ffc]
        wu = seq_v[pl.ds(al(rows + s * 256 + 256, 256), 256), ffc]
        cols = pl.ds(al(lax.rem(t, per_half) * 256, 256), 256)
        for r in range(rows // 256):
            rr = pl.ds(r * 256, 256)
            to = pl.ds(al((t // per_half) * rows + r * 256, 256), 256)
            out_v[to, cols] = (
                mm_nt(lkv_v[rr, ffc], wg) + mm_nt(seq_v[rr, ffc], wu)
            ).astype(BF16)
        return 0

    halves = []
    for h in range(dim // hh):
        wide_cols = pl.ds(h * hh, hh)
        lax.fori_loop(h * per_half, (h + 1) * per_half, norm_grad, 0)
        red = FsReduce(
            p,
            lambda b, h=h: out_v.at[pl.ds(al(h * rows + b * own, own), own)],
            fcore_v.at[:, :, wide_cols],
            fy_v.at[:, wide_cols],
            fss.at[4 * h],
            frs.at[4 * h],
        )
        red.start()
        if h > 0:
            halves[-1].mid(own)
        sc.tick(2)
        halves.append(red)
    lkv_in = local_copy(lkv_h, lkv_v)
    seq_in = local_copy(seq_h, seq_v)
    halves[-1].mid(own)
    sc.tick(4)
    for red in halves:
        red.end()
        red.wait_sends()
    gain_two = jnp.concatenate([gains[wide + r : wide + r + 1] for r in range(wide)], axis=1)
    gain_one = jnp.concatenate([gains[r : r + 1] for r in range(wide)], axis=1)
    gain_lat = gains[2 * wide : 2 * wide + 1]
    part_two = jnp.zeros((1, dim), F32)
    for m in range(2):
        rr = pl.ds(m * t2, t2)
        e = jnp.concatenate([red.value(rr) for red in halves], axis=1)
        v = middle[rr, :]
        inv = lax.rsqrt(jnp.mean(v * v, axis=-1, keepdims=True) + EPSILON)
        part_two += jnp.sum(e * v * inv, axis=0, keepdims=True)
        scaled = e * gain_two
        inner = jnp.mean(scaled * v, axis=-1, keepdims=True)
        g = dout[m].astype(F32) + inv * scaled - v * (inv * inv * inv * inner)
        gmid_v[rr, :] = g
        proj_v[pl.ds(al(p.f * own + m * t2, t2), t2), :] = g.astype(BF16)
    out_in = local_copy(out_h, out_v)
    gain_acc[0] = jnp.zeros(gain_acc.shape[1:], F32)
    for r in range(wide):
        gain_acc[0, pl.ds(wide + r, 1), :] = part_two[:, r * rank : (r + 1) * rank]
    ag = FsGather(p, lambda b: proj_v.at[pl.ds(al(b * own, own), own)], fss.at[1], frs.at[1])
    ag.start()
    sc.tick(4)
    ag.mid()
    sc.tick(2)
    out_in.wait()
    ag.end()
    ag.wait_sends()

    def back_out(j, _):
        cols = pl.ds(al(j * 256, 256), 256)
        for r in range(rows // 512):
            rr = pl.ds(r * 512, 512)
            gm_v[rr, cols] = mm(proj_v[rr, :], out_v[:, cols]).astype(BF16)
        return 0

    lax.fori_loop(0, heads * hd // 256, back_out, 0)
    sc.tick(2)
    mixed_in.wait()

    def grad_out(j, _):
        cols = pl.ds(al(j * 256, 256), 256)
        out_v[cols, :] = mm_tn(proj_v[:, cols], mixed_v[...]).astype(BF16)
        return 0

    lax.fori_loop(0, dim // 256, grad_out, 0)
    sc.tick(2)
    sc.add(out_v, 0, o_out, pieces[3])
    q_in.wait()
    lkv_in.wait()
    scale = hd ** (-0.5)
    half = hd // 2
    kcols, vcols = slice(rank, rank + hd), slice(rank + hd, rank + 2 * hd)
    causal = causal_bias(PROMPT)
    everything = slice(None)

    for m in range(2):
        k0, k1 = (group_rows(lkv_v, m, h2, kcols, own) for h2 in (0, 1))
        v0, v1 = (group_rows(lkv_v, m, h2, vcols, own) for h2 in (0, 1))
        low = bias[m]
        kv_acc[...] = jnp.zeros(kv_acc.shape, F32)

        def put_query(h, which, g):
            co = group_rows(cos, m, which, everything, own)
            si = group_rows(sin, m, which, everything, own)
            a, b = g[:, :half] * scale, g[:, half:] * scale
            c0 = pl.ds(al(h * hd, half), half)
            c1 = pl.ds(al(h * hd + half, half), half)
            put_rows(gm_v, m, which, c0, own, (a * co + b * si).astype(BF16))
            put_rows(gm_v, m, which, c1, own, (b * co - a * si).astype(BF16))

        def attend_back(h, _):
            cols = pl.ds(al(h * hd, hd), hd)
            q0 = group_rows(q_v, m, 0, cols, own)
            g0 = group_rows(gm_v, m, 0, cols, own)
            pr = softmax_parts(mm_nt(q0, k0) * scale + causal)
            gp = mm_nt(g0, v0)
            gsc = (pr * (gp - jnp.sum(pr * gp, axis=-1, keepdims=True))).astype(BF16)
            kv_acc[2] += mm_tn(pr.astype(BF16), g0)
            kv_acc[0] += mm_tn(gsc, q0)
            put_query(h, 0, mm(gsc, k0))
            q1 = group_rows(q_v, m, 1, cols, own)
            g1 = group_rows(gm_v, m, 1, cols, own)
            s0 = mm_nt(q1, k0) * scale
            s1 = mm_nt(q1, k1) * scale + low
            top = jnp.maximum(
                jnp.max(s0, axis=-1, keepdims=True), jnp.max(s1, axis=-1, keepdims=True)
            )
            e0, e1 = jnp.exp(s0 - top), jnp.exp(s1 - top)
            total = jnp.sum(e0, axis=-1, keepdims=True) + jnp.sum(e1, axis=-1, keepdims=True)
            p0, p1 = e0 / total, e1 / total
            gp0, gp1 = mm_nt(g1, v0), mm_nt(g1, v1)
            inner = jnp.sum(p0 * gp0, axis=-1, keepdims=True) + jnp.sum(
                p1 * gp1, axis=-1, keepdims=True
            )
            gs0 = (p0 * (gp0 - inner)).astype(BF16)
            gs1 = (p1 * (gp1 - inner)).astype(BF16)
            kv_acc[2] += mm_tn(p0.astype(BF16), g1)
            kv_acc[3] += mm_tn(p1.astype(BF16), g1)
            kv_acc[0] += mm_tn(gs0, q1)
            kv_acc[1] += mm_tn(gs1, q1)
            put_query(h, 1, mm(gs0, k0) + mm(gs1, k1))
            return 0

        lax.fori_loop(0, heads, attend_back, 0)
        for h2 in (0, 1):
            put_rows(proj_v, m, h2, kcols, own, (kv_acc[h2] * scale).astype(BF16))
            put_rows(proj_v, m, h2, vcols, own, kv_acc[2 + h2].astype(BF16))
        sc.tick(4)
    qb_in.wait()

    def back_latent(j, _):
        wr = pl.ds(al(j * 256, 256), 256)
        for r in range(rows // 512):
            rr = pl.ds(r * 512, 512)
            proj_v[rr, wr] = mm_nt(gm_v[rr, :], qb_v[wr, :]).astype(BF16)
        return 0

    lax.fori_loop(0, rank // 256, back_latent, 0)

    def grad_qb(j, _):
        cols = pl.ds(al(j * 256, 256), 256)
        qb_v[cols, :] = mm_tn(lkv_v[:, cols], gm_v[...]).astype(BF16)
        return 0

    lax.fori_loop(0, rank // 256, grad_qb, 0)
    narrow = pl.ds(0, kvw)
    red2 = FsReduce(
        p,
        lambda b: proj_v.at[pl.ds(al(b * own, own), own), narrow],
        fcore_v.at[:, :, narrow],
        fy_v.at[:, narrow],
        fss.at[2],
        frs.at[2],
    )
    red2.start()
    sc.tick(2)
    sc.add(qb_v, 0, o_qb, pieces[4])
    red2.mid(own)
    sc.tick(5)
    red2.end()
    red2.wait_sends()
    own_rows = pl.ds(al(p.f * own, own), own)
    part_lat = jnp.zeros((1, rank), F32)
    for m in range(2):
        rr = pl.ds(m * t2, t2)
        gr_rows = pl.ds(al(p.f * own + m * t2, t2), t2)
        e = red2.value(rr)
        v = latent[rr, :]
        inv = lax.rsqrt(jnp.mean(v * v, axis=-1, keepdims=True) + EPSILON)
        el = e[:, :rank]
        part_lat += jnp.sum(el * v * inv, axis=0, keepdims=True)
        scaled = el * gain_lat
        inner = jnp.mean(scaled * v, axis=-1, keepdims=True)
        gall_v[rr, :rank] = (inv * scaled - v * (inv * inv * inv * inner)).astype(BF16)
        co, si = cos[gr_rows, :], sin[gr_rows, :]
        a, b = e[:, rank : rank + half], e[:, rank + half : rank + hd]
        gall_v[rr, rank : rank + half] = (a * co + b * si).astype(BF16)
        gall_v[rr, rank + half : rank + hd] = (b * co - a * si).astype(BF16)
        gall_v[rr, rank + hd :] = e[:, rank + hd :].astype(BF16)
    gain_acc[0, pl.ds(2 * wide, 1), :] = part_lat
    seq_in.wait()

    def back_seq(j, _):
        wr = pl.ds(al(j * 256, 256), 256)
        gnorm_v[:, wr] = mm_nt(gall_v[...], seq_v[wr, :])
        return 0

    lax.fori_loop(0, dim // 256, back_seq, 0)
    sc.tick(2)
    span = NF * sr

    def grad_seq(j, _):
        cols = pl.ds(al(j * 256, 256), 256)
        g = mm_tn(normed[:, cols], gall_v[...]).astype(BF16)
        for i in range(256 // span):
            for fb in range(NF):
                seq_v[pl.ds(al(fb * ndp * sr + (j * (256 // span) + i) * sr, sr), sr), :] = g[
                    i * span + fb * sr : i * span + (fb + 1) * sr
                ]
        return 0

    lax.fori_loop(0, dim // 256, grad_seq, 0)
    srows = ndp * sr
    core3 = [lkv_v.at[pl.ds(0, srows)], lkv_v.at[pl.ds(srows, srows)]]

    def sblock(b):
        return seq_v.at[pl.ds(al(b * srows, srows), srows)]

    c1 = rcopy(sblock(p.f_yc), core3[1], fss.at[3, 1], frs.at[3, 1], p.to_core)
    c0 = rcopy(sblock(p.f_core), core3[0], fss.at[3, 0], frs.at[3, 0], p.to_core)
    mw = mixed_v.shape[1]
    cys = [
        rcopy(
            lkv_v.at[pl.ds(srows, srows), pl.ds(0, mw)],
            mixed_v.at[pl.ds(0, srows)],
            fss.at[3, 2],
            frs.at[3, 2],
            p.to_y,
        ),
        rcopy(
            lkv_v.at[pl.ds(srows, srows), pl.ds(mw, kvw - mw)],
            mixed_v.at[pl.ds(srows, srows), pl.ds(0, kvw - mw)],
            fss.at[3, 3],
            frs.at[3, 3],
            p.to_y,
        ),
    ]
    c1.start()
    c0.start()
    part_one = jnp.zeros((1, dim), F32)
    for m in range(2):
        rr = pl.ds(m * t2, t2)
        e = gnorm_v[rr, :]
        v = tok[m].astype(F32)
        inv = lax.rsqrt(jnp.mean(v * v, axis=-1, keepdims=True) + EPSILON)
        part_one += jnp.sum(e * v * inv, axis=0, keepdims=True)
        scaled = e * gain_one
        inner = jnp.mean(scaled * v, axis=-1, keepdims=True)
        o_in[m] = (gmid_v[rr, :] + inv * scaled - v * (inv * inv * inv * inner)).astype(BF16)
    for r in range(wide):
        gain_acc[0, pl.ds(r, 1), :] = part_one[:, r * rank : (r + 1) * rank]
    gain_steps = [
        rcopy(gain_acc.at[0], gain_rx.at[0], gs.at[0], gr.at[0], p.to_core),
        rcopy(gain_acc.at[1], gain_rx.at[1], gs.at[1], gr.at[1], p.to_y),
    ] + [
        rcopy(gain_acc.at[2 + b], gain_rx.at[2 + b], gs.at[2 + b], gr.at[2 + b], p.to_dp(bit))
        for b, bit in enumerate(p.bits)
    ]
    gain_steps[0].start()
    c1.wait_recv()

    def seq_y(t, _):
        t = al(t * 64, 64)
        a = pl.ds(srows + t, 64)
        b = pl.ds(al(p.f_y * srows + t, 64), 64)
        lkv_v[a, :] = lkv_v[a, :] + seq_v[b, :]
        return 0

    lax.fori_loop(0, srows // 64, seq_y, 0)
    for c in cys:
        c.start()
    for n in range(len(gain_steps)):
        gain_steps[n].wait_recv()
        gain_acc[n + 1] = gain_acc[n] + gain_rx[n]
        if n + 1 < len(gain_steps):
            gain_steps[n + 1].start()
        sc.tick(1)
    c0.wait_recv()
    for c in cys:
        c.wait_recv()

    def seq_f(t, _):
        t = al(t * 64, 64)
        a = pl.ds(t, 64)
        b = pl.ds(al(p.f * srows + t, 64), 64)
        a2 = pl.ds(srows + t, 64)
        seq_v[b, :mw] = (
            lkv_v[a, :mw].astype(F32) + seq_v[b, :mw].astype(F32) + mixed_v[a, :].astype(F32)
        ).astype(BF16)
        seq_v[b, mw:] = (
            lkv_v[a, mw:].astype(F32)
            + seq_v[b, mw:].astype(F32)
            + mixed_v[a2, : kvw - mw].astype(F32)
        ).astype(BF16)
        return 0

    lax.fori_loop(0, srows // 64, seq_f, 0)
    sc.add(seq_v, p.f * srows, o_seq, pieces[5])
    o_gain[...] = gain_acc[len(gain_steps)]
    for t in [c1, c0] + cys:
        t.wait_send()
    hid_in = local_copy(hid_h, lkv_v.at[:, ffc])

    def down_load(t):
        s = lax.rem(t, 2)
        return pltpu.make_async_copy(
            down_h.at[pl.ds(al(t * 256, 256), 256)],
            seq_v.at[pl.ds(al(p.f_core * srows + s * 256, 256), 256), ffc],
            tls.at[s],
        )

    down_load(0).start()
    sc.tick(2)
    hid_in.wait()

    def ffn_out(t, _):
        down_load(t).wait()

        @pl.when(t + 1 < n_tiles)
        def _():
            down_load(t + 1).start()

        w = seq_v[pl.ds(al(p.f_core * srows + lax.rem(t, 2) * 256, 256), 256), ffc]
        cols = pl.ds(al(t * 256, 256), 256)
        for r in range(rows // 256):
            rr = pl.ds(r * 256, 256)
            proj_v[rr, cols] = mm_nt(lkv_v[rr, ffc], w).astype(BF16)
        return 0

    lax.fori_loop(0, n_tiles, ffn_out, 0)
    red3 = FsReduce(
        p,
        lambda b: proj_v.at[pl.ds(al(b * own, own), own)],
        fcore_v,
        fy_v,
        fss.at[5],
        frs.at[5],
    )
    red3.start()
    sc.tick(2)
    red3.mid(own)
    sc.tick(5)
    red3.end()
    for m in range(2):
        rr = pl.ds(m * t2, t2)
        o_y[m] = (middle[rr, :] + red3.value(rr)).astype(BF16)
    sc.drain()
    red3.wait_sends()
    for t in gain_steps:
        t.wait_send()


def backward_call(ndp, tok, dout, middle, latent, normed, gains, cos, sin, bias, grads, ffn, saved):
    lkv, q, mixed, qb, out, seq = saved
    nz = ndp // 2
    own, dim = middle.shape
    rank = latent.shape[1]
    kvw = lkv.shape[1]
    hd = (kvw - rank) // 2
    heads = q.shape[1] // hd
    rows = NF * own
    sr = seq.shape[0] // (ndp * NF)
    shards = [(w.shape[0] // ndp, w.shape[1]) for w in grads] + [
        (out.shape[0] // ndp, out.shape[1]),
        (qb.shape[0] // ndp, qb.shape[1]),
        (sr, kvw),
    ]
    pieces = tuple(s[0] // piece_rows(s[0], nz) for s in shards)
    n = sum(pieces)
    slots, _, own_slots = scatter_ring(nz)
    nb = ndp.bit_length() - 1
    pr = max(piece_rows(s[0], nz) for s in shards)
    width = max(s[1] for s in shards)
    dma = pltpu.SemaphoreType.DMA
    scratch = [
        pltpu.VMEM((2, own, dim), BF16),
        pltpu.VMEM((own, dim), BF16),
        pltpu.VMEM((rows, dim), BF16),
        pltpu.VMEM((own, dim), F32),
        pltpu.VMEM((own, dim), F32),
        pltpu.VMEM(lkv.shape, BF16),
        pltpu.VMEM(q.shape, BF16),
        pltpu.VMEM(mixed.shape, BF16),
        pltpu.VMEM(q.shape, BF16),
        pltpu.VMEM((4, rows // 4, hd), F32),
        pltpu.VMEM(qb.shape, BF16),
        pltpu.VMEM(out.shape, BF16),
        pltpu.VMEM(seq.shape, BF16),
        pltpu.VMEM((own, kvw), BF16),
        pltpu.VMEM((2 + nb,) + gains.shape, F32),
        pltpu.VMEM((3 + nb,) + gains.shape, F32),
        pltpu.VMEM((slots, nz, pr, width), BF16),
        pltpu.VMEM((slots, nz - 1, pr, width), BF16),
        pltpu.VMEM((own_slots, nz, pr, width), BF16),
        pltpu.VMEM((slots, pr, width), F32),
        dma((slots, nz + nb - 1)),
        dma((slots, nz + nb - 1)),
        dma((slots, nz + 1)),
        pltpu.SemaphoreType.REGULAR((nb, nb)),
        dma((slots, nz)),
        dma((6, 4)),
        dma((6, 4)),
        dma((2 + nb,)),
        dma((2 + nb,)),
        dma((9,)),
        dma((4,)),
    ]
    return pl.pallas_call(
        functools.partial(backward_kernel, (ndp, own, dim, rank, hd, heads, pieces)),
        out_shape=tuple(jax.ShapeDtypeStruct(s, F32) for s in shards)
        + (
            jax.ShapeDtypeStruct(gains.shape, F32),
            jax.ShapeDtypeStruct(tok.shape, BF16),
            jax.ShapeDtypeStruct(tok.shape, BF16),
        ),
        in_specs=(VMEM,) * 9 + (ANY,) * 16,
        out_specs=(ANY,) * 6 + (VMEM,) * 3,
        scratch_shapes=scratch,
        compiler_params=pltpu.CompilerParams(
            collective_id=1, has_side_effects=True, vmem_limit_bytes=62 * 2**20
        ),
        name="backward_scatter",
    )(tok, dout, middle, latent, normed, gains, cos, sin, bias, *grads, *ffn, lkv, q, mixed, qb, out, seq)


def per_device(
    ndp,
    tokens,
    membership,
    d_output,
    gain_attn,
    w_qa,
    gain_latent,
    w_qb,
    w_key,
    w_value,
    w_out,
    gain_ffn,
    w_gate,
    w_up,
    w_down,
):
    micro, tlen, dim = tokens.shape
    own = micro * tlen
    rank = w_qa.shape[1]
    hd = w_key.shape[1]
    heads = w_qb.shape[1] // hd
    rows = NF * own
    wide = dim // rank
    labels, positions = jax.vmap(lambda r: layout(r, BLK))(membership[0])
    pos_rows = positions.reshape(micro, NF, tlen).transpose(1, 0, 2).reshape(rows)
    cos, sin = rope_tables(pos_rows, hd)
    tail = labels[:, PROMPT:]
    idx = jnp.arange(tail.shape[1], dtype=jnp.int32)
    seen = (idx[None, None, :] <= idx[None, :, None]) & (tail[:, None, :] == tail[:, :, None])
    bias = jnp.where(seen, 0.0, MASK_FILL).astype(F32)
    block = lax.axis_index("dp") * NF + lax.axis_index("fsdp")

    def spot(gain):
        width = gain.shape[0]
        count = ndp * NF
        at = lax.broadcasted_iota(jnp.int32, (count, width), 0) == block
        placed = jnp.where(at, gain.astype(F32)[None, :], 0.0)
        return placed.reshape(count * width // rank, rank)

    gain_sh = jnp.concatenate([spot(gain_attn), spot(gain_ffn), spot(gain_latent)], axis=0)
    gain_sh = jnp.pad(gain_sh, ((0, 8 - gain_sh.shape[0]), (0, 0)))
    seq_sh = jnp.concatenate([w_qa, w_key, w_value], axis=1)
    (
        qb_all,
        out_all,
        gate_all,
        up_all,
        down_all,
        seq_all,
        gains,
        lkv,
        q_all,
        mixed,
        latent,
        normed,
        middle,
        hidden,
        grad_gate,
        grad_up,
        gw_gate,
        gw_up,
        gw_down,
        early_gate,
    ) = forward_call(
        ndp, tokens, d_output, cos, sin, bias, seq_sh, gain_sh, w_qb, w_out, w_gate, w_up, w_down
    )
    o_gate, o_up, o_down, o_out, o_qb, o_seq, o_gain, input_grad, output = backward_call(
        ndp,
        tokens,
        d_output,
        middle,
        latent,
        normed,
        gains,
        cos,
        sin,
        bias,
        (gw_gate, gw_up, gw_down),
        (hidden, grad_gate, grad_up, gate_all, up_all, down_all, early_gate),
        (lkv, q_all, mixed, qb_all, out_all, seq_all),
    )

    def own_gain(flat, width):
        return lax.dynamic_slice_in_dim(flat.reshape(-1), block * width, width, 0)

    return (
        output,
        input_grad,
        own_gain(o_gain[:wide], gain_attn.shape[0]),
        o_seq[:, :rank],
        own_gain(o_gain[2 * wide], gain_latent.shape[0]),
        o_qb,
        o_seq[:, rank : rank + hd],
        o_seq[:, rank + hd :],
        o_out,
        own_gain(o_gain[wide : 2 * wide], gain_ffn.shape[0]),
        o_gate,
        o_up,
        o_down,
    )


def solution(mesh):
    both = ("dp", "fsdp")
    rowwise, vector = P(both, None), P(both)
    tok = P(None, both, None)
    head = P("dp", "fsdp")
    return jax.shard_map(
        functools.partial(per_device, mesh.shape["dp"]),
        mesh=mesh,
        in_specs=(
            tok,
            P("dp", None, None),
            tok,
            vector,
            rowwise,
            vector,
            head,
            rowwise,
            rowwise,
            head,
            vector,
            head,
            head,
            head,
        ),
        out_specs=(
            tok,
            tok,
            vector,
            rowwise,
            vector,
            head,
            rowwise,
            rowwise,
            head,
            vector,
            head,
            head,
            head,
        ),
        check_vma=False,
    )
```
